32 devices in a mesh: head: 2 (over x), blk: 16 (over z, y, core).
Axes of the slice: x: 2, y: 2, z: 4, core: 2. Of those that a mesh axis runs over, the one named last changes fastest.
Arguments:
- tokens: bfloat16 [8192, 1024], P(('head', 'blk')), may hold values from -6 to 6
- cotangent: bfloat16 [8192, 1024], P(('head', 'blk')), may hold values from -6 to 6
- norm1_gain: float32 [1024], P(('head', 'blk')), may hold values from 0.1 to 1.9
- w_query: float32 [1024, 1024], P(('head', 'blk')), may hold values from -0.1875 to 0.1875
- w_key: float32 [1024, 1024], P(('head', 'blk')), may hold values from -0.1875 to 0.1875
- w_value: float32 [1024, 1024], P(('head', 'blk')), may hold values from -0.1875 to 0.1875
- w_out: float32 [1024, 1024], P(('head', 'blk')), may hold values from -0.75 to 0.75
- norm2_gain: float32 [1024], P(('head', 'blk')), may hold values from 0.1 to 1.9
- w_gate: float32 [1024, 4096], P(('head', 'blk')), may hold values from -0.1875 to 0.1875
- w_up: float32 [1024, 4096], P(('head', 'blk')), may hold values from -0.1875 to 0.1875
- w_down: float32 [4096, 1024], P(('head', 'blk')), may hold values from -0.09375 to 0.09375
- block_anchor: int32 [64], replicated, may hold values from 0 to 63, each once
- seq_lengths: int32 [8], replicated, may hold values from 1 to 4096, 8192 in all
Outputs:
- output: bfloat16 [8192, 1024], P(('head', 'blk'))
- tokens_grad: bfloat16 [8192, 1024], P(('head', 'blk'))
- norm1_gain_grad: float32 [1024], P(('head', 'blk'))
- w_query_grad: float32 [1024, 1024], P(('head', 'blk'))
- w_key_grad: float32 [1024, 1024], P(('head', 'blk'))
- w_value_grad: float32 [1024, 1024], P(('head', 'blk'))
- w_out_grad: float32 [1024, 1024], P(('head', 'blk'))
- norm2_gain_grad: float32 [1024], P(('head', 'blk'))
- w_gate_grad: float32 [1024, 4096], P(('head', 'blk'))
- w_up_grad: float32 [1024, 4096], P(('head', 'blk'))
- w_down_grad: float32 [4096, 1024], P(('head', 'blk'))
The draws below stay inside these ranges and needn't reach their ends.
Inputs may be any that keep to these rules, and one draw needn't show every extreme that they name: `block_anchor`: a permutation of the 64 blocks. `seq_lengths`: they sum to 8192; the longest is exactly 4096.
All inputs are finite; a program needn't handle non-finite values.
Results may differ from the reference program's by a relative error of at most 0.04.
Values may be sent and summed in bfloat16 or wider, within the bound.
A program may use at most 384 MiB of HBM per device.

```python
import math
import jax
import jax.numpy as jnp
import numpy as np
from jax import lax

D = 1024
HEADS = 16
HEAD_DIM = 64
FF = 4096
BLOCK = 128
TOKENS = 8192
NBLOCKS = 64
LONGEST = 4096
NSEQ = 8


def levels(stream_key, dims, shards, smallest, top_value):
    factor_of = 1.0
    for dim, shards_of in shards:
        draws = jax.random.uniform(jax.random.fold_in(jax.random.fold_in(stream_key, 6), dim), (shards_of,), jnp.float32, smallest / len(shards), top_value / len(shards))
        factor_of = factor_of * jnp.repeat(jnp.exp(draws), dims[dim] // shards_of).reshape((-1,) + (1,) * (len(dims) - 1 - dim))
    return factor_of


def length_profile(number_of, total, most, skew):
    loads = [(1 << 20) // math.isqrt(rank ** skew) + 1 for rank in range(2, number_of + 1)]
    surplus, holding = total - most - (number_of - 1), [1] * (number_of - 1)
    while surplus > 0:
        candidates = [i for i in range(number_of - 1) if holding[i] < most]
        pool, remaining = sum([loads[i] for i in candidates]), surplus
        for i in candidates:
            extra = min(most - holding[i], max(1, remaining * loads[i] // pool), surplus)
            holding[i] = holding[i] + extra
            surplus = surplus - extra
    return np.array([most] + holding)


def uneven_parts(stream_key, number_of, total, most, lean):
    if number_of == 2:
        one = jax.random.randint(stream_key, (), max(1, total - most), min(most, total - 1) + 1)
        return jnp.stack([one, total - one])
    sizes = jnp.asarray(length_profile(number_of, total, most, lean), jnp.int32)
    couples = (number_of - 1) // 2
    donor, sink = sizes[1:1 + 2 * couples:2], sizes[2:2 + 2 * couples:2]
    room = jnp.minimum(donor - 1, most - sink)
    moved = jax.random.randint(jax.random.fold_in(stream_key, 1), (couples,), 0, 1 << 20) % (room + 1)
    sizes = sizes.at[1:1 + 2 * couples:2].set(donor - moved).at[2:2 + 2 * couples:2].set(sink + moved)
    return sizes[jax.random.permutation(jax.random.fold_in(stream_key, 2), number_of)]


def normal_values(rng, dims, scale, limit, pieces=(), kind=jnp.bfloat16):
    entries = jax.random.normal(rng, dims, jnp.float32) * scale
    if len(pieces) > 0:
        entries = levels(rng, dims, pieces, -0.22, 0.18) * entries
    return jnp.clip(entries, min=-limit, max=limit).astype(kind)


def setup_inputs(seed: int = 0) -> dict:
    key_of = jax.random.split(jax.random.key(seed), 14)
    return {
        "tokens": normal_values(key_of[0], (TOKENS, D), 1.0, 6.0, ((0, 32),)),
        "cotangent": normal_values(key_of[1], (TOKENS, D), 1.0, 6.0, ((0, 32),)),
        "norm1_gain": jnp.clip(1.0 + 0.18 * jax.random.normal(key_of[2], (D,), jnp.float32), 0.1, 1.9),
        "w_query": normal_values(key_of[3], (D, D), D ** -0.5, 0.1875, ((0, 32),), jnp.float32),
        "w_key": normal_values(key_of[4], (D, D), D ** -0.5, 0.1875, ((0, 32),), jnp.float32),
        "w_value": normal_values(key_of[5], (D, D), D ** -0.5, 0.1875, ((0, 32),), jnp.float32),
        "w_out": normal_values(key_of[6], (D, D), (D // 16) ** -0.5, 0.75, ((0, 32),), jnp.float32),
        "norm2_gain": jnp.clip(1.0 + 0.18 * jax.random.normal(key_of[7], (D,), jnp.float32), 0.1, 1.9),
        "w_gate": normal_values(key_of[8], (D, FF), D ** -0.5, 0.1875, ((0, 32),), jnp.float32),
        "w_up": normal_values(key_of[9], (D, FF), D ** -0.5, 0.1875, ((0, 32),), jnp.float32),
        "w_down": normal_values(key_of[10], (FF, D), FF ** -0.5, 0.09375, ((0, 32),), jnp.float32),
        "block_anchor": jax.random.permutation(key_of[11], NBLOCKS).astype(jnp.int32),
        "seq_lengths": uneven_parts(key_of[12], NSEQ, TOKENS, LONGEST, 2).astype(jnp.int32),
    }


epsilon = 1e-06
masked_value = -1e+30

@jax.custom_vjp
def low(v):
    return lax.optimization_barrier(v.astype(jnp.bfloat16)).astype(jnp.float32)

@jax.custom_vjp
def low_back(v):
    return v

def low_keep(v):
    return (low(v), None)

def low_pass(kept, grad):
    return (grad,)

def back_keep(v):
    return (v, None)

def back_low(kept, grad):
    return (low(grad),)
low.defvjp(low_keep, low_pass)
low_back.defvjp(back_keep, back_low)

def product(first, second):
    return jnp.dot(first, second, precision=lax.Precision.HIGHEST)

def rms_norm(values, gain_vec):
    return values * lax.rsqrt(lax.optimization_barrier(jnp.mean(values * values, axis=-1, keepdims=True)) + epsilon) * gain_vec

def reference(tokens, cotangent, norm1_gain, w_query, w_key, w_value, w_out, norm2_gain, w_gate, w_up, w_down, block_anchor, seq_lengths):
    block_total = TOKENS // BLOCK
    inverse_order = jnp.zeros((block_total,), jnp.int32).at[block_anchor].set(jnp.arange(block_total, dtype=jnp.int32))
    positions = jnp.arange(TOKENS, dtype=jnp.int32)
    seq_ends = jnp.cumsum(seq_lengths)
    segments = lax.optimization_barrier(jnp.sum((positions[:, None] >= seq_ends[None, :]).astype(jnp.int32), axis=1)).astype(jnp.int32)
    query_size = min(256, TOKENS)
    key_span = LONGEST + query_size
    padded_pos = jnp.concatenate([jnp.zeros((LONGEST,), jnp.int32), positions])
    padded_seg = jnp.concatenate([jnp.full((LONGEST,), -1, jnp.int32), segments])
    scale_factor = 1.0 / math.sqrt(HEAD_DIM)

    def attention(queries, key_rows, value_rows):
        padding = jnp.zeros((LONGEST, HEADS, HEAD_DIM), jnp.float32)
        padded_keys = jnp.concatenate([padding, key_rows])
        padded_values = jnp.concatenate([padding, value_rows])

        def one_block(first_row):
            query_block = lax.dynamic_slice_in_dim(queries, first_row, query_size)
            key_block = lax.dynamic_slice_in_dim(padded_keys, first_row, key_span)
            value_block = lax.dynamic_slice_in_dim(padded_values, first_row, key_span)
            query_pos = lax.dynamic_slice_in_dim(positions, first_row, query_size)
            query_seg = lax.dynamic_slice_in_dim(segments, first_row, query_size)
            key_pos = lax.dynamic_slice_in_dim(padded_pos, first_row, key_span)
            key_seg = lax.dynamic_slice_in_dim(padded_seg, first_row, key_span)
            visible = (query_seg[:, None] == key_seg[None, :]) & (key_pos[None, :] <= query_pos[:, None])
            scores = low_back(jnp.einsum('qhd,khd->hqk', query_block, key_block, precision=lax.Precision.HIGHEST) * scale_factor)
            probabilities = jax.nn.softmax(jnp.where(visible[None], scores, masked_value), axis=-1)
            return jnp.einsum('hqk,khd->qhd', low(probabilities), value_block, precision=lax.Precision.HIGHEST)
        first_rows = jnp.arange(TOKENS // query_size, dtype=jnp.int32) * query_size
        return lax.map(jax.checkpoint(one_block), first_rows).reshape(TOKENS, HEADS * HEAD_DIM)

    def forward(inputs, gain_one, query_w, key_w, value_w, out_w, gain_two, gate_w, up_w, down_w):
        rows_orig = inputs.reshape(block_total, BLOCK, D)[inverse_order].reshape(TOKENS, D)
        hidden_one = low(rms_norm(rows_orig, low(gain_one)))
        queries = low_back(low(product(hidden_one, low(query_w))))
        key_rows = low_back(low(product(hidden_one, low(key_w))))
        value_rows = low_back(low(product(hidden_one, low(value_w))))
        attended = attention(queries.reshape(TOKENS, HEADS, HEAD_DIM), key_rows.reshape(TOKENS, HEADS, HEAD_DIM), value_rows.reshape(TOKENS, HEADS, HEAD_DIM))
        attended = low_back(low(attended))
        residual = rows_orig + low_back(product(attended, low(out_w)))
        hidden_two = low(rms_norm(residual, low(gain_two)))
        gate_lin = low_back(product(hidden_two, low(gate_w)))
        up_lin = low_back(product(hidden_two, low(up_w)))
        hidden_mlp = low(jax.nn.silu(gate_lin) * up_lin)
        result = residual + low_back(product(hidden_mlp, low(down_w)))
        return result.reshape(block_total, BLOCK, D)[block_anchor].reshape(TOKENS, D)
    primal, pullback = jax.vjp(forward, tokens.astype(jnp.float32), norm1_gain, w_query, w_key, w_value, w_out, norm2_gain, w_gate, w_up, w_down)
    gradients = pullback(cotangent.astype(jnp.float32))
    return (primal.astype(jnp.bfloat16), gradients[0].astype(jnp.bfloat16), gradients[1], gradients[2], gradients[3], gradients[4], gradients[5], gradients[6], gradients[7], gradients[8], gradients[9])
```

```python
import functools

import jax
import jax.numpy as jnp
from jax import lax
from jax.experimental import pallas as pl
from jax.experimental.pallas import tpu as pltpu
from jax.sharding import Mesh
from jax.sharding import PartitionSpec as P

HEAD_DIM = 64
BLOCK = 128
PAIR = 128
EPS = 1e-06
MASKED = -1e30
QTILE = 256
KTILE = 512
AXES = ("head", "z", "y", "core")
IDS = pl.DeviceIdType.MESH
F32 = jnp.float32
BF16 = jnp.bfloat16
ANY = pl.BlockSpec(memory_space=pl.ANY)
VM = pl.BlockSpec(memory_space=pltpu.VMEM)
SM = pl.BlockSpec(memory_space=pltpu.SMEM)


def struct(shape, dtype=BF16):
    return jax.ShapeDtypeStruct(tuple(shape), dtype)


def nt_dot(a, b):
    return lax.dot_general(a, b, (((1,), (1,)), ((), ())), preferred_element_type=F32)


def tn_dot(a, b):
    return lax.dot_general(a, b, (((0,), (0,)), ((), ())), preferred_element_type=F32)


def dot(a, b):
    return jnp.dot(a, b, preferred_element_type=F32)


def selection(rows, columns, shift, first=0, last=None):
    last = columns if last is None else last
    row = lax.broadcasted_iota(jnp.int32, (rows, columns), 0)
    column = lax.broadcasted_iota(jnp.int32, (rows, columns), 1)
    hit = (row == column + shift) & (column >= first) & (column < last)
    return hit.astype(F32).astype(BF16)


class Place:
    def __init__(self, z_count):
        self.z_count = z_count
        self.x, self.z, self.y, self.c = (lax.axis_index(a) for a in AXES)
        self.g = self.x * 2 + self.y
        self.chip = (self.x * z_count + self.z) * 2 + self.y

    def sibling(self):
        return (self.x, self.z, self.y, 1 - self.c)

    def plane(self, k):
        return (self.x ^ (k >> 1), self.z, self.y ^ (k & 1), self.c)

    def line(self, k):
        return (self.x, self.z ^ k, self.y, self.c)

    def any_chip(self, k):
        return (self.x ^ ((k >> 1) & 1), self.z ^ (k >> 2), self.y ^ (k & 1), self.c)


def meet(peers):
    barrier = pltpu.get_barrier_semaphore()
    for peer in peers:
        pl.semaphore_signal(barrier, inc=1, device_id=peer, device_id_type=IDS)
    pl.semaphore_wait(barrier, len(peers))


def send(source, target, sems, recvs, index, device):
    copy = pltpu.make_async_remote_copy(
        src_ref=source,
        dst_ref=target,
        send_sem=sems.at[index],
        recv_sem=recvs.at[index],
        device_id=device,
        device_id_type=IDS,
    )
    copy.start()
    return copy


def move(source, target, sems, index):
    copy = pltpu.make_async_copy(source, target, sems.at[index])
    copy.start()
    return copy


def exchange(kernel, ident, out_shape, scratch, args, sent):
    return pl.pallas_call(
        kernel,
        out_shape=out_shape,
        in_specs=[ANY] * len(args),
        out_specs=jax.tree.map(lambda _: ANY, out_shape),
        scratch_shapes=scratch,
        compiler_params=pltpu.CompilerParams(
            collective_id=ident, has_side_effects=True, vmem_limit_bytes=48 << 20
        ),
        cost_estimate=pl.CostEstimate(flops=0, bytes_accessed=sent, transcendentals=0),
    )(*args)


DMA = pltpu.SemaphoreType.DMA


def first_kernel(zc, n_ref, w_ref, f_ref, ng_ref, wg_ref, fg_ref, ls, ps, pr, fs, fr, ws, wr, bs, br):
    me = Place(zc)
    chips = 4 * zc
    meet([me.any_chip(k) for k in range(1, chips)] + [me.sibling()])
    own = [
        move(w_ref.at[me.g], wg_ref.at[me.chip, me.c], ls, 0),
        move(n_ref, ng_ref.at[me.g], ls, 1),
        move(f_ref.at[me.g], fg_ref.at[me.g], ls, 2),
    ]
    pieces = []
    for k in range(1, chips):
        there = me.any_chip(k)
        their_g = there[0] * 2 + there[2]
        pieces.append(send(w_ref.at[their_g], wg_ref.at[me.chip, me.c], ws, wr, k, there))
    rows = [send(n_ref, ng_ref.at[me.g], ps, pr, k, me.plane(k)) for k in range(1, 4)]
    wide = []
    for k in range(1, 4):
        there = me.plane(k)
        their_g = there[0] * 2 + there[2]
        wide.append(send(f_ref.at[their_g], fg_ref.at[me.g], fs, fr, k, there))
    own[0].wait()
    for copy in pieces:
        copy.wait()
    relay = send(wg_ref.at[:, me.c], wg_ref.at[:, me.c], bs, br, 0, me.sibling())
    for copy in own[1:] + rows + wide:
        copy.wait()
    relay.wait()


def first_exchange(zc, normed, w_send, f_send):
    chips = 4 * zc
    rows, cols = w_send.shape[1:]
    return exchange(
        functools.partial(first_kernel, zc),
        1,
        (
            struct((4,) + normed.shape),
            struct((chips, 2, rows, cols)),
            struct(f_send.shape),
        ),
        [DMA((3,))] + [DMA((4,))] * 4 + [DMA((chips,))] * 2 + [DMA((1,))] * 2,
        (normed, w_send, f_send),
        4 << 20,
    )


def heads_kernel(zc, q_ref, c_ref, a_ref, cg_ref, ls, zs, zr, bs, br, ps, pr):
    me = Place(zc)
    per = zc // q_ref.shape[0]
    meet([me.line(k) for k in range(1, zc)] + [me.plane(k) for k in range(1, 4)] + [me.sibling()])
    own = [
        move(q_ref.at[me.z // per], a_ref.at[me.z, me.c], ls, 0),
        move(c_ref, cg_ref.at[me.g], ls, 1),
    ]
    over = []
    for k in range(1, zc):
        over.append(
            send(q_ref.at[(me.z ^ k) // per], a_ref.at[me.z, me.c], zs, zr, k, me.line(k))
        )
    rows = [send(c_ref, cg_ref.at[me.g], ps, pr, k, me.plane(k)) for k in range(1, 4)]
    own[0].wait()
    relays = [send(a_ref.at[me.z, me.c], a_ref.at[me.z, me.c], bs, br, 0, me.sibling())]
    for k in range(1, zc):
        over[k - 1].wait()
        there = me.z ^ k
        relays.append(
            send(a_ref.at[there, me.c], a_ref.at[there, me.c], bs, br, k, me.sibling())
        )
    for copy in relays + rows + own[1:]:
        copy.wait()


def heads_exchange(zc, packed, cotangent):
    return exchange(
        functools.partial(heads_kernel, zc),
        2,
        (struct((zc, 2) + packed.shape[1:]), struct((4,) + cotangent.shape)),
        [DMA((2,))] + [DMA((zc,))] * 4 + [DMA((4,))] * 2,
        (packed, cotangent),
        4 << 20,
    )


def back_kernel(zc, o_ref, r_ref, mine, theirs, ls, bs, br, ss, rs):
    me = Place(zc)
    chips = 4 * zc
    per = r_ref.shape[1]
    meet([me.any_chip(k) for k in range(1, chips)] + [me.sibling()])
    other = send(o_ref.at[:, 1 - me.c], theirs, bs, br, 0, me.sibling())
    own = move(o_ref.at[:, me.c], mine, ls, 0)
    own.wait()
    other.wait()
    mine[...] = mine[...] + theirs[...]
    head = me.g * (r_ref.shape[0] // 4) + me.z // per
    part = me.z % per
    keep = move(mine.at[me.z, me.g], r_ref.at[head, part], ls, 1)
    sends = []
    for k in range(1, chips):
        there = me.any_chip(k)
        their_g = there[0] * 2 + there[2]
        sends.append(send(mine.at[there[1], their_g], r_ref.at[head, part], ss, rs, k, there))
    keep.wait()
    for copy in sends:
        copy.wait()


def back_exchange(zc, heads, slabs):
    chips = 4 * zc
    per = 4 * zc // heads
    half = (zc,) + slabs.shape[2:]
    return exchange(
        functools.partial(back_kernel, zc),
        3,
        struct((heads, per) + slabs.shape[3:]),
        [pltpu.VMEM(half, BF16)] * 2 + [DMA((2,))] + [DMA((1,))] * 2 + [DMA((chips,))] * 2,
        (slabs,),
        2 << 20,
    )


def plane_kernel(zc, n_ref, ng_ref, ls, ps, pr):
    me = Place(zc)
    meet([me.plane(k) for k in range(1, 4)])
    own = move(n_ref, ng_ref.at[me.g], ls, 0)
    rows = [send(n_ref, ng_ref.at[me.g], ps, pr, k, me.plane(k)) for k in range(1, 4)]
    for copy in [own] + rows:
        copy.wait()


def plane_gather(zc, rows):
    return exchange(
        functools.partial(plane_kernel, zc),
        4,
        struct((4,) + rows.shape),
        [DMA((1,))] + [DMA((4,))] * 2,
        (rows,),
        2 << 20,
    )


def scatter_kernel(zc, p_ref, r_ref, ls, ps, pr):
    me = Place(zc)
    meet([me.plane(k) for k in range(1, 4)])
    own = move(p_ref.at[me.g], r_ref.at[me.g], ls, 0)
    rows = []
    for k in range(1, 4):
        there = me.plane(k)
        rows.append(
            send(p_ref.at[there[0] * 2 + there[2]], r_ref.at[me.g], ps, pr, k, there)
        )
    for copy in [own] + rows:
        copy.wait()


def plane_scatter(zc, parts):
    return exchange(
        functools.partial(scatter_kernel, zc),
        5,
        struct(parts.shape),
        [DMA((1,))] + [DMA((4,))] * 2,
        (parts,),
        4 << 20,
    )


def grads_kernel(zc, d_ref, a_ref, ls, ss, rs, bs, br):
    me = Place(zc)
    chips = 4 * zc
    group = d_ref.shape[0] // 4
    per = zc // group
    meet([me.any_chip(k) for k in range(1, chips)] + [me.sibling()])
    own = move(d_ref.at[me.g * group + me.z // per], a_ref.at[me.z, me.c, me.g], ls, 0)
    sends = []
    for k in range(1, chips):
        there = me.any_chip(k)
        head = (there[0] * 2 + there[2]) * group + there[1] // per
        sends.append(send(d_ref.at[head], a_ref.at[me.z, me.c, me.g], ss, rs, k, there))
    own.wait()
    for copy in sends:
        copy.wait()
    relay = send(a_ref.at[:, me.c], a_ref.at[:, me.c], bs, br, 0, me.sibling())
    relay.wait()


def grads_exchange(zc, slabs):
    chips = 4 * zc
    return exchange(
        functools.partial(grads_kernel, zc),
        6,
        struct((zc, 2, 4) + slabs.shape[1:]),
        [DMA((1,))] + [DMA((chips,))] * 2 + [DMA((1,))] * 2,
        (slabs,),
        2 << 20,
    )


def rows_kernel(zc, d_ref, p_ref, r_ref, o_ref, mine, theirs, ls, bs, br, ss, rs, ps, pr):
    me = Place(zc)
    per = r_ref.shape[1]
    meet([me.line(k) for k in range(1, zc)] + [me.plane(k) for k in range(1, 4)] + [me.sibling()])
    other = send(d_ref.at[:, 1 - me.c], theirs, bs, br, 0, me.sibling())
    own = move(d_ref.at[:, me.c], mine, ls, 0)
    keep = move(p_ref.at[me.g], o_ref.at[me.g], ls, 2)
    outs = []
    for k in range(1, 4):
        there = me.plane(k)
        outs.append(
            send(p_ref.at[there[0] * 2 + there[2]], o_ref.at[me.g], ps, pr, k, there)
        )
    own.wait()
    other.wait()
    mine[...] = mine[...] + theirs[...]
    head = me.z // per
    part = me.z % per
    stay = move(mine.at[me.z], r_ref.at[head, part], ls, 1)
    sends = []
    for k in range(1, zc):
        sends.append(send(mine.at[me.z ^ k], r_ref.at[head, part], ss, rs, k, me.line(k)))
    for copy in [keep, stay] + sends + outs:
        copy.wait()


def rows_exchange(zc, heads, grads, parts):
    group = heads // 4
    per = zc // group
    half = (zc,) + grads.shape[2:]
    return exchange(
        functools.partial(rows_kernel, zc),
        7,
        (struct((group, per) + grads.shape[2:]), struct(parts.shape)),
        [pltpu.VMEM(half, BF16)] * 2
        + [DMA((3,))]
        + [DMA((1,))] * 2
        + [DMA((zc,))] * 2
        + [DMA((4,))] * 2,
        (grads, parts),
        6 << 20,
    )


def last_kernel(zc, p_ref, w_ref, f_ref, r_ref, gw_ref, gf_ref, mine, theirs, ls, bs, br, ss, rs, ps, pr, fs, fr):
    me = Place(zc)
    chips = 4 * zc
    meet([me.any_chip(k) for k in range(1, chips)] + [me.sibling()])
    other = send(w_ref.at[:, 1 - me.c], theirs, bs, br, 0, me.sibling())
    own = move(w_ref.at[:, me.c], mine, ls, 0)
    keep = [move(p_ref.at[me.g], r_ref.at[me.g], ls, 1), move(f_ref.at[me.g], gf_ref.at[me.g], ls, 2)]
    outs = []
    for k in range(1, 4):
        there = me.plane(k)
        their_g = there[0] * 2 + there[2]
        outs.append(send(p_ref.at[their_g], r_ref.at[me.g], ps, pr, k, there))
        outs.append(send(f_ref.at[their_g], gf_ref.at[me.g], fs, fr, k, there))
    own.wait()
    other.wait()
    mine[...] = mine[...] + theirs[...]
    stay = move(mine.at[me.chip], gw_ref.at[me.z, me.g], ls, 3)
    sends = []
    for k in range(1, chips):
        there = me.any_chip(k)
        chip = (there[0] * zc + there[1]) * 2 + there[2]
        sends.append(send(mine.at[chip], gw_ref.at[me.z, me.g], ss, rs, k, there))
    for copy in keep + [stay] + sends + outs:
        copy.wait()


def last_exchange(zc, parts, w_parts, f_parts):
    chips = 4 * zc
    piece = w_parts.shape[2:]
    return exchange(
        functools.partial(last_kernel, zc),
        8,
        (struct(parts.shape), struct((zc, 4) + piece), struct(f_parts.shape)),
        [pltpu.VMEM((chips,) + piece, BF16)] * 2
        + [DMA((4,))]
        + [DMA((1,))] * 2
        + [DMA((chips,))] * 2
        + [DMA((4,))] * 4,
        (parts, w_parts, f_parts),
        6 << 20,
    )


def project_kernel(group, n_ref, w_ref, o_ref):
    qw = group * HEAD_DIM
    out = dot(n_ref[0], w_ref[...]).astype(BF16)
    for head in range(group):
        left = selection(qw, PAIR, head * HEAD_DIM, 0, HEAD_DIM)
        right = selection(qw, PAIR, head * HEAD_DIM - HEAD_DIM, HEAD_DIM, PAIR)
        slab = dot(out[:BLOCK, :qw], left) + dot(out[BLOCK:, :qw], right)
        o_ref[head, 0, :BLOCK] = slab.astype(BF16)
        start = qw + head * PAIR
        o_ref[head, 0, BLOCK:] = out[:, start : start + PAIR]


def project(group, rows, weights):
    count, per, width = rows.shape
    return pl.pallas_call(
        functools.partial(project_kernel, group),
        out_shape=struct((group, count, BLOCK + per, PAIR)),
        grid=(count,),
        in_specs=[
            pl.BlockSpec((1, per, width), lambda i: (i, 0, 0)),
            pl.BlockSpec(weights.shape, lambda i: (0, 0)),
        ],
        out_specs=pl.BlockSpec((group, 1, BLOCK + per, PAIR), lambda i: (0, i, 0, 0)),
        compiler_params=pltpu.CompilerParams(vmem_limit_bytes=32 << 20),
    )(rows, weights)


def unproject_kernel(group, d_ref, w_ref, m_ref, c_ref):
    qw = group * HEAD_DIM
    upper = jnp.zeros((BLOCK, qw), F32)
    lower = jnp.zeros((BLOCK, qw), F32)
    for head in range(group):
        slab = d_ref[head, 0, 0]
        for extra in range(1, d_ref.shape[1]):
            slab = slab + d_ref[head, extra, 0]
        left = selection(PAIR, qw, -head * HEAD_DIM, head * HEAD_DIM, (head + 1) * HEAD_DIM)
        right = selection(
            PAIR, qw, HEAD_DIM - head * HEAD_DIM, head * HEAD_DIM, (head + 1) * HEAD_DIM
        )
        upper = upper + dot(slab[:BLOCK], left)
        lower = lower + dot(slab[:BLOCK], right)
        start = qw + head * PAIR
        m_ref[0, :, start : start + PAIR] = slab[BLOCK:]
    m_ref[0, :BLOCK, :qw] = upper.astype(BF16)
    m_ref[0, BLOCK:, :qw] = lower.astype(BF16)
    c_ref[0] = nt_dot(m_ref[0], w_ref[...]).astype(BF16)


def unproject(grads, weights):
    group, parts, count, rows, _ = grads.shape
    per = rows - BLOCK
    width, cols = weights.shape
    return pl.pallas_call(
        functools.partial(unproject_kernel, group),
        out_shape=(struct((count, per, cols)), struct((count, per, width))),
        grid=(count,),
        in_specs=[
            pl.BlockSpec((group, parts, 1, rows, PAIR), lambda i: (0, 0, i, 0, 0)),
            pl.BlockSpec((width, cols), lambda i: (0, 0)),
        ],
        out_specs=(
            pl.BlockSpec((1, per, cols), lambda i: (i, 0, 0)),
            pl.BlockSpec((1, per, width), lambda i: (i, 0, 0)),
        ),
        compiler_params=pltpu.CompilerParams(vmem_limit_bytes=32 << 20),
    )(grads, weights)


def join_kernel(o_ref, x_ref, w_ref, ob_ref, r_ref, n_ref):
    heads = o_ref.shape[0]
    for block in range(2):
        for pair in range(heads // 2):
            total = jnp.zeros((BLOCK, PAIR), F32)
            for side in range(2):
                slab = o_ref[2 * pair + side, 0]
                for extra in range(1, o_ref.shape[1]):
                    slab = slab + o_ref[2 * pair + side, extra]
                pick = selection(
                    PAIR, PAIR, (block - side) * HEAD_DIM, side * HEAD_DIM, (side + 1) * HEAD_DIM
                )
                total = total + dot(slab, pick)
            ob_ref[block * BLOCK : (block + 1) * BLOCK, pair * PAIR : (pair + 1) * PAIR] = (
                total.astype(BF16)
            )
    residual = x_ref[...].astype(F32) + dot(ob_ref[...], w_ref[...])
    r_ref[...] = residual
    mean = jnp.mean(residual * residual, axis=-1, keepdims=True)
    n_ref[...] = (residual * lax.rsqrt(mean + EPS)).astype(BF16)


def join(slabs, tokens, w_out):
    shape = tokens.shape
    return pl.pallas_call(
        join_kernel,
        out_shape=(struct(shape), struct(shape, F32), struct(shape)),
        in_specs=[VM] * 3,
        out_specs=(VM,) * 3,
        compiler_params=pltpu.CompilerParams(vmem_limit_bytes=32 << 20),
    )(slabs, tokens, w_out)


def part_kernel(c_ref, t_ref, r_ref, w_ref, d_ref, a_ref, s_ref):
    total = c_ref[0].astype(F32)
    for i in range(1, c_ref.shape[0]):
        total = total + c_ref[i].astype(F32)
    residual = r_ref[...]
    scaling = lax.rsqrt(jnp.mean(residual * residual, axis=-1, keepdims=True) + EPS)
    normed = residual * scaling
    middle = jnp.mean(total * normed, axis=-1, keepdims=True)
    grad = t_ref[...].astype(F32) + scaling * (total - normed * middle)
    d_ref[...] = grad
    low = grad.astype(BF16)
    a_ref[...] = low
    heads = s_ref.shape[0]
    back = nt_dot(low, w_ref[...]).astype(BF16)
    for pair in range(heads // 2):
        both = back[:, pair * PAIR : (pair + 1) * PAIR]
        for side in range(2):
            left = selection(PAIR, PAIR, side * HEAD_DIM, 0, HEAD_DIM)
            right = selection(PAIR, PAIR, (side - 1) * HEAD_DIM, HEAD_DIM, PAIR)
            slab = dot(both[:BLOCK], left) + dot(both[BLOCK:], right)
            s_ref[2 * pair + side] = slab.astype(BF16)


def part(c_parts, cotangent, residual, w_out):
    shape = cotangent.shape
    heads = w_out.shape[0] // HEAD_DIM
    return pl.pallas_call(
        part_kernel,
        out_shape=(struct(shape, F32), struct(shape), struct((heads, BLOCK, PAIR))),
        in_specs=[VM] * 4,
        out_specs=(VM,) * 3,
        compiler_params=pltpu.CompilerParams(vmem_limit_bytes=32 << 20),
    )(c_parts, cotangent, residual, w_out)


def segment_start(position, lens_ref):
    start = jnp.zeros_like(position)
    end = 0
    for j in range(lens_ref.shape[0]):
        end = end + lens_ref[j]
        start = jnp.where(position >= end, end, start)
    return start


def tile_of(turn, workers, worker):
    forward = turn * workers + worker
    backward = turn * workers + workers - 1 - worker
    return jnp.where((turn & 1) == 0, forward, backward)


def key_bounds(first, lens_ref):
    low_start = segment_start(first, lens_ref)
    high_start = segment_start(first + QTILE - 1, lens_ref)
    low = low_start // KTILE
    high = (first + QTILE + KTILE - 1) // KTILE
    plain = jnp.clip((high_start + KTILE - 1) // KTILE, low, high)
    stop = jnp.clip((first + 1) // KTILE, plain, high)
    return low, plain, stop, high


def visible(first, tile, starts):
    key = tile * KTILE + lax.broadcasted_iota(jnp.int32, (KTILE, QTILE), 0)
    query = first + lax.broadcasted_iota(jnp.int32, (KTILE, QTILE), 1)
    return (key <= query) & (key >= starts)


def forward_kernel(
    workers, anchor_ref, lens_ref, who_ref, a_ref, o_ref, kv_ref, kvt_ref, q_ref, qt_ref, ot_ref, l_ref, inv, pick
):
    blocks = anchor_ref.shape[0]
    turns = q_ref.shape[0]
    per = QTILE // BLOCK
    worker = who_ref[0]

    def note(i, carry):
        inv[anchor_ref[i]] = i
        return carry

    lax.fori_loop(0, blocks, note, 0)
    for half in range(2):
        pick[half] = selection(PAIR, PAIR, half * HEAD_DIM, 0, HEAD_DIM)
        row = lax.broadcasted_iota(jnp.int32, (PAIR, PAIR), 0)
        column = lax.broadcasted_iota(jnp.int32, (PAIR, PAIR), 1)
        hit = (column == row + half * HEAD_DIM) & (row < HEAD_DIM)
        pick[2 + half] = hit.astype(F32).astype(BF16)
    same = lax.broadcasted_iota(jnp.int32, (PAIR, PAIR), 0)
    pick[4] = (same == lax.broadcasted_iota(jnp.int32, (PAIR, PAIR), 1)).astype(F32).astype(BF16)
    o_ref[...] = jnp.zeros_like(o_ref)

    def order(i, carry):
        where = inv[i]
        slab, half = where >> 1, where & 1
        block = a_ref[slab, pl.ds(pl.multiple_of(BLOCK + half * BLOCK, BLOCK), BLOCK), :]
        at = pl.ds(pl.multiple_of(i * BLOCK, BLOCK), BLOCK)
        kv_ref[at, :] = block
        kvt_ref[:, at] = nt_dot(pick[4], block).astype(BF16)
        return carry

    lax.fori_loop(0, blocks, order, 0)

    def one_tile(turn, carry):
        tile = tile_of(turn, workers, worker)
        first = tile * QTILE
        for b in range(per):
            where = inv[tile * per + b]
            slab, half = where >> 1, where & 1
            rows = a_ref[slab, :BLOCK, :]
            q_ref[turn, b * BLOCK : (b + 1) * BLOCK, :] = (dot(rows, pick[half]) * 0.125).astype(BF16)
            qt_ref[turn, :, b * BLOCK : (b + 1) * BLOCK] = (
                nt_dot(pick[2 + half], rows) * 0.125
            ).astype(BF16)
        query = qt_ref[turn]
        starts = segment_start(first + lax.broadcasted_iota(jnp.int32, (1, QTILE), 1), lens_ref)
        low, plain, stop, high = key_bounds(first, lens_ref)

        def step(masked, kt, state):
            top, total, acc = state
            at = pl.ds(pl.multiple_of(kt * KTILE, KTILE), KTILE)
            scores = dot(kv_ref[at, :], query)
            if masked:
                seen = visible(first, kt, starts)
                scores = jnp.where(seen, scores, MASKED)
            new_top = jnp.maximum(top, jnp.max(scores, axis=0, keepdims=True))
            factor = jnp.exp(top - new_top)
            weights = jnp.exp(scores - new_top)
            if masked:
                weights = jnp.where(seen, weights, 0.0)
            total = total * factor + jnp.sum(weights, axis=0, keepdims=True)
            acc = acc * factor + dot(kvt_ref[HEAD_DIM:, at], weights.astype(BF16))
            return (new_top, total, acc)

        state = (
            jnp.full((1, QTILE), MASKED, F32),
            jnp.zeros((1, QTILE), F32),
            jnp.zeros((HEAD_DIM, QTILE), F32),
        )
        state = lax.fori_loop(low, plain, functools.partial(step, True), state)
        state = lax.fori_loop(plain, stop, functools.partial(step, False), state)
        top, total, acc = lax.fori_loop(stop, high, functools.partial(step, True), state)
        out = acc / total
        ot_ref[turn] = out
        l_ref[turn] = top + jnp.log(total)
        narrow = out.astype(BF16)
        for b in range(per):
            where = inv[tile * per + b]
            slab, half = where >> 1, where & 1
            piece = tn_dot(narrow[:, b * BLOCK : (b + 1) * BLOCK], pick[2 + half, :HEAD_DIM, :])
            o_ref[slab] = o_ref[slab] + piece.astype(BF16)
        return carry

    lax.fori_loop(0, turns, one_tile, 0)


def attention_forward(workers, anchors, lengths, who, packed):
    slabs = packed.shape[0]
    rows = slabs * 2 * BLOCK
    turns = rows // QTILE // workers
    return pl.pallas_call(
        functools.partial(forward_kernel, workers),
        out_shape=(
            struct((slabs, BLOCK, PAIR)),
            struct((rows, PAIR)),
            struct((PAIR, rows)),
            struct((turns, QTILE, PAIR)),
            struct((turns, PAIR, QTILE)),
            struct((turns, HEAD_DIM, QTILE), F32),
            struct((turns, 1, QTILE), F32),
        ),
        in_specs=[SM, SM, SM, VM],
        out_specs=(VM,) * 7,
        scratch_shapes=[pltpu.SMEM((2 * slabs,), jnp.int32), pltpu.VMEM((5, PAIR, PAIR), BF16)],
        compiler_params=pltpu.CompilerParams(vmem_limit_bytes=60 << 20),
        cost_estimate=pl.CostEstimate(
            flops=rows * rows * 64, bytes_accessed=rows * 1024, transcendentals=rows * rows // 8
        ),
    )(anchors, lengths, who, packed)


def backward_kernel(
    workers,
    anchor_ref,
    lens_ref,
    who_ref,
    d_ref,
    kv_ref,
    kvt_ref,
    q_ref,
    qt_ref,
    ot_ref,
    l_ref,
    g_ref,
    inv,
    pick,
    dn,
    dt,
    acc,
):
    blocks = anchor_ref.shape[0]
    turns = q_ref.shape[0]
    per = QTILE // BLOCK
    worker = who_ref[0]

    def note(i, carry):
        inv[anchor_ref[i]] = i
        return carry

    lax.fori_loop(0, blocks, note, 0)
    row = lax.broadcasted_iota(jnp.int32, (PAIR, PAIR), 0)
    column = lax.broadcasted_iota(jnp.int32, (PAIR, PAIR), 1)
    for half in range(2):
        hit = (row - half * HEAD_DIM == column - HEAD_DIM) & (column >= HEAD_DIM)
        pick[half] = hit.astype(F32).astype(BF16)
        hit = (column - half * HEAD_DIM == row - HEAD_DIM) & (row >= HEAD_DIM)
        pick[2 + half] = hit.astype(F32).astype(BF16)
        hit = (column == row + half * HEAD_DIM) & (row < HEAD_DIM)
        pick[4 + half] = hit.astype(F32).astype(BF16)
    acc[...] = jnp.zeros_like(acc)
    g_ref[:, :BLOCK, :] = jnp.zeros((g_ref.shape[0], BLOCK, PAIR), BF16)

    def one_tile(turn, carry):
        tile = tile_of(turn, workers, worker)
        first = tile * QTILE
        for b in range(per):
            where = inv[tile * per + b]
            slab, half = where >> 1, where & 1
            rows = d_ref[slab]
            dn[b * BLOCK : (b + 1) * BLOCK, :] = dot(rows, pick[half]).astype(BF16)
            dt[:, b * BLOCK : (b + 1) * BLOCK] = nt_dot(pick[2 + half], rows).astype(BF16)
        query, query_rows = qt_ref[turn], q_ref[turn]
        grad, grad_rows = dt[...], dn[...]
        norm = l_ref[turn]
        delta = jnp.sum(grad[HEAD_DIM:].astype(F32) * ot_ref[turn], axis=0, keepdims=True)
        starts = segment_start(first + lax.broadcasted_iota(jnp.int32, (1, QTILE), 1), lens_ref)
        low, plain, stop, high = key_bounds(first, lens_ref)

        def step(masked, kt, total):
            at = pl.ds(pl.multiple_of(kt * KTILE, KTILE), KTILE)
            keys = kv_ref[at, :]
            weights = jnp.exp(dot(keys, query) - norm)
            if masked:
                weights = jnp.where(visible(first, kt, starts), weights, 0.0)
            score_grad = (weights * (dot(keys, grad) - delta)).astype(BF16)
            acc[at, :] += dot(score_grad, query_rows) + dot(weights.astype(BF16), grad_rows)
            return total + dot(kvt_ref[:HEAD_DIM, at], score_grad)

        total = jnp.zeros((HEAD_DIM, QTILE), F32)
        total = lax.fori_loop(low, plain, functools.partial(step, True), total)
        total = lax.fori_loop(plain, stop, functools.partial(step, False), total)
        total = lax.fori_loop(stop, high, functools.partial(step, True), total)
        narrow = (total * 0.125).astype(BF16)
        for b in range(per):
            where = inv[tile * per + b]
            slab, half = where >> 1, where & 1
            piece = tn_dot(narrow[:, b * BLOCK : (b + 1) * BLOCK], pick[4 + half, :HEAD_DIM, :])
            g_ref[slab, :BLOCK] = g_ref[slab, :BLOCK] + piece.astype(BF16)
        return carry

    lax.fori_loop(0, turns, one_tile, 0)

    def place(i, carry):
        where = inv[i]
        slab, half = where >> 1, where & 1
        at = pl.ds(pl.multiple_of(i * BLOCK, BLOCK), BLOCK)
        to = pl.ds(pl.multiple_of(BLOCK + half * BLOCK, BLOCK), BLOCK)
        g_ref[slab, to, :] = acc[at, :].astype(BF16)
        return carry

    lax.fori_loop(0, blocks, place, 0)


def attention_backward(workers, anchors, lengths, who, grads, kept):
    slabs = grads.shape[0]
    rows = slabs * 2 * BLOCK
    return pl.pallas_call(
        functools.partial(backward_kernel, workers),
        out_shape=struct((slabs, 3 * BLOCK, PAIR)),
        in_specs=[SM, SM, SM] + [VM] * 7,
        out_specs=VM,
        scratch_shapes=[
            pltpu.SMEM((2 * slabs,), jnp.int32),
            pltpu.VMEM((6, PAIR, PAIR), BF16),
            pltpu.VMEM((QTILE, PAIR), BF16),
            pltpu.VMEM((PAIR, QTILE), BF16),
            pltpu.VMEM((rows, PAIR), F32),
        ],
        compiler_params=pltpu.CompilerParams(vmem_limit_bytes=60 << 20),
        cost_estimate=pl.CostEstimate(
            flops=rows * rows * 160, bytes_accessed=rows * 1024, transcendentals=rows * rows // 8
        ),
    )(anchors, lengths, who, grads, *kept)


def norm_parts(values):
    scaling = lax.rsqrt(jnp.mean(values * values, axis=-1, keepdims=True) + EPS)
    return values * scaling, scaling


def body(
    zc,
    tokens,
    cotangent,
    norm1_gain,
    w_query,
    w_key,
    w_value,
    w_out,
    norm2_gain,
    w_gate,
    w_up,
    w_down,
    block_anchor,
    seq_lengths,
):
    own_rows, width = tokens.shape
    heads = width // HEAD_DIM
    group = heads // 4
    per_head = zc // group
    workers = 2 * per_head
    feature_rows = w_query.shape[0]
    hidden = w_gate.shape[1]
    units = w_down.shape[0]
    slice_units = hidden // 4

    low = lambda v: v.astype(BF16).astype(F32)
    gain1, gain2 = low(norm1_gain)[:, None], low(norm2_gain)[:, None]
    query_w, key_w, value_w = low(w_query), low(w_key), low(w_value)
    gate_w, up_w = low(w_gate), low(w_up)
    q_part = (gain1 * query_w).reshape(feature_rows, 4, group * HEAD_DIM)
    kv_part = jnp.stack(
        [
            (gain1 * key_w).reshape(feature_rows, 4, group, HEAD_DIM),
            (gain1 * value_w).reshape(feature_rows, 4, group, HEAD_DIM),
        ],
        axis=3,
    ).reshape(feature_rows, 4, group * PAIR)
    w_send = jnp.transpose(jnp.concatenate([q_part, kv_part], axis=2).astype(BF16), (1, 0, 2))

    def slices(weight):
        return jnp.transpose(
            weight.reshape(feature_rows, 2, zc, 2, 2 * units), (1, 3, 0, 2, 4)
        ).reshape(4, feature_rows, slice_units)

    f_send = jnp.stack([slices((gain2 * gate_w).astype(BF16)), slices((gain2 * up_w).astype(BF16))], axis=1)
    out_mat = lax.all_gather(w_out.astype(BF16), AXES, axis=0, tiled=True)

    inputs = tokens.astype(F32)
    normed_one, scaling_one = norm_parts(inputs)
    n1_all, qkv_w, f_all = first_exchange(zc, normed_one.astype(BF16), w_send, f_send)
    qkv_w = qkv_w.reshape(width, 3 * group * HEAD_DIM)

    ffn_in = jnp.concatenate([f_all.reshape(-1, slice_units), w_down.astype(BF16)], axis=0)
    ffn_all = lax.all_gather(ffn_in, ("z", "core"), axis=0, tiled=False)
    wide = 8 * feature_rows
    gate_up = jnp.transpose(
        ffn_all[:, :wide].reshape(zc, 2, 2, 2, 2, feature_rows, slice_units), (4, 2, 0, 3, 1, 5, 6)
    ).reshape(2, width, slice_units)
    gate_mat, up_mat = gate_up[0], gate_up[1]
    down_mat = ffn_all[:, wide:].reshape(slice_units, width)

    packed = project(group, n1_all, qkv_w)
    by_head, cot_all = heads_exchange(zc, packed, cotangent)

    anchors = jnp.transpose(block_anchor.reshape(2, zc, 2, 2, 2), (1, 3, 0, 2, 4)).reshape(-1)
    who = ((lax.axis_index("z") % per_head) * 2 + lax.axis_index("core")).astype(jnp.int32).reshape(1)
    slab_count = zc * 8
    o_slabs, *kept = attention_forward(
        workers, anchors, seq_lengths, who, by_head.reshape((slab_count,) + by_head.shape[3:])
    )
    o_rows = back_exchange(zc, heads, o_slabs.reshape(zc, 2, 4, BLOCK, PAIR))
    attn_rows, residual, normed_two = join(o_rows, tokens, out_mat)

    n2_all = plane_gather(zc, normed_two).reshape(-1, width)
    cot_rows = cot_all.reshape(-1, width)
    gate = dot(n2_all, gate_mat)
    up = dot(n2_all, up_mat)
    sig = jax.nn.sigmoid(gate)
    hid = (gate * sig * up).astype(BF16)
    out_parts = dot(hid, down_mat).astype(BF16)
    hid_grad = nt_dot(cot_rows, down_mat)
    gate_back = (hid_grad * up * sig * (1.0 + gate * (1.0 - sig))).astype(BF16)
    up_back = (hid_grad * gate * sig).astype(BF16)
    c2_parts = (nt_dot(gate_back, gate_mat) + nt_dot(up_back, up_mat)).astype(BF16)
    gate_grad = tn_dot(n2_all, gate_back).astype(BF16)
    up_grad = tn_dot(n2_all, up_back).astype(BF16)
    down_grad = tn_dot(hid, cot_rows).astype(BF16)

    c2_all = plane_scatter(zc, c2_parts.reshape(4, own_rows, width))
    residual_grad, branch_back, do_slabs = part(c2_all, cotangent, residual, out_mat)
    do_heads = grads_exchange(zc, do_slabs)

    out_w_grad = tn_dot(attn_rows, branch_back).astype(BF16)

    def by_owner(grad):
        cols = grad.shape[-1]
        return jnp.transpose(
            grad.reshape(2, zc, 2, 2, feature_rows, cols), (1, 3, 0, 2, 4, 5)
        ).reshape(zc * 2, 4, 1, feature_rows, cols)

    shares = jnp.concatenate(
        [
            jnp.concatenate(
                [by_owner(gate_grad), by_owner(up_grad), by_owner(out_w_grad)], axis=2
            ).reshape(zc * 2, -1, width),
            down_grad.reshape(zc * 2, units, width),
        ],
        axis=1,
    )
    rows_each = shares.shape[1]
    shares = lax.psum_scatter(
        shares.reshape(zc * 2 * rows_each, width), ("z", "core"), scatter_dimension=0, tiled=True
    )
    down_share = shares[rows_each - units :]
    ffn_share = shares[: rows_each - units].reshape(4, 3, feature_rows, width)

    grad_heads = attention_backward(
        workers, anchors, seq_lengths, who, do_heads.reshape(slab_count, BLOCK, PAIR), kept
    )
    grad_rows, out_all = rows_exchange(
        zc,
        heads,
        grad_heads.reshape(zc, 2, 4, 3 * BLOCK, PAIR),
        out_parts.reshape(4, own_rows, width),
    )
    qkv_grad, c1_parts = unproject(grad_rows, qkv_w)
    w_grad = tn_dot(n1_all.reshape(-1, width), qkv_grad.reshape(-1, qkv_grad.shape[-1])).astype(BF16)
    c1_all, w_all, f_grad = last_exchange(
        zc, c1_parts, w_grad.reshape(4 * zc, 2, feature_rows, -1), ffn_share
    )

    output = (residual + jnp.sum(out_all.astype(F32), axis=0)).astype(BF16)
    c1 = jnp.sum(c1_all.astype(F32), axis=0)
    middle = jnp.mean(c1 * normed_one, axis=-1, keepdims=True)
    tokens_grad = (residual_grad + scaling_one * (c1 - normed_one * middle)).astype(BF16)

    w_sum = jnp.sum(w_all.astype(F32), axis=0)
    q_cols = group * HEAD_DIM
    query_raw = jnp.transpose(w_sum[:, :, :q_cols], (1, 0, 2)).reshape(feature_rows, width)
    kv_raw = w_sum[:, :, q_cols:].reshape(4, feature_rows, group, 2, HEAD_DIM)
    key_raw = jnp.transpose(kv_raw[:, :, :, 0], (1, 0, 2, 3)).reshape(feature_rows, width)
    value_raw = jnp.transpose(kv_raw[:, :, :, 1], (1, 0, 2, 3)).reshape(feature_rows, width)
    gain1_grad = jnp.sum(query_raw * query_w + key_raw * key_w + value_raw * value_w, axis=1)

    def unslice(grad):
        return jnp.transpose(
            grad.astype(F32).reshape(2, 2, feature_rows, zc, 2 * units), (2, 0, 3, 1, 4)
        ).reshape(feature_rows, hidden)

    gate_raw, up_raw = unslice(f_grad[:, 0]), unslice(f_grad[:, 1])
    gain2_grad = jnp.sum(gate_raw * gate_w + up_raw * up_w, axis=1)
    out_share = jnp.sum(f_grad[:, 2].astype(F32), axis=0)
    return (
        output,
        tokens_grad,
        gain1_grad,
        gain1 * query_raw,
        gain1 * key_raw,
        gain1 * value_raw,
        out_share,
        gain2_grad,
        gain2 * gate_raw,
        gain2 * up_raw,
        down_share.astype(F32),
    )


def solution(mesh):
    blk = mesh.shape["blk"]
    grid = Mesh(mesh.devices.reshape(mesh.shape["head"], blk // 4, 2, 2), AXES)
    rows, vector, whole = P(AXES, None), P(AXES), P()
    return jax.shard_map(
        functools.partial(body, blk // 4),
        mesh=grid,
        in_specs=(rows, rows, vector, rows, rows, rows, rows, vector, rows, rows, rows, whole, whole),
        out_specs=(rows, rows, vector, rows, rows, rows, rows, vector, rows, rows, rows),
        check_vma=False,
    )
```

```python
import functools

import jax
import jax.numpy as jnp
from jax import lax
from jax.experimental import pallas as pl
from jax.experimental.pallas import tpu as pltpu
from jax.sharding import Mesh
from jax.sharding import PartitionSpec as P

HEAD_DIM = 64
BLOCK = 128
PAIR = 128
EPS = 1e-06
MASKED = -1e30
QTILE = 256
KTILE = 512
AXES = ("head", "z", "y", "core")
IDS = pl.DeviceIdType.MESH
F32 = jnp.float32
BF16 = jnp.bfloat16
ANY = pl.BlockSpec(memory_space=pl.ANY)
VM = pl.BlockSpec(memory_space=pltpu.VMEM)
SM = pl.BlockSpec(memory_space=pltpu.SMEM)


def struct(shape, dtype=BF16):
    return jax.ShapeDtypeStruct(tuple(shape), dtype)


def nt_dot(a, b):
    return lax.dot_general(a, b, (((1,), (1,)), ((), ())), preferred_element_type=F32)


def tn_dot(a, b):
    return lax.dot_general(a, b, (((0,), (0,)), ((), ())), preferred_element_type=F32)


def dot(a, b):
    return jnp.dot(a, b, preferred_element_type=F32)


def selection(rows, columns, shift, first=0, last=None):
    last = columns if last is None else last
    row = lax.broadcasted_iota(jnp.int32, (rows, columns), 0)
    column = lax.broadcasted_iota(jnp.int32, (rows, columns), 1)
    hit = (row == column + shift) & (column >= first) & (column < last)
    return hit.astype(F32).astype(BF16)


class Place:
    def __init__(self, z_count):
        self.x, self.z, self.y, self.c = (lax.axis_index(a) for a in AXES)
        self.g = self.x * 2 + self.y
        self.chip = (self.x * z_count + self.z) * 2 + self.y

    def sibling(self):
        return (self.x, self.z, self.y, 1 - self.c)

    def plane(self, k):
        return (self.x ^ (k // 2), self.z, self.y ^ (k % 2), self.c)

    def line(self, k):
        return (self.x, self.z ^ k, self.y, self.c)

    def any_chip(self, k):
        return (self.x ^ (k // 2 % 2), self.z ^ (k // 4), self.y ^ (k % 2), self.c)


def meet(peers):
    barrier = pltpu.get_barrier_semaphore()
    for peer in peers:
        pl.semaphore_signal(barrier, inc=1, device_id=peer, device_id_type=IDS)
    pl.semaphore_wait(barrier, len(peers))


def trip(source, target, sems, index, device):
    return pltpu.make_async_remote_copy(
        src_ref=source,
        dst_ref=target,
        send_sem=sems[0].at[index],
        recv_sem=sems[1].at[index],
        device_id=device,
        device_id_type=IDS,
    )


def send(*given):
    copy = trip(*given)
    copy.start()
    return copy


def move(source, target, sems, index):
    copy = pltpu.make_async_copy(source, target, sems.at[index])
    copy.start()
    return copy


DMA = pltpu.SemaphoreType.DMA


def both(count):
    return [DMA((count,)), DMA((count,))]


def exchange(kernel, ident, out_shape, in_specs, out_specs, scratch, args, flops, sent):
    return pl.pallas_call(
        kernel,
        out_shape=out_shape,
        in_specs=in_specs,
        out_specs=out_specs,
        scratch_shapes=scratch,
        compiler_params=pltpu.CompilerParams(
            collective_id=ident, has_side_effects=True, vmem_limit_bytes=56 << 20
        ),
        cost_estimate=pl.CostEstimate(flops=flops, bytes_accessed=sent, transcendentals=0),
    )(*args)


def head_kernel(
    zc,
    group,
    t_ref,
    w_ref,
    f_ref,
    o_ref,
    ng_ref,
    wg_ref,
    fg_ref,
    og_ref,
    a_ref,
    rows,
    weights,
    packed,
    ls,
    w0,
    w1,
    n0,
    n1,
    f0,
    f1,
    o0,
    o1,
    p0,
    p1,
    z0,
    z1,
    b0,
    b1,
    s0,
    s1,
):
    me = Place(zc)
    chips = 4 * zc
    per = zc // group
    qw = group * HEAD_DIM
    width = t_ref.shape[1]
    x = t_ref[...].astype(F32)
    rows[0] = (x * lax.rsqrt(jnp.mean(x * x, axis=-1, keepdims=True) + EPS)).astype(BF16)
    meet([me.any_chip(k) for k in range(1, chips)] + [me.sibling()])
    local = [
        move(w_ref.at[me.g], weights.at[me.chip, me.c], ls, 0),
        move(o_ref, og_ref.at[me.x, me.z, me.y, me.c], ls, 1),
        move(f_ref.at[me.g], fg_ref.at[me.g], ls, 2),
    ]
    pieces = []
    for k in reversed(range(1, chips)):
        there = me.any_chip(k)
        their_g = there[0] * 2 + there[2]
        pieces.append(
            send(w_ref.at[their_g], weights.at[me.chip, me.c], (w0, w1), k, there)
        )
    outs = [
        send(o_ref, og_ref.at[me.x, me.z, me.y, me.c], (o0, o1), k, me.line(k))
        for k in range(1, zc)
    ]
    blocks = [send(rows.at[0], rows.at[k], (n0, n1), k, me.plane(k)) for k in range(1, 4)]
    wide = []
    for k in range(1, 4):
        there = me.plane(k)
        their_g = there[0] * 2 + there[2]
        wide.append(send(f_ref.at[their_g], fg_ref.at[me.g], (f0, f1), k, there))
    local[0].wait()
    for copy in pieces:
        copy.wait()
    relay = send(
        weights.at[:, me.c], weights.at[:, me.c], (s0, s1), 0, me.sibling()
    )
    relay.wait()
    kept = [move(weights, wg_ref, ls, 3)]

    def project(k, carry):
        @pl.when(k > 0)
        def _():
            trip(rows.at[0], rows.at[k], (n0, n1), k, me.plane(k)).wait_recv()

        at = (me.x ^ (k // 2)) * 2 + (me.y ^ (k % 2))
        out = dot(rows[k], weights[...].reshape(width, 3 * qw)).astype(BF16)
        for head in range(group):
            left = selection(qw, PAIR, head * HEAD_DIM, 0, HEAD_DIM)
            right = selection(qw, PAIR, head * HEAD_DIM - HEAD_DIM, HEAD_DIM, PAIR)
            slab = dot(out[:BLOCK, :qw], left) + dot(out[BLOCK:, :qw], right)
            packed[head, k, :BLOCK] = slab.astype(BF16)
            start = qw + head * PAIR
            packed[head, k, BLOCK:] = out[:, start : start + PAIR]
        for over in range(1, zc):
            trip(
                packed.at[(me.z ^ over) // per, k],
                a_ref.at[me.z, me.c, at],
                (z0, z1),
                k * zc + over,
                me.line(over),
            ).start()
        trip(
            packed.at[me.z // per, k], a_ref.at[me.z, me.c, at], (b0, b1), k * zc, me.sibling()
        ).start()
        pltpu.make_async_copy(
            packed.at[me.z // per, k], a_ref.at[me.z, me.c, at], ls.at[4 + k]
        ).start()
        return carry

    lax.fori_loop(0, 4, project, 0)
    kept.append(move(rows, ng_ref, ls, 8))
    for copy in outs + local[1:2]:
        copy.wait()
    mine = og_ref.at[me.x, :, me.y, me.c]
    out_rows = [send(mine, mine, (p0, p1), k, me.plane(k)) for k in range(1, 4)]

    def pass_on(step, carry):
        k, over = step // (zc - 1), step % (zc - 1) + 1
        at = (me.x ^ (k // 2)) * 2 + (me.y ^ (k % 2))
        there = me.z ^ over
        trip(
            packed.at[there // per, k],
            a_ref.at[me.z, me.c, at],
            (z0, z1),
            k * zc + over,
            me.line(over),
        ).wait()
        landed = a_ref.at[there, me.c, at]
        trip(landed, landed, (b0, b1), k * zc + over, me.sibling()).start()
        return carry

    lax.fori_loop(0, 4 * (zc - 1), pass_on, 0)
    for copy in out_rows:
        copy.wait()
    every = og_ref.at[:, :, :, me.c]
    last = send(every, every, (s0, s1), 1, me.sibling())

    def finish(step, carry):
        k, over = step // zc, step % zc
        at = (me.x ^ (k // 2)) * 2 + (me.y ^ (k % 2))
        landed = a_ref.at[me.z ^ over, me.c, at]
        trip(landed, landed, (b0, b1), k * zc + over, me.sibling()).wait()
        return carry

    lax.fori_loop(0, 4 * zc, finish, 0)
    for k in range(4):
        pltpu.make_async_copy(
            packed.at[me.z // per, k], a_ref.at[me.z, me.c, me.g], ls.at[4 + k]
        ).wait()
    for copy in [last] + local[2:] + kept + wide:
        copy.wait()
    for copy in blocks:
        copy.wait_send()


def head_exchange(zc, group, tokens, w_send, f_send, w_out):
    chips = 4 * zc
    own, width = tokens.shape
    piece = w_send.shape[1:]
    return exchange(
        functools.partial(head_kernel, zc, group),
        1,
        (
            struct((4, own, width)),
            struct((chips, 2) + piece),
            struct(f_send.shape),
            struct((2, zc, 2, 2) + w_out.shape),
            struct((zc, 2, 4, BLOCK + own, PAIR)),
        ),
        [VM, ANY, ANY, ANY],
        (ANY,) * 5,
        [
            pltpu.VMEM((4, own, width), BF16),
            pltpu.VMEM((chips, 2) + piece, BF16),
            pltpu.VMEM((group, 4, BLOCK + own, PAIR), BF16),
            DMA((9,)),
        ]
        + both(chips)
        + both(4)
        + both(4)
        + both(zc)
        + both(4)
        + both(4 * zc)
        + both(4 * zc)
        + both(2),
        (tokens, w_send, f_send, w_out),
        2 * 4 * own * width * width,
        16 << 20,
    )


def join_kernel(zc, s_ref, x_ref, w_ref, ob_ref, r_ref, n_ref, mine, theirs, slabs, ls, b0, b1, c0, c1):
    me = Place(zc)
    chips = 4 * zc
    heads, per = slabs.shape[:2]
    meet([me.any_chip(k) for k in range(1, chips)] + [me.sibling()])
    other = send(s_ref.at[:, 1 - me.c], theirs, (b0, b1), 0, me.sibling())
    own = move(s_ref.at[:, me.c], mine, ls, 0)
    own.wait()
    other.wait()
    mine[...] = mine[...] + theirs[...]
    head = me.g * (heads // 4) + me.z // per
    place = me.z % per
    keep = move(mine.at[me.z, me.g], slabs.at[head, place], ls, 1)
    sends = []
    for k in reversed(range(1, chips)):
        there = me.any_chip(k)
        their_g = there[0] * 2 + there[2]
        sends.append(
            send(mine.at[there[1], their_g], slabs.at[head, place], (c0, c1), k, there)
        )
    keep.wait()
    for copy in sends:
        copy.wait()
    for block in range(2):
        for pair in range(heads // 2):
            total = jnp.zeros((BLOCK, PAIR), F32)
            for side in range(2):
                slab = slabs[2 * pair + side, 0]
                for extra in range(1, per):
                    slab = slab + slabs[2 * pair + side, extra]
                pick = selection(
                    PAIR, PAIR, (block - side) * HEAD_DIM, side * HEAD_DIM, (side + 1) * HEAD_DIM
                )
                total = total + dot(slab, pick)
            ob_ref[block * BLOCK : (block + 1) * BLOCK, pair * PAIR : (pair + 1) * PAIR] = (
                total.astype(BF16)
            )
    residual = x_ref[...].astype(F32) + dot(ob_ref[...], w_ref[...])
    r_ref[...] = residual
    mean = jnp.mean(residual * residual, axis=-1, keepdims=True)
    n_ref[...] = (residual * lax.rsqrt(mean + EPS)).astype(BF16)


def join_exchange(zc, heads, slabs, tokens, w_out):
    chips = 4 * zc
    per = 4 * zc // heads
    half = (zc,) + slabs.shape[2:]
    shape = tokens.shape
    return exchange(
        functools.partial(join_kernel, zc),
        2,
        (struct(shape), struct(shape, F32), struct(shape)),
        [ANY, VM, VM],
        (VM,) * 3,
        [
            pltpu.VMEM(half, BF16),
            pltpu.VMEM(half, BF16),
            pltpu.VMEM((heads, per) + slabs.shape[3:], BF16),
            DMA((2,)),
        ]
        + both(1)
        + both(chips),
        (slabs, tokens, w_out),
        2 * shape[0] * shape[1] * shape[1],
        4 << 20,
    )


def middle_kernel(
    zc,
    n_ref,
    ca_ref,
    cb_ref,
    cc_ref,
    cd_ref,
    f_ref,
    wo_ref,
    r_ref,
    ob_ref,
    out_ref,
    dr_ref,
    sh_ref,
    do_ref,
    rows,
    cots,
    gate_w,
    up_w,
    down_w,
    hid,
    dgate,
    dup,
    c_out,
    c_in,
    stage,
    slabs,
    ls,
    n0,
    n1,
    c0,
    c1,
    d0,
    d1,
    b0,
    b1,
):
    me = Place(zc)
    chips = 4 * zc
    width = n_ref.shape[1]
    heads = slabs.shape[0]
    group = heads // 4
    per = zc // group
    loads = []
    for g in range(4):
        x, y = g // 2, g % 2
        loads.append(move(f_ref.at[:, :, 2 * g], gate_w.at[x, :, y], ls, 3 * g))
        loads.append(move(f_ref.at[:, :, 2 * g + 1], up_w.at[x, :, y], ls, 3 * g + 1))
    loads.append(move(f_ref.at[:, :, 8:], down_w, ls, 2))
    rows[0] = n_ref[...]
    for k, ref in enumerate((ca_ref, cb_ref, cc_ref, cd_ref)):
        cots[k] = ref[...]
    meet([me.any_chip(k) for k in range(1, chips)] + [me.sibling()])
    gathers = [send(rows.at[0], rows.at[k], (n0, n1), k, me.plane(k)) for k in range(1, 4)]
    for copy in loads:
        copy.wait()
    square = (width, width)

    def block(k, carry):
        @pl.when(k > 0)
        def _():
            trip(rows.at[0], rows.at[k], (n0, n1), k, me.plane(k)).wait_recv()

        gate_mat, up_mat = gate_w[...].reshape(square), up_w[...].reshape(square)
        gate = dot(rows[k], gate_mat)
        up = dot(rows[k], up_mat)
        back = nt_dot(cots[k], down_w[...].reshape(square))
        sig = jax.nn.sigmoid(gate)
        soft = gate * sig
        hid[k] = (soft * up).astype(BF16)
        dgate[k] = (back * up * sig * (1.0 + gate * (1.0 - sig))).astype(BF16)
        dup[k] = (back * soft).astype(BF16)
        c_out[k] = (nt_dot(dgate[k], gate_mat) + nt_dot(dup[k], up_mat)).astype(BF16)

        @pl.when(k > 0)
        def _():
            trip(c_out.at[k], c_in.at[k], (c0, c1), k, me.plane(k)).start()

        return carry

    lax.fori_loop(0, 4, block, 0)

    def finish_out(k, carry):
        out_ref[k] = dot(hid[k], down_w[...].reshape(square)).astype(BF16)
        return carry

    lax.fori_loop(0, 4, finish_out, 0)
    all_rows = (4 * n_ref.shape[0], width)
    left_t = stage.shape[0]
    stage_sq = [stage.at[i] for i in range(left_t)]

    def weight_grad(left, right, slot):
        chunk = 256
        for first in range(0, width, chunk):
            value = tn_dot(left[:, first : first + chunk], right).astype(BF16)
            stage[slot, first : first + chunk] = value

    shares = []

    def share(slot, which, by_rows):
        parts = stage_sq[slot].reshape(2, zc, 2, 2, width // (8 * zc), width)
        for g in range(4):
            x, y = g // 2, g % 2
            shares.append(
                move(parts.at[x, :, y], sh_ref.at[:, :, 3 * g + which], ls, 12 + 3 * g + which)
            )

    flat = lambda ref: ref[...].reshape(all_rows)
    weight_grad(flat(rows), flat(dgate), 0)
    share(0, 0, True)
    weight_grad(flat(rows), flat(dup), 1)
    share(1, 1, True)
    weight_grad(flat(hid), flat(cots), 2)
    shares.append(
        move(stage_sq[2].reshape(zc, 2, 4, width // (8 * zc), width), sh_ref.at[:, :, 12:], ls, 24)
    )
    total = c_out[0].astype(F32)
    for k in range(1, 4):
        trip(c_out.at[k], c_in.at[k], (c0, c1), k, me.plane(k)).wait_recv()
        total = total + c_in[k].astype(F32)
    residual = r_ref[...]
    scaling = lax.rsqrt(jnp.mean(residual * residual, axis=-1, keepdims=True) + EPS)
    normed = residual * scaling
    middle = jnp.mean(total * normed, axis=-1, keepdims=True)
    grad = cots[0].astype(F32) + scaling * (total - normed * middle)
    dr_ref[...] = grad
    low = grad.astype(BF16)
    back = nt_dot(low, wo_ref[...]).astype(BF16)
    for pair in range(heads // 2):
        two = back[:, pair * PAIR : (pair + 1) * PAIR]
        for side in range(2):
            left = selection(PAIR, PAIR, side * HEAD_DIM, 0, HEAD_DIM)
            right = selection(PAIR, PAIR, (side - 1) * HEAD_DIM, HEAD_DIM, PAIR)
            slab = dot(two[:BLOCK], left) + dot(two[BLOCK:], right)
            slabs[2 * pair + side] = slab.astype(BF16)
    to = do_ref.at[me.z, me.c, me.g]
    own = move(slabs.at[me.g * group + me.z // per], to, ls, 25)
    sends = []
    for k in reversed(range(1, chips)):
        there = me.any_chip(k)
        head = (there[0] * 2 + there[2]) * group + there[1] // per
        sends.append(send(slabs.at[head], to, (d0, d1), k, there))
    weight_grad(ob_ref[...], low, 3)
    share(3, 2, True)
    own.wait()
    for copy in sends:
        copy.wait()
    half = do_ref.at[:, me.c]
    relay = send(half, half, (b0, b1), 0, me.sibling())
    for copy in shares:
        copy.wait()
    for copy in gathers:
        copy.wait_send()
    for k in range(1, 4):
        trip(c_out.at[k], c_in.at[k], (c0, c1), k, me.plane(k)).wait_send()
    relay.wait()


def middle_exchange(zc, normed, cots, weights, w_out, residual, attn_rows):
    chips = 4 * zc
    own, width = normed.shape
    heads = width // HEAD_DIM
    piece = width // (8 * zc)
    blocks = pltpu.VMEM((4, own, width), BF16)
    wide = pltpu.VMEM((2, zc, 2, 2, piece, width), BF16)
    return exchange(
        functools.partial(middle_kernel, zc),
        3,
        (
            struct((4, own, width)),
            struct((own, width), F32),
            struct((zc, 2, 16, piece, width)),
            struct((zc, 2, 4, BLOCK, PAIR)),
        ),
        [VM] * 5 + [ANY] + [VM] * 3,
        (VM, VM, ANY, ANY),
        [blocks, blocks, wide, wide, pltpu.VMEM((zc, 2, 4, piece, width), BF16)]
        + [blocks] * 5
        + [pltpu.VMEM((4, width, width), BF16), pltpu.VMEM((heads, BLOCK, PAIR), BF16), DMA((26,))]
        + both(4)
        + both(4)
        + both(chips)
        + both(1),
        (normed, *cots, weights, w_out, residual, attn_rows),
        2 * 4 * own * width * width * 9,
        64 << 20,
    )


def tail_kernel(
    zc,
    d_ref,
    n_ref,
    w_ref,
    x_ref,
    g_ref,
    tg_ref,
    gw_ref,
    mine,
    theirs,
    landed,
    grads,
    c_out,
    c_in,
    stage,
    other_w,
    ls,
    b0,
    b1,
    z0,
    z1,
    c0,
    c1,
    s0,
    s1,
    w0,
    w1,
):
    me = Place(zc)
    chips = 4 * zc
    group, per = landed.shape[:2]
    qw = group * HEAD_DIM
    meet([me.any_chip(k) for k in range(1, chips)] + [me.sibling()])
    head, place = me.z // per, me.z % per

    def slot(k):
        return (me.x ^ (k // 2)) * 2 + (me.y ^ (k % 2))

    order = (3, 2, 1, 0)
    halves = []
    for k in order:
        halves.append(
            (
                send(d_ref.at[:, 1 - me.c, slot(k)], theirs.at[k], (b0, b1), k, me.sibling()),
                move(d_ref.at[:, me.c, slot(k)], mine.at[k], ls, k),
            )
        )
    for k, (far, near) in zip(order, halves):
        near.wait()
        far.wait()
        mine[k] = mine[k] + theirs[k]
        for over in range(1, zc):
            send(
                mine.at[k, me.z ^ over],
                landed.at[head, place, k],
                (z0, z1),
                k * zc + over,
                me.line(over),
            )
        move(mine.at[k, me.z], landed.at[head, place, k], ls, 4 + k)

    def block(step, carry):
        k = 3 - step
        pltpu.make_async_copy(
            mine.at[k, me.z], landed.at[head, place, k], ls.at[4 + k]
        ).wait()
        for over in range(1, zc):
            trip(
                mine.at[k, me.z ^ over],
                landed.at[head, place, k],
                (z0, z1),
                k * zc + over,
                me.line(over),
            ).wait()
        upper = jnp.zeros((BLOCK, qw), F32)
        lower = jnp.zeros((BLOCK, qw), F32)
        for h in range(group):
            slab = landed[h, 0, k]
            for extra in range(1, per):
                slab = slab + landed[h, extra, k]
            first, last = h * HEAD_DIM, (h + 1) * HEAD_DIM
            upper = upper + dot(slab[:BLOCK], selection(PAIR, qw, -first, first, last))
            lower = lower + dot(slab[:BLOCK], selection(PAIR, qw, HEAD_DIM - first, first, last))
            start = qw + h * PAIR
            grads[k, :, start : start + PAIR] = slab[BLOCK:]
        grads[k, :BLOCK, :qw] = upper.astype(BF16)
        grads[k, BLOCK:, :qw] = lower.astype(BF16)
        c_out[k] = nt_dot(grads[k], w_ref[...]).astype(BF16)

        @pl.when(k > 0)
        def _():
            trip(c_out.at[k], c_in.at[k], (c0, c1), k, me.plane(k)).start()

        return carry

    lax.fori_loop(0, 4, block, 0)
    width, cols = w_ref.shape
    all_rows = 4 * n_ref.shape[1]
    normed_all = n_ref[...].reshape(all_rows, width)
    grads_all = grads[...].reshape(all_rows, cols)
    piece = stage.shape[2]
    chunk = 256
    each = chunk // (2 * piece)
    for first in range(0, width, chunk):
        value = tn_dot(normed_all[:, first : first + chunk], grads_all).astype(BF16)
        at = first // (2 * piece)
        stage[at : at + each] = value.reshape(each, 2, piece, cols)
    swap = send(stage.at[:, 1 - me.c], other_w, (s0, s1), 0, me.sibling())
    swap.wait()

    def add(i, carry):
        other_w[i] = stage[i, me.c] + other_w[i]
        return carry

    lax.fori_loop(0, chips, add, 0)
    stay = move(other_w.at[me.chip], gw_ref.at[me.z, me.g], ls, 8)
    sends = []
    for k in reversed(range(1, chips)):
        there = me.any_chip(k)
        chip = (there[0] * zc + there[1]) * 2 + there[2]
        sends.append(send(other_w.at[chip], gw_ref.at[me.z, me.g], (w0, w1), k, there))
    total = c_out[0].astype(F32)
    for k in range(1, 4):
        trip(c_out.at[k], c_in.at[k], (c0, c1), k, me.plane(k)).wait()
        total = total + c_in[k].astype(F32)
    x = x_ref[...].astype(F32)
    scaling = lax.rsqrt(jnp.mean(x * x, axis=-1, keepdims=True) + EPS)
    normed = x * scaling
    middle = jnp.mean(total * normed, axis=-1, keepdims=True)
    tg_ref[...] = (g_ref[...] + scaling * (total - normed * middle)).astype(BF16)
    stay.wait()
    for copy in sends:
        copy.wait()


def tail_exchange(zc, group, slab_grads, n_all, weights, tokens, residual_grad):
    chips = 4 * zc
    per = zc // group
    own, width = tokens.shape
    cols = weights.shape[1]
    slab = slab_grads.shape[3:]
    piece = width // (2 * chips)
    blocks = pltpu.VMEM((4, own, width), BF16)
    return exchange(
        functools.partial(tail_kernel, zc),
        4,
        (struct((own, width)), struct((zc, 4, piece, cols))),
        [ANY] + [VM] * 4,
        (VM, ANY),
        [
            pltpu.VMEM((4, zc) + slab, BF16),
            pltpu.VMEM((4, zc) + slab, BF16),
            pltpu.VMEM((group, per, 4) + slab, BF16),
            pltpu.VMEM((4, own, cols), BF16),
            blocks,
            blocks,
            pltpu.VMEM((chips, 2, piece, cols), BF16),
            pltpu.VMEM((chips, piece, cols), BF16),
            DMA((9,)),
        ]
        + both(4)
        + both(4 * zc)
        + both(4)
        + both(1)
        + both(chips),
        (slab_grads, n_all, weights, tokens, residual_grad),
        2 * 4 * own * width * cols * 2,
        24 << 20,
    )


def share_kernel(zc, f_ref, gf_ref, ls, f0, f1):
    me = Place(zc)
    meet([me.plane(k) for k in range(1, 4)])
    copies = [move(f_ref.at[me.g], gf_ref.at[me.g], ls, 0)]
    for k in range(1, 4):
        there = me.plane(k)
        copies.append(
            send(f_ref.at[there[0] * 2 + there[2]], gf_ref.at[me.g], (f0, f1), k, there)
        )
    for copy in copies:
        copy.wait()


def share_exchange(zc, shares):
    return exchange(
        functools.partial(share_kernel, zc),
        5,
        struct(shares.shape),
        [ANY],
        ANY,
        [DMA((1,))] + both(4),
        (shares,),
        0,
        2 << 20,
    )


def segment_start(position, lens_ref):
    start = jnp.zeros_like(position)
    end = 0
    for j in range(lens_ref.shape[0]):
        end = end + lens_ref[j]
        start = jnp.where(position >= end, end, start)
    return start


def tile_of(turn, workers, worker):
    forward = turn * workers + worker
    backward = turn * workers + workers - 1 - worker
    return jnp.where((turn & 1) == 0, forward, backward)


def key_bounds(first, lens_ref):
    low_start = segment_start(first, lens_ref)
    high_start = segment_start(first + QTILE - 1, lens_ref)
    low = low_start // KTILE
    high = (first + QTILE + KTILE - 1) // KTILE
    plain = jnp.clip((high_start + KTILE - 1) // KTILE, low, high)
    stop = jnp.clip((first + 1) // KTILE, plain, high)
    return low, plain, stop, high


def visible(first, tile, starts):
    key = tile * KTILE + lax.broadcasted_iota(jnp.int32, (KTILE, QTILE), 0)
    query = first + lax.broadcasted_iota(jnp.int32, (KTILE, QTILE), 1)
    return (key <= query) & (key >= starts)


def forward_kernel(
    workers, anchor_ref, lens_ref, who_ref, a_ref, o_ref, kv_ref, kvt_ref, q_ref, qt_ref, ot_ref, l_ref, inv, pick
):
    blocks = anchor_ref.shape[0]
    turns = q_ref.shape[0]
    per = QTILE // BLOCK
    worker = who_ref[0]

    def note(i, carry):
        inv[anchor_ref[i]] = i
        return carry

    lax.fori_loop(0, blocks, note, 0)
    for half in range(2):
        pick[half] = selection(PAIR, PAIR, half * HEAD_DIM, 0, HEAD_DIM)
        row = lax.broadcasted_iota(jnp.int32, (PAIR, PAIR), 0)
        column = lax.broadcasted_iota(jnp.int32, (PAIR, PAIR), 1)
        hit = (column == row + half * HEAD_DIM) & (row < HEAD_DIM)
        pick[2 + half] = hit.astype(F32).astype(BF16)
    same = lax.broadcasted_iota(jnp.int32, (PAIR, PAIR), 0)
    pick[4] = (same == lax.broadcasted_iota(jnp.int32, (PAIR, PAIR), 1)).astype(F32).astype(BF16)
    o_ref[...] = jnp.zeros_like(o_ref)

    def order(i, carry):
        where = inv[i]
        slab, half = where >> 1, where & 1
        block = a_ref[slab, pl.ds(pl.multiple_of(BLOCK + half * BLOCK, BLOCK), BLOCK), :]
        at = pl.ds(pl.multiple_of(i * BLOCK, BLOCK), BLOCK)
        kv_ref[at, :] = block
        kvt_ref[:, at] = nt_dot(pick[4], block).astype(BF16)
        return carry

    lax.fori_loop(0, blocks, order, 0)

    def one_tile(turn, carry):
        tile = tile_of(turn, workers, worker)
        first = tile * QTILE
        for b in range(per):
            where = inv[tile * per + b]
            slab, half = where >> 1, where & 1
            rows = a_ref[slab, :BLOCK, :]
            q_ref[turn, b * BLOCK : (b + 1) * BLOCK, :] = (dot(rows, pick[half]) * 0.125).astype(BF16)
            qt_ref[turn, :, b * BLOCK : (b + 1) * BLOCK] = (
                nt_dot(pick[2 + half], rows) * 0.125
            ).astype(BF16)
        query = qt_ref[turn]
        starts = segment_start(first + lax.broadcasted_iota(jnp.int32, (1, QTILE), 1), lens_ref)
        low, plain, stop, high = key_bounds(first, lens_ref)

        def step(masked, kt, state):
            top, total, acc = state
            at = pl.ds(pl.multiple_of(kt * KTILE, KTILE), KTILE)
            scores = dot(kv_ref[at, :], query)
            if masked:
                seen = visible(first, kt, starts)
                scores = jnp.where(seen, scores, MASKED)
            new_top = jnp.maximum(top, jnp.max(scores, axis=0, keepdims=True))
            factor = jnp.exp(top - new_top)
            weights = jnp.exp(scores - new_top)
            if masked:
                weights = jnp.where(seen, weights, 0.0)
            total = total * factor + jnp.sum(weights, axis=0, keepdims=True)
            acc = acc * factor + dot(kvt_ref[HEAD_DIM:, at], weights.astype(BF16))
            return (new_top, total, acc)

        state = (
            jnp.full((1, QTILE), MASKED, F32),
            jnp.zeros((1, QTILE), F32),
            jnp.zeros((HEAD_DIM, QTILE), F32),
        )
        state = lax.fori_loop(low, plain, functools.partial(step, True), state)
        state = lax.fori_loop(plain, stop, functools.partial(step, False), state)
        top, total, acc = lax.fori_loop(stop, high, functools.partial(step, True), state)
        out = acc / total
        ot_ref[turn] = out
        l_ref[turn] = top + jnp.log(total)
        narrow = out.astype(BF16)
        for b in range(per):
            where = inv[tile * per + b]
            slab, half = where >> 1, where & 1
            piece = tn_dot(narrow[:, b * BLOCK : (b + 1) * BLOCK], pick[2 + half, :HEAD_DIM, :])
            o_ref[slab] = o_ref[slab] + piece.astype(BF16)
        return carry

    lax.fori_loop(0, turns, one_tile, 0)


def attention_forward(workers, anchors, lengths, who, packed):
    slabs = packed.shape[0]
    rows = slabs * 2 * BLOCK
    turns = rows // QTILE // workers
    return pl.pallas_call(
        functools.partial(forward_kernel, workers),
        out_shape=(
            struct((slabs, BLOCK, PAIR)),
            struct((rows, PAIR)),
            struct((PAIR, rows)),
            struct((turns, QTILE, PAIR)),
            struct((turns, PAIR, QTILE)),
            struct((turns, HEAD_DIM, QTILE), F32),
            struct((turns, 1, QTILE), F32),
        ),
        in_specs=[SM, SM, SM, VM],
        out_specs=(VM,) * 7,
        scratch_shapes=[pltpu.SMEM((2 * slabs,), jnp.int32), pltpu.VMEM((5, PAIR, PAIR), BF16)],
        compiler_params=pltpu.CompilerParams(vmem_limit_bytes=60 << 20),
        cost_estimate=pl.CostEstimate(
            flops=rows * rows * 64, bytes_accessed=rows * 1024, transcendentals=rows * rows // 8
        ),
    )(anchors, lengths, who, packed)


def backward_kernel(
    workers,
    anchor_ref,
    lens_ref,
    who_ref,
    d_ref,
    kv_ref,
    kvt_ref,
    q_ref,
    qt_ref,
    ot_ref,
    l_ref,
    g_ref,
    inv,
    pick,
    dn,
    dt,
    acc,
):
    blocks = anchor_ref.shape[0]
    turns = q_ref.shape[0]
    per = QTILE // BLOCK
    worker = who_ref[0]

    def note(i, carry):
        inv[anchor_ref[i]] = i
        return carry

    lax.fori_loop(0, blocks, note, 0)
    row = lax.broadcasted_iota(jnp.int32, (PAIR, PAIR), 0)
    column = lax.broadcasted_iota(jnp.int32, (PAIR, PAIR), 1)
    for half in range(2):
        hit = (row - half * HEAD_DIM == column - HEAD_DIM) & (column >= HEAD_DIM)
        pick[half] = hit.astype(F32).astype(BF16)
        hit = (column - half * HEAD_DIM == row - HEAD_DIM) & (row >= HEAD_DIM)
        pick[2 + half] = hit.astype(F32).astype(BF16)
        hit = (column == row + half * HEAD_DIM) & (row < HEAD_DIM)
        pick[4 + half] = hit.astype(F32).astype(BF16)
    acc[...] = jnp.zeros_like(acc)
    g_ref[:, :BLOCK, :] = jnp.zeros((g_ref.shape[0], BLOCK, PAIR), BF16)

    def one_tile(turn, carry):
        tile = tile_of(turn, workers, worker)
        first = tile * QTILE
        for b in range(per):
            where = inv[tile * per + b]
            slab, half = where >> 1, where & 1
            rows = d_ref[slab]
            dn[b * BLOCK : (b + 1) * BLOCK, :] = dot(rows, pick[half]).astype(BF16)
            dt[:, b * BLOCK : (b + 1) * BLOCK] = nt_dot(pick[2 + half], rows).astype(BF16)
        query, query_rows = qt_ref[turn], q_ref[turn]
        grad, grad_rows = dt[...], dn[...]
        norm = l_ref[turn]
        delta = jnp.sum(grad[HEAD_DIM:].astype(F32) * ot_ref[turn], axis=0, keepdims=True)
        starts = segment_start(first + lax.broadcasted_iota(jnp.int32, (1, QTILE), 1), lens_ref)
        low, plain, stop, high = key_bounds(first, lens_ref)

        def step(masked, kt, total):
            at = pl.ds(pl.multiple_of(kt * KTILE, KTILE), KTILE)
            keys = kv_ref[at, :]
            weights = jnp.exp(dot(keys, query) - norm)
            if masked:
                weights = jnp.where(visible(first, kt, starts), weights, 0.0)
            score_grad = (weights * (dot(keys, grad) - delta)).astype(BF16)
            acc[at, :] += dot(score_grad, query_rows) + dot(weights.astype(BF16), grad_rows)
            return total + dot(kvt_ref[:HEAD_DIM, at], score_grad)

        total = jnp.zeros((HEAD_DIM, QTILE), F32)
        total = lax.fori_loop(low, plain, functools.partial(step, True), total)
        total = lax.fori_loop(plain, stop, functools.partial(step, False), total)
        total = lax.fori_loop(stop, high, functools.partial(step, True), total)
        narrow = (total * 0.125).astype(BF16)
        for b in range(per):
            where = inv[tile * per + b]
            slab, half = where >> 1, where & 1
            piece = tn_dot(narrow[:, b * BLOCK : (b + 1) * BLOCK], pick[4 + half, :HEAD_DIM, :])
            g_ref[slab, :BLOCK] = g_ref[slab, :BLOCK] + piece.astype(BF16)
        return carry

    lax.fori_loop(0, turns, one_tile, 0)

    def place(i, carry):
        where = inv[i]
        slab, half = where >> 1, where & 1
        at = pl.ds(pl.multiple_of(i * BLOCK, BLOCK), BLOCK)
        to = pl.ds(pl.multiple_of(BLOCK + half * BLOCK, BLOCK), BLOCK)
        g_ref[slab, to, :] = acc[at, :].astype(BF16)
        return carry

    lax.fori_loop(0, blocks, place, 0)


def attention_backward(workers, anchors, lengths, who, grads, kept):
    slabs = grads.shape[0]
    rows = slabs * 2 * BLOCK
    return pl.pallas_call(
        functools.partial(backward_kernel, workers),
        out_shape=struct((slabs, 3 * BLOCK, PAIR)),
        in_specs=[SM, SM, SM] + [VM] * 7,
        out_specs=VM,
        scratch_shapes=[
            pltpu.SMEM((2 * slabs,), jnp.int32),
            pltpu.VMEM((6, PAIR, PAIR), BF16),
            pltpu.VMEM((QTILE, PAIR), BF16),
            pltpu.VMEM((PAIR, QTILE), BF16),
            pltpu.VMEM((rows, PAIR), F32),
        ],
        compiler_params=pltpu.CompilerParams(vmem_limit_bytes=60 << 20),
        cost_estimate=pl.CostEstimate(
            flops=rows * rows * 160, bytes_accessed=rows * 1024, transcendentals=rows * rows // 8
        ),
    )(anchors, lengths, who, grads, *kept)


def around(value, k):
    return lax.ppermute(value, ("head", "y"), [(i, i ^ k) for i in range(4)])


def body(
    zc,
    tokens,
    cotangent,
    norm1_gain,
    w_query,
    w_key,
    w_value,
    w_out,
    norm2_gain,
    w_gate,
    w_up,
    w_down,
    block_anchor,
    seq_lengths,
):
    width = tokens.shape[1]
    heads = width // HEAD_DIM
    group = heads // 4
    per_head = zc // group
    workers = 2 * per_head
    feature_rows = w_query.shape[0]
    hidden = w_gate.shape[1]
    units = w_down.shape[0]
    slice_units = hidden // 4

    low = lambda v: v.astype(BF16).astype(F32)
    gain1, gain2 = low(norm1_gain)[:, None], low(norm2_gain)[:, None]
    query_w, key_w, value_w = low(w_query), low(w_key), low(w_value)
    gate_w, up_w = low(w_gate), low(w_up)
    q_part = (gain1 * query_w).reshape(feature_rows, 4, group * HEAD_DIM)
    kv_part = jnp.stack(
        [
            (gain1 * key_w).reshape(feature_rows, 4, group, HEAD_DIM),
            (gain1 * value_w).reshape(feature_rows, 4, group, HEAD_DIM),
        ],
        axis=3,
    ).reshape(feature_rows, 4, group * PAIR)
    w_send = jnp.transpose(jnp.concatenate([q_part, kv_part], axis=2).astype(BF16), (1, 0, 2))

    def slices(weight):
        return jnp.transpose(
            weight.reshape(feature_rows, 2, zc, 2, 2 * units), (1, 3, 0, 2, 4)
        ).reshape(4, feature_rows, slice_units)

    f_send = jnp.stack([slices((gain2 * gate_w).astype(BF16)), slices((gain2 * up_w).astype(BF16))], axis=1)

    n1_all, qkv_w, f_all, out_all, by_head = head_exchange(
        zc, group, tokens, w_send, f_send, w_out.astype(BF16)
    )
    qkv_w = qkv_w.reshape(width, 3 * group * HEAD_DIM)
    out_mat = out_all.reshape(width, width)

    ffn_in = jnp.concatenate(
        [f_all.reshape(8, feature_rows, width), w_down.astype(BF16).reshape(4, feature_rows, width)], axis=0
    )
    ffn_all = lax.all_gather(ffn_in, ("z", "core"), axis=0, tiled=False).reshape(
        zc, 2, 12, feature_rows, width
    )
    by_head, near = lax.optimization_barrier((by_head, cotangent))
    cots = [cotangent] + [around(near, k) for k in range(1, 4)]

    anchors = jnp.transpose(block_anchor.reshape(2, zc, 2, 2, 2), (1, 3, 0, 2, 4)).reshape(-1)
    who = ((lax.axis_index("z") % per_head) * 2 + lax.axis_index("core")).astype(jnp.int32).reshape(1)
    slab_count = zc * 8
    o_slabs, *kept = attention_forward(
        workers, anchors, seq_lengths, who, by_head.reshape((slab_count,) + by_head.shape[3:])
    )
    attn_rows, residual, normed_two = join_exchange(
        zc, heads, o_slabs.reshape(zc, 2, 4, BLOCK, PAIR), tokens, out_mat
    )
    out_parts, residual_grad, shares, do_heads = middle_exchange(
        zc, normed_two, cots, ffn_all, out_mat, residual, attn_rows
    )
    outs = [out_parts[0]] + [around(out_parts[k], k) for k in range(1, 4)]
    shares = lax.psum_scatter(
        shares.reshape(zc * 2 * 16, feature_rows, width), ("z", "core"), scatter_dimension=0, tiled=True
    )
    grad_heads = attention_backward(
        workers, anchors, seq_lengths, who, do_heads.reshape(slab_count, BLOCK, PAIR), kept
    )
    tokens_grad, w_all = tail_exchange(
        zc,
        group,
        grad_heads.reshape(zc, 2, 4, 3 * BLOCK, PAIR),
        n1_all,
        qkv_w,
        tokens,
        residual_grad,
    )
    shares, tokens_grad = lax.optimization_barrier((shares, tokens_grad))
    f_grad = share_exchange(zc, shares[:12].reshape(4, 3, feature_rows, width))
    down_share = shares[12:].reshape(units, width)

    output = (residual + sum(v.astype(F32) for v in outs)).astype(BF16)
    w_sum = jnp.sum(w_all.astype(F32), axis=0)
    q_cols = group * HEAD_DIM
    query_raw = jnp.transpose(w_sum[:, :, :q_cols], (1, 0, 2)).reshape(feature_rows, width)
    kv_raw = w_sum[:, :, q_cols:].reshape(4, feature_rows, group, 2, HEAD_DIM)
    key_raw = jnp.transpose(kv_raw[:, :, :, 0], (1, 0, 2, 3)).reshape(feature_rows, width)
    value_raw = jnp.transpose(kv_raw[:, :, :, 1], (1, 0, 2, 3)).reshape(feature_rows, width)
    gain1_grad = jnp.sum(query_raw * query_w + key_raw * key_w + value_raw * value_w, axis=1)

    def unslice(grad):
        return jnp.transpose(
            grad.astype(F32).reshape(2, 2, feature_rows, zc, 2 * units), (2, 0, 3, 1, 4)
        ).reshape(feature_rows, hidden)

    gate_raw, up_raw = unslice(f_grad[:, 0]), unslice(f_grad[:, 1])
    gain2_grad = jnp.sum(gate_raw * gate_w + up_raw * up_w, axis=1)
    out_share = jnp.sum(f_grad[:, 2].astype(F32), axis=0)
    return (
        output,
        tokens_grad,
        gain1_grad,
        gain1 * query_raw,
        gain1 * key_raw,
        gain1 * value_raw,
        out_share,
        gain2_grad,
        gain2 * gate_raw,
        gain2 * up_raw,
        down_share.astype(F32),
    )


def solution(mesh):
    blk = mesh.shape["blk"]
    grid = Mesh(mesh.devices.reshape(mesh.shape["head"], blk // 4, 2, 2), AXES)
    rows, vector, whole = P(AXES, None), P(AXES), P()
    return jax.shard_map(
        functools.partial(body, blk // 4),
        mesh=grid,
        in_specs=(rows, rows, vector, rows, rows, rows, rows, vector, rows, rows, rows, whole, whole),
        out_specs=(rows, rows, vector, rows, rows, rows, rows, vector, rows, rows, rows),
        check_vma=False,
    )
```

```python
import functools

import jax
import jax.numpy as jnp
from jax import lax
from jax.experimental import pallas as pl
from jax.experimental.pallas import tpu as pltpu
from jax.sharding import Mesh
from jax.sharding import PartitionSpec as P

HEAD_DIM = 64
BLOCK = 128
PAIR = 128
EPS = 1e-06
MASKED = -1e30
LOWEST = -1e20
QTILE = 512
KTILE = 512
AXES = ("head", "z", "y", "core")
IDS = pl.DeviceIdType.MESH
F32 = jnp.float32
BF16 = jnp.bfloat16
ANY = pl.BlockSpec(memory_space=pl.ANY)
VM = pl.BlockSpec(memory_space=pltpu.VMEM)
SM = pl.BlockSpec(memory_space=pltpu.SMEM)


def struct(shape, dtype=BF16):
    return jax.ShapeDtypeStruct(tuple(shape), dtype)


def nt_dot(a, b):
    return lax.dot_general(a, b, (((1,), (1,)), ((), ())), preferred_element_type=F32)


def tn_dot(a, b):
    return lax.dot_general(a, b, (((0,), (0,)), ((), ())), preferred_element_type=F32)


def dot(a, b):
    return jnp.dot(a, b, preferred_element_type=F32)


def selection(rows, columns, shift, first=0, last=None):
    last = columns if last is None else last
    row = lax.broadcasted_iota(jnp.int32, (rows, columns), 0)
    column = lax.broadcasted_iota(jnp.int32, (rows, columns), 1)
    hit = (row == column + shift) & (column >= first) & (column < last)
    return hit.astype(F32).astype(BF16)


def pair_up(first, first_half, second, second_half):
    lane = lax.broadcasted_iota(jnp.int32, first.shape, 1)
    left = first if first_half == 0 else pltpu.roll(first, HEAD_DIM, 1)
    right = second if second_half == 1 else pltpu.roll(second, HEAD_DIM, 1)
    return jnp.where(lane < HEAD_DIM, left, right)


def column_of(row):
    count = row.shape[1]
    i = lax.broadcasted_iota(jnp.int32, (count, count), 0)
    j = lax.broadcasted_iota(jnp.int32, (count, count), 1)
    return jnp.sum(jnp.where(i == j, row, 0.0), axis=1, keepdims=True)


def row_of(column):
    count = column.shape[0]
    i = lax.broadcasted_iota(jnp.int32, (count, count), 0)
    j = lax.broadcasted_iota(jnp.int32, (count, count), 1)
    return jnp.sum(jnp.where(i == j, column, 0.0), axis=0, keepdims=True)


def low(value):
    return value.astype(BF16).astype(F32)


def lanes(index):
    return slice(index * PAIR, (index + 1) * PAIR)


class Place:
    def __init__(self, z_count):
        self.x, self.z, self.y, self.c = (lax.axis_index(a) for a in AXES)
        self.g = self.x * 2 + self.y
        self.chip = (self.x * z_count + self.z) * 2 + self.y

    def sibling(self):
        return (self.x, self.z, self.y, 1 - self.c)

    def plane(self, k):
        return (self.x ^ (k // 2), self.z, self.y ^ (k % 2), self.c)

    def line(self, k):
        return (self.x, self.z ^ k, self.y, self.c)

    def any_chip(self, k):
        return (self.x ^ (k // 2 % 2), self.z ^ (k // 4), self.y ^ (k % 2), self.c)


def meet(peers):
    barrier = pltpu.get_barrier_semaphore()
    for peer in peers:
        pl.semaphore_signal(barrier, inc=1, device_id=peer, device_id_type=IDS)
    pl.semaphore_wait(barrier, len(peers))


def trip(source, target, sems, index, device):
    return pltpu.make_async_remote_copy(
        src_ref=source,
        dst_ref=target,
        send_sem=sems[0].at[index],
        recv_sem=sems[1].at[index],
        device_id=device,
        device_id_type=IDS,
    )


def send(*given):
    copy = trip(*given)
    copy.start()
    return copy


def move(source, target, sems, index):
    copy = pltpu.make_async_copy(source, target, sems.at[index])
    copy.start()
    return copy


DMA = pltpu.SemaphoreType.DMA


def both(count):
    return [DMA((count,)), DMA((count,))]


def exchange(kernel, ident, out_shape, in_specs, out_specs, scratch, args, flops, sent):
    return pl.pallas_call(
        kernel,
        out_shape=out_shape,
        in_specs=in_specs,
        out_specs=out_specs,
        scratch_shapes=scratch,
        compiler_params=pltpu.CompilerParams(
            collective_id=ident, has_side_effects=True, vmem_limit_bytes=56 << 20
        ),
        cost_estimate=pl.CostEstimate(flops=flops, bytes_accessed=sent, transcendentals=0),
    )(*args)


def head_kernel(
    zc,
    group,
    t_ref,
    q_w,
    k_w,
    v_w,
    o_w,
    g_w,
    u_w,
    d_w,
    gain1,
    gain2,
    ng_ref,
    wg_ref,
    fg_ref,
    og_ref,
    a_ref,
    w_ref,
    f_ref,
    o_ref,
    e_ref,
    rows,
    weights,
    packed,
    ls,
    w0,
    w1,
    n0,
    n1,
    f0,
    f1,
    o0,
    o1,
    p0,
    p1,
    z0,
    z1,
    b0,
    b1,
    s0,
    s1,
):
    me = Place(zc)
    chips = 4 * zc
    per = zc // group
    qw = group * HEAD_DIM
    width = t_ref.shape[1]
    first_gain, second_gain = column_of(low(gain1[...])), column_of(low(gain2[...]))
    for g in range(4):
        at = slice(g * qw, (g + 1) * qw)
        w_ref[g, :, :qw] = (first_gain * low(q_w[:, at])).astype(BF16)
        for pair in range(group // 2):
            at = lanes(g * group // 2 + pair)
            key, value = first_gain * low(k_w[:, at]), first_gain * low(v_w[:, at])
            for half in range(2):
                start = qw + (2 * pair + half) * PAIR
                w_ref[g, :, start : start + PAIR] = pair_up(key, half, value, half).astype(BF16)
    o_ref[...] = o_w[...].astype(BF16)
    e_ref[...] = d_w[...].astype(BF16).reshape(e_ref.shape)
    x = t_ref[...].astype(F32)
    rows[0] = (x * lax.rsqrt(jnp.mean(x * x, axis=-1, keepdims=True) + EPS)).astype(BF16)
    meet([me.any_chip(k) for k in range(1, chips)] + [me.sibling()])
    local = [
        move(w_ref.at[me.g], weights.at[me.chip, me.c], ls, 0),
        move(o_ref, og_ref.at[me.x, me.z, me.y, me.c], ls, 1),
    ]
    pieces = []
    for k in reversed(range(1, chips)):
        there = me.any_chip(k)
        their_g = there[0] * 2 + there[2]
        pieces.append(
            send(w_ref.at[their_g], weights.at[me.chip, me.c], (w0, w1), k, there)
        )
    outs = [
        send(o_ref, og_ref.at[me.x, me.z, me.y, me.c], (o0, o1), k, me.line(k))
        for k in range(1, zc)
    ]
    blocks = [send(rows.at[0], rows.at[k], (n0, n1), k, me.plane(k)) for k in range(1, 4)]
    units = g_w.shape[1] // (4 * zc)
    for which, ref in enumerate((g_w, u_w)):
        for g in range(4):
            px, py = g // 2, g % 2
            if units % PAIR == 0:
                for z in range(zc):
                    at = ((px * zc + z) * 2 + py) * units
                    f_ref[g, which, :, z * units : (z + 1) * units] = (
                        second_gain * low(ref[:, at : at + units])
                    ).astype(BF16)
            else:
                for z in range(0, zc, 2):
                    near, far = (second_gain * low(ref[:, lanes(px * zc + i)]) for i in (z, z + 1))
                    f_ref[g, which, :, lanes(z // 2)] = pair_up(near, py, far, py).astype(BF16)
    wide = [
        move(f_ref.at[me.g], fg_ref.at[pl.ds(2 * me.g, 2)], ls, 2),
        move(e_ref, fg_ref.at[pl.ds(8, 4)], ls, 9),
    ]
    for k in range(1, 4):
        there = me.plane(k)
        their_g = there[0] * 2 + there[2]
        wide.append(send(f_ref.at[their_g], fg_ref.at[pl.ds(2 * me.g, 2)], (f0, f1), k, there))
    local[0].wait()
    for copy in pieces:
        copy.wait()
    relay = send(
        weights.at[:, me.c], weights.at[:, me.c], (s0, s1), 0, me.sibling()
    )
    relay.wait()
    kept = [move(weights, wg_ref, ls, 3)]

    def project(k, carry):
        @pl.when(k > 0)
        def _():
            trip(rows.at[0], rows.at[k], (n0, n1), k, me.plane(k)).wait_recv()

        at = (me.x ^ (k // 2)) * 2 + (me.y ^ (k % 2))
        out = dot(rows[k], weights[...].reshape(width, 3 * qw)).astype(BF16)
        for head in range(group):
            left = selection(qw, PAIR, head * HEAD_DIM, 0, HEAD_DIM)
            right = selection(qw, PAIR, head * HEAD_DIM - HEAD_DIM, HEAD_DIM, PAIR)
            slab = dot(out[:BLOCK, :qw], left) + dot(out[BLOCK:, :qw], right)
            packed[head, k, :BLOCK] = slab.astype(BF16)
            start = qw + head * PAIR
            packed[head, k, BLOCK:] = out[:, start : start + PAIR]
        for over in range(1, zc):
            trip(
                packed.at[(me.z ^ over) // per, k],
                a_ref.at[me.z, me.c, at],
                (z0, z1),
                k * zc + over,
                me.line(over),
            ).start()
        trip(
            packed.at[me.z // per, k], a_ref.at[me.z, me.c, at], (b0, b1), k * zc, me.sibling()
        ).start()
        pltpu.make_async_copy(
            packed.at[me.z // per, k], a_ref.at[me.z, me.c, at], ls.at[4 + k]
        ).start()
        return carry

    lax.fori_loop(0, 4, project, 0)
    kept.append(move(rows, ng_ref, ls, 8))
    for copy in outs + local[1:2]:
        copy.wait()
    mine = og_ref.at[me.x, :, me.y, me.c]
    out_rows = [send(mine, mine, (p0, p1), k, me.plane(k)) for k in range(1, 4)]

    def pass_on(step, carry):
        k, over = step // (zc - 1), step % (zc - 1) + 1
        at = (me.x ^ (k // 2)) * 2 + (me.y ^ (k % 2))
        there = me.z ^ over
        trip(
            packed.at[there // per, k],
            a_ref.at[me.z, me.c, at],
            (z0, z1),
            k * zc + over,
            me.line(over),
        ).wait()
        landed = a_ref.at[there, me.c, at]
        trip(landed, landed, (b0, b1), k * zc + over, me.sibling()).start()
        return carry

    lax.fori_loop(0, 4 * (zc - 1), pass_on, 0)
    for copy in out_rows:
        copy.wait()
    every = og_ref.at[:, :, :, me.c]
    last = send(every, every, (s0, s1), 1, me.sibling())

    def finish(step, carry):
        k, over = step // zc, step % zc
        at = (me.x ^ (k // 2)) * 2 + (me.y ^ (k % 2))
        landed = a_ref.at[me.z ^ over, me.c, at]
        trip(landed, landed, (b0, b1), k * zc + over, me.sibling()).wait()
        return carry

    lax.fori_loop(0, 4 * zc, finish, 0)
    for k in range(4):
        pltpu.make_async_copy(
            packed.at[me.z // per, k], a_ref.at[me.z, me.c, me.g], ls.at[4 + k]
        ).wait()
    for copy in [last] + kept + wide:
        copy.wait()
    for copy in blocks:
        copy.wait_send()


def head_exchange(zc, group, tokens, matrices, gains):
    chips = 4 * zc
    own, width = tokens.shape
    count = matrices[0].shape[0]
    piece = (count, 3 * group * HEAD_DIM)
    return exchange(
        functools.partial(head_kernel, zc, group),
        1,
        (
            struct((4, own, width)),
            struct((chips, 2) + piece),
            struct((12, count, width)),
            struct((2, zc, 2, 2, count, width)),
            struct((zc, 2, 4, BLOCK + own, PAIR)),
        ),
        [VM] * 10,
        (ANY,) * 5,
        [
            pltpu.VMEM((4,) + piece, BF16),
            pltpu.VMEM((4, 2, count, width), BF16),
            pltpu.VMEM((count, width), BF16),
            pltpu.VMEM((4, count, width), BF16),
            pltpu.VMEM((4, own, width), BF16),
            pltpu.VMEM((chips, 2) + piece, BF16),
            pltpu.VMEM((group, 4, BLOCK + own, PAIR), BF16),
            DMA((10,)),
        ]
        + both(chips)
        + both(4)
        + both(4)
        + both(zc)
        + both(4)
        + both(4 * zc)
        + both(4 * zc)
        + both(2),
        (tokens, *matrices, *(g.reshape(1, -1) for g in gains)),
        2 * 4 * own * width * width,
        16 << 20,
    )


def join_kernel(zc, s_ref, x_ref, w_ref, ob_ref, r_ref, n_ref, mine, theirs, slabs, ls, b0, b1, c0, c1):
    me = Place(zc)
    chips = 4 * zc
    heads, per = slabs.shape[:2]
    meet([me.any_chip(k) for k in range(1, chips)] + [me.sibling()])
    other = send(s_ref.at[:, 1 - me.c], theirs, (b0, b1), 0, me.sibling())
    own = move(s_ref.at[:, me.c], mine, ls, 0)
    own.wait()
    other.wait()
    mine[...] = mine[...] + theirs[...]
    head = me.g * (heads // 4) + me.z // per
    place = me.z % per
    keep = move(mine.at[me.z, me.g], slabs.at[head, place], ls, 1)
    sends = []
    for k in reversed(range(1, chips)):
        there = me.any_chip(k)
        their_g = there[0] * 2 + there[2]
        sends.append(
            send(mine.at[there[1], their_g], slabs.at[head, place], (c0, c1), k, there)
        )
    keep.wait()
    for copy in sends:
        copy.wait()
    for block in range(2):
        for pair in range(heads // 2):
            total = jnp.zeros((BLOCK, PAIR), F32)
            for side in range(2):
                slab = slabs[2 * pair + side, 0]
                for extra in range(1, per):
                    slab = slab + slabs[2 * pair + side, extra]
                pick = selection(
                    PAIR, PAIR, (block - side) * HEAD_DIM, side * HEAD_DIM, (side + 1) * HEAD_DIM
                )
                total = total + dot(slab, pick)
            ob_ref[block * BLOCK : (block + 1) * BLOCK, pair * PAIR : (pair + 1) * PAIR] = (
                total.astype(BF16)
            )
    residual = x_ref[...].astype(F32) + dot(ob_ref[...], w_ref[...])
    r_ref[...] = residual
    mean = jnp.mean(residual * residual, axis=-1, keepdims=True)
    n_ref[...] = (residual * lax.rsqrt(mean + EPS)).astype(BF16)


def join_exchange(zc, heads, slabs, tokens, w_out):
    chips = 4 * zc
    per = 4 * zc // heads
    half = (zc,) + slabs.shape[2:]
    shape = tokens.shape
    return exchange(
        functools.partial(join_kernel, zc),
        2,
        (struct(shape), struct(shape, F32), struct(shape)),
        [ANY, VM, VM],
        (VM,) * 3,
        [
            pltpu.VMEM(half, BF16),
            pltpu.VMEM(half, BF16),
            pltpu.VMEM((heads, per) + slabs.shape[3:], BF16),
            DMA((2,)),
        ]
        + both(1)
        + both(chips),
        (slabs, tokens, w_out),
        2 * shape[0] * shape[1] * shape[1],
        4 << 20,
    )


def middle_kernel(
    zc,
    n_ref,
    ca_ref,
    cb_ref,
    cc_ref,
    cd_ref,
    f_ref,
    out_ref,
    cs_ref,
    sh_ref,
    rows,
    cots,
    gate_w,
    up_w,
    down_w,
    hid,
    dgate,
    dup,
    c_out,
    c_in,
    stage,
    ls,
    n0,
    n1,
    c0,
    c1,
):
    me = Place(zc)
    width = n_ref.shape[1]
    rows[0] = n_ref[...]
    meet([me.plane(k) for k in range(1, 4)])
    farthest = send(rows.at[0], rows.at[3], (n0, n1), 3, me.plane(3))
    loads = []
    for g in range(4):
        x, y = g // 2, g % 2
        loads.append(move(f_ref.at[:, :, 2 * g], gate_w.at[x, :, y], ls, 3 * g))
        loads.append(move(f_ref.at[:, :, 2 * g + 1], up_w.at[x, :, y], ls, 3 * g + 1))
    loads.append(move(f_ref.at[:, :, 8:], down_w, ls, 2))
    for k, ref in enumerate((ca_ref, cb_ref, cc_ref, cd_ref)):
        cots[k] = ref[...]
    for copy in loads:
        copy.wait()
    square = (width, width)

    def block(step, carry):
        k = jnp.where(step == 0, 0, jnp.where(step == 1, 3, step - 1))

        @pl.when(step > 0)
        def _():
            trip(rows.at[0], rows.at[k], (n0, n1), k, me.plane(k)).wait_recv()

        gate_mat, up_mat = gate_w[...].reshape(square), up_w[...].reshape(square)
        gate = dot(rows[k], gate_mat)
        up = dot(rows[k], up_mat)
        back = nt_dot(cots[k], down_w[...].reshape(square))
        sig = jax.nn.sigmoid(gate)
        soft = gate * sig
        hid[k] = (soft * up).astype(BF16)
        dgate[k] = (back * up * sig * (1.0 + gate * (1.0 - sig))).astype(BF16)
        dup[k] = (back * soft).astype(BF16)
        c_out[k] = (nt_dot(dgate[k], gate_mat) + nt_dot(dup[k], up_mat)).astype(BF16)

        @pl.when(step > 0)
        def _():
            trip(c_out.at[k], c_in.at[k], (c0, c1), k, me.plane(k)).start()

        @pl.when(step == 0)
        def _():
            trip(rows.at[0], rows.at[3], (n0, n1), 3, me.plane(3)).wait_send()
            for near in (1, 2):
                trip(rows.at[0], rows.at[near], (n0, n1), near, me.plane(near)).start()

        return carry

    lax.fori_loop(0, 4, block, 0)
    all_rows = (4 * n_ref.shape[0], width)

    def weight_grad(left, right, slot):
        chunk = 256
        for first in range(0, width, chunk):
            value = tn_dot(left[:, first : first + chunk], right).astype(BF16)
            stage[slot, first : first + chunk] = value

    shares = []
    piece = width // (8 * zc)

    def share(slot, which):
        parts = stage.at[slot].reshape(2, zc, 2, 2, piece, width)
        for g in range(4):
            x, y = g // 2, g % 2
            shares.append(
                move(parts.at[x, :, y], sh_ref.at[:, :, 2 * g + which], ls, 12 + 2 * g + which)
            )

    flat = lambda ref: ref[...].reshape(all_rows)
    weight_grad(flat(rows), flat(dgate), 0)
    share(0, 0)
    weight_grad(flat(rows), flat(dup), 1)
    share(1, 1)
    weight_grad(flat(hid), flat(cots), 2)
    shares.append(
        move(stage.at[2].reshape(zc, 2, 4, piece, width), sh_ref.at[:, :, 8:], ls, 20)
    )

    def finish_out(k, carry):
        out_ref[k] = dot(hid[k], down_w[...].reshape(square)).astype(BF16)
        return carry

    lax.fori_loop(0, 4, finish_out, 0)
    total = c_out[0].astype(F32)
    for k in range(1, 4):
        trip(c_out.at[k], c_in.at[k], (c0, c1), k, me.plane(k)).wait()
        total = total + c_in[k].astype(F32)
    cs_ref[...] = total
    for copy in shares:
        copy.wait()
    for near in (1, 2):
        trip(rows.at[0], rows.at[near], (n0, n1), near, me.plane(near)).wait_send()


def middle_exchange(zc, normed, cots, weights):
    own, width = normed.shape
    piece = width // (8 * zc)
    blocks = pltpu.VMEM((4, own, width), BF16)
    wide = pltpu.VMEM((2, zc, 2, 2, piece, width), BF16)
    return exchange(
        functools.partial(middle_kernel, zc),
        3,
        (
            struct((4, own, width)),
            struct((own, width), F32),
            struct((zc, 2, 12, piece, width)),
        ),
        [VM] * 5 + [ANY],
        (VM, VM, ANY),
        [blocks, blocks, wide, wide, pltpu.VMEM((zc, 2, 4, piece, width), BF16)]
        + [blocks] * 5
        + [pltpu.VMEM((3, width, width), BF16), DMA((21,))]
        + both(4)
        + both(4),
        (normed, *cots, weights),
        2 * 4 * own * width * width * 9,
        64 << 20,
    )


def turn_kernel(
    zc,
    c_ref,
    t_ref,
    r_ref,
    wo_ref,
    ob_ref,
    op_ref,
    dr_ref,
    do_ref,
    dw_ref,
    out_ref,
    slabs,
    stage,
    o_in,
    ls,
    d0,
    d1,
    b0,
    b1,
    o0,
    o1,
):
    me = Place(zc)
    chips = 4 * zc
    heads = slabs.shape[0]
    group = heads // 4
    per = zc // group
    width = t_ref.shape[1]
    meet([me.any_chip(k) for k in range(1, chips)] + [me.sibling()])
    outs = [send(op_ref.at[k], o_in.at[k], (o0, o1), k, me.plane(k)) for k in (3, 1, 2)]
    outs.append(move(op_ref.at[0], o_in.at[0], ls, 5))
    total, residual = c_ref[...], r_ref[...]
    scaling = lax.rsqrt(jnp.mean(residual * residual, axis=-1, keepdims=True) + EPS)
    normed = residual * scaling
    middle = jnp.mean(total * normed, axis=-1, keepdims=True)
    grad = t_ref[...].astype(F32) + scaling * (total - normed * middle)
    dr_ref[...] = grad
    narrow = grad.astype(BF16)
    back = nt_dot(narrow, wo_ref[...]).astype(BF16)
    for pair in range(heads // 2):
        two = back[:, pair * PAIR : (pair + 1) * PAIR]
        for side in range(2):
            left = selection(PAIR, PAIR, side * HEAD_DIM, 0, HEAD_DIM)
            right = selection(PAIR, PAIR, (side - 1) * HEAD_DIM, HEAD_DIM, PAIR)
            slab = dot(two[:BLOCK], left) + dot(two[BLOCK:], right)
            slabs[2 * pair + side] = slab.astype(BF16)
    to = do_ref.at[me.z, me.c, me.g]
    own = move(slabs.at[me.g * group + me.z // per], to, ls, 0)
    sends = []
    for k in reversed(range(1, chips)):
        there = me.any_chip(k)
        head = (there[0] * 2 + there[2]) * group + there[1] // per
        sends.append(send(slabs.at[head], to, (d0, d1), k, there))
    chunk = 256
    attended = ob_ref[...]
    for first in range(0, width, chunk):
        stage[first : first + chunk] = tn_dot(attended[:, first : first + chunk], narrow).astype(BF16)
    parts = stage.reshape(2, zc, 2, 2, width // (8 * zc), width)
    keeps = []
    for k in range(4):
        there = me.plane(k)
        keeps.append(move(parts.at[there[0], :, there[2]], dw_ref.at[k], ls, 1 + k))
    own.wait()
    for copy in sends:
        copy.wait()
    half = do_ref.at[:, me.c]
    relay = send(half, half, (b0, b1), 0, me.sibling())
    for copy in outs:
        copy.wait()
    final = residual
    for k in range(4):
        final = final + o_in[k].astype(F32)
    out_ref[...] = final.astype(BF16)
    for copy in keeps:
        copy.wait()
    relay.wait()


def turn_exchange(zc, c_sum, cotangent, residual, w_out, attn_rows, out_parts):
    chips = 4 * zc
    own, width = cotangent.shape
    heads = width // HEAD_DIM
    return exchange(
        functools.partial(turn_kernel, zc),
        6,
        (
            struct((own, width), F32),
            struct((zc, 2, 4, BLOCK, PAIR)),
            struct((4, zc, 2, width // (8 * zc), width)),
            struct((own, width)),
        ),
        [VM] * 5 + [ANY],
        (VM, ANY, ANY, VM),
        [
            pltpu.VMEM((heads, BLOCK, PAIR), BF16),
            pltpu.VMEM((width, width), BF16),
            pltpu.VMEM((4, own, width), BF16),
            DMA((6,)),
        ]
        + both(chips)
        + both(1)
        + both(4),
        (c_sum, cotangent, residual, w_out, attn_rows, out_parts),
        2 * 2 * own * width * width,
        8 << 20,
    )


def tail_kernel(
    zc,
    d_ref,
    n_ref,
    w_ref,
    x_ref,
    g_ref,
    v_ref,
    tg_ref,
    gw_ref,
    go_ref,
    o_in,
    o_mine,
    o_theirs,
    o_land,
    mine,
    theirs,
    landed,
    grads,
    c_out,
    c_in,
    stage,
    other_w,
    ls,
    b0,
    b1,
    z0,
    z1,
    c0,
    c1,
    s0,
    s1,
    w0,
    w1,
    q0,
    q1,
    v0,
    v1,
):
    me = Place(zc)
    chips = 4 * zc
    group, per = landed.shape[:2]
    qw = group * HEAD_DIM
    meet([me.any_chip(k) for k in range(1, chips)] + [me.sibling()])
    head, place = me.z // per, me.z % per

    def slot(k):
        return (me.x ^ (k // 2)) * 2 + (me.y ^ (k % 2))

    order = (3, 2, 1, 0)
    halves = []
    for k in order:
        halves.append(
            (
                send(d_ref.at[:, 1 - me.c, slot(k)], theirs.at[k], (b0, b1), k, me.sibling()),
                move(d_ref.at[:, me.c, slot(k)], mine.at[k], ls, k),
            )
        )
    o_parts = [move(v_ref.at[0], o_in.at[0], ls, 9)]
    for k in (3, 1, 2):
        o_parts.append(send(v_ref.at[k], o_in.at[k], (v0, v1), k, me.plane(k)))
    for k, (far, near) in zip(order, halves):
        near.wait()
        far.wait()
        mine[k] = mine[k] + theirs[k]
        for over in range(1, zc):
            send(
                mine.at[k, me.z ^ over],
                landed.at[head, place, k],
                (z0, z1),
                k * zc + over,
                me.line(over),
            )
        move(mine.at[k, me.z], landed.at[head, place, k], ls, 4 + k)

    def block(step, carry):
        k = 3 - step
        pltpu.make_async_copy(
            mine.at[k, me.z], landed.at[head, place, k], ls.at[4 + k]
        ).wait()
        for over in range(1, zc):
            trip(
                mine.at[k, me.z ^ over],
                landed.at[head, place, k],
                (z0, z1),
                k * zc + over,
                me.line(over),
            ).wait()
        upper = jnp.zeros((BLOCK, qw), F32)
        lower = jnp.zeros((BLOCK, qw), F32)
        for h in range(group):
            slab = landed[h, 0, k]
            for extra in range(1, per):
                slab = slab + landed[h, extra, k]
            first, last = h * HEAD_DIM, (h + 1) * HEAD_DIM
            upper = upper + dot(slab[:BLOCK], selection(PAIR, qw, -first, first, last))
            lower = lower + dot(slab[:BLOCK], selection(PAIR, qw, HEAD_DIM - first, first, last))
            start = qw + h * PAIR
            grads[k, :, start : start + PAIR] = slab[BLOCK:]
        grads[k, :BLOCK, :qw] = upper.astype(BF16)
        grads[k, BLOCK:, :qw] = lower.astype(BF16)
        c_out[k] = nt_dot(grads[k], w_ref[...]).astype(BF16)

        @pl.when(k > 0)
        def _():
            trip(c_out.at[k], c_in.at[k], (c0, c1), k, me.plane(k)).start()

        return carry

    lax.fori_loop(0, 4, block, 0)
    for copy in o_parts:
        copy.wait()
    o_sum = o_in[0].astype(F32)
    for k in range(1, 4):
        o_sum = o_sum + o_in[k].astype(F32)
    o_mine[...] = o_sum.astype(BF16)
    o_swap = send(o_mine.at[:, 1 - me.c], o_theirs, (s0, s1), 1, me.sibling())
    width, cols = w_ref.shape
    all_rows = 4 * n_ref.shape[1]
    normed_all = n_ref[...].reshape(all_rows, width)
    grads_all = grads[...].reshape(all_rows, cols)
    piece = stage.shape[2]
    chunk = 256
    each = chunk // (2 * piece)
    for first in range(0, width, chunk):
        value = tn_dot(normed_all[:, first : first + chunk], grads_all).astype(BF16)
        at = first // (2 * piece)
        stage[at : at + each] = value.reshape(each, 2, piece, cols)
    swap = send(stage.at[:, 1 - me.c], other_w, (s0, s1), 0, me.sibling())
    o_swap.wait()
    o_theirs[...] = o_theirs[...] + o_mine[:, me.c]
    sends = [
        send(o_theirs.at[me.z ^ k], o_land.at[k], (q0, q1), k, me.line(k)) for k in range(1, zc)
    ]
    swap.wait()

    def add(i, carry):
        other_w[i] = stage[i, me.c] + other_w[i]
        return carry

    lax.fori_loop(0, chips, add, 0)
    stay = move(other_w.at[me.chip], gw_ref.at[me.z, me.g], ls, 8)
    for k in reversed(range(1, chips)):
        there = me.any_chip(k)
        chip = (there[0] * zc + there[1]) * 2 + there[2]
        sends.append(send(other_w.at[chip], gw_ref.at[me.z, me.g], (w0, w1), k, there))
    total = c_out[0].astype(F32)
    for k in range(1, 4):
        trip(c_out.at[k], c_in.at[k], (c0, c1), k, me.plane(k)).wait()
        total = total + c_in[k].astype(F32)
    x = x_ref[...].astype(F32)
    scaling = lax.rsqrt(jnp.mean(x * x, axis=-1, keepdims=True) + EPS)
    normed = x * scaling
    middle = jnp.mean(total * normed, axis=-1, keepdims=True)
    tg_ref[...] = (g_ref[...] + scaling * (total - normed * middle)).astype(BF16)
    stay.wait()
    for copy in sends:
        copy.wait()
    o_sum = o_theirs[me.z].astype(F32)
    for k in range(1, zc):
        o_sum = o_sum + o_land[k].astype(F32)
    go_ref[...] = o_sum


def tail_exchange(zc, group, slab_grads, n_all, weights, tokens, residual_grad, out_grads):
    chips = 4 * zc
    per = zc // group
    own, width = tokens.shape
    cols = weights.shape[1]
    slab = slab_grads.shape[3:]
    piece = width // (2 * chips)
    blocks = pltpu.VMEM((4, own, width), BF16)
    return exchange(
        functools.partial(tail_kernel, zc),
        4,
        (struct((own, width)), struct((zc, 4, piece, cols)), struct((piece, width), F32)),
        [ANY] + [VM] * 4 + [ANY],
        (VM, ANY, VM),
        [
            pltpu.VMEM((4, zc, 2, piece, width), BF16),
            pltpu.VMEM((zc, 2, piece, width), BF16),
            pltpu.VMEM((zc, piece, width), BF16),
            pltpu.VMEM((zc, piece, width), BF16),
            pltpu.VMEM((4, zc) + slab, BF16),
            pltpu.VMEM((4, zc) + slab, BF16),
            pltpu.VMEM((group, per, 4) + slab, BF16),
            pltpu.VMEM((4, own, cols), BF16),
            blocks,
            blocks,
            pltpu.VMEM((chips, 2, piece, cols), BF16),
            pltpu.VMEM((chips, piece, cols), BF16),
            DMA((10,)),
        ]
        + both(4)
        + both(4 * zc)
        + both(4)
        + both(2)
        + both(chips)
        + both(zc)
        + both(4),
        (slab_grads, n_all, weights, tokens, residual_grad, out_grads),
        2 * 4 * own * width * cols * 2,
        24 << 20,
    )


def share_kernel(zc, f_ref, gf_ref, ls, f0, f1):
    me = Place(zc)
    meet([me.plane(k) for k in range(1, 4)])
    copies = []
    for k in (3, 1, 2):
        there = me.plane(k)
        part = f_ref.at[pl.ds(2 * (there[0] * 2 + there[2]), 2)]
        copies.append(send(part, gf_ref.at[me.g], (f0, f1), k, there))
    copies.append(move(f_ref.at[pl.ds(2 * me.g, 2)], gf_ref.at[me.g], ls, 0))
    for copy in copies:
        copy.wait()


def share_exchange(zc, shares):
    return exchange(
        functools.partial(share_kernel, zc),
        5,
        struct((4, 2) + shares.shape[1:]),
        [ANY],
        ANY,
        [DMA((1,))] + both(4),
        (shares,),
        0,
        2 << 20,
    )


def last_kernel(
    zc,
    group,
    t_ref,
    o_ref,
    wo_ref,
    gw_ref,
    gf_ref,
    ds_ref,
    q_w,
    k_w,
    v_w,
    g_w,
    u_w,
    gain1,
    gain2,
    tg_ref,
    out_ref,
    go_ref,
    g1_ref,
    q_ref,
    k_ref,
    v_ref,
    g2_ref,
    g_ref,
    u_ref,
    d_ref,
):
    tg_ref[...] = t_ref[...]
    out_ref[...] = o_ref[...]
    go_ref[...] = wo_ref[...]
    d_ref[...] = ds_ref[8:].astype(F32).reshape(d_ref.shape)
    first_gain, second_gain = column_of(low(gain1[...])), column_of(low(gain2[...]))
    count = q_w.shape[0]
    qw = group * HEAD_DIM
    score = jnp.zeros((count, PAIR), F32)
    for g in range(4):
        raw = gw_ref[0, g].astype(F32)
        for z in range(1, zc):
            raw = raw + gw_ref[z, g].astype(F32)
        for pair in range(group // 2):
            at = lanes(g * group // 2 + pair)
            start = qw + 2 * pair * PAIR
            even, odd = raw[:, start : start + PAIR], raw[:, start + PAIR : start + 2 * PAIR]
            query = raw[:, lanes(pair)]
            key, value = pair_up(even, 0, odd, 0), pair_up(even, 1, odd, 1)
            score = score + query * low(q_w[:, at]) + key * low(k_w[:, at]) + value * low(v_w[:, at])
            q_ref[:, at] = first_gain * query
            k_ref[:, at] = first_gain * key
            v_ref[:, at] = first_gain * value
    g1_ref[...] = row_of(jnp.sum(score, axis=1, keepdims=True))
    units = g_w.shape[1] // (4 * zc)
    score = jnp.zeros((count, PAIR), F32)
    for which, (weight, target) in enumerate(((g_w, g_ref), (u_w, u_ref))):
        for chunk in range(weight.shape[1] // PAIR):
            if units % PAIR == 0:
                owner, piece = divmod(chunk, units // PAIR)
                x, z, y = owner // (2 * zc), owner // 2 % zc, owner % 2
                raw = gf_ref[2 * x + y, which, :, lanes(z * units // PAIR + piece)].astype(F32)
            else:
                x, z = chunk // zc, chunk % zc
                near = gf_ref[2 * x, which, :, lanes(z // 2)].astype(F32)
                far = gf_ref[2 * x + 1, which, :, lanes(z // 2)].astype(F32)
                raw = pair_up(near, z % 2, far, z % 2)
            score = score + raw * low(weight[:, lanes(chunk)])
            target[:, lanes(chunk)] = second_gain * raw
    g2_ref[...] = row_of(jnp.sum(score, axis=1, keepdims=True))


def last_step(zc, group, tokens_grad, output, out_share, w_all, f_all, shares, matrices, gains):
    own, width = output.shape
    count, hidden = matrices[3].shape
    return pl.pallas_call(
        functools.partial(last_kernel, zc, group),
        out_shape=(
            struct((own, width)),
            struct((own, width)),
            struct((count, width), F32),
            struct((1, count), F32),
            struct((count, width), F32),
            struct((count, width), F32),
            struct((count, width), F32),
            struct((1, count), F32),
            struct((count, hidden), F32),
            struct((count, hidden), F32),
            struct((4 * count, width), F32),
        ),
        in_specs=[VM] * 13,
        out_specs=(VM,) * 11,
        compiler_params=pltpu.CompilerParams(vmem_limit_bytes=32 << 20),
    )(
        tokens_grad,
        output,
        out_share,
        w_all,
        f_all,
        shares,
        *matrices,
        *(g.reshape(1, -1) for g in gains),
    )


def segment_start(position, lens_ref):
    start = jnp.zeros_like(position)
    end = 0
    for j in range(lens_ref.shape[0]):
        end = end + lens_ref[j]
        start = jnp.where(position >= end, end, start)
    return start


def note_tiles(workers, worker, tiles, lens_ref, mine):
    turns = tiles // workers

    def snake(turn, carry):
        forward = turn * workers + worker
        backward = turn * workers + workers - 1 - worker
        mine[turn] = jnp.where((turn & 1) == 0, forward, backward)
        return carry

    def weigh(step, ahead):
        turn = turns - 1 - step
        loads = []
        for tile in (2 * turn, 2 * turn + 1):
            first, _, _, last = key_bounds(tile * QTILE, lens_ref)
            loads.append(last - first)
        lighter_first = loads[0] <= loads[1]
        first_to_zero = jnp.where(ahead > 0, lighter_first, loads[0] > loads[1])
        mine[turn] = 2 * turn + jnp.where(first_to_zero, worker, 1 - worker)
        return ahead + jnp.where(first_to_zero, loads[0] - loads[1], loads[1] - loads[0])

    if workers == 2:
        lax.fori_loop(0, turns, weigh, 0)
    else:
        lax.fori_loop(0, turns, snake, 0)


def key_bounds(first, lens_ref):
    low_start = segment_start(first, lens_ref)
    high_start = segment_start(first + QTILE - 1, lens_ref)
    low = low_start // KTILE
    high = (first + QTILE + KTILE - 1) // KTILE
    plain = jnp.clip((high_start + KTILE - 1) // KTILE, low, high)
    stop = jnp.clip((first + 1) // KTILE, plain, high)
    return low, plain, stop, high


def visible(first, tile, starts):
    key = tile * KTILE + lax.broadcasted_iota(jnp.int32, (KTILE, QTILE), 0)
    query = first + lax.broadcasted_iota(jnp.int32, (KTILE, QTILE), 1)
    return (key <= query) & (key >= starts)


def note_places(anchor_ref, inv):
    def note(i, carry):
        inv[anchor_ref[i]] = i
        return carry

    lax.fori_loop(0, anchor_ref.shape[0], note, 0)


def half_lanes(rows, half):
    lane = lax.broadcasted_iota(jnp.int32, rows.shape, 1)
    return jnp.where((lane // HEAD_DIM) == half, rows, jnp.zeros_like(rows))


def fold(rows, columns, first):
    row = lax.broadcasted_iota(jnp.int32, (rows, columns), 0)
    column = lax.broadcasted_iota(jnp.int32, (rows, columns), 1)
    return (row % HEAD_DIM == column - first).astype(F32).astype(BF16)


def unfold(rows, columns, first):
    row = lax.broadcasted_iota(jnp.int32, (rows, columns), 0)
    column = lax.broadcasted_iota(jnp.int32, (rows, columns), 1)
    return (column % HEAD_DIM == row - first).astype(F32).astype(BF16)


def forward_kernel(
    workers, anchor_ref, lens_ref, who_ref, a_ref, o_ref, kv_ref, kvt_ref, q_ref, qt_ref, ot_ref, l_ref, inv, mine, raw
):
    blocks = anchor_ref.shape[0]
    turns = q_ref.shape[0]
    per = QTILE // BLOCK
    worker = who_ref[0]
    note_places(anchor_ref, inv)
    note_tiles(workers, worker, turns * workers, lens_ref, mine)
    o_ref[...] = jnp.zeros_like(o_ref)
    same = selection(PAIR, PAIR, 0)

    def order(step, carry):
        for b in range(per):
            i = step * per + b
            where = inv[i]
            slab, half = where >> 1, where & 1
            at = pl.ds(pl.multiple_of(i * BLOCK, BLOCK), BLOCK)
            kv_ref[at, :] = a_ref[slab, pl.ds(pl.multiple_of(BLOCK + half * BLOCK, BLOCK), BLOCK), :]
        at = pl.ds(pl.multiple_of(step * QTILE, QTILE), QTILE)
        kvt_ref[:, at] = nt_dot(same, kv_ref[at, :]).astype(BF16)
        return carry

    lax.fori_loop(0, blocks // per, order, 0)

    def one_tile(turn, carry):
        tile = mine[turn]
        first = tile * QTILE
        for b in range(per):
            where = inv[tile * per + b]
            raw[b * BLOCK : (b + 1) * BLOCK, :] = half_lanes(a_ref[where >> 1, :BLOCK, :], where & 1)
        q_ref[turn] = (dot(raw[...], fold(PAIR, PAIR, 0)) * 0.125).astype(BF16)
        qt_ref[turn] = (nt_dot(unfold(PAIR, PAIR, 0), raw[...]) * 0.125).astype(BF16)
        query = qt_ref[turn]
        starts = segment_start(first + lax.broadcasted_iota(jnp.int32, (1, QTILE), 1), lens_ref)
        low, plain, stop, high = key_bounds(first, lens_ref)

        def step(masked, kt, state):
            top, total, acc = state
            at = pl.ds(pl.multiple_of(kt * KTILE, KTILE), KTILE)
            scores = dot(kv_ref[at, :], query)
            if masked:
                scores = jnp.where(visible(first, kt, starts), scores, MASKED)
            new_top = jnp.maximum(top, jnp.max(scores, axis=0, keepdims=True))
            factor = jnp.exp(top - new_top)
            weights = jnp.exp(scores - new_top)
            total = total * factor + jnp.sum(weights, axis=0, keepdims=True)
            acc = acc * factor + dot(kvt_ref[HEAD_DIM:, at], weights.astype(BF16))
            return (new_top, total, acc)

        state = (
            jnp.full((1, QTILE), LOWEST, F32),
            jnp.zeros((1, QTILE), F32),
            jnp.zeros((HEAD_DIM, QTILE), F32),
        )
        state = lax.fori_loop(low, plain, functools.partial(step, True), state)
        state = lax.fori_loop(plain, stop, functools.partial(step, False), state)
        top, total, acc = lax.fori_loop(stop, high, functools.partial(step, True), state)
        out = acc / total
        ot_ref[turn] = out
        l_ref[turn] = top + jnp.log(total)
        wide = tn_dot(out.astype(BF16), unfold(HEAD_DIM, PAIR, 0)).astype(BF16)
        for b in range(per):
            where = inv[tile * per + b]
            slab = where >> 1
            o_ref[slab] = o_ref[slab] + half_lanes(wide[b * BLOCK : (b + 1) * BLOCK], where & 1)
        return carry

    lax.fori_loop(0, turns, one_tile, 0)


def attention_forward(workers, anchors, lengths, who, packed):
    slabs = packed.shape[0]
    rows = slabs * 2 * BLOCK
    turns = rows // QTILE // workers
    return pl.pallas_call(
        functools.partial(forward_kernel, workers),
        out_shape=(
            struct((slabs, BLOCK, PAIR)),
            struct((rows, PAIR)),
            struct((PAIR, rows)),
            struct((turns, QTILE, PAIR)),
            struct((turns, PAIR, QTILE)),
            struct((turns, HEAD_DIM, QTILE), F32),
            struct((turns, 1, QTILE), F32),
        ),
        in_specs=[SM, SM, SM, VM],
        out_specs=(VM,) * 7,
        scratch_shapes=[
            pltpu.SMEM((2 * slabs,), jnp.int32),
            pltpu.SMEM((turns,), jnp.int32),
            pltpu.VMEM((QTILE, PAIR), BF16),
        ],
        compiler_params=pltpu.CompilerParams(vmem_limit_bytes=60 << 20),
        cost_estimate=pl.CostEstimate(
            flops=rows * rows * 64, bytes_accessed=rows * 1024, transcendentals=rows * rows // 8
        ),
    )(anchors, lengths, who, packed)


def backward_kernel(
    workers,
    anchor_ref,
    lens_ref,
    who_ref,
    d_ref,
    kv_ref,
    kvt_ref,
    q_ref,
    qt_ref,
    ot_ref,
    l_ref,
    g_ref,
    inv,
    mine,
    raw,
    dn,
    dt,
    acc,
):
    blocks = anchor_ref.shape[0]
    turns = q_ref.shape[0]
    per = QTILE // BLOCK
    worker = who_ref[0]
    note_places(anchor_ref, inv)
    note_tiles(workers, worker, turns * workers, lens_ref, mine)
    acc[...] = jnp.zeros_like(acc)
    g_ref[:, :BLOCK, :] = jnp.zeros((g_ref.shape[0], BLOCK, PAIR), BF16)

    def one_tile(turn, carry):
        tile = mine[turn]
        first = tile * QTILE
        for b in range(per):
            where = inv[tile * per + b]
            raw[b * BLOCK : (b + 1) * BLOCK, :] = half_lanes(d_ref[where >> 1], where & 1)
        dn[...] = dot(raw[...], fold(PAIR, PAIR, HEAD_DIM)).astype(BF16)
        dt[...] = nt_dot(unfold(PAIR, PAIR, HEAD_DIM), raw[...]).astype(BF16)
        query, query_rows = qt_ref[turn], q_ref[turn]
        grad, grad_rows = dt[...], dn[...]
        norm = l_ref[turn]
        delta = jnp.sum(grad[HEAD_DIM:].astype(F32) * ot_ref[turn], axis=0, keepdims=True)
        starts = segment_start(first + lax.broadcasted_iota(jnp.int32, (1, QTILE), 1), lens_ref)
        low, plain, stop, high = key_bounds(first, lens_ref)

        def step(masked, kt, total):
            at = pl.ds(pl.multiple_of(kt * KTILE, KTILE), KTILE)
            keys = kv_ref[at, :]
            scores = dot(keys, query)
            if masked:
                scores = jnp.where(visible(first, kt, starts), scores, MASKED)
            weights = jnp.exp(scores - norm)
            score_grad = (weights * (dot(keys, grad) - delta)).astype(BF16)
            acc[at, :] += dot(score_grad, query_rows) + dot(weights.astype(BF16), grad_rows)
            return total + dot(kvt_ref[:HEAD_DIM, at], score_grad)

        total = jnp.zeros((HEAD_DIM, QTILE), F32)
        total = lax.fori_loop(low, plain, functools.partial(step, True), total)
        total = lax.fori_loop(plain, stop, functools.partial(step, False), total)
        total = lax.fori_loop(stop, high, functools.partial(step, True), total)
        wide = tn_dot((total * 0.125).astype(BF16), unfold(HEAD_DIM, PAIR, 0)).astype(BF16)
        for b in range(per):
            where = inv[tile * per + b]
            slab = where >> 1
            g_ref[slab, :BLOCK] = g_ref[slab, :BLOCK] + half_lanes(
                wide[b * BLOCK : (b + 1) * BLOCK], where & 1
            )
        return carry

    lax.fori_loop(0, turns, one_tile, 0)

    def place(step, carry):
        for b in range(per):
            i = step * per + b
            where = inv[i]
            slab, half = where >> 1, where & 1
            at = pl.ds(pl.multiple_of(i * BLOCK, BLOCK), BLOCK)
            to = pl.ds(pl.multiple_of(BLOCK + half * BLOCK, BLOCK), BLOCK)
            g_ref[slab, to, :] = acc[at, :].astype(BF16)
        return carry

    lax.fori_loop(0, blocks // per, place, 0)


def attention_backward(workers, anchors, lengths, who, grads, kept):
    slabs = grads.shape[0]
    rows = slabs * 2 * BLOCK
    return pl.pallas_call(
        functools.partial(backward_kernel, workers),
        out_shape=struct((slabs, 3 * BLOCK, PAIR)),
        in_specs=[SM, SM, SM] + [VM] * 7,
        out_specs=VM,
        scratch_shapes=[
            pltpu.SMEM((2 * slabs,), jnp.int32),
            pltpu.SMEM((rows // QTILE // workers,), jnp.int32),
            pltpu.VMEM((QTILE, PAIR), BF16),
            pltpu.VMEM((QTILE, PAIR), BF16),
            pltpu.VMEM((PAIR, QTILE), BF16),
            pltpu.VMEM((rows, PAIR), F32),
        ],
        compiler_params=pltpu.CompilerParams(vmem_limit_bytes=60 << 20),
        cost_estimate=pl.CostEstimate(
            flops=rows * rows * 160, bytes_accessed=rows * 1024, transcendentals=rows * rows // 8
        ),
    )(anchors, lengths, who, grads, *kept)


def around(value, k):
    return lax.ppermute(value, ("head", "y"), [(i, i ^ k) for i in range(4)])


def body(
    zc,
    tokens,
    cotangent,
    norm1_gain,
    w_query,
    w_key,
    w_value,
    w_out,
    norm2_gain,
    w_gate,
    w_up,
    w_down,
    block_anchor,
    seq_lengths,
):
    width = tokens.shape[1]
    heads = width // HEAD_DIM
    group = heads // 4
    per_head = zc // group
    workers = 2 * per_head
    feature_rows = w_query.shape[0]

    n1_all, qkv_w, ffn_in, out_all, by_head = head_exchange(
        zc,
        group,
        tokens,
        (w_query, w_key, w_value, w_out, w_gate, w_up, w_down),
        (norm1_gain, norm2_gain),
    )
    qkv_w = qkv_w.reshape(width, 3 * group * HEAD_DIM)
    out_mat = out_all.reshape(width, width)

    ffn_all = lax.all_gather(ffn_in, ("z", "core"), axis=0, tiled=False).reshape(
        zc, 2, 12, feature_rows, width
    )
    by_head, near = lax.optimization_barrier((by_head, cotangent))
    cots = [cotangent] + [around(near, k) for k in range(1, 4)]

    anchors = jnp.transpose(block_anchor.reshape(2, zc, 2, 2, 2), (1, 3, 0, 2, 4)).reshape(-1)
    who = ((lax.axis_index("z") % per_head) * 2 + lax.axis_index("core")).astype(jnp.int32).reshape(1)
    slab_count = zc * 8
    o_slabs, *kept = attention_forward(
        workers, anchors, seq_lengths, who, by_head.reshape((slab_count,) + by_head.shape[3:])
    )
    attn_rows, residual, normed_two = join_exchange(
        zc, heads, o_slabs.reshape(zc, 2, 4, BLOCK, PAIR), tokens, out_mat
    )
    out_parts, c_sum, shares = middle_exchange(zc, normed_two, cots, ffn_all)
    shares = lax.psum_scatter(
        shares.reshape(zc * 2 * 12, feature_rows, width), ("z", "core"), scatter_dimension=0, tiled=True
    )
    residual_grad, do_heads, out_grads, output = turn_exchange(
        zc, c_sum, cotangent, residual, out_mat, attn_rows, out_parts
    )
    grad_heads = attention_backward(
        workers, anchors, seq_lengths, who, do_heads.reshape(slab_count, BLOCK, PAIR), kept
    )
    tokens_grad, w_all, out_share = tail_exchange(
        zc,
        group,
        grad_heads.reshape(zc, 2, 4, 3 * BLOCK, PAIR),
        n1_all,
        qkv_w,
        tokens,
        residual_grad,
        out_grads,
    )
    shares, w_all = lax.optimization_barrier((shares, w_all))
    (
        tokens_grad,
        output,
        out_grad,
        gain1_grad,
        query_grad,
        key_grad,
        value_grad,
        gain2_grad,
        gate_grad,
        up_grad,
        down_grad,
    ) = last_step(
        zc,
        group,
        tokens_grad,
        output,
        out_share,
        w_all,
        share_exchange(zc, shares),
        shares,
        (w_query, w_key, w_value, w_gate, w_up),
        (norm1_gain, norm2_gain),
    )
    return (
        output,
        tokens_grad,
        gain1_grad.reshape(-1),
        query_grad,
        key_grad,
        value_grad,
        out_grad,
        gain2_grad.reshape(-1),
        gate_grad,
        up_grad,
        down_grad,
    )


def solution(mesh):
    blk = mesh.shape["blk"]
    grid = Mesh(mesh.devices.reshape(mesh.shape["head"], blk // 4, 2, 2), AXES)
    rows, vector, whole = P(AXES, None), P(AXES), P()
    return jax.shard_map(
        functools.partial(body, blk // 4),
        mesh=grid,
        in_specs=(rows, rows, vector, rows, rows, rows, rows, vector, rows, rows, rows, whole, whole),
        out_specs=(rows, rows, vector, rows, rows, rows, rows, vector, rows, rows, rows),
        check_vma=False,
    )
```

```python
import functools

import jax
import jax.numpy as jnp
from jax import lax
from jax.experimental import pallas as pl
from jax.experimental.pallas import tpu as pltpu
from jax.sharding import Mesh
from jax.sharding import PartitionSpec as P

HEAD_DIM = 64
BLOCK = 128
PAIR = 128
EPS = 1e-06
MASKED = -1e30
LOWEST = -1e20
QTILE = 512
KTILE = 512
TURNED = 2048
AXES = ("head", "z", "y", "core")
IDS = pl.DeviceIdType.MESH
F32 = jnp.float32
BF16 = jnp.bfloat16
ANY = pl.BlockSpec(memory_space=pl.ANY)
VM = pl.BlockSpec(memory_space=pltpu.VMEM)
SM = pl.BlockSpec(memory_space=pltpu.SMEM)


def struct(shape, dtype=BF16):
    return jax.ShapeDtypeStruct(tuple(shape), dtype)


def nt_dot(a, b):
    return lax.dot_general(a, b, (((1,), (1,)), ((), ())), preferred_element_type=F32)


def tn_dot(a, b):
    return lax.dot_general(a, b, (((0,), (0,)), ((), ())), preferred_element_type=F32)


def dot(a, b):
    return jnp.dot(a, b, preferred_element_type=F32)


def selection(rows, columns, shift, first=0, last=None):
    last = columns if last is None else last
    row = lax.broadcasted_iota(jnp.int32, (rows, columns), 0)
    column = lax.broadcasted_iota(jnp.int32, (rows, columns), 1)
    hit = (row == column + shift) & (column >= first) & (column < last)
    return hit.astype(F32).astype(BF16)


def pair_up(first, first_half, second, second_half):
    lane = lax.broadcasted_iota(jnp.int32, first.shape, 1)
    left = first if first_half == 0 else pltpu.roll(first, HEAD_DIM, 1)
    right = second if second_half == 1 else pltpu.roll(second, HEAD_DIM, 1)
    return jnp.where(lane < HEAD_DIM, left, right)


def column_of(row):
    count = row.shape[1]
    i = lax.broadcasted_iota(jnp.int32, (count, count), 0)
    j = lax.broadcasted_iota(jnp.int32, (count, count), 1)
    return jnp.sum(jnp.where(i == j, row, 0.0), axis=1, keepdims=True)


def row_of(column):
    count = column.shape[0]
    i = lax.broadcasted_iota(jnp.int32, (count, count), 0)
    j = lax.broadcasted_iota(jnp.int32, (count, count), 1)
    return jnp.sum(jnp.where(i == j, column, 0.0), axis=0, keepdims=True)


def low(value):
    return value.astype(BF16).astype(F32)


def lanes(index):
    return slice(index * PAIR, (index + 1) * PAIR)


class Place:
    def __init__(self, z_count):
        self.x, self.z, self.y, self.c = (lax.axis_index(a) for a in AXES)
        self.g = self.x * 2 + self.y
        self.chip = (self.x * z_count + self.z) * 2 + self.y

    def sibling(self):
        return (self.x, self.z, self.y, 1 - self.c)

    def plane(self, k):
        return (self.x ^ (k // 2), self.z, self.y ^ (k % 2), self.c)

    def line(self, k):
        return (self.x, self.z ^ k, self.y, self.c)

    def any_chip(self, k):
        return (self.x ^ (k // 2 % 2), self.z ^ (k // 4), self.y ^ (k % 2), self.c)


def meet(peers):
    barrier = pltpu.get_barrier_semaphore()
    for peer in peers:
        pl.semaphore_signal(barrier, inc=1, device_id=peer, device_id_type=IDS)
    pl.semaphore_wait(barrier, len(peers))


def trip(source, target, sems, index, device):
    return pltpu.make_async_remote_copy(
        src_ref=source,
        dst_ref=target,
        send_sem=sems[0].at[index],
        recv_sem=sems[1].at[index],
        device_id=device,
        device_id_type=IDS,
    )


def send(*given):
    copy = trip(*given)
    copy.start()
    return copy


def move(source, target, sems, index):
    copy = pltpu.make_async_copy(source, target, sems.at[index])
    copy.start()
    return copy


DMA = pltpu.SemaphoreType.DMA


def both(count):
    return [DMA((count,)), DMA((count,))]


def exchange(kernel, ident, out_shape, in_specs, out_specs, scratch, args, flops, sent):
    return pl.pallas_call(
        kernel,
        out_shape=out_shape,
        in_specs=in_specs,
        out_specs=out_specs,
        scratch_shapes=scratch,
        compiler_params=pltpu.CompilerParams(
            collective_id=ident, has_side_effects=True, vmem_limit_bytes=60 << 20
        ),
        cost_estimate=pl.CostEstimate(flops=flops, bytes_accessed=sent, transcendentals=0),
    )(*args)


def head_kernel(
    zc,
    group,
    t_ref,
    q_w,
    k_w,
    v_w,
    g_w,
    u_w,
    d_w,
    o_w,
    t2_ref,
    gain1,
    gain2,
    ng_ref,
    wg_ref,
    fg_ref,
    a_ref,
    ca_ref,
    cb_ref,
    cc_ref,
    wo_ref,
    w_ref,
    f_ref,
    e_ref,
    rows,
    weights,
    packed,
    ls,
    w0,
    w1,
    n0,
    n1,
    f0,
    f1,
    z0,
    z1,
    b0,
    b1,
    s0,
    s1,
    t0,
    t1,
):
    me = Place(zc)
    chips = 4 * zc
    per = zc // group
    qw = group * HEAD_DIM
    width = t_ref.shape[1]
    first_gain, second_gain = column_of(low(gain1[...])), column_of(low(gain2[...]))
    for g in range(4):
        at = slice(g * qw, (g + 1) * qw)
        w_ref[g, :, :qw] = (first_gain * low(q_w[:, at])).astype(BF16)
        for pair in range(group // 2):
            at = lanes(g * group // 2 + pair)
            key, value = first_gain * low(k_w[:, at]), first_gain * low(v_w[:, at])
            for half in range(2):
                start = qw + (2 * pair + half) * PAIR
                w_ref[g, :, start : start + PAIR] = pair_up(key, half, value, half).astype(BF16)
    e_ref[...] = d_w[...].astype(BF16).reshape(e_ref.shape)
    wo_ref[...] = o_w[...].astype(BF16)
    x = t_ref[...].astype(F32)
    rows[0] = (x * lax.rsqrt(jnp.mean(x * x, axis=-1, keepdims=True) + EPS)).astype(BF16)
    meet([me.any_chip(k) for k in range(1, chips)] + [me.sibling()])
    local = [move(w_ref.at[me.g], weights.at[me.chip, me.c], ls, 0)]
    pieces = []
    for k in reversed(range(1, chips)):
        there = me.any_chip(k)
        their_g = there[0] * 2 + there[2]
        pieces.append(
            send(w_ref.at[their_g], weights.at[me.chip, me.c], (w0, w1), k, there)
        )
    blocks = [send(rows.at[0], rows.at[k], (n0, n1), k, me.plane(k)) for k in range(1, 4)]
    units = g_w.shape[1] // (4 * zc)
    for which, ref in enumerate((g_w, u_w)):
        for g in range(4):
            px, py = g // 2, g % 2
            if units % PAIR == 0:
                for z in range(zc):
                    at = ((px * zc + z) * 2 + py) * units
                    f_ref[g, which, :, z * units : (z + 1) * units] = (
                        second_gain * low(ref[:, at : at + units])
                    ).astype(BF16)
            else:
                for z in range(0, zc, 2):
                    near, far = (second_gain * low(ref[:, lanes(px * zc + i)]) for i in (z, z + 1))
                    f_ref[g, which, :, lanes(z // 2)] = pair_up(near, py, far, py).astype(BF16)
    wide = [
        move(f_ref.at[me.g], fg_ref.at[pl.ds(2 * me.g, 2)], ls, 2),
        move(e_ref, fg_ref.at[pl.ds(8, 4)], ls, 9),
    ]
    for k in range(1, 4):
        there = me.plane(k)
        their_g = there[0] * 2 + there[2]
        wide.append(send(f_ref.at[their_g], fg_ref.at[pl.ds(2 * me.g, 2)], (f0, f1), k, there))
    for k, ref in ((3, cc_ref), (1, ca_ref), (2, cb_ref)):
        wide.append(send(t2_ref, ref, (t0, t1), k, me.plane(k)))
    local[0].wait()
    for copy in pieces:
        copy.wait()
    relay = send(
        weights.at[:, me.c], weights.at[:, me.c], (s0, s1), 0, me.sibling()
    )
    relay.wait()
    kept = [move(weights, wg_ref, ls, 3)]

    def project(k, carry):
        @pl.when(k > 0)
        def _():
            trip(rows.at[0], rows.at[k], (n0, n1), k, me.plane(k)).wait_recv()

        at = (me.x ^ (k // 2)) * 2 + (me.y ^ (k % 2))
        out = dot(rows[k], weights[...].reshape(width, 3 * qw))
        for head in range(group):
            two, half = out[:, lanes(head // 2)], head % 2
            packed[head, k, :BLOCK] = pair_up(two[:BLOCK], half, two[BLOCK:], half).astype(BF16)
            start = qw + head * PAIR
            packed[head, k, BLOCK:] = out[:, start : start + PAIR].astype(BF16)
        for over in range(1, zc):
            trip(
                packed.at[(me.z ^ over) // per, k],
                a_ref.at[me.z, me.c, at],
                (z0, z1),
                k * zc + over,
                me.line(over),
            ).start()
        trip(
            packed.at[me.z // per, k], a_ref.at[me.z, me.c, at], (b0, b1), k * zc, me.sibling()
        ).start()
        pltpu.make_async_copy(
            packed.at[me.z // per, k], a_ref.at[me.z, me.c, at], ls.at[4 + k]
        ).start()
        return carry

    lax.fori_loop(0, 4, project, 0)
    kept.append(move(rows, ng_ref, ls, 8))

    def pass_on(step, carry):
        k, over = step // (zc - 1), step % (zc - 1) + 1
        at = (me.x ^ (k // 2)) * 2 + (me.y ^ (k % 2))
        there = me.z ^ over
        trip(
            packed.at[there // per, k],
            a_ref.at[me.z, me.c, at],
            (z0, z1),
            k * zc + over,
            me.line(over),
        ).wait()
        landed = a_ref.at[there, me.c, at]
        trip(landed, landed, (b0, b1), k * zc + over, me.sibling()).start()
        return carry

    lax.fori_loop(0, 4 * (zc - 1), pass_on, 0)

    def finish(step, carry):
        k, over = step // zc, step % zc
        at = (me.x ^ (k // 2)) * 2 + (me.y ^ (k % 2))
        landed = a_ref.at[me.z ^ over, me.c, at]
        trip(landed, landed, (b0, b1), k * zc + over, me.sibling()).wait()
        return carry

    lax.fori_loop(0, 4 * zc, finish, 0)
    for k in range(4):
        pltpu.make_async_copy(
            packed.at[me.z // per, k], a_ref.at[me.z, me.c, me.g], ls.at[4 + k]
        ).wait()
    for copy in kept + wide:
        copy.wait()
    for copy in blocks:
        copy.wait_send()


def head_exchange(zc, group, tokens, matrices, cotangent, gains):
    chips = 4 * zc
    own, width = tokens.shape
    count = matrices[0].shape[0]
    piece = (count, 3 * group * HEAD_DIM)
    return exchange(
        functools.partial(head_kernel, zc, group),
        1,
        (
            struct((4, own, width)),
            struct((chips, 2) + piece),
            struct((12, count, width)),
            struct((zc, 2, 4, BLOCK + own, PAIR)),
            struct((own, width)),
            struct((own, width)),
            struct((own, width)),
            struct((count, width)),
        ),
        [VM] * 8 + [ANY] + [VM] * 2,
        (ANY,) * 7 + (VM,),
        [
            pltpu.VMEM((4,) + piece, BF16),
            pltpu.VMEM((4, 2, count, width), BF16),
            pltpu.VMEM((4, count, width), BF16),
            pltpu.VMEM((4, own, width), BF16),
            pltpu.VMEM((chips, 2) + piece, BF16),
            pltpu.VMEM((group, 4, BLOCK + own, PAIR), BF16),
            DMA((10,)),
        ]
        + both(chips)
        + both(4)
        + both(4)
        + both(4 * zc)
        + both(4 * zc)
        + both(1)
        + both(4),
        (tokens, *matrices, cotangent, *(g.reshape(1, -1) for g in gains)),
        2 * 4 * own * width * width,
        16 << 20,
    )


def join_kernel(
    zc,
    s_ref,
    x_ref,
    *rest,
):
    w_refs, rest = rest[:zc], rest[zc:]
    ob_ref, r_ref, n_ref, og_ref, mine, theirs, slabs, all_w, ls, b0, b1, c0, c1, p0, p1 = rest
    me = Place(zc)
    chips = 4 * zc
    heads, per = slabs.shape[:2]
    for k, ref in enumerate(w_refs):
        all_w[me.x, me.z ^ k, me.y, me.c] = ref[...]
    meet([me.any_chip(k) for k in range(1, chips)] + [me.sibling()])
    column = all_w.at[me.x, :, me.y, me.c]
    planes = [send(column, column, (p0, p1), k, me.plane(k)) for k in range(1, 4)]
    other = send(s_ref.at[:, 1 - me.c], theirs, (b0, b1), 0, me.sibling())
    own = move(s_ref.at[:, me.c], mine, ls, 0)
    own.wait()
    other.wait()
    mine[...] = mine[...] + theirs[...]
    head = me.g * (heads // 4) + me.z // per
    place = me.z % per
    keep = move(mine.at[me.z, me.g], slabs.at[head, place], ls, 1)
    sends = []
    for k in reversed(range(1, chips)):
        there = me.any_chip(k)
        their_g = there[0] * 2 + there[2]
        sends.append(
            send(mine.at[there[1], their_g], slabs.at[head, place], (c0, c1), k, there)
        )
    for copy in planes:
        copy.wait()
    half = all_w.at[:, :, :, me.c]
    relay = send(half, half, (p0, p1), 0, me.sibling())
    keep.wait()
    for copy in sends:
        copy.wait()
    for block in range(2):
        for pair in range(heads // 2):
            sides = []
            for side in range(2):
                slab = slabs[2 * pair + side, 0].astype(F32)
                for extra in range(1, per):
                    slab = slab + slabs[2 * pair + side, extra].astype(F32)
                sides.append(slab)
            ob_ref[block * BLOCK : (block + 1) * BLOCK, lanes(pair)] = pair_up(
                sides[0], block, sides[1], block
            ).astype(BF16)
    relay.wait()
    save = move(all_w, og_ref, ls, 2)
    residual = x_ref[...].astype(F32) + dot(ob_ref[...], all_w[...].reshape(x_ref.shape[1], x_ref.shape[1]))
    r_ref[...] = residual
    mean = jnp.mean(residual * residual, axis=-1, keepdims=True)
    n_ref[...] = (residual * lax.rsqrt(mean + EPS)).astype(BF16)
    save.wait()


def join_exchange(zc, heads, slabs, tokens, w_parts):
    chips = 4 * zc
    per = 4 * zc // heads
    half = (zc,) + slabs.shape[2:]
    shape = tokens.shape
    whole = (2, zc, 2, 2) + w_parts[0].shape
    return exchange(
        functools.partial(join_kernel, zc),
        2,
        (struct(shape), struct(shape, F32), struct(shape), struct(whole)),
        [ANY, VM] + [VM] * zc,
        (VM,) * 3 + (ANY,),
        [
            pltpu.VMEM(half, BF16),
            pltpu.VMEM(half, BF16),
            pltpu.VMEM((heads, per) + slabs.shape[3:], BF16),
            pltpu.VMEM(whole, BF16),
            DMA((3,)),
        ]
        + both(1)
        + both(chips)
        + both(4),
        (slabs, tokens, *w_parts),
        2 * shape[0] * shape[1] * shape[1],
        4 << 20,
    )


def middle_kernel(
    zc,
    n_ref,
    ca_ref,
    cb_ref,
    cc_ref,
    cd_ref,
    f_ref,
    oa_ref,
    ob_ref,
    oc_ref,
    od_ref,
    cs_ref,
    sh_ref,
    rows,
    cots,
    gate_w,
    up_w,
    down_w,
    hid,
    dgate,
    dup,
    c_out,
    c_in,
    stage,
    ls,
    n0,
    n1,
    c0,
    c1,
):
    me = Place(zc)
    width = n_ref.shape[1]
    rows[0] = n_ref[...]
    meet([me.plane(k) for k in range(1, 4)])
    farthest = send(rows.at[0], rows.at[3], (n0, n1), 3, me.plane(3))
    loads = []
    for g in range(4):
        x, y = g // 2, g % 2
        loads.append(move(f_ref.at[:, :, 2 * g], gate_w.at[x, :, y], ls, 3 * g))
        loads.append(move(f_ref.at[:, :, 2 * g + 1], up_w.at[x, :, y], ls, 3 * g + 1))
    loads.append(move(f_ref.at[:, :, 8:], down_w, ls, 2))
    for k, ref in enumerate((ca_ref, cb_ref, cc_ref, cd_ref)):
        cots[k] = ref[...]
    for copy in loads:
        copy.wait()
    square = (width, width)

    def block(step, carry):
        k = jnp.where(step == 0, 0, jnp.where(step == 1, 3, step - 1))

        @pl.when(step > 0)
        def _():
            trip(rows.at[0], rows.at[k], (n0, n1), k, me.plane(k)).wait_recv()

        gate_mat, up_mat = gate_w[...].reshape(square), up_w[...].reshape(square)
        gate = dot(rows[k], gate_mat)
        up = dot(rows[k], up_mat)
        back = nt_dot(cots[k], down_w[...].reshape(square))
        sig = jax.nn.sigmoid(gate)
        soft = gate * sig
        hid[k] = (soft * up).astype(BF16)
        dgate[k] = (back * up * sig * (1.0 + gate * (1.0 - sig))).astype(BF16)
        dup[k] = (back * soft).astype(BF16)
        c_out[k] = (nt_dot(dgate[k], gate_mat) + nt_dot(dup[k], up_mat)).astype(BF16)

        @pl.when(step > 0)
        def _():
            trip(c_out.at[k], c_in.at[k], (c0, c1), k, me.plane(k)).start()

        @pl.when(step == 0)
        def _():
            trip(rows.at[0], rows.at[3], (n0, n1), 3, me.plane(3)).wait_send()
            for near in (1, 2):
                trip(rows.at[0], rows.at[near], (n0, n1), near, me.plane(near)).start()

        return carry

    lax.fori_loop(0, 4, block, 0)
    all_rows = (4 * n_ref.shape[0], width)

    def weight_grad(left, right, slot):
        chunk = 256
        for first in range(0, width, chunk):
            value = tn_dot(left[:, first : first + chunk], right).astype(BF16)
            stage[slot, first : first + chunk] = value

    shares = []
    piece = width // (8 * zc)

    def share(slot, which):
        parts = stage.at[slot].reshape(2, zc, 2, 2, piece, width)
        for g in range(4):
            x, y = g // 2, g % 2
            shares.append(
                move(parts.at[x, :, y], sh_ref.at[:, :, 2 * g + which], ls, 12 + 2 * g + which)
            )

    flat = lambda ref: ref[...].reshape(all_rows)
    weight_grad(flat(rows), flat(dgate), 0)
    share(0, 0)
    weight_grad(flat(rows), flat(dup), 1)
    share(1, 1)
    weight_grad(flat(hid), flat(cots), 2)
    shares.append(
        move(stage.at[2].reshape(zc, 2, 4, piece, width), sh_ref.at[:, :, 8:], ls, 20)
    )

    for k, ref in enumerate((oa_ref, ob_ref, oc_ref, od_ref)):
        ref[...] = dot(hid[k], down_w[...].reshape(square)).astype(BF16)
    total = c_out[0].astype(F32)
    for k in range(1, 4):
        trip(c_out.at[k], c_in.at[k], (c0, c1), k, me.plane(k)).wait()
        total = total + c_in[k].astype(F32)
    cs_ref[...] = total
    for copy in shares:
        copy.wait()
    for near in (1, 2):
        trip(rows.at[0], rows.at[near], (n0, n1), near, me.plane(near)).wait_send()


def middle_exchange(zc, normed, cots, weights):
    own, width = normed.shape
    piece = width // (8 * zc)
    blocks = pltpu.VMEM((4, own, width), BF16)
    wide = pltpu.VMEM((2, zc, 2, 2, piece, width), BF16)
    return exchange(
        functools.partial(middle_kernel, zc),
        3,
        (
            *[struct((own, width))] * 4,
            struct((own, width), F32),
            struct((zc, 2, 12, piece, width)),
        ),
        [VM] * 5 + [ANY],
        (VM,) * 5 + (ANY,),
        [blocks, blocks, wide, wide, pltpu.VMEM((zc, 2, 4, piece, width), BF16)]
        + [blocks] * 5
        + [pltpu.VMEM((3, width, width), BF16), DMA((21,))]
        + both(4)
        + both(4),
        (normed, *cots, weights),
        2 * 4 * own * width * width * 9,
        64 << 20,
    )


def turn_kernel(
    zc,
    c_ref,
    t_ref,
    r_ref,
    wo_ref,
    ob_ref,
    dr_ref,
    do_ref,
    dw_ref,
    slabs,
    stage,
    ls,
    d0,
    d1,
    b0,
    b1,
):
    me = Place(zc)
    chips = 4 * zc
    heads = slabs.shape[0]
    group = heads // 4
    per = zc // group
    width = t_ref.shape[1]
    meet([me.any_chip(k) for k in range(1, chips)] + [me.sibling()])
    total, residual = c_ref[...], r_ref[...]
    scaling = lax.rsqrt(jnp.mean(residual * residual, axis=-1, keepdims=True) + EPS)
    normed = residual * scaling
    middle = jnp.mean(total * normed, axis=-1, keepdims=True)
    grad = t_ref[...].astype(F32) + scaling * (total - normed * middle)
    dr_ref[...] = grad
    narrow = grad.astype(BF16)
    back = nt_dot(narrow, wo_ref[...])
    for pair in range(heads // 2):
        two = back[:, lanes(pair)]
        for side in range(2):
            slabs[2 * pair + side] = pair_up(two[:BLOCK], side, two[BLOCK:], side).astype(BF16)
    to = do_ref.at[me.z, me.c, me.g]
    own = move(slabs.at[me.g * group + me.z // per], to, ls, 0)
    sends = []
    for k in reversed(range(1, chips)):
        there = me.any_chip(k)
        head = (there[0] * 2 + there[2]) * group + there[1] // per
        sends.append(send(slabs.at[head], to, (d0, d1), k, there))
    chunk = 256
    attended = ob_ref[...]
    for first in range(0, width, chunk):
        stage[first : first + chunk] = tn_dot(attended[:, first : first + chunk], narrow).astype(BF16)
    parts = stage.reshape(2, zc, 2, 2, width // (8 * zc), width)
    keeps = []
    for k in range(4):
        there = me.plane(k)
        keeps.append(move(parts.at[there[0], :, there[2]], dw_ref.at[k], ls, 1 + k))
    own.wait()
    for copy in sends:
        copy.wait()
    half = do_ref.at[:, me.c]
    relay = send(half, half, (b0, b1), 0, me.sibling())
    for copy in keeps:
        copy.wait()
    relay.wait()


def turn_exchange(zc, c_sum, cotangent, residual, w_out, attn_rows):
    chips = 4 * zc
    own, width = cotangent.shape
    heads = width // HEAD_DIM
    return exchange(
        functools.partial(turn_kernel, zc),
        6,
        (
            struct((own, width), F32),
            struct((zc, 2, 4, BLOCK, PAIR)),
            struct((4, zc, 2, width // (8 * zc), width)),
        ),
        [VM] * 5,
        (VM, ANY, ANY),
        [
            pltpu.VMEM((heads, BLOCK, PAIR), BF16),
            pltpu.VMEM((width, width), BF16),
            DMA((5,)),
        ]
        + both(chips)
        + both(1),
        (c_sum, cotangent, residual, w_out, attn_rows),
        2 * 2 * own * width * width,
        8 << 20,
    )


def tail_kernel(
    zc,
    d_ref,
    n_ref,
    w_ref,
    x_ref,
    g_ref,
    v_ref,
    f_ref,
    r_ref,
    ya_ref,
    yb_ref,
    yc_ref,
    yd_ref,
    tg_ref,
    gw_ref,
    go_ref,
    gf_ref,
    out_ref,
    r_in,
    y_in,
    o_in,
    o_mine,
    o_theirs,
    o_land,
    mine,
    theirs,
    landed,
    grads,
    c_out,
    c_in,
    stage,
    other_w,
    ls,
    b0,
    b1,
    z0,
    z1,
    c0,
    c1,
    s0,
    s1,
    w0,
    w1,
    q0,
    q1,
    v0,
    v1,
    f0,
    f1,
):
    me = Place(zc)
    chips = 4 * zc
    group, per = landed.shape[:2]
    qw = group * HEAD_DIM
    meet([me.any_chip(k) for k in range(1, chips)] + [me.sibling()])
    head, place = me.z // per, me.z % per

    def slot(k):
        return (me.x ^ (k // 2)) * 2 + (me.y ^ (k % 2))

    order = (3, 2, 1, 0)
    halves = []
    for k in order:
        halves.append(
            (
                send(d_ref.at[:, 1 - me.c, slot(k)], theirs.at[k], (b0, b1), k, me.sibling()),
                move(d_ref.at[:, me.c, slot(k)], mine.at[k], ls, k),
            )
        )
    o_parts = [move(v_ref.at[0], o_in.at[0], ls, 9)]
    for k in (3, 1, 2):
        o_parts.append(send(v_ref.at[k], o_in.at[k], (v0, v1), k, me.plane(k)))
    f_parts = [move(f_ref.at[pl.ds(2 * me.g, 2)], gf_ref.at[me.g], ls, 10)]
    for k in (3, 1, 2):
        there = me.plane(k)
        part = f_ref.at[pl.ds(2 * (there[0] * 2 + there[2]), 2)]
        f_parts.append(send(part, gf_ref.at[me.g], (f0, f1), k, there))
    out_parts = [move(r_ref, r_in, ls, 11)]
    for i, ref in enumerate((ya_ref, yb_ref, yc_ref, yd_ref)):
        out_parts.append(move(ref, y_in.at[i], ls, 12 + i))
    for k, (far, near) in zip(order, halves):
        near.wait()
        far.wait()
        mine[k] = mine[k] + theirs[k]
        for over in range(1, zc):
            send(
                mine.at[k, me.z ^ over],
                landed.at[head, place, k],
                (z0, z1),
                k * zc + over,
                me.line(over),
            )
        move(mine.at[k, me.z], landed.at[head, place, k], ls, 4 + k)

    for copy in out_parts:
        copy.wait()
    final = r_in[...]
    for i in range(4):
        final = final + y_in[i].astype(F32)
    out_ref[...] = final.astype(BF16)

    def block(step, carry):
        k = 3 - step
        pltpu.make_async_copy(
            mine.at[k, me.z], landed.at[head, place, k], ls.at[4 + k]
        ).wait()
        for over in range(1, zc):
            trip(
                mine.at[k, me.z ^ over],
                landed.at[head, place, k],
                (z0, z1),
                k * zc + over,
                me.line(over),
            ).wait()
        for pair in range(group // 2):
            sides = []
            for side in range(2):
                h = 2 * pair + side
                slab = landed[h, 0, k]
                for extra in range(1, per):
                    slab = slab + landed[h, extra, k]
                start = qw + h * PAIR
                grads[k, :, start : start + PAIR] = slab[BLOCK:]
                sides.append(slab[:BLOCK].astype(F32))
            for b in range(2):
                grads[k, b * BLOCK : (b + 1) * BLOCK, lanes(pair)] = pair_up(
                    sides[0], b, sides[1], b
                ).astype(BF16)

        @pl.when(k > 0)
        def _():
            c_out[k] = nt_dot(grads[k], w_ref[...]).astype(BF16)
            trip(c_out.at[k], c_in.at[k], (c0, c1), k, me.plane(k)).start()

        return carry

    lax.fori_loop(0, 4, block, 0)
    for copy in o_parts:
        copy.wait()
    o_sum = o_in[0].astype(F32)
    for k in range(1, 4):
        o_sum = o_sum + o_in[k].astype(F32)
    o_mine[...] = o_sum.astype(BF16)
    o_swap = send(o_mine.at[:, 1 - me.c], o_theirs, (s0, s1), 1, me.sibling())
    width, cols = w_ref.shape
    all_rows = 4 * n_ref.shape[1]
    normed_all = n_ref[...].reshape(all_rows, width)
    grads_all = grads[...].reshape(all_rows, cols)
    piece = stage.shape[2]
    chunk = 256
    each = chunk // (2 * piece)
    swaps = []
    for first in range(0, width, chunk):
        value = tn_dot(normed_all[:, first : first + chunk], grads_all).astype(BF16)
        at = first // (2 * piece)
        stage[at : at + each] = value.reshape(each, 2, piece, cols)
        swaps.append(
            send(
                stage.at[at : at + each, 1 - me.c],
                other_w.at[at : at + each],
                (s0, s1),
                2 + first // chunk,
                me.sibling(),
            )
        )
    o_swap.wait()
    o_theirs[...] = o_theirs[...] + o_mine[:, me.c]
    sends = [
        send(o_theirs.at[me.z ^ k], o_land.at[k], (q0, q1), k, me.line(k)) for k in range(1, zc)
    ]
    c_out[0] = nt_dot(grads[0], w_ref[...]).astype(BF16)
    for swap in swaps:
        swap.wait()

    def add(i, carry):
        other_w[i] = stage[i, me.c] + other_w[i]
        return carry

    lax.fori_loop(0, chips, add, 0)
    stay = move(other_w.at[me.chip], gw_ref.at[me.z, me.g], ls, 8)
    for k in reversed(range(1, chips)):
        there = me.any_chip(k)
        chip = (there[0] * zc + there[1]) * 2 + there[2]
        sends.append(send(other_w.at[chip], gw_ref.at[me.z, me.g], (w0, w1), k, there))
    total = c_out[0].astype(F32)
    for k in range(1, 4):
        trip(c_out.at[k], c_in.at[k], (c0, c1), k, me.plane(k)).wait()
        total = total + c_in[k].astype(F32)
    x = x_ref[...].astype(F32)
    scaling = lax.rsqrt(jnp.mean(x * x, axis=-1, keepdims=True) + EPS)
    normed = x * scaling
    middle = jnp.mean(total * normed, axis=-1, keepdims=True)
    tg_ref[...] = (g_ref[...] + scaling * (total - normed * middle)).astype(BF16)
    stay.wait()
    for copy in sends + f_parts:
        copy.wait()
    o_sum = o_theirs[me.z].astype(F32)
    for k in range(1, zc):
        o_sum = o_sum + o_land[k].astype(F32)
    go_ref[...] = o_sum


def tail_exchange(zc, group, slab_grads, n_all, weights, tokens, residual_grad, out_grads, shares, residual, outs):
    chips = 4 * zc
    per = zc // group
    own, width = tokens.shape
    cols = weights.shape[1]
    slab = slab_grads.shape[3:]
    piece = width // (2 * chips)
    blocks = pltpu.VMEM((4, own, width), BF16)
    return exchange(
        functools.partial(tail_kernel, zc),
        4,
        (
            struct((own, width)),
            struct((zc, 4, piece, cols)),
            struct((piece, width), F32),
            struct((4, 2, piece, width)),
            struct((own, width)),
        ),
        [ANY] + [VM] * 4 + [ANY] * 7,
        (VM, ANY, VM, ANY, VM),
        [
            pltpu.VMEM((own, width), F32),
            pltpu.VMEM((4, own, width), BF16),
            pltpu.VMEM((4, zc, 2, piece, width), BF16),
            pltpu.VMEM((zc, 2, piece, width), BF16),
            pltpu.VMEM((zc, piece, width), BF16),
            pltpu.VMEM((zc, piece, width), BF16),
            pltpu.VMEM((4, zc) + slab, BF16),
            pltpu.VMEM((4, zc) + slab, BF16),
            pltpu.VMEM((group, per, 4) + slab, BF16),
            pltpu.VMEM((4, own, cols), BF16),
            blocks,
            blocks,
            pltpu.VMEM((chips, 2, piece, cols), BF16),
            pltpu.VMEM((chips, piece, cols), BF16),
            DMA((16,)),
        ]
        + both(4)
        + both(4 * zc)
        + both(4)
        + both(2 + width // 256)
        + both(chips)
        + both(zc)
        + both(4)
        + both(4),
        (slab_grads, n_all, weights, tokens, residual_grad, out_grads, shares, residual, *outs),
        2 * 4 * own * width * cols * 2,
        24 << 20,
    )


def last_kernel(
    zc,
    group,
    t_any,
    o_any,
    wo_any,
    gw_any,
    gf_any,
    ds_any,
    q_any,
    k_any,
    v_any,
    g_any,
    u_any,
    gain1,
    gain2,
    tg_ref,
    out_ref,
    go_ref,
    g1_ref,
    q_ref,
    k_ref,
    v_ref,
    g2_ref,
    g_ref,
    u_ref,
    d_ref,
    gw_ref,
    gf_ref,
    ds_ref,
    q_w,
    k_w,
    v_w,
    g_w,
    u_w,
    ls,
):
    given = (gw_any, q_any, k_any, v_any, gf_any, g_any, u_any, ds_any, t_any, o_any, wo_any)
    taken = (gw_ref, q_w, k_w, v_w, gf_ref, g_w, u_w, ds_ref, tg_ref, out_ref, go_ref)
    copies = [move(a, b, ls, i) for i, (a, b) in enumerate(zip(given, taken))]
    for copy in copies:
        copy.wait()
    d_ref[...] = ds_ref[8:].astype(F32).reshape(d_ref.shape)
    first_gain, second_gain = column_of(low(gain1[...])), column_of(low(gain2[...]))
    count = q_w.shape[0]
    qw = group * HEAD_DIM
    score = jnp.zeros((count, PAIR), F32)
    for g in range(4):
        raw = gw_ref[0, g].astype(F32)
        for z in range(1, zc):
            raw = raw + gw_ref[z, g].astype(F32)
        for pair in range(group // 2):
            at = lanes(g * group // 2 + pair)
            start = qw + 2 * pair * PAIR
            even, odd = raw[:, start : start + PAIR], raw[:, start + PAIR : start + 2 * PAIR]
            query = raw[:, lanes(pair)]
            key, value = pair_up(even, 0, odd, 0), pair_up(even, 1, odd, 1)
            score = score + query * low(q_w[:, at]) + key * low(k_w[:, at]) + value * low(v_w[:, at])
            q_ref[:, at] = first_gain * query
            k_ref[:, at] = first_gain * key
            v_ref[:, at] = first_gain * value
    g1_ref[...] = row_of(jnp.sum(score, axis=1, keepdims=True))
    units = g_w.shape[1] // (4 * zc)
    score = jnp.zeros((count, PAIR), F32)
    for which, (weight, target) in enumerate(((g_w, g_ref), (u_w, u_ref))):
        for chunk in range(weight.shape[1] // PAIR):
            if units % PAIR == 0:
                owner, piece = divmod(chunk, units // PAIR)
                x, z, y = owner // (2 * zc), owner // 2 % zc, owner % 2
                raw = gf_ref[2 * x + y, which, :, lanes(z * units // PAIR + piece)].astype(F32)
            else:
                x, z = chunk // zc, chunk % zc
                near = gf_ref[2 * x, which, :, lanes(z // 2)].astype(F32)
                far = gf_ref[2 * x + 1, which, :, lanes(z // 2)].astype(F32)
                raw = pair_up(near, z % 2, far, z % 2)
            score = score + raw * low(weight[:, lanes(chunk)])
            target[:, lanes(chunk)] = second_gain * raw
    g2_ref[...] = row_of(jnp.sum(score, axis=1, keepdims=True))


def last_step(zc, group, tokens_grad, output, out_share, w_all, f_all, shares, matrices, gains):
    own, width = output.shape
    count, hidden = matrices[3].shape
    return pl.pallas_call(
        functools.partial(last_kernel, zc, group),
        out_shape=(
            struct((own, width)),
            struct((own, width)),
            struct((count, width), F32),
            struct((1, count), F32),
            struct((count, width), F32),
            struct((count, width), F32),
            struct((count, width), F32),
            struct((1, count), F32),
            struct((count, hidden), F32),
            struct((count, hidden), F32),
            struct((4 * count, width), F32),
        ),
        in_specs=[ANY] * 11 + [VM] * 2,
        out_specs=(VM,) * 11,
        scratch_shapes=[
            pltpu.VMEM(v.shape, v.dtype) for v in (w_all, f_all, shares, *matrices)
        ]
        + [DMA((11,))],
        compiler_params=pltpu.CompilerParams(vmem_limit_bytes=60 << 20),
    )(
        tokens_grad,
        output,
        out_share,
        w_all,
        f_all,
        shares,
        *matrices,
        *(g.reshape(1, -1) for g in gains),
    )


def segment_start(position, lens_ref):
    start = jnp.zeros_like(position)
    end = 0
    for j in range(lens_ref.shape[0]):
        end = end + lens_ref[j]
        start = jnp.where(position >= end, end, start)
    return start


def note_tiles(workers, worker, tiles, lens_ref, mine):
    turns = tiles // workers

    def snake(turn, carry):
        forward = turn * workers + worker
        backward = turn * workers + workers - 1 - worker
        mine[turn] = jnp.where((turn & 1) == 0, forward, backward)
        return carry

    def weigh(step, ahead):
        turn = turns - 1 - step
        loads = []
        for tile in (2 * turn, 2 * turn + 1):
            first, _, _, last = key_bounds(tile * QTILE, lens_ref)
            loads.append(last - first)
        lighter_first = loads[0] <= loads[1]
        first_to_zero = jnp.where(ahead > 0, lighter_first, loads[0] > loads[1])
        mine[turn] = 2 * turn + jnp.where(first_to_zero, worker, 1 - worker)
        return ahead + jnp.where(first_to_zero, loads[0] - loads[1], loads[1] - loads[0])

    if workers == 2:
        lax.fori_loop(0, turns, weigh, 0)
    else:
        lax.fori_loop(0, turns, snake, 0)


def key_bounds(first, lens_ref):
    low_start = segment_start(first, lens_ref)
    high_start = segment_start(first + QTILE - 1, lens_ref)
    low = low_start // KTILE
    high = (first + QTILE + KTILE - 1) // KTILE
    plain = jnp.clip((high_start + KTILE - 1) // KTILE, low, high)
    stop = jnp.clip((first + 1) // KTILE, plain, high)
    return low, plain, stop, high


def visible(first, tile, starts):
    key = tile * KTILE + lax.broadcasted_iota(jnp.int32, (KTILE, QTILE), 0)
    query = first + lax.broadcasted_iota(jnp.int32, (KTILE, QTILE), 1)
    return (key <= query) & (key >= starts)


def note_places(anchor_ref, inv):
    def note(i, carry):
        inv[anchor_ref[i]] = i
        return carry

    lax.fori_loop(0, anchor_ref.shape[0], note, 0)


def half_lanes(rows, half):
    lane = lax.broadcasted_iota(jnp.int32, rows.shape, 1)
    return jnp.where((lane // HEAD_DIM) == half, rows, jnp.zeros_like(rows))


def fold(rows, columns, first):
    row = lax.broadcasted_iota(jnp.int32, (rows, columns), 0)
    column = lax.broadcasted_iota(jnp.int32, (rows, columns), 1)
    return (row % HEAD_DIM == column - first).astype(F32).astype(BF16)


def unfold(rows, columns, first):
    row = lax.broadcasted_iota(jnp.int32, (rows, columns), 0)
    column = lax.broadcasted_iota(jnp.int32, (rows, columns), 1)
    return (column % HEAD_DIM == row - first).astype(F32).astype(BF16)


def forward_kernel(
    workers, anchor_ref, lens_ref, who_ref, a_ref, o_ref, kv_ref, kvt_ref, q_ref, qt_ref, ot_ref, l_ref, inv, mine, raw
):
    blocks = anchor_ref.shape[0]
    turns = qt_ref.shape[0]
    per = QTILE // BLOCK
    worker = who_ref[0]
    note_places(anchor_ref, inv)
    note_tiles(workers, worker, turns * workers, lens_ref, mine)
    o_ref[...] = jnp.zeros_like(o_ref)
    same = selection(PAIR, PAIR, 0)

    def order(step, carry):
        for b in range(per):
            i = step * per + b
            where = inv[i]
            slab, half = where >> 1, where & 1
            at = pl.ds(pl.multiple_of(i * BLOCK, BLOCK), BLOCK)
            kv_ref[at, :] = a_ref[slab, pl.ds(pl.multiple_of(BLOCK + half * BLOCK, BLOCK), BLOCK), :]
        return carry

    lax.fori_loop(0, blocks // per, order, 0)

    def flip(step, carry):
        at = pl.ds(pl.multiple_of(step * TURNED, TURNED), TURNED)
        kvt_ref[:, at] = nt_dot(same, kv_ref[at, :]).astype(BF16)
        return carry

    lax.fori_loop(0, blocks * BLOCK // TURNED, flip, 0)

    def one_tile(turn, carry):
        tile = mine[turn]
        first = tile * QTILE
        for b in range(per):
            where = inv[tile * per + b]
            raw[b * BLOCK : (b + 1) * BLOCK, :] = half_lanes(a_ref[where >> 1, :BLOCK, :], where & 1)
        q_ref[turn] = (dot(raw[...], fold(PAIR, PAIR, 0)) * 0.125).astype(BF16)
        qt_ref[turn] = (nt_dot(unfold(PAIR, PAIR, 0), raw[...]) * 0.125).astype(BF16)
        query = qt_ref[turn]
        starts = segment_start(first + lax.broadcasted_iota(jnp.int32, (1, QTILE), 1), lens_ref)
        low, plain, stop, high = key_bounds(first, lens_ref)

        def step(masked, kt, state):
            top, total, acc = state
            at = pl.ds(pl.multiple_of(kt * KTILE, KTILE), KTILE)
            scores = dot(kv_ref[at, :], query)
            if masked:
                scores = jnp.where(visible(first, kt, starts), scores, MASKED)
            new_top = jnp.maximum(top, jnp.max(scores, axis=0, keepdims=True))
            factor = jnp.exp(top - new_top)
            weights = jnp.exp(scores - new_top)
            total = total * factor + jnp.sum(weights, axis=0, keepdims=True)
            acc = acc * factor + dot(kvt_ref[HEAD_DIM:, at], weights.astype(BF16))
            return (new_top, total, acc)

        state = (
            jnp.full((1, QTILE), LOWEST, F32),
            jnp.zeros((1, QTILE), F32),
            jnp.zeros((HEAD_DIM, QTILE), F32),
        )
        state = lax.fori_loop(low, plain, functools.partial(step, True), state)
        state = lax.fori_loop(plain, stop, functools.partial(step, False), state)
        top, total, acc = lax.fori_loop(stop, high, functools.partial(step, True), state)
        out = acc / total
        ot_ref[turn] = out
        l_ref[turn] = top + jnp.log(total)
        wide = tn_dot(out.astype(BF16), unfold(HEAD_DIM, PAIR, 0)).astype(BF16)
        for b in range(per):
            where = inv[tile * per + b]
            slab = where >> 1
            o_ref[slab] = o_ref[slab] + half_lanes(wide[b * BLOCK : (b + 1) * BLOCK], where & 1)
        return carry

    lax.fori_loop(0, turns, one_tile, 0)


def attention_forward(workers, anchors, lengths, who, packed):
    slabs = packed.shape[0]
    rows = slabs * 2 * BLOCK
    turns = rows // QTILE // workers
    return pl.pallas_call(
        functools.partial(forward_kernel, workers),
        out_shape=(
            struct((slabs, BLOCK, PAIR)),
            struct((rows, PAIR)),
            struct((PAIR, rows)),
            struct((turns, QTILE, PAIR)),
            struct((turns, PAIR, QTILE)),
            struct((turns, HEAD_DIM, QTILE), F32),
            struct((turns, 1, QTILE), F32),
        ),
        in_specs=[SM, SM, SM, VM],
        out_specs=(VM,) * 7,
        scratch_shapes=[
            pltpu.SMEM((2 * slabs,), jnp.int32),
            pltpu.SMEM((turns,), jnp.int32),
            pltpu.VMEM((QTILE, PAIR), BF16),
        ],
        compiler_params=pltpu.CompilerParams(vmem_limit_bytes=60 << 20),
        cost_estimate=pl.CostEstimate(
            flops=rows * rows * 64, bytes_accessed=rows * 1024, transcendentals=rows * rows // 8
        ),
    )(anchors, lengths, who, packed)


def backward_kernel(
    workers,
    anchor_ref,
    lens_ref,
    who_ref,
    d_ref,
    kv_ref,
    kvt_ref,
    q_ref,
    qt_ref,
    ot_ref,
    l_ref,
    g_ref,
    inv,
    mine,
    raw,
    both_rows,
    dt,
    acc,
):
    blocks = anchor_ref.shape[0]
    turns = qt_ref.shape[0]
    per = QTILE // BLOCK
    worker = who_ref[0]
    note_places(anchor_ref, inv)
    note_tiles(workers, worker, turns * workers, lens_ref, mine)
    acc[...] = jnp.zeros_like(acc)
    g_ref[:, :BLOCK, :] = jnp.zeros((g_ref.shape[0], BLOCK, PAIR), BF16)

    def one_tile(turn, carry):
        tile = mine[turn]
        first = tile * QTILE
        for b in range(per):
            where = inv[tile * per + b]
            raw[b * BLOCK : (b + 1) * BLOCK, :] = half_lanes(d_ref[where >> 1], where & 1)
        both_rows[:QTILE] = q_ref[turn]
        both_rows[QTILE:] = dot(raw[...], fold(PAIR, PAIR, HEAD_DIM)).astype(BF16)
        dt[...] = nt_dot(unfold(PAIR, PAIR, HEAD_DIM), raw[...]).astype(BF16)
        query, grad = qt_ref[turn], dt[...]
        norm = l_ref[turn]
        delta = jnp.sum(grad[HEAD_DIM:].astype(F32) * ot_ref[turn], axis=0, keepdims=True)
        starts = segment_start(first + lax.broadcasted_iota(jnp.int32, (1, QTILE), 1), lens_ref)
        low, plain, stop, high = key_bounds(first, lens_ref)

        def step(masked, kt, total):
            at = pl.ds(pl.multiple_of(kt * KTILE, KTILE), KTILE)
            keys = kv_ref[at, :]
            scores = dot(keys, query)
            if masked:
                scores = jnp.where(visible(first, kt, starts), scores, MASKED)
            weights = jnp.exp(scores - norm)
            score_grad = (weights * (dot(keys, grad) - delta)).astype(BF16)
            both_grads = jnp.concatenate([score_grad, weights.astype(BF16)], axis=1)
            acc[at, :] += dot(both_grads, both_rows[...])
            return total + dot(kvt_ref[:HEAD_DIM, at], score_grad)

        total = jnp.zeros((HEAD_DIM, QTILE), F32)
        total = lax.fori_loop(low, plain, functools.partial(step, True), total)
        total = lax.fori_loop(plain, stop, functools.partial(step, False), total)
        total = lax.fori_loop(stop, high, functools.partial(step, True), total)
        wide = tn_dot((total * 0.125).astype(BF16), unfold(HEAD_DIM, PAIR, 0)).astype(BF16)
        for b in range(per):
            where = inv[tile * per + b]
            slab = where >> 1
            g_ref[slab, :BLOCK] = g_ref[slab, :BLOCK] + half_lanes(
                wide[b * BLOCK : (b + 1) * BLOCK], where & 1
            )
        return carry

    lax.fori_loop(0, turns, one_tile, 0)

    def place(step, carry):
        for b in range(per):
            i = step * per + b
            where = inv[i]
            slab, half = where >> 1, where & 1
            at = pl.ds(pl.multiple_of(i * BLOCK, BLOCK), BLOCK)
            to = pl.ds(pl.multiple_of(BLOCK + half * BLOCK, BLOCK), BLOCK)
            g_ref[slab, to, :] = acc[at, :].astype(BF16)
        return carry

    lax.fori_loop(0, blocks // per, place, 0)


def attention_backward(workers, anchors, lengths, who, grads, kept):
    slabs = grads.shape[0]
    rows = slabs * 2 * BLOCK
    return pl.pallas_call(
        functools.partial(backward_kernel, workers),
        out_shape=struct((slabs, 3 * BLOCK, PAIR)),
        in_specs=[SM, SM, SM] + [VM] * 7,
        out_specs=VM,
        scratch_shapes=[
            pltpu.SMEM((2 * slabs,), jnp.int32),
            pltpu.SMEM((rows // QTILE // workers,), jnp.int32),
            pltpu.VMEM((QTILE, PAIR), BF16),
            pltpu.VMEM((2 * QTILE, PAIR), BF16),
            pltpu.VMEM((PAIR, QTILE), BF16),
            pltpu.VMEM((rows, PAIR), F32),
        ],
        compiler_params=pltpu.CompilerParams(vmem_limit_bytes=60 << 20),
        cost_estimate=pl.CostEstimate(
            flops=rows * rows * 160, bytes_accessed=rows * 1024, transcendentals=rows * rows // 8
        ),
    )(anchors, lengths, who, grads, *kept)


def around(value, k):
    return lax.ppermute(value, ("head", "y"), [(i, i ^ k) for i in range(4)])


def along(value, k):
    return lax.ppermute(value, "z", [(i, i ^ k) for i in range(lax.axis_size("z"))])


def body(
    zc,
    tokens,
    cotangent,
    norm1_gain,
    w_query,
    w_key,
    w_value,
    w_out,
    norm2_gain,
    w_gate,
    w_up,
    w_down,
    block_anchor,
    seq_lengths,
):
    width = tokens.shape[1]
    heads = width // HEAD_DIM
    group = heads // 4
    per_head = zc // group
    workers = 2 * per_head
    feature_rows = w_query.shape[0]

    n1_all, qkv_w, ffn_in, by_head, *near, w_o = head_exchange(
        zc,
        group,
        tokens,
        (w_query, w_key, w_value, w_gate, w_up, w_down, w_out),
        cotangent,
        (norm1_gain, norm2_gain),
    )
    cots = [cotangent] + near
    w_parts = [w_o] + [along(w_o, k) for k in range(1, zc)]
    qkv_w = qkv_w.reshape(width, 3 * group * HEAD_DIM)

    ffn_all = lax.all_gather(ffn_in, ("z", "core"), axis=0, tiled=False).reshape(
        zc, 2, 12, feature_rows, width
    )

    anchors = jnp.transpose(block_anchor.reshape(2, zc, 2, 2, 2), (1, 3, 0, 2, 4)).reshape(-1)
    who = ((lax.axis_index("z") % per_head) * 2 + lax.axis_index("core")).astype(jnp.int32).reshape(1)
    slab_count = zc * 8
    o_slabs, *kept = attention_forward(
        workers, anchors, seq_lengths, who, by_head.reshape((slab_count,) + by_head.shape[3:])
    )
    attn_rows, residual, normed_two, out_mat = join_exchange(
        zc, heads, o_slabs.reshape(zc, 2, 4, BLOCK, PAIR), tokens, w_parts
    )
    out_mat = out_mat.reshape(width, width)
    *out_parts, c_sum, shares = middle_exchange(zc, normed_two, cots, ffn_all)
    shares = lax.psum_scatter(
        shares.reshape(zc * 2 * 12, feature_rows, width), ("z", "core"), scatter_dimension=0, tiled=True
    )
    residual_grad, do_heads, out_grads = turn_exchange(
        zc, c_sum, cotangent, residual, out_mat, attn_rows
    )
    do_heads, *out_parts = lax.optimization_barrier((do_heads, *out_parts))
    outs = [out_parts[0]] + [around(out_parts[k], k) for k in range(1, 4)]
    grad_heads = attention_backward(
        workers, anchors, seq_lengths, who, do_heads.reshape(slab_count, BLOCK, PAIR), kept
    )
    tokens_grad, w_all, out_share, f_all, output = tail_exchange(
        zc,
        group,
        grad_heads.reshape(zc, 2, 4, 3 * BLOCK, PAIR),
        n1_all,
        qkv_w,
        tokens,
        residual_grad,
        out_grads,
        shares,
        residual,
        outs,
    )
    (
        tokens_grad,
        output,
        out_grad,
        gain1_grad,
        query_grad,
        key_grad,
        value_grad,
        gain2_grad,
        gate_grad,
        up_grad,
        down_grad,
    ) = last_step(
        zc,
        group,
        tokens_grad,
        output,
        out_share,
        w_all,
        f_all,
        shares,
        (w_query, w_key, w_value, w_gate, w_up),
        (norm1_gain, norm2_gain),
    )
    return (
        output,
        tokens_grad,
        gain1_grad.reshape(-1),
        query_grad,
        key_grad,
        value_grad,
        out_grad,
        gain2_grad.reshape(-1),
        gate_grad,
        up_grad,
        down_grad,
    )


def solution(mesh):
    blk = mesh.shape["blk"]
    grid = Mesh(mesh.devices.reshape(mesh.shape["head"], blk // 4, 2, 2), AXES)
    rows, vector, whole = P(AXES, None), P(AXES), P()
    return jax.shard_map(
        functools.partial(body, blk // 4),
        mesh=grid,
        in_specs=(rows, rows, vector, rows, rows, rows, rows, vector, rows, rows, rows, whole, whole),
        out_specs=(rows, rows, vector, rows, rows, rows, rows, vector, rows, rows, rows),
        check_vma=False,
    )
```

```python
import functools

import jax
import jax.numpy as jnp
from jax import lax
from jax.experimental import pallas as pl
from jax.experimental.pallas import tpu as pltpu
from jax.sharding import Mesh
from jax.sharding import PartitionSpec as P

HEAD_DIM = 64
BLOCK = 128
PAIR = 128
EPS = 1e-06
MASKED = -1e30
LOWEST = -1e20
QTILE = 512
KTILE = 512
TURNED = 2048
AXES = ("head", "z", "y", "core")
IDS = pl.DeviceIdType.MESH
F32 = jnp.float32
BF16 = jnp.bfloat16
ANY = pl.BlockSpec(memory_space=pl.ANY)
VM = pl.BlockSpec(memory_space=pltpu.VMEM)
SM = pl.BlockSpec(memory_space=pltpu.SMEM)


def struct(shape, dtype=BF16):
    return jax.ShapeDtypeStruct(tuple(shape), dtype)


def nt_dot(a, b):
    return lax.dot_general(a, b, (((1,), (1,)), ((), ())), preferred_element_type=F32)


def tn_dot(a, b):
    return lax.dot_general(a, b, (((0,), (0,)), ((), ())), preferred_element_type=F32)


def dot(a, b):
    return jnp.dot(a, b, preferred_element_type=F32)


def selection(rows, columns, shift, first=0, last=None):
    last = columns if last is None else last
    row = lax.broadcasted_iota(jnp.int32, (rows, columns), 0)
    column = lax.broadcasted_iota(jnp.int32, (rows, columns), 1)
    hit = (row == column + shift) & (column >= first) & (column < last)
    return hit.astype(F32).astype(BF16)


def pair_up(first, first_half, second, second_half):
    lane = lax.broadcasted_iota(jnp.int32, first.shape, 1)
    left = first if first_half == 0 else pltpu.roll(first, HEAD_DIM, 1)
    right = second if second_half == 1 else pltpu.roll(second, HEAD_DIM, 1)
    return jnp.where(lane < HEAD_DIM, left, right)


def column_of(row):
    count = row.shape[1]
    i = lax.broadcasted_iota(jnp.int32, (count, count), 0)
    j = lax.broadcasted_iota(jnp.int32, (count, count), 1)
    return jnp.sum(jnp.where(i == j, row, 0.0), axis=1, keepdims=True)


def row_of(column):
    count = column.shape[0]
    i = lax.broadcasted_iota(jnp.int32, (count, count), 0)
    j = lax.broadcasted_iota(jnp.int32, (count, count), 1)
    return jnp.sum(jnp.where(i == j, column, 0.0), axis=0, keepdims=True)


def low(value):
    return value.astype(BF16).astype(F32)


def lanes(index):
    return slice(index * PAIR, (index + 1) * PAIR)


class Place:
    def __init__(self, z_count):
        self.x, self.z, self.y, self.c = (lax.axis_index(a) for a in AXES)
        self.g = self.x * 2 + self.y
        self.chip = (self.x * z_count + self.z) * 2 + self.y

    def sibling(self):
        return (self.x, self.z, self.y, 1 - self.c)

    def plane(self, k):
        return (self.x ^ (k // 2), self.z, self.y ^ (k % 2), self.c)

    def line(self, k):
        return (self.x, self.z ^ k, self.y, self.c)

    def any_chip(self, k):
        return (self.x ^ (k // 2 % 2), self.z ^ (k // 4), self.y ^ (k % 2), self.c)


def meet(peers):
    barrier = pltpu.get_barrier_semaphore()
    for peer in peers:
        pl.semaphore_signal(barrier, inc=1, device_id=peer, device_id_type=IDS)
    pl.semaphore_wait(barrier, len(peers))


def trip(source, target, sems, index, device):
    return pltpu.make_async_remote_copy(
        src_ref=source,
        dst_ref=target,
        send_sem=sems[0].at[index],
        recv_sem=sems[1].at[index],
        device_id=device,
        device_id_type=IDS,
    )


def send(*given):
    copy = trip(*given)
    copy.start()
    return copy


def move(source, target, sems, index):
    copy = pltpu.make_async_copy(source, target, sems.at[index])
    copy.start()
    return copy


DMA = pltpu.SemaphoreType.DMA


def both(count):
    return [DMA((count,)), DMA((count,))]


def exchange(kernel, ident, out_shape, in_specs, out_specs, scratch, args, flops, sent):
    return pl.pallas_call(
        kernel,
        out_shape=out_shape,
        in_specs=in_specs,
        out_specs=out_specs,
        scratch_shapes=scratch,
        compiler_params=pltpu.CompilerParams(
            collective_id=ident, has_side_effects=True, vmem_limit_bytes=60 << 20
        ),
        cost_estimate=pl.CostEstimate(flops=flops, bytes_accessed=sent, transcendentals=0),
    )(*args)


def head_kernel(
    zc,
    group,
    t_ref,
    q_w,
    k_w,
    v_w,
    g_w,
    u_w,
    d_w,
    o_w,
    t2_ref,
    gain1,
    gain2,
    ng_ref,
    wg_ref,
    fg_ref,
    a_ref,
    ca_ref,
    cb_ref,
    og_ref,
    w_ref,
    f_ref,
    e_ref,
    wo_ref,
    rows,
    weights,
    packed,
    ls,
    w0,
    w1,
    n0,
    n1,
    f0,
    f1,
    z0,
    z1,
    b0,
    b1,
    s0,
    s1,
    t0,
    t1,
    o0,
    o1,
):
    me = Place(zc)
    chips = 4 * zc
    per = zc // group
    qw = group * HEAD_DIM
    width = t_ref.shape[1]
    first_gain, second_gain = column_of(low(gain1[...])), column_of(low(gain2[...]))
    for g in range(4):
        at = slice(g * qw, (g + 1) * qw)
        w_ref[g, :, :qw] = (first_gain * low(q_w[:, at])).astype(BF16)
        for pair in range(group // 2):
            at = lanes(g * group // 2 + pair)
            key, value = first_gain * low(k_w[:, at]), first_gain * low(v_w[:, at])
            for half in range(2):
                start = qw + (2 * pair + half) * PAIR
                w_ref[g, :, start : start + PAIR] = pair_up(key, half, value, half).astype(BF16)
    e_ref[...] = d_w[...].astype(BF16).reshape(e_ref.shape)
    wo_ref[...] = o_w[...].astype(BF16)
    x = t_ref[...].astype(F32)
    rows[0] = (x * lax.rsqrt(jnp.mean(x * x, axis=-1, keepdims=True) + EPS)).astype(BF16)
    meet([me.any_chip(k) for k in range(1, chips)] + [me.sibling()])
    here = og_ref.at[me.z]
    local = [move(w_ref.at[me.g], weights.at[me.chip, me.c], ls, 0), move(wo_ref, here, ls, 1)]
    pieces = []
    for k in reversed(range(1, chips)):
        there = me.any_chip(k)
        their_g = there[0] * 2 + there[2]
        pieces.append(
            send(w_ref.at[their_g], weights.at[me.chip, me.c], (w0, w1), k, there)
        )
    outs = [send(wo_ref, here, (o0, o1), k, me.line(k)) for k in range(1, zc)]
    blocks = [send(rows.at[0], rows.at[k], (n0, n1), k, me.plane(k)) for k in range(1, 4)]
    units = g_w.shape[1] // (4 * zc)
    for which, ref in enumerate((g_w, u_w)):
        for g in range(4):
            px, py = g // 2, g % 2
            if units % PAIR == 0:
                for z in range(zc):
                    at = ((px * zc + z) * 2 + py) * units
                    f_ref[g, which, :, z * units : (z + 1) * units] = (
                        second_gain * low(ref[:, at : at + units])
                    ).astype(BF16)
            else:
                for z in range(0, zc, 2):
                    near, far = (second_gain * low(ref[:, lanes(px * zc + i)]) for i in (z, z + 1))
                    f_ref[g, which, :, lanes(z // 2)] = pair_up(near, py, far, py).astype(BF16)
    wide = [
        move(f_ref.at[me.g], fg_ref.at[me.x, me.y, pl.ds(0, 2)], ls, 2),
        move(e_ref, fg_ref.at[:, :, 2], ls, 9),
    ]
    for k in range(1, 4):
        there = me.plane(k)
        their_g = there[0] * 2 + there[2]
        wide.append(
            send(f_ref.at[their_g], fg_ref.at[me.x, me.y, pl.ds(0, 2)], (f0, f1), k, there)
        )
    for k, ref in ((1, ca_ref), (2, cb_ref)):
        wide.append(send(t2_ref, ref, (t0, t1), k, me.plane(k)))
    local[0].wait()
    for copy in pieces:
        copy.wait()
    relay = send(
        weights.at[:, me.c], weights.at[:, me.c], (s0, s1), 0, me.sibling()
    )
    relay.wait()
    kept = [move(weights, wg_ref, ls, 3)]

    def project(k, carry):
        @pl.when(k > 0)
        def _():
            trip(rows.at[0], rows.at[k], (n0, n1), k, me.plane(k)).wait_recv()

        at = (me.x ^ (k // 2)) * 2 + (me.y ^ (k % 2))
        out = dot(rows[k], weights[...].reshape(width, 3 * qw))
        for head in range(group):
            two, half = out[:, lanes(head // 2)], head % 2
            packed[head, k, :BLOCK] = pair_up(two[:BLOCK], half, two[BLOCK:], half).astype(BF16)
            start = qw + head * PAIR
            packed[head, k, BLOCK:] = out[:, start : start + PAIR].astype(BF16)
        for over in range(1, zc):
            trip(
                packed.at[(me.z ^ over) // per, k],
                a_ref.at[me.z, me.c, at],
                (z0, z1),
                k * zc + over,
                me.line(over),
            ).start()
        trip(
            packed.at[me.z // per, k], a_ref.at[me.z, me.c, at], (b0, b1), k * zc, me.sibling()
        ).start()
        pltpu.make_async_copy(
            packed.at[me.z // per, k], a_ref.at[me.z, me.c, at], ls.at[4 + k]
        ).start()
        return carry

    lax.fori_loop(0, 4, project, 0)
    kept.append(move(rows, ng_ref, ls, 8))

    def pass_on(step, carry):
        k, over = step // (zc - 1), step % (zc - 1) + 1
        at = (me.x ^ (k // 2)) * 2 + (me.y ^ (k % 2))
        there = me.z ^ over
        trip(
            packed.at[there // per, k],
            a_ref.at[me.z, me.c, at],
            (z0, z1),
            k * zc + over,
            me.line(over),
        ).wait()
        landed = a_ref.at[there, me.c, at]
        trip(landed, landed, (b0, b1), k * zc + over, me.sibling()).start()
        return carry

    lax.fori_loop(0, 4 * (zc - 1), pass_on, 0)

    def finish(step, carry):
        k, over = step // zc, step % zc
        at = (me.x ^ (k // 2)) * 2 + (me.y ^ (k % 2))
        landed = a_ref.at[me.z ^ over, me.c, at]
        trip(landed, landed, (b0, b1), k * zc + over, me.sibling()).wait()
        return carry

    lax.fori_loop(0, 4 * zc, finish, 0)
    for k in range(4):
        pltpu.make_async_copy(
            packed.at[me.z // per, k], a_ref.at[me.z, me.c, me.g], ls.at[4 + k]
        ).wait()
    for copy in kept + wide + outs + local[1:]:
        copy.wait()
    for copy in blocks:
        copy.wait_send()


def head_exchange(zc, group, tokens, matrices, cotangent, gains):
    chips = 4 * zc
    own, width = tokens.shape
    count = matrices[0].shape[0]
    piece = (count, 3 * group * HEAD_DIM)
    return exchange(
        functools.partial(head_kernel, zc, group),
        1,
        (
            struct((4, own, width)),
            struct((chips, 2) + piece),
            struct((2, 2, 3, count, width)),
            struct((zc, 2, 4, BLOCK + own, PAIR)),
            struct((own, width)),
            struct((own, width)),
            struct((zc, count, width)),
        ),
        [VM] * 8 + [ANY] + [VM] * 2,
        (ANY,) * 7,
        [
            pltpu.VMEM((4,) + piece, BF16),
            pltpu.VMEM((4, 2, count, width), BF16),
            pltpu.VMEM((2, 2, count, width), BF16),
            pltpu.VMEM((count, width), BF16),
            pltpu.VMEM((4, own, width), BF16),
            pltpu.VMEM((chips, 2) + piece, BF16),
            pltpu.VMEM((group, 4, BLOCK + own, PAIR), BF16),
            DMA((10,)),
        ]
        + both(chips)
        + both(4)
        + both(4)
        + both(4 * zc)
        + both(4 * zc)
        + both(1)
        + both(4)
        + both(zc),
        (tokens, *matrices, cotangent, *(g.reshape(1, -1) for g in gains)),
        2 * 4 * own * width * width,
        16 << 20,
    )


def join_kernel(
    zc,
    s_ref,
    x_ref,
    w_ref,
    ob_ref,
    r_ref,
    n_ref,
    og_ref,
    mine,
    theirs,
    slabs,
    all_w,
    ls,
    b0,
    b1,
    c0,
    c1,
    p0,
    p1,
):
    me = Place(zc)
    chips = 4 * zc
    heads, per = slabs.shape[:2]
    meet([me.any_chip(k) for k in range(1, chips)] + [me.sibling()])
    other = send(s_ref.at[:, 1 - me.c], theirs, (b0, b1), 0, me.sibling())
    own = move(s_ref.at[:, me.c], mine, ls, 0)
    column = all_w.at[me.x, :, me.y, me.c]
    planes = []
    for k in range(1, 4):
        there = me.plane(k)
        planes.append(send(w_ref, column, (p0, p1), k, there))
    planes.append(move(w_ref, column, ls, 2))
    own.wait()
    other.wait()
    mine[...] = mine[...] + theirs[...]
    head = me.g * (heads // 4) + me.z // per
    place = me.z % per
    keep = move(mine.at[me.z, me.g], slabs.at[head, place], ls, 1)
    sends = []
    for k in reversed(range(1, chips)):
        there = me.any_chip(k)
        their_g = there[0] * 2 + there[2]
        sends.append(
            send(mine.at[there[1], their_g], slabs.at[head, place], (c0, c1), k, there)
        )
    for copy in planes:
        copy.wait()
    half = all_w.at[:, :, :, me.c]
    relay = send(half, half, (p0, p1), 0, me.sibling())
    keep.wait()
    for copy in sends:
        copy.wait()
    for block in range(2):
        for pair in range(heads // 2):
            sides = []
            for side in range(2):
                slab = slabs[2 * pair + side, 0].astype(F32)
                for extra in range(1, per):
                    slab = slab + slabs[2 * pair + side, extra].astype(F32)
                sides.append(slab)
            ob_ref[block * BLOCK : (block + 1) * BLOCK, lanes(pair)] = pair_up(
                sides[0], block, sides[1], block
            ).astype(BF16)
    relay.wait()
    save = move(all_w, og_ref, ls, 3)
    square = (x_ref.shape[1], x_ref.shape[1])
    residual = x_ref[...].astype(F32) + dot(ob_ref[...], all_w[...].reshape(square))
    r_ref[...] = residual
    mean = jnp.mean(residual * residual, axis=-1, keepdims=True)
    n_ref[...] = (residual * lax.rsqrt(mean + EPS)).astype(BF16)
    save.wait()


def join_exchange(zc, heads, slabs, tokens, w_column):
    chips = 4 * zc
    per = 4 * zc // heads
    half = (zc,) + slabs.shape[2:]
    shape = tokens.shape
    whole = (2, zc, 2, 2) + w_column.shape[1:]
    return exchange(
        functools.partial(join_kernel, zc),
        2,
        (struct(shape), struct(shape, F32), struct(shape), struct(whole)),
        [ANY, VM, ANY],
        (VM,) * 3 + (ANY,),
        [
            pltpu.VMEM(half, BF16),
            pltpu.VMEM(half, BF16),
            pltpu.VMEM((heads, per) + slabs.shape[3:], BF16),
            pltpu.VMEM(whole, BF16),
            DMA((4,)),
        ]
        + both(1)
        + both(chips)
        + both(4),
        (slabs, tokens, w_column),
        0,
        0,
    )


def middle_kernel(zc, n_ref, ca_ref, cb_ref, cc_ref, cd_ref, *rest):
    f_refs, rest = rest[: zc // 2 + 1], rest[zc // 2 + 1 :]
    oa_ref, ob_ref, oc_ref, od_ref, cs_ref, sh_ref, rows, cots, gate_w, up_w, down_w, *rest = rest
    hid, dgate, dup, c_out, c_in, stage, ls, n0, n1, c0, c1, f0, f1, h0, h1 = rest
    me = Place(zc)
    width = n_ref.shape[1]
    rows[0] = n_ref[...]
    meet([me.plane(k) for k in range(1, 4)] + [me.line(1), me.sibling()])
    farthest = send(rows.at[0], rows.at[3], (n0, n1), 3, me.plane(3))
    def places(there):
        return (
            gate_w.at[:, there, :, me.c],
            up_w.at[:, there, :, me.c],
            down_w.at[there, me.c],
        )

    given = dict(zip([1, *range(0, zc, 2)], f_refs))
    hops, loads = [], []
    for k in range(2, zc, 2):
        for i, place in enumerate(places(me.z ^ k)):
            hops.append(send(given[k].at[:, :, i], place, (h0, h1), 3 * k + i, me.line(1)))
    for k, ref in given.items():
        for i, place in enumerate(places(me.z ^ k)):
            loads.append(send(ref.at[:, :, i], place, (f0, f1), 3 * k + i, me.sibling()))
            loads.append(move(ref.at[:, :, i], place, ls, 21 + 3 * k + i))
    for k, ref in enumerate((ca_ref, cb_ref, cc_ref, cd_ref)):
        cots[k] = ref[...]
    farthest.wait_send()
    near_rows = [send(rows.at[0], rows.at[k], (n0, n1), k, me.plane(k)) for k in (1, 2)]
    for copy in hops:
        copy.wait()
    for k in range(3, zc, 2):
        for i, place in enumerate(places(me.z ^ k)):
            loads.append(send(place, place, (f0, f1), 3 * k + i, me.sibling()))
    for copy in loads:
        copy.wait()
    square = (width, width)

    def block(step, carry):
        k = jnp.where(step == 0, 0, jnp.where(step == 1, 3, step - 1))

        @pl.when(step > 0)
        def _():
            trip(rows.at[0], rows.at[k], (n0, n1), k, me.plane(k)).wait_recv()

        gate_mat, up_mat = gate_w[...].reshape(square), up_w[...].reshape(square)
        gate = dot(rows[k], gate_mat)
        up = dot(rows[k], up_mat)
        back = nt_dot(cots[k], down_w[...].reshape(square))
        sig = jax.nn.sigmoid(gate)
        soft = gate * sig
        hid[k] = (soft * up).astype(BF16)
        dgate[k] = (back * up * sig * (1.0 + gate * (1.0 - sig))).astype(BF16)
        dup[k] = (back * soft).astype(BF16)
        c_out[k] = (nt_dot(dgate[k], gate_mat) + nt_dot(dup[k], up_mat)).astype(BF16)

        @pl.when(step > 0)
        def _():
            trip(c_out.at[k], c_in.at[k], (c0, c1), k, me.plane(k)).start()

        return carry

    lax.fori_loop(0, 4, block, 0)
    all_rows = (4 * n_ref.shape[0], width)

    def weight_grad(left, right, slot):
        chunk = 256
        for first in range(0, width, chunk):
            value = tn_dot(left[:, first : first + chunk], right).astype(BF16)
            stage[slot, first : first + chunk] = value

    shares = []
    piece = width // (8 * zc)

    def share(slot, which):
        parts = stage.at[slot].reshape(2, zc, 2, 2, piece, width)
        for g in range(4):
            x, y = g // 2, g % 2
            shares.append(
                move(parts.at[x, :, y], sh_ref.at[:, :, 2 * g + which], ls, 12 + 2 * g + which)
            )

    flat = lambda ref: ref[...].reshape(all_rows)
    weight_grad(flat(rows), flat(dgate), 0)
    share(0, 0)
    weight_grad(flat(rows), flat(dup), 1)
    share(1, 1)
    weight_grad(flat(hid), flat(cots), 2)
    shares.append(
        move(stage.at[2].reshape(zc, 2, 4, piece, width), sh_ref.at[:, :, 8:], ls, 20)
    )

    for k, ref in enumerate((oa_ref, ob_ref, oc_ref, od_ref)):
        ref[...] = dot(hid[k], down_w[...].reshape(square)).astype(BF16)
    total = c_out[0].astype(F32)
    for k in range(1, 4):
        trip(c_out.at[k], c_in.at[k], (c0, c1), k, me.plane(k)).wait()
        total = total + c_in[k].astype(F32)
    cs_ref[...] = total
    for copy in shares:
        copy.wait()
    for copy in near_rows:
        copy.wait_send()


def middle_exchange(zc, normed, cots, weights):
    own, width = normed.shape
    piece = width // (8 * zc)
    blocks = pltpu.VMEM((4, own, width), BF16)
    wide = pltpu.VMEM((2, zc, 2, 2, piece, width), BF16)
    return exchange(
        functools.partial(middle_kernel, zc),
        3,
        (
            *[struct((own, width))] * 4,
            struct((own, width), F32),
            struct((zc, 2, 12, piece, width)),
        ),
        [VM] * 5 + [ANY] * len(weights),
        (VM,) * 5 + (ANY,),
        [blocks, blocks, wide, wide, pltpu.VMEM((zc, 2, 2, 2, piece, width), BF16)]
        + [blocks] * 5
        + [pltpu.VMEM((3, width, width), BF16), DMA((21 + 3 * zc,))]
        + both(4)
        + both(4)
        + both(3 * zc)
        + both(3 * zc),
        (normed, *cots, *weights),
        2 * 4 * own * width * width * 9,
        64 << 20,
    )


def turn_kernel(
    zc,
    c_ref,
    t_ref,
    r_ref,
    wo_ref,
    ob_ref,
    dr_ref,
    do_ref,
    dw_ref,
    slabs,
    stage,
    ls,
    d0,
    d1,
    b0,
    b1,
):
    me = Place(zc)
    chips = 4 * zc
    heads = slabs.shape[0]
    group = heads // 4
    per = zc // group
    width = t_ref.shape[1]
    meet([me.any_chip(k) for k in range(1, chips)] + [me.sibling()])
    total, residual = c_ref[...], r_ref[...]
    scaling = lax.rsqrt(jnp.mean(residual * residual, axis=-1, keepdims=True) + EPS)
    normed = residual * scaling
    middle = jnp.mean(total * normed, axis=-1, keepdims=True)
    grad = t_ref[...].astype(F32) + scaling * (total - normed * middle)
    dr_ref[...] = grad
    narrow = grad.astype(BF16)
    back = nt_dot(narrow, wo_ref[...])
    for pair in range(heads // 2):
        two = back[:, lanes(pair)]
        for side in range(2):
            slabs[2 * pair + side] = pair_up(two[:BLOCK], side, two[BLOCK:], side).astype(BF16)
    to = do_ref.at[me.z, me.c, me.g]
    own = move(slabs.at[me.g * group + me.z // per], to, ls, 0)
    sends = []
    for k in reversed(range(1, chips)):
        there = me.any_chip(k)
        head = (there[0] * 2 + there[2]) * group + there[1] // per
        sends.append(send(slabs.at[head], to, (d0, d1), k, there))
    chunk = 256
    attended = ob_ref[...]
    for first in range(0, width, chunk):
        stage[first : first + chunk] = tn_dot(attended[:, first : first + chunk], narrow).astype(BF16)
    parts = stage.reshape(2, zc, 2, 2, width // (8 * zc), width)
    keeps = []
    for k in range(4):
        there = me.plane(k)
        keeps.append(move(parts.at[there[0], :, there[2]], dw_ref.at[k], ls, 1 + k))
    own.wait()
    for copy in sends:
        copy.wait()
    half = do_ref.at[:, me.c]
    relay = send(half, half, (b0, b1), 0, me.sibling())
    for copy in keeps:
        copy.wait()
    relay.wait()


def turn_exchange(zc, c_sum, cotangent, residual, w_out, attn_rows):
    chips = 4 * zc
    own, width = cotangent.shape
    heads = width // HEAD_DIM
    return exchange(
        functools.partial(turn_kernel, zc),
        6,
        (
            struct((own, width), F32),
            struct((zc, 2, 4, BLOCK, PAIR)),
            struct((4, zc, 2, width // (8 * zc), width)),
        ),
        [VM] * 5,
        (VM, ANY, ANY),
        [
            pltpu.VMEM((heads, BLOCK, PAIR), BF16),
            pltpu.VMEM((width, width), BF16),
            DMA((5,)),
        ]
        + both(chips)
        + both(1),
        (c_sum, cotangent, residual, w_out, attn_rows),
        2 * 2 * own * width * width,
        8 << 20,
    )


def tail_kernel(
    zc,
    d_ref,
    n_ref,
    w_ref,
    x_ref,
    g_ref,
    v_ref,
    f_ref,
    r_ref,
    ya_ref,
    yb_ref,
    yc_ref,
    yd_ref,
    tg_ref,
    gw_ref,
    go_ref,
    gf_ref,
    out_ref,
    r_in,
    y_in,
    o_in,
    o_mine,
    o_theirs,
    o_land,
    mine,
    theirs,
    landed,
    grads,
    c_out,
    c_in,
    stage,
    other_w,
    ls,
    b0,
    b1,
    z0,
    z1,
    c0,
    c1,
    s0,
    s1,
    w0,
    w1,
    q0,
    q1,
    v0,
    v1,
    f0,
    f1,
):
    me = Place(zc)
    chips = 4 * zc
    group, per = landed.shape[:2]
    qw = group * HEAD_DIM
    meet([me.any_chip(k) for k in range(1, chips)] + [me.sibling()])
    head, place = me.z // per, me.z % per

    def slot(k):
        return (me.x ^ (k // 2)) * 2 + (me.y ^ (k % 2))

    order = (3, 2, 1, 0)
    halves = []
    for k in order:
        halves.append(
            (
                send(d_ref.at[:, 1 - me.c, slot(k)], theirs.at[k], (b0, b1), k, me.sibling()),
                move(d_ref.at[:, me.c, slot(k)], mine.at[k], ls, k),
            )
        )
    o_parts = [move(v_ref.at[0], o_in.at[0], ls, 9)]
    for k in (3, 1, 2):
        o_parts.append(send(v_ref.at[k], o_in.at[k], (v0, v1), k, me.plane(k)))
    f_parts = [move(f_ref.at[pl.ds(2 * me.g, 2)], gf_ref.at[me.g], ls, 10)]
    for k in (3, 1, 2):
        there = me.plane(k)
        part = f_ref.at[pl.ds(2 * (there[0] * 2 + there[2]), 2)]
        f_parts.append(send(part, gf_ref.at[me.g], (f0, f1), k, there))
    out_parts = [move(r_ref, r_in, ls, 11)]
    for i, ref in enumerate((ya_ref, yb_ref, yc_ref, yd_ref)):
        out_parts.append(move(ref, y_in.at[i], ls, 12 + i))
    for k, (far, near) in zip(order, halves):
        near.wait()
        far.wait()
        mine[k] = mine[k] + theirs[k]
        for over in range(1, zc):
            send(
                mine.at[k, me.z ^ over],
                landed.at[head, place, k],
                (z0, z1),
                k * zc + over,
                me.line(over),
            )
        move(mine.at[k, me.z], landed.at[head, place, k], ls, 4 + k)

    for copy in out_parts:
        copy.wait()
    final = r_in[...]
    for i in range(4):
        final = final + y_in[i].astype(F32)
    out_ref[...] = final.astype(BF16)

    def block(step, carry):
        k = 3 - step
        pltpu.make_async_copy(
            mine.at[k, me.z], landed.at[head, place, k], ls.at[4 + k]
        ).wait()
        for over in range(1, zc):
            trip(
                mine.at[k, me.z ^ over],
                landed.at[head, place, k],
                (z0, z1),
                k * zc + over,
                me.line(over),
            ).wait()
        for pair in range(group // 2):
            sides = []
            for side in range(2):
                h = 2 * pair + side
                slab = landed[h, 0, k]
                for extra in range(1, per):
                    slab = slab + landed[h, extra, k]
                start = qw + h * PAIR
                grads[k, :, start : start + PAIR] = slab[BLOCK:]
                sides.append(slab[:BLOCK].astype(F32))
            for b in range(2):
                grads[k, b * BLOCK : (b + 1) * BLOCK, lanes(pair)] = pair_up(
                    sides[0], b, sides[1], b
                ).astype(BF16)

        @pl.when(k > 0)
        def _():
            c_out[k] = nt_dot(grads[k], w_ref[...]).astype(BF16)
            trip(c_out.at[k], c_in.at[k], (c0, c1), k, me.plane(k)).start()

        return carry

    lax.fori_loop(0, 3, block, 0)
    for copy in o_parts:
        copy.wait()
    o_sum = o_in[0].astype(F32)
    for k in range(1, 4):
        o_sum = o_sum + o_in[k].astype(F32)
    o_mine[...] = o_sum.astype(BF16)
    o_swap = send(o_mine.at[:, 1 - me.c], o_theirs, (s0, s1), 1, me.sibling())
    o_swap.wait()
    o_theirs[...] = o_theirs[...] + o_mine[:, me.c]
    sends = [
        send(o_theirs.at[me.z ^ k], o_land.at[k], (q0, q1), k, me.line(k)) for k in range(1, zc)
    ]
    lax.fori_loop(3, 4, block, 0)
    width, cols = w_ref.shape
    all_rows = 4 * n_ref.shape[1]
    normed_all = n_ref[...].reshape(all_rows, width)
    grads_all = grads[...].reshape(all_rows, cols)
    piece = stage.shape[2]
    chunk = 256
    each = chunk // (2 * piece)
    swaps = []
    for first in range(0, width, chunk):
        value = tn_dot(normed_all[:, first : first + chunk], grads_all).astype(BF16)
        at = first // (2 * piece)
        stage[at : at + each] = value.reshape(each, 2, piece, cols)
        swaps.append(
            send(
                stage.at[at : at + each, 1 - me.c],
                other_w.at[at : at + each],
                (s0, s1),
                2 + first // chunk,
                me.sibling(),
            )
        )
    c_out[0] = nt_dot(grads[0], w_ref[...]).astype(BF16)
    for swap in swaps:
        swap.wait()

    def add(i, carry):
        other_w[i] = stage[i, me.c] + other_w[i]
        return carry

    lax.fori_loop(0, chips, add, 0)
    stay = move(other_w.at[me.chip], gw_ref.at[me.z, me.g], ls, 8)
    for k in reversed(range(1, chips)):
        there = me.any_chip(k)
        chip = (there[0] * zc + there[1]) * 2 + there[2]
        sends.append(send(other_w.at[chip], gw_ref.at[me.z, me.g], (w0, w1), k, there))
    total = c_out[0].astype(F32)
    for k in range(1, 4):
        trip(c_out.at[k], c_in.at[k], (c0, c1), k, me.plane(k)).wait()
        total = total + c_in[k].astype(F32)
    x = x_ref[...].astype(F32)
    scaling = lax.rsqrt(jnp.mean(x * x, axis=-1, keepdims=True) + EPS)
    normed = x * scaling
    middle = jnp.mean(total * normed, axis=-1, keepdims=True)
    tg_ref[...] = (g_ref[...] + scaling * (total - normed * middle)).astype(BF16)
    stay.wait()
    for copy in sends + f_parts:
        copy.wait()
    o_sum = o_theirs[me.z].astype(F32)
    for k in range(1, zc):
        o_sum = o_sum + o_land[k].astype(F32)
    go_ref[...] = o_sum


def tail_exchange(zc, group, slab_grads, n_all, weights, tokens, residual_grad, out_grads, shares, residual, outs):
    chips = 4 * zc
    per = zc // group
    own, width = tokens.shape
    cols = weights.shape[1]
    slab = slab_grads.shape[3:]
    piece = width // (2 * chips)
    blocks = pltpu.VMEM((4, own, width), BF16)
    return exchange(
        functools.partial(tail_kernel, zc),
        4,
        (
            struct((own, width)),
            struct((zc, 4, piece, cols)),
            struct((piece, width), F32),
            struct((4, 2, piece, width)),
            struct((own, width)),
        ),
        [ANY] + [VM] * 4 + [ANY] * 7,
        (VM, ANY, VM, ANY, VM),
        [
            pltpu.VMEM((own, width), F32),
            pltpu.VMEM((4, own, width), BF16),
            pltpu.VMEM((4, zc, 2, piece, width), BF16),
            pltpu.VMEM((zc, 2, piece, width), BF16),
            pltpu.VMEM((zc, piece, width), BF16),
            pltpu.VMEM((zc, piece, width), BF16),
            pltpu.VMEM((4, zc) + slab, BF16),
            pltpu.VMEM((4, zc) + slab, BF16),
            pltpu.VMEM((group, per, 4) + slab, BF16),
            pltpu.VMEM((4, own, cols), BF16),
            blocks,
            blocks,
            pltpu.VMEM((chips, 2, piece, cols), BF16),
            pltpu.VMEM((chips, piece, cols), BF16),
            DMA((16,)),
        ]
        + both(4)
        + both(4 * zc)
        + both(4)
        + both(2 + width // 256)
        + both(chips)
        + both(zc)
        + both(4)
        + both(4),
        (slab_grads, n_all, weights, tokens, residual_grad, out_grads, shares, residual, *outs),
        2 * 4 * own * width * cols * 2,
        24 << 20,
    )


def last_kernel(
    zc,
    group,
    t_any,
    o_any,
    wo_any,
    gw_any,
    gf_any,
    ds_any,
    q_any,
    k_any,
    v_any,
    g_any,
    u_any,
    gain1,
    gain2,
    tg_ref,
    out_ref,
    go_ref,
    g1_ref,
    q_ref,
    k_ref,
    v_ref,
    g2_ref,
    g_ref,
    u_ref,
    d_ref,
    gw_ref,
    gf_ref,
    ds_ref,
    q_w,
    k_w,
    v_w,
    g_w,
    u_w,
    ls,
):
    given = (gw_any, q_any, k_any, v_any, gf_any, g_any, u_any, ds_any, t_any, o_any, wo_any)
    taken = (gw_ref, q_w, k_w, v_w, gf_ref, g_w, u_w, ds_ref, tg_ref, out_ref, go_ref)
    copies = [move(a, b, ls, i) for i, (a, b) in enumerate(zip(given, taken))]
    for copy in copies:
        copy.wait()
    d_ref[...] = ds_ref[8:].astype(F32).reshape(d_ref.shape)
    first_gain, second_gain = column_of(low(gain1[...])), column_of(low(gain2[...]))
    count = q_w.shape[0]
    qw = group * HEAD_DIM
    score = jnp.zeros((count, PAIR), F32)
    for g in range(4):
        raw = gw_ref[0, g].astype(F32)
        for z in range(1, zc):
            raw = raw + gw_ref[z, g].astype(F32)
        for pair in range(group // 2):
            at = lanes(g * group // 2 + pair)
            start = qw + 2 * pair * PAIR
            even, odd = raw[:, start : start + PAIR], raw[:, start + PAIR : start + 2 * PAIR]
            query = raw[:, lanes(pair)]
            key, value = pair_up(even, 0, odd, 0), pair_up(even, 1, odd, 1)
            score = score + query * low(q_w[:, at]) + key * low(k_w[:, at]) + value * low(v_w[:, at])
            q_ref[:, at] = first_gain * query
            k_ref[:, at] = first_gain * key
            v_ref[:, at] = first_gain * value
    g1_ref[...] = row_of(jnp.sum(score, axis=1, keepdims=True))
    units = g_w.shape[1] // (4 * zc)
    score = jnp.zeros((count, PAIR), F32)
    for which, (weight, target) in enumerate(((g_w, g_ref), (u_w, u_ref))):
        for chunk in range(weight.shape[1] // PAIR):
            if units % PAIR == 0:
                owner, piece = divmod(chunk, units // PAIR)
                x, z, y = owner // (2 * zc), owner // 2 % zc, owner % 2
                raw = gf_ref[2 * x + y, which, :, lanes(z * units // PAIR + piece)].astype(F32)
            else:
                x, z = chunk // zc, chunk % zc
                near = gf_ref[2 * x, which, :, lanes(z // 2)].astype(F32)
                far = gf_ref[2 * x + 1, which, :, lanes(z // 2)].astype(F32)
                raw = pair_up(near, z % 2, far, z % 2)
            score = score + raw * low(weight[:, lanes(chunk)])
            target[:, lanes(chunk)] = second_gain * raw
    g2_ref[...] = row_of(jnp.sum(score, axis=1, keepdims=True))


def last_step(zc, group, tokens_grad, output, out_share, w_all, f_all, shares, matrices, gains):
    own, width = output.shape
    count, hidden = matrices[3].shape
    return pl.pallas_call(
        functools.partial(last_kernel, zc, group),
        out_shape=(
            struct((own, width)),
            struct((own, width)),
            struct((count, width), F32),
            struct((1, count), F32),
            struct((count, width), F32),
            struct((count, width), F32),
            struct((count, width), F32),
            struct((1, count), F32),
            struct((count, hidden), F32),
            struct((count, hidden), F32),
            struct((4 * count, width), F32),
        ),
        in_specs=[ANY] * 11 + [VM] * 2,
        out_specs=(VM,) * 11,
        scratch_shapes=[
            pltpu.VMEM(v.shape, v.dtype) for v in (w_all, f_all, shares, *matrices)
        ]
        + [DMA((11,))],
        compiler_params=pltpu.CompilerParams(vmem_limit_bytes=60 << 20),
    )(
        tokens_grad,
        output,
        out_share,
        w_all,
        f_all,
        shares,
        *matrices,
        *(g.reshape(1, -1) for g in gains),
    )


def segment_start(position, lens_ref):
    start = jnp.zeros_like(position)
    end = 0
    for j in range(lens_ref.shape[0]):
        end = end + lens_ref[j]
        start = jnp.where(position >= end, end, start)
    return start


def note_tiles(workers, worker, tiles, lens_ref, mine):
    turns = tiles // workers

    def snake(turn, carry):
        forward = turn * workers + worker
        backward = turn * workers + workers - 1 - worker
        mine[turn] = jnp.where((turn & 1) == 0, forward, backward)
        return carry

    def weigh(step, ahead):
        turn = turns - 1 - step
        loads = []
        for tile in (2 * turn, 2 * turn + 1):
            first, _, _, last = key_bounds(tile * QTILE, lens_ref)
            loads.append(last - first)
        lighter_first = loads[0] <= loads[1]
        first_to_zero = jnp.where(ahead > 0, lighter_first, loads[0] > loads[1])
        mine[turn] = 2 * turn + jnp.where(first_to_zero, worker, 1 - worker)
        return ahead + jnp.where(first_to_zero, loads[0] - loads[1], loads[1] - loads[0])

    if workers == 2:
        lax.fori_loop(0, turns, weigh, 0)
    else:
        lax.fori_loop(0, turns, snake, 0)


def key_bounds(first, lens_ref):
    low_start = segment_start(first, lens_ref)
    high_start = segment_start(first + QTILE - 1, lens_ref)
    low = low_start // KTILE
    high = (first + QTILE + KTILE - 1) // KTILE
    plain = jnp.clip((high_start + KTILE - 1) // KTILE, low, high)
    stop = jnp.clip((first + 1) // KTILE, plain, high)
    return low, plain, stop, high


def visible(first, tile, starts):
    key = tile * KTILE + lax.broadcasted_iota(jnp.int32, (KTILE, QTILE), 0)
    query = first + lax.broadcasted_iota(jnp.int32, (KTILE, QTILE), 1)
    return (key <= query) & (key >= starts)


def note_places(anchor_ref, inv):
    def note(i, carry):
        inv[anchor_ref[i]] = i
        return carry

    lax.fori_loop(0, anchor_ref.shape[0], note, 0)


def half_lanes(rows, half):
    lane = lax.broadcasted_iota(jnp.int32, rows.shape, 1)
    return jnp.where((lane // HEAD_DIM) == half, rows, jnp.zeros_like(rows))


def fold(rows, columns, first):
    row = lax.broadcasted_iota(jnp.int32, (rows, columns), 0)
    column = lax.broadcasted_iota(jnp.int32, (rows, columns), 1)
    return (row % HEAD_DIM == column - first).astype(F32).astype(BF16)


def unfold(rows, columns, first):
    row = lax.broadcasted_iota(jnp.int32, (rows, columns), 0)
    column = lax.broadcasted_iota(jnp.int32, (rows, columns), 1)
    return (column % HEAD_DIM == row - first).astype(F32).astype(BF16)


def forward_kernel(
    workers, anchor_ref, lens_ref, who_ref, a_ref, o_ref, kv_ref, kvt_ref, q_ref, qt_ref, ot_ref, l_ref, inv, mine, raw
):
    blocks = anchor_ref.shape[0]
    turns = qt_ref.shape[0]
    per = QTILE // BLOCK
    worker = who_ref[0]
    note_places(anchor_ref, inv)
    note_tiles(workers, worker, turns * workers, lens_ref, mine)
    o_ref[...] = jnp.zeros_like(o_ref)
    same = selection(PAIR, PAIR, 0)

    def order(step, carry):
        for b in range(per):
            i = step * per + b
            where = inv[i]
            slab, half = where >> 1, where & 1
            at = pl.ds(pl.multiple_of(i * BLOCK, BLOCK), BLOCK)
            kv_ref[at, :] = a_ref[slab, pl.ds(pl.multiple_of(BLOCK + half * BLOCK, BLOCK), BLOCK), :]
        return carry

    lax.fori_loop(0, blocks // per, order, 0)

    def flip(step, carry):
        at = pl.ds(pl.multiple_of(step * TURNED, TURNED), TURNED)
        kvt_ref[:, at] = nt_dot(same, kv_ref[at, :]).astype(BF16)
        return carry

    lax.fori_loop(0, blocks * BLOCK // TURNED, flip, 0)

    def one_tile(turn, carry):
        tile = mine[turn]
        first = tile * QTILE
        for b in range(per):
            where = inv[tile * per + b]
            raw[b * BLOCK : (b + 1) * BLOCK, :] = half_lanes(a_ref[where >> 1, :BLOCK, :], where & 1)
        q_ref[turn] = (dot(raw[...], fold(PAIR, PAIR, 0)) * 0.125).astype(BF16)
        qt_ref[turn] = (nt_dot(unfold(PAIR, PAIR, 0), raw[...]) * 0.125).astype(BF16)
        query = qt_ref[turn]
        starts = segment_start(first + lax.broadcasted_iota(jnp.int32, (1, QTILE), 1), lens_ref)
        low, plain, stop, high = key_bounds(first, lens_ref)

        def step(masked, kt, state):
            top, total, acc = state
            at = pl.ds(pl.multiple_of(kt * KTILE, KTILE), KTILE)
            scores = dot(kv_ref[at, :], query)
            if masked:
                scores = jnp.where(visible(first, kt, starts), scores, MASKED)
            new_top = jnp.maximum(top, jnp.max(scores, axis=0, keepdims=True))
            factor = jnp.exp(top - new_top)
            weights = jnp.exp(scores - new_top)
            total = total * factor + jnp.sum(weights, axis=0, keepdims=True)
            acc = acc * factor + dot(kvt_ref[HEAD_DIM:, at], weights.astype(BF16))
            return (new_top, total, acc)

        state = (
            jnp.full((1, QTILE), LOWEST, F32),
            jnp.zeros((1, QTILE), F32),
            jnp.zeros((HEAD_DIM, QTILE), F32),
        )
        state = lax.fori_loop(low, plain, functools.partial(step, True), state)
        state = lax.fori_loop(plain, stop, functools.partial(step, False), state)
        top, total, acc = lax.fori_loop(stop, high, functools.partial(step, True), state)
        out = acc / total
        ot_ref[turn] = out
        l_ref[turn] = top + jnp.log(total)
        wide = tn_dot(out.astype(BF16), unfold(HEAD_DIM, PAIR, 0)).astype(BF16)
        for b in range(per):
            where = inv[tile * per + b]
            slab = where >> 1
            o_ref[slab] = o_ref[slab] + half_lanes(wide[b * BLOCK : (b + 1) * BLOCK], where & 1)
        return carry

    lax.fori_loop(0, turns, one_tile, 0)


def attention_forward(workers, anchors, lengths, who, packed):
    slabs = packed.shape[0]
    rows = slabs * 2 * BLOCK
    turns = rows // QTILE // workers
    return pl.pallas_call(
        functools.partial(forward_kernel, workers),
        out_shape=(
            struct((slabs, BLOCK, PAIR)),
            struct((rows, PAIR)),
            struct((PAIR, rows)),
            struct((turns, QTILE, PAIR)),
            struct((turns, PAIR, QTILE)),
            struct((turns, HEAD_DIM, QTILE), F32),
            struct((turns, 1, QTILE), F32),
        ),
        in_specs=[SM, SM, SM, VM],
        out_specs=(VM,) * 7,
        scratch_shapes=[
            pltpu.SMEM((2 * slabs,), jnp.int32),
            pltpu.SMEM((turns,), jnp.int32),
            pltpu.VMEM((QTILE, PAIR), BF16),
        ],
        compiler_params=pltpu.CompilerParams(vmem_limit_bytes=60 << 20),
        cost_estimate=pl.CostEstimate(
            flops=rows * rows * 64, bytes_accessed=rows * 1024, transcendentals=rows * rows // 8
        ),
    )(anchors, lengths, who, packed)


def backward_kernel(
    workers,
    anchor_ref,
    lens_ref,
    who_ref,
    d_ref,
    kv_ref,
    kvt_ref,
    q_ref,
    qt_ref,
    ot_ref,
    l_ref,
    g_ref,
    inv,
    mine,
    raw,
    both_rows,
    dt,
    acc,
):
    blocks = anchor_ref.shape[0]
    turns = qt_ref.shape[0]
    per = QTILE // BLOCK
    worker = who_ref[0]
    note_places(anchor_ref, inv)
    note_tiles(workers, worker, turns * workers, lens_ref, mine)
    acc[...] = jnp.zeros_like(acc)
    g_ref[:, :BLOCK, :] = jnp.zeros((g_ref.shape[0], BLOCK, PAIR), BF16)

    def one_tile(turn, carry):
        tile = mine[turn]
        first = tile * QTILE
        for b in range(per):
            where = inv[tile * per + b]
            raw[b * BLOCK : (b + 1) * BLOCK, :] = half_lanes(d_ref[where >> 1], where & 1)
        both_rows[:QTILE] = q_ref[turn]
        both_rows[QTILE:] = dot(raw[...], fold(PAIR, PAIR, HEAD_DIM)).astype(BF16)
        dt[...] = nt_dot(unfold(PAIR, PAIR, HEAD_DIM), raw[...]).astype(BF16)
        query, grad = qt_ref[turn], dt[...]
        norm = l_ref[turn]
        delta = jnp.sum(grad[HEAD_DIM:].astype(F32) * ot_ref[turn], axis=0, keepdims=True)
        starts = segment_start(first + lax.broadcasted_iota(jnp.int32, (1, QTILE), 1), lens_ref)
        low, plain, stop, high = key_bounds(first, lens_ref)

        def step(masked, kt, total):
            at = pl.ds(pl.multiple_of(kt * KTILE, KTILE), KTILE)
            keys = kv_ref[at, :]
            scores = dot(keys, query)
            if masked:
                scores = jnp.where(visible(first, kt, starts), scores, MASKED)
            weights = jnp.exp(scores - norm)
            score_grad = (weights * (dot(keys, grad) - delta)).astype(BF16)
            both_grads = jnp.concatenate([score_grad, weights.astype(BF16)], axis=1)
            acc[at, :] += dot(both_grads, both_rows[...])
            return total + dot(kvt_ref[:HEAD_DIM, at], score_grad)

        total = jnp.zeros((HEAD_DIM, QTILE), F32)
        total = lax.fori_loop(low, plain, functools.partial(step, True), total)
        total = lax.fori_loop(plain, stop, functools.partial(step, False), total)
        total = lax.fori_loop(stop, high, functools.partial(step, True), total)
        wide = tn_dot((total * 0.125).astype(BF16), unfold(HEAD_DIM, PAIR, 0)).astype(BF16)
        for b in range(per):
            where = inv[tile * per + b]
            slab = where >> 1
            g_ref[slab, :BLOCK] = g_ref[slab, :BLOCK] + half_lanes(
                wide[b * BLOCK : (b + 1) * BLOCK], where & 1
            )
        return carry

    lax.fori_loop(0, turns, one_tile, 0)

    def place(step, carry):
        for b in range(per):
            i = step * per + b
            where = inv[i]
            slab, half = where >> 1, where & 1
            at = pl.ds(pl.multiple_of(i * BLOCK, BLOCK), BLOCK)
            to = pl.ds(pl.multiple_of(BLOCK + half * BLOCK, BLOCK), BLOCK)
            g_ref[slab, to, :] = acc[at, :].astype(BF16)
        return carry

    lax.fori_loop(0, blocks // per, place, 0)


def attention_backward(workers, anchors, lengths, who, grads, kept):
    slabs = grads.shape[0]
    rows = slabs * 2 * BLOCK
    return pl.pallas_call(
        functools.partial(backward_kernel, workers),
        out_shape=struct((slabs, 3 * BLOCK, PAIR)),
        in_specs=[SM, SM, SM] + [VM] * 7,
        out_specs=VM,
        scratch_shapes=[
            pltpu.SMEM((2 * slabs,), jnp.int32),
            pltpu.SMEM((rows // QTILE // workers,), jnp.int32),
            pltpu.VMEM((QTILE, PAIR), BF16),
            pltpu.VMEM((2 * QTILE, PAIR), BF16),
            pltpu.VMEM((PAIR, QTILE), BF16),
            pltpu.VMEM((rows, PAIR), F32),
        ],
        compiler_params=pltpu.CompilerParams(vmem_limit_bytes=60 << 20),
        cost_estimate=pl.CostEstimate(
            flops=rows * rows * 160, bytes_accessed=rows * 1024, transcendentals=rows * rows // 8
        ),
    )(anchors, lengths, who, grads, *kept)


def around(value, k):
    return lax.ppermute(value, ("head", "y"), [(i, i ^ k) for i in range(4)])


def along(value, k):
    return lax.ppermute(value, "z", [(i, i ^ k) for i in range(lax.axis_size("z"))])


def doubling(pieces, first, last):
    while first >= last:
        pieces = {**pieces, **{k + first: along(pieces[k], first) for k in pieces}}
        first //= 2
    return pieces


def body(
    zc,
    tokens,
    cotangent,
    norm1_gain,
    w_query,
    w_key,
    w_value,
    w_out,
    norm2_gain,
    w_gate,
    w_up,
    w_down,
    block_anchor,
    seq_lengths,
):
    width = tokens.shape[1]
    heads = width // HEAD_DIM
    group = heads // 4
    per_head = zc // group
    workers = 2 * per_head
    feature_rows = w_query.shape[0]

    n1_all, qkv_w, ffn_own, by_head, *near, w_column = head_exchange(
        zc,
        group,
        tokens,
        (w_query, w_key, w_value, w_gate, w_up, w_down, w_out),
        cotangent,
        (norm1_gain, norm2_gain),
    )
    qkv_w = qkv_w.reshape(width, 3 * group * HEAD_DIM)

    ffn_own, far = lax.optimization_barrier((ffn_own, cotangent))
    cots = [cotangent] + near + [around(far, 3)]
    ffn_parts = doubling({0: ffn_own}, zc // 2, 2)
    close = along(ffn_own, 1)

    anchors = jnp.transpose(block_anchor.reshape(2, zc, 2, 2, 2), (1, 3, 0, 2, 4)).reshape(-1)
    who = ((lax.axis_index("z") % per_head) * 2 + lax.axis_index("core")).astype(jnp.int32).reshape(1)
    slab_count = zc * 8
    o_slabs, *kept = attention_forward(
        workers, anchors, seq_lengths, who, by_head.reshape((slab_count,) + by_head.shape[3:])
    )
    attn_rows, residual, normed_two, out_mat = join_exchange(
        zc, heads, o_slabs.reshape(zc, 2, 4, BLOCK, PAIR), tokens, w_column
    )
    out_mat = out_mat.reshape(width, width)
    *out_parts, c_sum, shares = middle_exchange(
        zc, normed_two, cots, [close] + [ffn_parts[k] for k in range(0, zc, 2)]
    )
    shares = lax.psum_scatter(
        shares.reshape(zc * 2 * 12, feature_rows, width), ("z", "core"), scatter_dimension=0, tiled=True
    )
    residual_grad, do_heads, out_grads = turn_exchange(
        zc, c_sum, cotangent, residual, out_mat, attn_rows
    )
    do_heads, *out_parts = lax.optimization_barrier((do_heads, *out_parts))
    outs = [out_parts[0]] + [around(out_parts[k], k) for k in range(1, 4)]
    grad_heads = attention_backward(
        workers, anchors, seq_lengths, who, do_heads.reshape(slab_count, BLOCK, PAIR), kept
    )
    tokens_grad, w_all, out_share, f_all, output = tail_exchange(
        zc,
        group,
        grad_heads.reshape(zc, 2, 4, 3 * BLOCK, PAIR),
        n1_all,
        qkv_w,
        tokens,
        residual_grad,
        out_grads,
        shares,
        residual,
        outs,
    )
    (
        tokens_grad,
        output,
        out_grad,
        gain1_grad,
        query_grad,
        key_grad,
        value_grad,
        gain2_grad,
        gate_grad,
        up_grad,
        down_grad,
    ) = last_step(
        zc,
        group,
        tokens_grad,
        output,
        out_share,
        w_all,
        f_all,
        shares,
        (w_query, w_key, w_value, w_gate, w_up),
        (norm1_gain, norm2_gain),
    )
    return (
        output,
        tokens_grad,
        gain1_grad.reshape(-1),
        query_grad,
        key_grad,
        value_grad,
        out_grad,
        gain2_grad.reshape(-1),
        gate_grad,
        up_grad,
        down_grad,
    )


def solution(mesh):
    blk = mesh.shape["blk"]
    grid = Mesh(mesh.devices.reshape(mesh.shape["head"], blk // 4, 2, 2), AXES)
    rows, vector, whole = P(AXES, None), P(AXES), P()
    return jax.shard_map(
        functools.partial(body, blk // 4),
        mesh=grid,
        in_specs=(rows, rows, vector, rows, rows, rows, rows, vector, rows, rows, rows, whole, whole),
        out_specs=(rows, rows, vector, rows, rows, rows, rows, vector, rows, rows, rows),
        check_vma=False,
    )
```

```python
import functools

import jax
import jax.numpy as jnp
from jax import lax
from jax.experimental import pallas as pl
from jax.experimental.pallas import tpu as pltpu
from jax.sharding import Mesh
from jax.sharding import PartitionSpec as P

HEAD_DIM = 64
BLOCK = 128
PAIR = 128
EPS = 1e-06
MASKED = -1e30
LOWEST = -1e20
QTILE = 512
KTILE = 512
TURNED = 2048
AXES = ("head", "z", "y", "core")
IDS = pl.DeviceIdType.MESH
F32 = jnp.float32
BF16 = jnp.bfloat16
ANY = pl.BlockSpec(memory_space=pl.ANY)
VM = pl.BlockSpec(memory_space=pltpu.VMEM)
SM = pl.BlockSpec(memory_space=pltpu.SMEM)


def struct(shape, dtype=BF16):
    return jax.ShapeDtypeStruct(tuple(shape), dtype)


def nt_dot(a, b):
    return lax.dot_general(a, b, (((1,), (1,)), ((), ())), preferred_element_type=F32)


def tn_dot(a, b):
    return lax.dot_general(a, b, (((0,), (0,)), ((), ())), preferred_element_type=F32)


def dot(a, b):
    return jnp.dot(a, b, preferred_element_type=F32)


def selection(rows, columns, shift, first=0, last=None):
    last = columns if last is None else last
    row = lax.broadcasted_iota(jnp.int32, (rows, columns), 0)
    column = lax.broadcasted_iota(jnp.int32, (rows, columns), 1)
    hit = (row == column + shift) & (column >= first) & (column < last)
    return hit.astype(F32).astype(BF16)


def pair_up(first, first_half, second, second_half):
    lane = lax.broadcasted_iota(jnp.int32, first.shape, 1)
    left = first if first_half == 0 else pltpu.roll(first, HEAD_DIM, 1)
    right = second if second_half == 1 else pltpu.roll(second, HEAD_DIM, 1)
    return jnp.where(lane < HEAD_DIM, left, right)


def column_of(row):
    count = row.shape[1]
    i = lax.broadcasted_iota(jnp.int32, (count, count), 0)
    j = lax.broadcasted_iota(jnp.int32, (count, count), 1)
    return jnp.sum(jnp.where(i == j, row, 0.0), axis=1, keepdims=True)


def row_of(column):
    count = column.shape[0]
    i = lax.broadcasted_iota(jnp.int32, (count, count), 0)
    j = lax.broadcasted_iota(jnp.int32, (count, count), 1)
    return jnp.sum(jnp.where(i == j, column, 0.0), axis=0, keepdims=True)


def low(value):
    return value.astype(BF16).astype(F32)


def lanes(index):
    return slice(index * PAIR, (index + 1) * PAIR)


class Place:
    def __init__(self, z_count):
        self.x, self.z, self.y, self.c = (lax.axis_index(a) for a in AXES)
        self.g = self.x * 2 + self.y
        self.chip = (self.x * z_count + self.z) * 2 + self.y

    def sibling(self):
        return (self.x, self.z, self.y, 1 - self.c)

    def plane(self, k):
        return (self.x ^ (k // 2), self.z, self.y ^ (k % 2), self.c)

    def line(self, k):
        return (self.x, self.z ^ k, self.y, self.c)

    def any_chip(self, k):
        return (self.x ^ (k // 2 % 2), self.z ^ (k // 4), self.y ^ (k % 2), self.c)


def greet(peers):
    barrier = pltpu.get_barrier_semaphore()
    for peer in peers:
        pl.semaphore_signal(barrier, inc=1, device_id=peer, device_id_type=IDS)
    return lambda: pl.semaphore_wait(barrier, len(peers))


def trip(source, target, sems, index, device):
    return pltpu.make_async_remote_copy(
        src_ref=source,
        dst_ref=target,
        send_sem=sems[0].at[index],
        recv_sem=sems[1].at[index],
        device_id=device,
        device_id_type=IDS,
    )


def send(*given):
    copy = trip(*given)
    copy.start()
    return copy


def move(source, target, sems, index):
    copy = pltpu.make_async_copy(source, target, sems.at[index])
    copy.start()
    return copy


DMA = pltpu.SemaphoreType.DMA


def both(count):
    return [DMA((count,)), DMA((count,))]


def exchange(kernel, ident, out_shape, in_specs, out_specs, scratch, args, flops, sent):
    return pl.pallas_call(
        kernel,
        out_shape=out_shape,
        in_specs=in_specs,
        out_specs=out_specs,
        scratch_shapes=scratch,
        compiler_params=pltpu.CompilerParams(
            collective_id=ident, has_side_effects=True, vmem_limit_bytes=60 << 20
        ),
        cost_estimate=pl.CostEstimate(flops=flops, bytes_accessed=sent, transcendentals=0),
    )(*args)


def head_kernel(
    zc,
    group,
    t_ref,
    q_w,
    k_w,
    v_w,
    g_w,
    u_w,
    d_w,
    o_w,
    gain1,
    gain2,
    ng_ref,
    wg_ref,
    fg_ref,
    a_ref,
    og_ref,
    w_ref,
    f_ref,
    e_ref,
    wo_ref,
    rows,
    weights,
    packed,
    ls,
    w0,
    w1,
    n0,
    n1,
    f0,
    f1,
    z0,
    z1,
    b0,
    b1,
    s0,
    s1,
    o0,
    o1,
    p0,
    p1,
):
    me = Place(zc)
    chips = 4 * zc
    per = zc // group
    qw = group * HEAD_DIM
    width = t_ref.shape[1]
    met = greet([me.any_chip(k) for k in range(1, chips)] + [me.sibling()])
    first_gain, second_gain = column_of(low(gain1[...])), column_of(low(gain2[...]))
    for g in range(4):
        at = slice(g * qw, (g + 1) * qw)
        w_ref[g, :, :qw] = (first_gain * low(q_w[:, at])).astype(BF16)
        for pair in range(group // 2):
            at = lanes(g * group // 2 + pair)
            key, value = first_gain * low(k_w[:, at]), first_gain * low(v_w[:, at])
            for half in range(2):
                start = qw + (2 * pair + half) * PAIR
                w_ref[g, :, start : start + PAIR] = pair_up(key, half, value, half).astype(BF16)
    e_ref[...] = d_w[...].astype(BF16).reshape(e_ref.shape)
    wo_ref[...] = o_w[...].astype(BF16)
    x = t_ref[...].astype(F32)
    rows[0] = (x * lax.rsqrt(jnp.mean(x * x, axis=-1, keepdims=True) + EPS)).astype(BF16)
    met()
    here = og_ref.at[me.x, me.z, me.y, me.c]
    local = [move(w_ref.at[me.g], weights.at[me.chip, me.c], ls, 0), move(wo_ref, here, ls, 1)]
    pieces = []
    for k in reversed(range(1, chips)):
        there = me.any_chip(k)
        their_g = there[0] * 2 + there[2]
        pieces.append(
            send(w_ref.at[their_g], weights.at[me.chip, me.c], (w0, w1), k, there)
        )
    outs = [send(wo_ref, here, (o0, o1), k, me.line(k)) for k in range(1, zc)]
    blocks = [send(rows.at[0], rows.at[k], (n0, n1), k, me.plane(k)) for k in range(1, 4)]
    units = g_w.shape[1] // (4 * zc)
    for which, ref in enumerate((g_w, u_w)):
        for g in range(4):
            px, py = g // 2, g % 2
            if units % PAIR == 0:
                for z in range(zc):
                    at = ((px * zc + z) * 2 + py) * units
                    f_ref[g, which, :, z * units : (z + 1) * units] = (
                        second_gain * low(ref[:, at : at + units])
                    ).astype(BF16)
            else:
                for z in range(0, zc, 2):
                    near, far = (second_gain * low(ref[:, lanes(px * zc + i)]) for i in (z, z + 1))
                    f_ref[g, which, :, lanes(z // 2)] = pair_up(near, py, far, py).astype(BF16)
    wide = [
        move(f_ref.at[me.g], fg_ref.at[me.x, me.y, pl.ds(0, 2)], ls, 2),
        move(e_ref, fg_ref.at[:, :, 2], ls, 9),
    ]
    for k in range(1, 4):
        there = me.plane(k)
        their_g = there[0] * 2 + there[2]
        wide.append(
            send(f_ref.at[their_g], fg_ref.at[me.x, me.y, pl.ds(0, 2)], (f0, f1), k, there)
        )
    local[0].wait()
    for copy in pieces:
        copy.wait()
    relay = send(
        weights.at[:, me.c], weights.at[:, me.c], (s0, s1), 0, me.sibling()
    )
    relay.wait()
    kept = [move(weights, wg_ref, ls, 3)]

    def project(k, carry):
        @pl.when(k > 0)
        def _():
            trip(rows.at[0], rows.at[k], (n0, n1), k, me.plane(k)).wait_recv()

        at = (me.x ^ (k // 2)) * 2 + (me.y ^ (k % 2))
        out = dot(rows[k], weights[...].reshape(width, 3 * qw))
        for head in range(group):
            two, half = out[:, lanes(head // 2)], head % 2
            packed[head, k, :BLOCK] = pair_up(two[:BLOCK], half, two[BLOCK:], half).astype(BF16)
            start = qw + head * PAIR
            packed[head, k, BLOCK:] = out[:, start : start + PAIR].astype(BF16)
        for over in range(1, zc):
            trip(
                packed.at[(me.z ^ over) // per, k],
                a_ref.at[me.z, me.c, at],
                (z0, z1),
                k * zc + over,
                me.line(over),
            ).start()
        trip(
            packed.at[me.z // per, k], a_ref.at[me.z, me.c, at], (b0, b1), k * zc, me.sibling()
        ).start()
        pltpu.make_async_copy(
            packed.at[me.z // per, k], a_ref.at[me.z, me.c, at], ls.at[4 + k]
        ).start()
        return carry

    lax.fori_loop(0, 4, project, 0)
    kept.append(move(rows, ng_ref, ls, 8))
    for copy in outs + local[1:]:
        copy.wait()
    column = og_ref.at[me.x, :, me.y, me.c]
    out_rows = [send(column, column, (p0, p1), k, me.plane(k)) for k in range(1, 4)]

    def pass_on(step, carry):
        k, over = step // (zc - 1), step % (zc - 1) + 1
        at = (me.x ^ (k // 2)) * 2 + (me.y ^ (k % 2))
        there = me.z ^ over
        trip(
            packed.at[there // per, k],
            a_ref.at[me.z, me.c, at],
            (z0, z1),
            k * zc + over,
            me.line(over),
        ).wait()
        landed = a_ref.at[there, me.c, at]
        trip(landed, landed, (b0, b1), k * zc + over, me.sibling()).start()
        return carry

    lax.fori_loop(0, 4 * (zc - 1), pass_on, 0)
    for copy in out_rows:
        copy.wait()
    every = og_ref.at[:, :, :, me.c]
    last = send(every, every, (s0, s1), 1, me.sibling())

    def finish(step, carry):
        k, over = step // zc, step % zc
        at = (me.x ^ (k // 2)) * 2 + (me.y ^ (k % 2))
        landed = a_ref.at[me.z ^ over, me.c, at]
        trip(landed, landed, (b0, b1), k * zc + over, me.sibling()).wait()
        return carry

    lax.fori_loop(0, 4 * zc, finish, 0)
    for k in range(4):
        pltpu.make_async_copy(
            packed.at[me.z // per, k], a_ref.at[me.z, me.c, me.g], ls.at[4 + k]
        ).wait()
    for copy in [last] + kept + wide:
        copy.wait()
    for copy in blocks:
        copy.wait_send()


def head_exchange(zc, group, tokens, matrices, gains):
    chips = 4 * zc
    own, width = tokens.shape
    count = matrices[0].shape[0]
    piece = (count, 3 * group * HEAD_DIM)
    return exchange(
        functools.partial(head_kernel, zc, group),
        1,
        (
            struct((4, own, width)),
            struct((chips, 2) + piece),
            struct((2, 2, 3, count, width)),
            struct((zc, 2, 4, BLOCK + own, PAIR)),
            struct((2, zc, 2, 2, count, width)),
        ),
        [VM] * 10,
        (ANY,) * 5,
        [
            pltpu.VMEM((4,) + piece, BF16),
            pltpu.VMEM((4, 2, count, width), BF16),
            pltpu.VMEM((2, 2, count, width), BF16),
            pltpu.VMEM((count, width), BF16),
            pltpu.VMEM((4, own, width), BF16),
            pltpu.VMEM((chips, 2) + piece, BF16),
            pltpu.VMEM((group, 4, BLOCK + own, PAIR), BF16),
            DMA((10,)),
        ]
        + both(chips)
        + both(4)
        + both(4)
        + both(4 * zc)
        + both(4 * zc)
        + both(2)
        + both(zc)
        + both(4),
        (tokens, *matrices, *(g.reshape(1, -1) for g in gains)),
        2 * 4 * own * width * width,
        16 << 20,
    )


def join_kernel(zc, s_ref, x_ref, w_ref, ob_ref, r_ref, n_ref, mine, theirs, slabs, ls, b0, b1, c0, c1):
    me = Place(zc)
    chips = 4 * zc
    heads, per = slabs.shape[:2]
    greet([me.any_chip(k) for k in range(1, chips)] + [me.sibling()])()
    other = send(s_ref.at[:, 1 - me.c], theirs, (b0, b1), 0, me.sibling())
    own = move(s_ref.at[:, me.c], mine, ls, 0)
    own.wait()
    other.wait()
    mine[...] = mine[...] + theirs[...]
    head = me.g * (heads // 4) + me.z // per
    place = me.z % per
    keep = move(mine.at[me.z, me.g], slabs.at[head, place], ls, 1)
    sends = []
    for k in reversed(range(1, chips)):
        there = me.any_chip(k)
        their_g = there[0] * 2 + there[2]
        sends.append(
            send(mine.at[there[1], their_g], slabs.at[head, place], (c0, c1), k, there)
        )
    keep.wait()
    for copy in sends:
        copy.wait()
    for block in range(2):
        for pair in range(heads // 2):
            sides = []
            for side in range(2):
                slab = slabs[2 * pair + side, 0].astype(F32)
                for extra in range(1, per):
                    slab = slab + slabs[2 * pair + side, extra].astype(F32)
                sides.append(slab)
            ob_ref[block * BLOCK : (block + 1) * BLOCK, lanes(pair)] = pair_up(
                sides[0], block, sides[1], block
            ).astype(BF16)
    residual = x_ref[...].astype(F32) + dot(ob_ref[...], w_ref[...])
    r_ref[...] = residual
    mean = jnp.mean(residual * residual, axis=-1, keepdims=True)
    n_ref[...] = (residual * lax.rsqrt(mean + EPS)).astype(BF16)


def join_exchange(zc, heads, slabs, tokens, w_out):
    chips = 4 * zc
    per = 4 * zc // heads
    half = (zc,) + slabs.shape[2:]
    shape = tokens.shape
    return exchange(
        functools.partial(join_kernel, zc),
        2,
        (struct(shape), struct(shape, F32), struct(shape)),
        [ANY, VM, VM],
        (VM,) * 3,
        [
            pltpu.VMEM(half, BF16),
            pltpu.VMEM(half, BF16),
            pltpu.VMEM((heads, per) + slabs.shape[3:], BF16),
            DMA((2,)),
        ]
        + both(1)
        + both(chips),
        (slabs, tokens, w_out),
        0,
        0,
    )


def middle_kernel(zc, n_ref, ca_ref, cb_ref, cc_ref, cd_ref, *rest):
    f_refs, rest = rest[: zc // 2 + 1], rest[zc // 2 + 1 :]
    oa_ref, ob_ref, oc_ref, od_ref, cs_ref, sh_ref, rows, cots, gate_w, up_w, down_w, *rest = rest
    hid, dgate, dup, c_out, c_in, stage, o_out, ls, n0, n1, c0, c1, f0, f1, h0, h1 = rest
    me = Place(zc)
    width = n_ref.shape[1]
    met = greet([me.plane(k) for k in range(1, 4)] + [me.line(1), me.sibling()])
    move(n_ref, rows.at[0], ls, 15).wait()
    met()
    farthest = send(rows.at[0], rows.at[3], (n0, n1), 3, me.plane(3))
    def places(there):
        return (
            gate_w.at[:, there, :, me.c],
            up_w.at[:, there, :, me.c],
            down_w.at[there, me.c],
        )

    given = dict(zip([1, *range(0, zc, 2)], f_refs))
    hops, loads = [], []
    for k in range(2, zc, 2):
        for i, place in enumerate(places(me.z ^ k)):
            hops.append(send(given[k].at[:, :, i], place, (h0, h1), 3 * k + i, me.line(1)))
    for k, ref in given.items():
        for i, place in enumerate(places(me.z ^ k)):
            loads.append(send(ref.at[:, :, i], place, (f0, f1), 3 * k + i, me.sibling()))
            loads.append(move(ref.at[:, :, i], place, ls, 21 + 3 * k + i))
    for k, ref in enumerate((ca_ref, cb_ref, cc_ref, cd_ref)):
        loads.append(move(ref, cots.at[k], ls, 16 + k))
    farthest.wait_send()
    near_rows = [send(rows.at[0], rows.at[k], (n0, n1), k, me.plane(k)) for k in (1, 2)]
    for copy in hops:
        copy.wait()
    for k in range(3, zc, 2):
        for i, place in enumerate(places(me.z ^ k)):
            loads.append(send(place, place, (f0, f1), 3 * k + i, me.sibling()))
    for copy in loads:
        copy.wait()
    square = (width, width)

    def block(step, carry):
        k = jnp.where(step == 0, 3, jnp.where(step == 3, 0, step))

        @pl.when(step < 3)
        def _():
            trip(rows.at[0], rows.at[k], (n0, n1), k, me.plane(k)).wait_recv()

        gate_mat, up_mat = gate_w[...].reshape(square), up_w[...].reshape(square)
        gate = dot(rows[k], gate_mat)
        up = dot(rows[k], up_mat)
        back = nt_dot(cots[k], down_w[...].reshape(square))
        sig = jax.nn.sigmoid(gate)
        soft = gate * sig
        hid[k] = (soft * up).astype(BF16)
        dgate[k] = (back * up * sig * (1.0 + gate * (1.0 - sig))).astype(BF16)
        dup[k] = (back * soft).astype(BF16)
        c_out[k] = (nt_dot(dgate[k], gate_mat) + nt_dot(dup[k], up_mat)).astype(BF16)

        @pl.when(step < 3)
        def _():
            trip(c_out.at[k], c_in.at[k], (c0, c1), k, me.plane(k)).start()

        return carry

    lax.fori_loop(0, 4, block, 0)
    all_rows = (4 * n_ref.shape[0], width)

    def weight_grad(left, right, slot):
        chunk = 256
        for first in range(0, width, chunk):
            value = tn_dot(left[:, first : first + chunk], right).astype(BF16)
            stage[slot, first : first + chunk] = value

    shares = []
    piece = width // (8 * zc)

    def share(slot, which):
        parts = stage.at[slot].reshape(2, zc, 2, 2, piece, width)
        for g in range(4):
            x, y = g // 2, g % 2
            shares.append(
                move(parts.at[x, :, y], sh_ref.at[:, :, 2 * g + which], ls, 12 + 2 * g + which)
            )

    flat = lambda ref: ref[...].reshape(all_rows)
    weight_grad(flat(rows), flat(dgate), 0)
    share(0, 0)
    weight_grad(flat(rows), flat(dup), 1)
    share(1, 1)
    weight_grad(flat(hid), flat(cots), 2)
    shares.append(
        move(stage.at[2].reshape(zc, 2, 4, piece, width), sh_ref.at[:, :, 8:], ls, 20)
    )

    for k, ref in enumerate((oa_ref, ob_ref, oc_ref, od_ref)):
        o_out[k] = dot(hid[k], down_w[...].reshape(square)).astype(BF16).reshape(ref.shape)
        shares.append(move(o_out.at[k], ref, ls, k))
    total = c_out[0].astype(F32)
    for k in range(1, 4):
        trip(c_out.at[k], c_in.at[k], (c0, c1), k, me.plane(k)).wait()
        total = total + c_in[k].astype(F32)
    cs_ref[...] = total
    for copy in shares:
        copy.wait()
    for copy in near_rows:
        copy.wait_send()


def middle_exchange(zc, normed, cots, weights):
    own, width = normed.shape
    piece = width // (8 * zc)
    blocks = pltpu.VMEM((4, own, width), BF16)
    wide = pltpu.VMEM((2, zc, 2, 2, piece, width), BF16)
    return exchange(
        functools.partial(middle_kernel, zc),
        3,
        (
            *[struct((zc, 2, piece, width))] * 4,
            struct((own, width), F32),
            struct((zc, 2, 12, piece, width)),
        ),
        [ANY] * (5 + len(weights)),
        (ANY,) * 4 + (VM, ANY),
        [blocks, blocks, wide, wide, pltpu.VMEM((zc, 2, 2, 2, piece, width), BF16)]
        + [blocks] * 5
        + [pltpu.VMEM((3, width, width), BF16), pltpu.VMEM((4, zc, 2, piece, width), BF16), DMA((21 + 3 * zc,))]
        + both(4)
        + both(4)
        + both(3 * zc)
        + both(3 * zc),
        (normed, *cots, *weights),
        2 * 4 * own * width * width * 9,
        64 << 20,
    )


def turn_kernel(
    zc,
    c_ref,
    t_ref,
    r_ref,
    wo_ref,
    ob_ref,
    yb_ref,
    yc_ref,
    dr_ref,
    do_ref,
    va_ref,
    vb_ref,
    vc_ref,
    vd_ref,
    nb_ref,
    nc_ref,
    slabs,
    stage,
    wo_in,
    ob_in,
    ls,
    d0,
    d1,
    b0,
    b1,
    y0,
    y1,
):
    me = Place(zc)
    chips = 4 * zc
    heads = slabs.shape[0]
    group = heads // 4
    per = zc // group
    width = t_ref.shape[1]
    met = greet([me.any_chip(k) for k in range(1, chips)] + [me.sibling()])
    loads = [move(wo_ref, wo_in, ls, 5), move(ob_ref, ob_in, ls, 6)]
    total, residual = c_ref[...], r_ref[...]
    scaling = lax.rsqrt(jnp.mean(residual * residual, axis=-1, keepdims=True) + EPS)
    normed = residual * scaling
    middle = jnp.mean(total * normed, axis=-1, keepdims=True)
    grad = t_ref[...].astype(F32) + scaling * (total - normed * middle)
    dr_ref[...] = grad
    narrow = grad.astype(BF16)
    loads[0].wait()
    back = nt_dot(narrow, wo_in[...])
    for pair in range(heads // 2):
        two = back[:, lanes(pair)]
        for side in range(2):
            slabs[2 * pair + side] = pair_up(two[:BLOCK], side, two[BLOCK:], side).astype(BF16)
    met()
    to = do_ref.at[me.z, me.c, me.g]
    own = move(slabs.at[me.g * group + me.z // per], to, ls, 0)
    sends = []
    for k in reversed(range(1, chips)):
        there = me.any_chip(k)
        head = (there[0] * 2 + there[2]) * group + there[1] // per
        sends.append(send(slabs.at[head], to, (d0, d1), k, there))
    sends.append(send(yb_ref, nb_ref, (y0, y1), 1, me.plane(1)))
    sends.append(send(yc_ref, nc_ref, (y0, y1), 2, me.plane(2)))
    chunk = 256
    loads[1].wait()
    attended = ob_in[...]
    for first in range(0, width, chunk):
        stage[first : first + chunk] = tn_dot(attended[:, first : first + chunk], narrow).astype(BF16)
    parts = stage.reshape(2, zc, 2, 2, width // (8 * zc), width)
    keeps = []
    for k, ref in enumerate((va_ref, vb_ref, vc_ref, vd_ref)):
        there = me.plane(k)
        keeps.append(move(parts.at[there[0], :, there[2]], ref, ls, 1 + k))
    own.wait()
    for copy in sends[:-2]:
        copy.wait()
    half = do_ref.at[:, me.c]
    relay = send(half, half, (b0, b1), 0, me.sibling())
    for copy in keeps + sends[-2:]:
        copy.wait()
    relay.wait()


def turn_exchange(zc, c_sum, cotangent, residual, w_out, attn_rows, near):
    chips = 4 * zc
    own, width = cotangent.shape
    heads = width // HEAD_DIM
    return exchange(
        functools.partial(turn_kernel, zc),
        6,
        (
            struct((own, width), F32),
            struct((zc, 2, 4, BLOCK, PAIR)),
            *[struct((zc, 2, width // (8 * zc), width))] * 6,
        ),
        [VM] * 3 + [ANY] * 4,
        (VM,) + (ANY,) * 7,
        [
            pltpu.VMEM((heads, BLOCK, PAIR), BF16),
            pltpu.VMEM((width, width), BF16),
            pltpu.VMEM((width, width), BF16),
            pltpu.VMEM((own, width), BF16),
            DMA((7,)),
        ]
        + both(chips)
        + both(1)
        + both(3),
        (c_sum, cotangent, residual, w_out, attn_rows, *near),
        2 * 2 * own * width * width,
        8 << 20,
    )


def tail_kernel(
    zc,
    d_ref,
    n_any,
    w_any,
    x_any,
    g_any,
    f_ref,
    r_ref,
    ya_ref,
    yb_ref,
    yc_ref,
    yd_ref,
    va_ref,
    vb_ref,
    vc_ref,
    vd_ref,
    tg_ref,
    gw_ref,
    go_ref,
    gf_ref,
    out_ref,
    n_ref,
    w_ref,
    x_ref,
    g_ref,
    r_in,
    y_in,
    o_mine,
    o_theirs,
    o_land,
    mine,
    theirs,
    landed,
    grads,
    c_out,
    c_in,
    stage,
    other_w,
    ls,
    b0,
    b1,
    z0,
    z1,
    c0,
    c1,
    s0,
    s1,
    w0,
    w1,
    q0,
    q1,
    f0,
    f1,
):
    me = Place(zc)
    chips = 4 * zc
    group, per = landed.shape[:2]
    qw = group * HEAD_DIM
    greet([me.any_chip(k) for k in range(1, chips)] + [me.sibling()])()
    head, place = me.z // per, me.z % per

    def slot(k):
        return (me.x ^ (k // 2)) * 2 + (me.y ^ (k % 2))

    order = (3, 2, 1, 0)
    halves = []
    for k in order:
        halves.append(
            (
                send(d_ref.at[:, 1 - me.c, slot(k)], theirs.at[k], (b0, b1), k, me.sibling()),
                move(d_ref.at[:, me.c, slot(k)], mine.at[k], ls, k),
            )
        )
    given = ((w_any, w_ref), (n_any, n_ref), (g_any, g_ref), (x_any, x_ref))
    loads = [move(source, target, ls, 20 + i) for i, (source, target) in enumerate(given)]
    f_parts = [move(f_ref.at[pl.ds(2 * me.g, 2)], gf_ref.at[me.g], ls, 10)]
    for k in (3, 1, 2):
        there = me.plane(k)
        part = f_ref.at[pl.ds(2 * (there[0] * 2 + there[2]), 2)]
        f_parts.append(send(part, gf_ref.at[me.g], (f0, f1), k, there))
    out_parts = [move(r_ref, r_in, ls, 11)]
    for i, ref in enumerate((ya_ref, yb_ref, yc_ref, yd_ref)):
        out_parts.append(move(ref, y_in.at[i, 0], ls, 12 + i))
    for i, ref in enumerate((va_ref, vb_ref, vc_ref, vd_ref)):
        out_parts.append(move(ref, y_in.at[i, 1], ls, 16 + i))
    for k, (far, near) in zip(order, halves):
        near.wait()
        far.wait()
        mine[k] = mine[k] + theirs[k]
        for over in range(1, zc):
            send(
                mine.at[k, me.z ^ over],
                landed.at[head, place, k],
                (z0, z1),
                k * zc + over,
                me.line(over),
            )
        move(mine.at[k, me.z], landed.at[head, place, k], ls, 4 + k)

    for copy in out_parts + loads:
        copy.wait()
    final = r_in[...]
    o_sum = jnp.zeros(o_mine.shape, F32)
    for i in range(4):
        final = final + y_in[i, 0].astype(F32).reshape(final.shape)
        o_sum = o_sum + y_in[i, 1].astype(F32)
    out_ref[...] = final.astype(BF16)
    o_mine[...] = o_sum.astype(BF16)
    o_swap = send(o_mine.at[:, 1 - me.c], o_theirs, (s0, s1), 1, me.sibling())

    def block(step, carry):
        k = 3 - step
        pltpu.make_async_copy(
            mine.at[k, me.z], landed.at[head, place, k], ls.at[4 + k]
        ).wait()
        for over in range(1, zc):
            trip(
                mine.at[k, me.z ^ over],
                landed.at[head, place, k],
                (z0, z1),
                k * zc + over,
                me.line(over),
            ).wait()
        for pair in range(group // 2):
            sides = []
            for side in range(2):
                h = 2 * pair + side
                slab = landed[h, 0, k]
                for extra in range(1, per):
                    slab = slab + landed[h, extra, k]
                start = qw + h * PAIR
                grads[k, :, start : start + PAIR] = slab[BLOCK:]
                sides.append(slab[:BLOCK].astype(F32))
            for b in range(2):
                grads[k, b * BLOCK : (b + 1) * BLOCK, lanes(pair)] = pair_up(
                    sides[0], b, sides[1], b
                ).astype(BF16)

        @pl.when(k > 0)
        def _():
            c_out[k] = nt_dot(grads[k], w_ref[...]).astype(BF16)
            trip(c_out.at[k], c_in.at[k], (c0, c1), k, me.plane(k)).start()

        return carry

    o_swap.wait()
    o_theirs[...] = o_theirs[...] + o_mine[:, me.c]
    sends = [
        send(o_theirs.at[me.z ^ k], o_land.at[k], (q0, q1), k, me.line(k)) for k in range(1, zc)
    ]
    lax.fori_loop(0, 4, block, 0)
    width, cols = w_ref.shape
    all_rows = 4 * n_ref.shape[1]
    normed_all = n_ref[...].reshape(all_rows, width)
    grads_all = grads[...].reshape(all_rows, cols)
    piece = stage.shape[2]
    chunk = 256
    each = chunk // (2 * piece)
    swaps = []
    for first in range(0, width, chunk):
        value = tn_dot(normed_all[:, first : first + chunk], grads_all).astype(BF16)
        at = first // (2 * piece)
        stage[at : at + each] = value.reshape(each, 2, piece, cols)
        swaps.append(
            send(
                stage.at[at : at + each, 1 - me.c],
                other_w.at[at : at + each],
                (s0, s1),
                2 + first // chunk,
                me.sibling(),
            )
        )
    c_out[0] = nt_dot(grads[0], w_ref[...]).astype(BF16)
    for swap in swaps:
        swap.wait()

    def add(i, carry):
        other_w[i] = stage[i, me.c] + other_w[i]
        return carry

    lax.fori_loop(0, chips, add, 0)
    stay = move(other_w.at[me.chip], gw_ref.at[me.z, me.g], ls, 8)
    for k in reversed(range(1, chips)):
        there = me.any_chip(k)
        chip = (there[0] * zc + there[1]) * 2 + there[2]
        sends.append(send(other_w.at[chip], gw_ref.at[me.z, me.g], (w0, w1), k, there))
    total = c_out[0].astype(F32)
    for k in range(1, 4):
        trip(c_out.at[k], c_in.at[k], (c0, c1), k, me.plane(k)).wait()
        total = total + c_in[k].astype(F32)
    x = x_ref[...].astype(F32)
    scaling = lax.rsqrt(jnp.mean(x * x, axis=-1, keepdims=True) + EPS)
    normed = x * scaling
    middle = jnp.mean(total * normed, axis=-1, keepdims=True)
    tg_ref[...] = (g_ref[...] + scaling * (total - normed * middle)).astype(BF16)
    stay.wait()
    for copy in sends + f_parts:
        copy.wait()
    o_sum = o_theirs[me.z].astype(F32)
    for k in range(1, zc):
        o_sum = o_sum + o_land[k].astype(F32)
    go_ref[...] = o_sum


def tail_exchange(zc, group, slab_grads, n_all, weights, tokens, residual_grad, shares, residual, packs):
    chips = 4 * zc
    per = zc // group
    own, width = tokens.shape
    cols = weights.shape[1]
    slab = slab_grads.shape[3:]
    piece = width // (2 * chips)
    blocks = pltpu.VMEM((4, own, width), BF16)
    return exchange(
        functools.partial(tail_kernel, zc),
        4,
        (
            struct((own, width)),
            struct((zc, 4, piece, cols)),
            struct((piece, width), F32),
            struct((4, 2, piece, width)),
            struct((own, width)),
        ),
        [ANY] * 15,
        (VM, ANY, VM, ANY, VM),
        [
            pltpu.VMEM((4, own, width), BF16),
            pltpu.VMEM((width, cols), BF16),
            pltpu.VMEM((own, width), BF16),
            pltpu.VMEM((own, width), F32),
            pltpu.VMEM((own, width), F32),
            pltpu.VMEM((4, 2, zc, 2, piece, width), BF16),
            pltpu.VMEM((zc, 2, piece, width), BF16),
            pltpu.VMEM((zc, piece, width), BF16),
            pltpu.VMEM((zc, piece, width), BF16),
            pltpu.VMEM((4, zc) + slab, BF16),
            pltpu.VMEM((4, zc) + slab, BF16),
            pltpu.VMEM((group, per, 4) + slab, BF16),
            pltpu.VMEM((4, own, cols), BF16),
            blocks,
            blocks,
            pltpu.VMEM((chips, 2, piece, cols), BF16),
            pltpu.VMEM((chips, piece, cols), BF16),
            DMA((24,)),
        ]
        + both(4)
        + both(4 * zc)
        + both(4)
        + both(2 + width // 256)
        + both(chips)
        + both(zc)
        + both(4),
        (slab_grads, n_all, weights, tokens, residual_grad, shares, residual, *packs),
        2 * 4 * own * width * cols * 2,
        24 << 20,
    )


def last_kernel(
    zc,
    group,
    t_any,
    o_any,
    wo_any,
    gw_any,
    gf_any,
    ds_any,
    q_any,
    k_any,
    v_any,
    g_any,
    u_any,
    gain1,
    gain2,
    tg_ref,
    out_ref,
    go_ref,
    g1_ref,
    q_ref,
    k_ref,
    v_ref,
    g2_ref,
    g_ref,
    u_ref,
    d_ref,
    gw_ref,
    gf_ref,
    ds_ref,
    q_w,
    k_w,
    v_w,
    g_w,
    u_w,
    ls,
):
    given = (gw_any, q_any, k_any, v_any, gf_any, g_any, u_any, ds_any, t_any, o_any, wo_any)
    taken = (gw_ref, q_w, k_w, v_w, gf_ref, g_w, u_w, ds_ref, tg_ref, out_ref, go_ref)
    copies = [move(a, b, ls, i) for i, (a, b) in enumerate(zip(given, taken))]
    for copy in copies:
        copy.wait()
    d_ref[...] = ds_ref[8:].astype(F32).reshape(d_ref.shape)
    first_gain, second_gain = column_of(low(gain1[...])), column_of(low(gain2[...]))
    count = q_w.shape[0]
    qw = group * HEAD_DIM
    score = jnp.zeros((count, PAIR), F32)
    for g in range(4):
        raw = gw_ref[0, g].astype(F32)
        for z in range(1, zc):
            raw = raw + gw_ref[z, g].astype(F32)
        for pair in range(group // 2):
            at = lanes(g * group // 2 + pair)
            start = qw + 2 * pair * PAIR
            even, odd = raw[:, start : start + PAIR], raw[:, start + PAIR : start + 2 * PAIR]
            query = raw[:, lanes(pair)]
            key, value = pair_up(even, 0, odd, 0), pair_up(even, 1, odd, 1)
            score = score + query * low(q_w[:, at]) + key * low(k_w[:, at]) + value * low(v_w[:, at])
            q_ref[:, at] = first_gain * query
            k_ref[:, at] = first_gain * key
            v_ref[:, at] = first_gain * value
    g1_ref[...] = row_of(jnp.sum(score, axis=1, keepdims=True))
    units = g_w.shape[1] // (4 * zc)
    score = jnp.zeros((count, PAIR), F32)
    for which, (weight, target) in enumerate(((g_w, g_ref), (u_w, u_ref))):
        for chunk in range(weight.shape[1] // PAIR):
            if units % PAIR == 0:
                owner, piece = divmod(chunk, units // PAIR)
                x, z, y = owner // (2 * zc), owner // 2 % zc, owner % 2
                raw = gf_ref[2 * x + y, which, :, lanes(z * units // PAIR + piece)].astype(F32)
            else:
                x, z = chunk // zc, chunk % zc
                near = gf_ref[2 * x, which, :, lanes(z // 2)].astype(F32)
                far = gf_ref[2 * x + 1, which, :, lanes(z // 2)].astype(F32)
                raw = pair_up(near, z % 2, far, z % 2)
            score = score + raw * low(weight[:, lanes(chunk)])
            target[:, lanes(chunk)] = second_gain * raw
    g2_ref[...] = row_of(jnp.sum(score, axis=1, keepdims=True))


def last_step(zc, group, tokens_grad, output, out_share, w_all, f_all, shares, matrices, gains):
    own, width = output.shape
    count, hidden = matrices[3].shape
    return pl.pallas_call(
        functools.partial(last_kernel, zc, group),
        out_shape=(
            struct((own, width)),
            struct((own, width)),
            struct((count, width), F32),
            struct((1, count), F32),
            struct((count, width), F32),
            struct((count, width), F32),
            struct((count, width), F32),
            struct((1, count), F32),
            struct((count, hidden), F32),
            struct((count, hidden), F32),
            struct((4 * count, width), F32),
        ),
        in_specs=[ANY] * 11 + [VM] * 2,
        out_specs=(VM,) * 11,
        scratch_shapes=[
            pltpu.VMEM(v.shape, v.dtype) for v in (w_all, f_all, shares, *matrices)
        ]
        + [DMA((11,))],
        compiler_params=pltpu.CompilerParams(vmem_limit_bytes=60 << 20),
    )(
        tokens_grad,
        output,
        out_share,
        w_all,
        f_all,
        shares,
        *matrices,
        *(g.reshape(1, -1) for g in gains),
    )


def segment_start(position, lens_ref):
    start = jnp.zeros_like(position)
    end = 0
    for j in range(lens_ref.shape[0]):
        end = end + lens_ref[j]
        start = jnp.where(position >= end, end, start)
    return start


def note_tiles(workers, worker, tiles, lens_ref, mine):
    turns = tiles // workers

    def snake(turn, carry):
        forward = turn * workers + worker
        backward = turn * workers + workers - 1 - worker
        mine[turn] = jnp.where((turn & 1) == 0, forward, backward)
        return carry

    def weigh(step, ahead):
        turn = turns - 1 - step
        loads = []
        for tile in (2 * turn, 2 * turn + 1):
            first, _, _, last = key_bounds(tile * QTILE, lens_ref)
            loads.append(last - first)
        lighter_first = loads[0] <= loads[1]
        first_to_zero = jnp.where(ahead > 0, lighter_first, loads[0] > loads[1])
        mine[turn] = 2 * turn + jnp.where(first_to_zero, worker, 1 - worker)
        return ahead + jnp.where(first_to_zero, loads[0] - loads[1], loads[1] - loads[0])

    if workers == 2:
        lax.fori_loop(0, turns, weigh, 0)
    else:
        lax.fori_loop(0, turns, snake, 0)


def key_bounds(first, lens_ref):
    low_start = segment_start(first, lens_ref)
    high_start = segment_start(first + QTILE - 1, lens_ref)
    low = low_start // KTILE
    high = (first + QTILE + KTILE - 1) // KTILE
    plain = jnp.clip((high_start + KTILE - 1) // KTILE, low, high)
    stop = jnp.clip((first + 1) // KTILE, plain, high)
    return low, plain, stop, high


def visible(first, tile, starts):
    key = tile * KTILE + lax.broadcasted_iota(jnp.int32, (KTILE, QTILE), 0)
    query = first + lax.broadcasted_iota(jnp.int32, (KTILE, QTILE), 1)
    return (key <= query) & (key >= starts)


def note_places(anchor_ref, inv):
    def note(i, carry):
        inv[anchor_ref[i]] = i
        return carry

    lax.fori_loop(0, anchor_ref.shape[0], note, 0)


def half_lanes(rows, half):
    lane = lax.broadcasted_iota(jnp.int32, rows.shape, 1)
    return jnp.where((lane // HEAD_DIM) == half, rows, jnp.zeros_like(rows))


def fold(rows, columns, first):
    row = lax.broadcasted_iota(jnp.int32, (rows, columns), 0)
    column = lax.broadcasted_iota(jnp.int32, (rows, columns), 1)
    return (row % HEAD_DIM == column - first).astype(F32).astype(BF16)


def unfold(rows, columns, first):
    row = lax.broadcasted_iota(jnp.int32, (rows, columns), 0)
    column = lax.broadcasted_iota(jnp.int32, (rows, columns), 1)
    return (column % HEAD_DIM == row - first).astype(F32).astype(BF16)


def forward_kernel(
    workers, anchor_ref, lens_ref, who_ref, a_ref, o_ref, kv_ref, kvt_ref, q_ref, qt_ref, ot_ref, l_ref, inv, mine, raw
):
    blocks = anchor_ref.shape[0]
    turns = qt_ref.shape[0]
    per = QTILE // BLOCK
    worker = who_ref[0]
    note_places(anchor_ref, inv)
    note_tiles(workers, worker, turns * workers, lens_ref, mine)
    o_ref[...] = jnp.zeros_like(o_ref)
    same = selection(PAIR, PAIR, 0)

    def order(step, carry):
        for b in range(per):
            i = step * per + b
            where = inv[i]
            slab, half = where >> 1, where & 1
            at = pl.ds(pl.multiple_of(i * BLOCK, BLOCK), BLOCK)
            kv_ref[at, :] = a_ref[slab, pl.ds(pl.multiple_of(BLOCK + half * BLOCK, BLOCK), BLOCK), :]
        return carry

    lax.fori_loop(0, blocks // per, order, 0)

    def flip(step, carry):
        at = pl.ds(pl.multiple_of(step * TURNED, TURNED), TURNED)
        kvt_ref[:, at] = nt_dot(same, kv_ref[at, :]).astype(BF16)
        return carry

    lax.fori_loop(0, blocks * BLOCK // TURNED, flip, 0)

    def one_tile(turn, carry):
        tile = mine[turn]
        first = tile * QTILE
        for b in range(per):
            where = inv[tile * per + b]
            raw[b * BLOCK : (b + 1) * BLOCK, :] = half_lanes(a_ref[where >> 1, :BLOCK, :], where & 1)
        q_ref[turn] = (dot(raw[...], fold(PAIR, PAIR, 0)) * 0.125).astype(BF16)
        qt_ref[turn] = (nt_dot(unfold(PAIR, PAIR, 0), raw[...]) * 0.125).astype(BF16)
        query = qt_ref[turn]
        starts = segment_start(first + lax.broadcasted_iota(jnp.int32, (1, QTILE), 1), lens_ref)
        low, plain, stop, high = key_bounds(first, lens_ref)

        def step(masked, kt, state):
            top, total, acc = state
            at = pl.ds(pl.multiple_of(kt * KTILE, KTILE), KTILE)
            scores = dot(kv_ref[at, :], query)
            if masked:
                scores = jnp.where(visible(first, kt, starts), scores, MASKED)
            new_top = jnp.maximum(top, jnp.max(scores, axis=0, keepdims=True))
            factor = jnp.exp(top - new_top)
            weights = jnp.exp(scores - new_top)
            total = total * factor + jnp.sum(weights, axis=0, keepdims=True)
            acc = acc * factor + dot(kvt_ref[HEAD_DIM:, at], weights.astype(BF16))
            return (new_top, total, acc)

        state = (
            jnp.full((1, QTILE), LOWEST, F32),
            jnp.zeros((1, QTILE), F32),
            jnp.zeros((HEAD_DIM, QTILE), F32),
        )
        state = lax.fori_loop(low, plain, functools.partial(step, True), state)
        state = lax.fori_loop(plain, stop, functools.partial(step, False), state)
        top, total, acc = lax.fori_loop(stop, high, functools.partial(step, True), state)
        out = acc / total
        ot_ref[turn] = out
        l_ref[turn] = top + jnp.log(total)
        wide = tn_dot(out.astype(BF16), unfold(HEAD_DIM, PAIR, 0)).astype(BF16)
        for b in range(per):
            where = inv[tile * per + b]
            slab = where >> 1
            o_ref[slab] = o_ref[slab] + half_lanes(wide[b * BLOCK : (b + 1) * BLOCK], where & 1)
        return carry

    lax.fori_loop(0, turns, one_tile, 0)


def attention_forward(workers, anchors, lengths, who, packed):
    slabs = packed.shape[0]
    rows = slabs * 2 * BLOCK
    turns = rows // QTILE // workers
    return pl.pallas_call(
        functools.partial(forward_kernel, workers),
        out_shape=(
            struct((slabs, BLOCK, PAIR)),
            struct((rows, PAIR)),
            struct((PAIR, rows)),
            struct((turns, QTILE, PAIR)),
            struct((turns, PAIR, QTILE)),
            struct((turns, HEAD_DIM, QTILE), F32),
            struct((turns, 1, QTILE), F32),
        ),
        in_specs=[SM, SM, SM, VM],
        out_specs=(VM,) * 7,
        scratch_shapes=[
            pltpu.SMEM((2 * slabs,), jnp.int32),
            pltpu.SMEM((turns,), jnp.int32),
            pltpu.VMEM((QTILE, PAIR), BF16),
        ],
        compiler_params=pltpu.CompilerParams(vmem_limit_bytes=60 << 20),
        cost_estimate=pl.CostEstimate(
            flops=rows * rows * 64, bytes_accessed=rows * 1024, transcendentals=rows * rows // 8
        ),
    )(anchors, lengths, who, packed)


def backward_kernel(
    workers,
    anchor_ref,
    lens_ref,
    who_ref,
    d_ref,
    kv_ref,
    kvt_ref,
    q_ref,
    qt_ref,
    ot_ref,
    l_ref,
    g_ref,
    inv,
    mine,
    raw,
    both_rows,
    dt,
    acc,
):
    blocks = anchor_ref.shape[0]
    turns = qt_ref.shape[0]
    per = QTILE // BLOCK
    worker = who_ref[0]
    note_places(anchor_ref, inv)
    note_tiles(workers, worker, turns * workers, lens_ref, mine)
    acc[...] = jnp.zeros_like(acc)
    g_ref[:, :BLOCK, :] = jnp.zeros((g_ref.shape[0], BLOCK, PAIR), BF16)

    def one_tile(turn, carry):
        tile = mine[turn]
        first = tile * QTILE
        for b in range(per):
            where = inv[tile * per + b]
            raw[b * BLOCK : (b + 1) * BLOCK, :] = half_lanes(d_ref[where >> 1], where & 1)
        both_rows[:QTILE] = q_ref[turn]
        both_rows[QTILE:] = dot(raw[...], fold(PAIR, PAIR, HEAD_DIM)).astype(BF16)
        dt[...] = nt_dot(unfold(PAIR, PAIR, HEAD_DIM), raw[...]).astype(BF16)
        query, grad = qt_ref[turn], dt[...]
        norm = l_ref[turn]
        delta = jnp.sum(grad[HEAD_DIM:].astype(F32) * ot_ref[turn], axis=0, keepdims=True)
        starts = segment_start(first + lax.broadcasted_iota(jnp.int32, (1, QTILE), 1), lens_ref)
        low, plain, stop, high = key_bounds(first, lens_ref)

        def step(masked, kt, total):
            at = pl.ds(pl.multiple_of(kt * KTILE, KTILE), KTILE)
            keys = kv_ref[at, :]
            scores = dot(keys, query)
            if masked:
                scores = jnp.where(visible(first, kt, starts), scores, MASKED)
            weights = jnp.exp(scores - norm)
            score_grad = (weights * (dot(keys, grad) - delta)).astype(BF16)
            both_grads = jnp.concatenate([score_grad, weights.astype(BF16)], axis=1)
            acc[at, :] += dot(both_grads, both_rows[...])
            return total + dot(kvt_ref[:HEAD_DIM, at], score_grad)

        total = jnp.zeros((HEAD_DIM, QTILE), F32)
        total = lax.fori_loop(low, plain, functools.partial(step, True), total)
        total = lax.fori_loop(plain, stop, functools.partial(step, False), total)
        total = lax.fori_loop(stop, high, functools.partial(step, True), total)
        wide = tn_dot((total * 0.125).astype(BF16), unfold(HEAD_DIM, PAIR, 0)).astype(BF16)
        for b in range(per):
            where = inv[tile * per + b]
            slab = where >> 1
            g_ref[slab, :BLOCK] = g_ref[slab, :BLOCK] + half_lanes(
                wide[b * BLOCK : (b + 1) * BLOCK], where & 1
            )
        return carry

    lax.fori_loop(0, turns, one_tile, 0)

    def place(step, carry):
        for b in range(per):
            i = step * per + b
            where = inv[i]
            slab, half = where >> 1, where & 1
            at = pl.ds(pl.multiple_of(i * BLOCK, BLOCK), BLOCK)
            to = pl.ds(pl.multiple_of(BLOCK + half * BLOCK, BLOCK), BLOCK)
            g_ref[slab, to, :] = acc[at, :].astype(BF16)
        return carry

    lax.fori_loop(0, blocks // per, place, 0)


def attention_backward(workers, anchors, lengths, who, grads, kept):
    slabs = grads.shape[0]
    rows = slabs * 2 * BLOCK
    return pl.pallas_call(
        functools.partial(backward_kernel, workers),
        out_shape=struct((slabs, 3 * BLOCK, PAIR)),
        in_specs=[SM, SM, SM] + [VM] * 7,
        out_specs=VM,
        scratch_shapes=[
            pltpu.SMEM((2 * slabs,), jnp.int32),
            pltpu.SMEM((rows // QTILE // workers,), jnp.int32),
            pltpu.VMEM((QTILE, PAIR), BF16),
            pltpu.VMEM((2 * QTILE, PAIR), BF16),
            pltpu.VMEM((PAIR, QTILE), BF16),
            pltpu.VMEM((rows, PAIR), F32),
        ],
        compiler_params=pltpu.CompilerParams(vmem_limit_bytes=60 << 20),
        cost_estimate=pl.CostEstimate(
            flops=rows * rows * 160, bytes_accessed=rows * 1024, transcendentals=rows * rows // 8
        ),
    )(anchors, lengths, who, grads, *kept)


def around(value, k):
    return lax.ppermute(value, ("head", "y"), [(i, i ^ k) for i in range(4)])


def along(value, k):
    return lax.ppermute(value, "z", [(i, i ^ k) for i in range(lax.axis_size("z"))])


def doubling(pieces, first, last):
    while first >= last:
        pieces = {**pieces, **{k + first: along(pieces[k], first) for k in pieces}}
        first //= 2
    return pieces


def body(
    zc,
    tokens,
    cotangent,
    norm1_gain,
    w_query,
    w_key,
    w_value,
    w_out,
    norm2_gain,
    w_gate,
    w_up,
    w_down,
    block_anchor,
    seq_lengths,
):
    width = tokens.shape[1]
    heads = width // HEAD_DIM
    group = heads // 4
    per_head = zc // group
    workers = 2 * per_head
    feature_rows = w_query.shape[0]

    n1_all, qkv_w, ffn_own, by_head, out_mat = head_exchange(
        zc,
        group,
        tokens,
        (w_query, w_key, w_value, w_gate, w_up, w_down, w_out),
        (norm1_gain, norm2_gain),
    )
    qkv_w = qkv_w.reshape(width, 3 * group * HEAD_DIM)

    out_mat, sent = lax.optimization_barrier((out_mat.reshape(width, width), cotangent))
    cots = [cotangent] + [around(sent, k) for k in range(1, 4)]
    ffn_parts = doubling({0: ffn_own}, zc // 2, 2)
    close = along(ffn_own, 1)

    anchors = jnp.transpose(block_anchor.reshape(2, zc, 2, 2, 2), (1, 3, 0, 2, 4)).reshape(-1)
    who = ((lax.axis_index("z") % per_head) * 2 + lax.axis_index("core")).astype(jnp.int32).reshape(1)
    slab_count = zc * 8
    o_slabs, *kept = attention_forward(
        workers, anchors, seq_lengths, who, by_head.reshape((slab_count,) + by_head.shape[3:])
    )
    attn_rows, residual, normed_two = join_exchange(
        zc, heads, o_slabs.reshape(zc, 2, 4, BLOCK, PAIR), tokens, out_mat
    )
    *out_parts, c_sum, shares = middle_exchange(
        zc, normed_two, cots, [close] + [ffn_parts[k] for k in range(0, zc, 2)]
    )
    shares = lax.psum_scatter(
        shares.reshape(zc * 2 * 12, feature_rows, width), ("z", "core"), scatter_dimension=0, tiled=True
    )
    residual_grad, do_heads, *packs = turn_exchange(
        zc, c_sum, cotangent, residual, out_mat, attn_rows, out_parts[1:3]
    )
    w_grads, near = packs[:4], packs[4:]
    do_heads, far = lax.optimization_barrier((do_heads, out_parts[3]))
    packs = [out_parts[0], *near, around(far, 3), w_grads[0]]
    packs += [around(w_grads[k], k) for k in range(1, 4)]
    grad_heads = attention_backward(
        workers, anchors, seq_lengths, who, do_heads.reshape(slab_count, BLOCK, PAIR), kept
    )
    tokens_grad, w_all, out_share, f_all, output = tail_exchange(
        zc,
        group,
        grad_heads.reshape(zc, 2, 4, 3 * BLOCK, PAIR),
        n1_all,
        qkv_w,
        tokens,
        residual_grad,
        shares,
        residual,
        packs,
    )
    (
        tokens_grad,
        output,
        out_grad,
        gain1_grad,
        query_grad,
        key_grad,
        value_grad,
        gain2_grad,
        gate_grad,
        up_grad,
        down_grad,
    ) = last_step(
        zc,
        group,
        tokens_grad,
        output,
        out_share,
        w_all,
        f_all,
        shares,
        (w_query, w_key, w_value, w_gate, w_up),
        (norm1_gain, norm2_gain),
    )
    return (
        output,
        tokens_grad,
        gain1_grad.reshape(-1),
        query_grad,
        key_grad,
        value_grad,
        out_grad,
        gain2_grad.reshape(-1),
        gate_grad,
        up_grad,
        down_grad,
    )


def solution(mesh):
    blk = mesh.shape["blk"]
    grid = Mesh(mesh.devices.reshape(mesh.shape["head"], blk // 4, 2, 2), AXES)
    rows, vector, whole = P(AXES, None), P(AXES), P()
    return jax.shard_map(
        functools.partial(body, blk // 4),
        mesh=grid,
        in_specs=(rows, rows, vector, rows, rows, rows, rows, vector, rows, rows, rows, whole, whole),
        out_specs=(rows, rows, vector, rows, rows, rows, rows, vector, rows, rows, rows),
        check_vma=False,
    )
```

```python
import functools

import jax
import jax.numpy as jnp
from jax import lax
from jax.experimental import pallas as pl
from jax.experimental.pallas import tpu as pltpu
from jax.sharding import Mesh
from jax.sharding import PartitionSpec as P

HEAD_DIM = 64
BLOCK = 128
PAIR = 128
EPS = 1e-06
MASKED = -1e30
LOWEST = -1e20
QTILE = 512
KTILE = 512
TURNED = 2048
AXES = ("head", "z", "y", "core")
IDS = pl.DeviceIdType.MESH
F32 = jnp.float32
BF16 = jnp.bfloat16
ANY = pl.BlockSpec(memory_space=pl.ANY)
VM = pl.BlockSpec(memory_space=pltpu.VMEM)
SM = pl.BlockSpec(memory_space=pltpu.SMEM)


def struct(shape, dtype=BF16):
    return jax.ShapeDtypeStruct(tuple(shape), dtype)


def nt_dot(a, b):
    return lax.dot_general(a, b, (((1,), (1,)), ((), ())), preferred_element_type=F32)


def tn_dot(a, b):
    return lax.dot_general(a, b, (((0,), (0,)), ((), ())), preferred_element_type=F32)


def dot(a, b):
    return jnp.dot(a, b, preferred_element_type=F32)


def selection(rows, columns, shift, first=0, last=None):
    last = columns if last is None else last
    row = lax.broadcasted_iota(jnp.int32, (rows, columns), 0)
    column = lax.broadcasted_iota(jnp.int32, (rows, columns), 1)
    hit = (row == column + shift) & (column >= first) & (column < last)
    return hit.astype(F32).astype(BF16)


def pair_up(first, first_half, second, second_half):
    lane = lax.broadcasted_iota(jnp.int32, first.shape, 1)
    left = first if first_half == 0 else pltpu.roll(first, HEAD_DIM, 1)
    right = second if second_half == 1 else pltpu.roll(second, HEAD_DIM, 1)
    return jnp.where(lane < HEAD_DIM, left, right)


def column_of(row):
    count = row.shape[1]
    i = lax.broadcasted_iota(jnp.int32, (count, count), 0)
    j = lax.broadcasted_iota(jnp.int32, (count, count), 1)
    return jnp.sum(jnp.where(i == j, row, 0.0), axis=1, keepdims=True)


def row_of(column):
    count = column.shape[0]
    i = lax.broadcasted_iota(jnp.int32, (count, count), 0)
    j = lax.broadcasted_iota(jnp.int32, (count, count), 1)
    return jnp.sum(jnp.where(i == j, column, 0.0), axis=0, keepdims=True)


def low(value):
    return value.astype(BF16).astype(F32)


def lanes(index):
    return slice(index * PAIR, (index + 1) * PAIR)


class Place:
    def __init__(self, z_count):
        self.x, self.z, self.y, self.c = (lax.axis_index(a) for a in AXES)
        self.g = self.x * 2 + self.y
        self.chip = (self.x * z_count + self.z) * 2 + self.y

    def sibling(self):
        return (self.x, self.z, self.y, 1 - self.c)

    def plane(self, k):
        return (self.x ^ (k // 2), self.z, self.y ^ (k % 2), self.c)

    def line(self, k):
        return (self.x, self.z ^ k, self.y, self.c)

    def any_chip(self, k):
        return (self.x ^ (k // 2 % 2), self.z ^ (k // 4), self.y ^ (k % 2), self.c)


def greet(peers):
    barrier = pltpu.get_barrier_semaphore()
    for peer in peers:
        pl.semaphore_signal(barrier, inc=1, device_id=peer, device_id_type=IDS)
    return lambda: pl.semaphore_wait(barrier, len(peers))


def trip(source, target, sems, index, device):
    return pltpu.make_async_remote_copy(
        src_ref=source,
        dst_ref=target,
        send_sem=sems[0].at[index],
        recv_sem=sems[1].at[index],
        device_id=device,
        device_id_type=IDS,
    )


def send(*given):
    copy = trip(*given)
    copy.start()
    return copy


def move(source, target, sems, index):
    copy = pltpu.make_async_copy(source, target, sems.at[index])
    copy.start()
    return copy


DMA = pltpu.SemaphoreType.DMA


def both(count):
    return [DMA((count,)), DMA((count,))]


def exchange(kernel, ident, out_shape, in_specs, out_specs, scratch, args, flops, sent):
    return pl.pallas_call(
        kernel,
        out_shape=out_shape,
        in_specs=in_specs,
        out_specs=out_specs,
        scratch_shapes=scratch,
        compiler_params=pltpu.CompilerParams(
            collective_id=ident, has_side_effects=True, vmem_limit_bytes=60 << 20
        ),
        cost_estimate=pl.CostEstimate(flops=flops, bytes_accessed=sent, transcendentals=0),
    )(*args)


def head_kernel(
    zc,
    group,
    t_ref,
    q_w,
    k_w,
    v_w,
    g_w,
    u_w,
    d_w,
    o_w,
    gain1,
    gain2,
    ng_ref,
    wg_ref,
    fg_ref,
    a_ref,
    og_ref,
    w_ref,
    f_ref,
    e_ref,
    wo_ref,
    rows,
    weights,
    packed,
    ls,
    w0,
    w1,
    n0,
    n1,
    f0,
    f1,
    z0,
    z1,
    b0,
    b1,
    s0,
    s1,
    o0,
    o1,
    p0,
    p1,
):
    me = Place(zc)
    chips = 4 * zc
    per = zc // group
    qw = group * HEAD_DIM
    width = t_ref.shape[1]
    met = greet([me.any_chip(k) for k in range(1, chips)] + [me.sibling()])
    first_gain, second_gain = column_of(low(gain1[...])), column_of(low(gain2[...]))
    for g in range(4):
        at = slice(g * qw, (g + 1) * qw)
        w_ref[g, :, :qw] = (first_gain * low(q_w[:, at])).astype(BF16)
        for pair in range(group // 2):
            at = lanes(g * group // 2 + pair)
            key, value = first_gain * low(k_w[:, at]), first_gain * low(v_w[:, at])
            for half in range(2):
                start = qw + (2 * pair + half) * PAIR
                w_ref[g, :, start : start + PAIR] = pair_up(key, half, value, half).astype(BF16)
    e_ref[...] = d_w[...].astype(BF16).reshape(e_ref.shape)
    wo_ref[...] = o_w[...].astype(BF16)
    x = t_ref[...].astype(F32)
    rows[0] = (x * lax.rsqrt(jnp.mean(x * x, axis=-1, keepdims=True) + EPS)).astype(BF16)
    met()
    here = og_ref.at[me.x, me.z, me.y, me.c]
    local = [move(w_ref.at[me.g], weights.at[me.chip, me.c], ls, 0), move(wo_ref, here, ls, 1)]
    pieces = []
    for k in reversed(range(1, chips)):
        there = me.any_chip(k)
        their_g = there[0] * 2 + there[2]
        pieces.append(
            send(w_ref.at[their_g], weights.at[me.chip, me.c], (w0, w1), k, there)
        )
    outs = [send(wo_ref, here, (o0, o1), k, me.line(k)) for k in range(1, zc)]
    blocks = [send(rows.at[0], rows.at[k], (n0, n1), k, me.plane(k)) for k in range(1, 4)]
    units = g_w.shape[1] // (4 * zc)
    for which, ref in enumerate((g_w, u_w)):
        for g in range(4):
            px, py = g // 2, g % 2
            if units % PAIR == 0:
                for z in range(zc):
                    at = ((px * zc + z) * 2 + py) * units
                    f_ref[g, which, :, z * units : (z + 1) * units] = (
                        second_gain * low(ref[:, at : at + units])
                    ).astype(BF16)
            else:
                for z in range(0, zc, 2):
                    near, far = (second_gain * low(ref[:, lanes(px * zc + i)]) for i in (z, z + 1))
                    f_ref[g, which, :, lanes(z // 2)] = pair_up(near, py, far, py).astype(BF16)
    wide = [
        move(f_ref.at[me.g], fg_ref.at[me.x, me.y, pl.ds(0, 2)], ls, 2),
        move(e_ref, fg_ref.at[:, :, 2], ls, 9),
    ]
    for k in range(1, 4):
        there = me.plane(k)
        their_g = there[0] * 2 + there[2]
        wide.append(
            send(f_ref.at[their_g], fg_ref.at[me.x, me.y, pl.ds(0, 2)], (f0, f1), k, there)
        )
    local[0].wait()
    for copy in pieces:
        copy.wait()
    relay = send(
        weights.at[:, me.c], weights.at[:, me.c], (s0, s1), 0, me.sibling()
    )
    relay.wait()
    kept = [move(weights, wg_ref, ls, 3)]

    def project(k, carry):
        @pl.when(k > 0)
        def _():
            trip(rows.at[0], rows.at[k], (n0, n1), k, me.plane(k)).wait_recv()

        at = (me.x ^ (k // 2)) * 2 + (me.y ^ (k % 2))
        out = dot(rows[k], weights[...].reshape(width, 3 * qw))
        for head in range(group):
            two, half = out[:, lanes(head // 2)], head % 2
            packed[head, k, :BLOCK] = pair_up(two[:BLOCK], half, two[BLOCK:], half).astype(BF16)
            start = qw + head * PAIR
            packed[head, k, BLOCK:] = out[:, start : start + PAIR].astype(BF16)
        for over in range(1, zc):
            trip(
                packed.at[(me.z ^ over) // per, k],
                a_ref.at[me.z, me.c, at],
                (z0, z1),
                k * zc + over,
                me.line(over),
            ).start()
        trip(
            packed.at[me.z // per, k], a_ref.at[me.z, me.c, at], (b0, b1), k * zc, me.sibling()
        ).start()
        pltpu.make_async_copy(
            packed.at[me.z // per, k], a_ref.at[me.z, me.c, at], ls.at[4 + k]
        ).start()
        return carry

    lax.fori_loop(0, 4, project, 0)
    kept.append(move(rows, ng_ref, ls, 8))
    for copy in outs + local[1:]:
        copy.wait()
    column = og_ref.at[me.x, :, me.y, me.c]
    out_rows = [send(column, column, (p0, p1), k, me.plane(k)) for k in range(1, 4)]

    def pass_on(step, carry):
        k, over = step // (zc - 1), step % (zc - 1) + 1
        at = (me.x ^ (k // 2)) * 2 + (me.y ^ (k % 2))
        there = me.z ^ over
        trip(
            packed.at[there // per, k],
            a_ref.at[me.z, me.c, at],
            (z0, z1),
            k * zc + over,
            me.line(over),
        ).wait()
        landed = a_ref.at[there, me.c, at]
        trip(landed, landed, (b0, b1), k * zc + over, me.sibling()).start()
        return carry

    lax.fori_loop(0, 4 * (zc - 1), pass_on, 0)
    for copy in out_rows:
        copy.wait()
    every = og_ref.at[:, :, :, me.c]
    last = send(every, every, (s0, s1), 1, me.sibling())

    def finish(step, carry):
        k, over = step // zc, step % zc
        at = (me.x ^ (k // 2)) * 2 + (me.y ^ (k % 2))
        landed = a_ref.at[me.z ^ over, me.c, at]
        trip(landed, landed, (b0, b1), k * zc + over, me.sibling()).wait()
        return carry

    lax.fori_loop(0, 4 * zc, finish, 0)
    for k in range(4):
        pltpu.make_async_copy(
            packed.at[me.z // per, k], a_ref.at[me.z, me.c, me.g], ls.at[4 + k]
        ).wait()
    for copy in [last] + kept + wide:
        copy.wait()
    for copy in blocks:
        copy.wait_send()


def head_exchange(zc, group, tokens, matrices, gains):
    chips = 4 * zc
    own, width = tokens.shape
    count = matrices[0].shape[0]
    piece = (count, 3 * group * HEAD_DIM)
    return exchange(
        functools.partial(head_kernel, zc, group),
        1,
        (
            struct((4, own, width)),
            struct((chips, 2) + piece),
            struct((2, 2, 3, count, width)),
            struct((zc, 2, 4, BLOCK + own, PAIR)),
            struct((2, zc, 2, 2, count, width)),
        ),
        [VM] * 10,
        (ANY,) * 5,
        [
            pltpu.VMEM((4,) + piece, BF16),
            pltpu.VMEM((4, 2, count, width), BF16),
            pltpu.VMEM((2, 2, count, width), BF16),
            pltpu.VMEM((count, width), BF16),
            pltpu.VMEM((4, own, width), BF16),
            pltpu.VMEM((chips, 2) + piece, BF16),
            pltpu.VMEM((group, 4, BLOCK + own, PAIR), BF16),
            DMA((10,)),
        ]
        + both(chips)
        + both(4)
        + both(4)
        + both(4 * zc)
        + both(4 * zc)
        + both(2)
        + both(zc)
        + both(4),
        (tokens, *matrices, *(g.reshape(1, -1) for g in gains)),
        2 * 4 * own * width * width,
        16 << 20,
    )


def join_kernel(zc, s_ref, x_ref, w_ref, ob_ref, r_ref, n_ref, mine, theirs, slabs, ls, b0, b1, c0, c1):
    me = Place(zc)
    chips = 4 * zc
    heads, per = slabs.shape[:2]
    greet([me.any_chip(k) for k in range(1, chips)] + [me.sibling()])()
    other = send(s_ref.at[:, 1 - me.c], theirs, (b0, b1), 0, me.sibling())
    own = move(s_ref.at[:, me.c], mine, ls, 0)
    own.wait()
    other.wait()
    mine[...] = mine[...] + theirs[...]
    head = me.g * (heads // 4) + me.z // per
    place = me.z % per
    keep = move(mine.at[me.z, me.g], slabs.at[head, place], ls, 1)
    sends = []
    for k in reversed(range(1, chips)):
        there = me.any_chip(k)
        their_g = there[0] * 2 + there[2]
        sends.append(
            send(mine.at[there[1], their_g], slabs.at[head, place], (c0, c1), k, there)
        )
    keep.wait()
    for copy in sends:
        copy.wait()
    for block in range(2):
        for pair in range(heads // 2):
            sides = []
            for side in range(2):
                slab = slabs[2 * pair + side, 0].astype(F32)
                for extra in range(1, per):
                    slab = slab + slabs[2 * pair + side, extra].astype(F32)
                sides.append(slab)
            ob_ref[block * BLOCK : (block + 1) * BLOCK, lanes(pair)] = pair_up(
                sides[0], block, sides[1], block
            ).astype(BF16)
    residual = x_ref[...].astype(F32) + dot(ob_ref[...], w_ref[...])
    r_ref[...] = residual
    mean = jnp.mean(residual * residual, axis=-1, keepdims=True)
    n_ref[...] = (residual * lax.rsqrt(mean + EPS)).astype(BF16)


def join_exchange(zc, heads, slabs, tokens, w_out):
    chips = 4 * zc
    per = 4 * zc // heads
    half = (zc,) + slabs.shape[2:]
    shape = tokens.shape
    return exchange(
        functools.partial(join_kernel, zc),
        2,
        (struct(shape), struct(shape, F32), struct(shape)),
        [ANY, VM, VM],
        (VM,) * 3,
        [
            pltpu.VMEM(half, BF16),
            pltpu.VMEM(half, BF16),
            pltpu.VMEM((heads, per) + slabs.shape[3:], BF16),
            DMA((2,)),
        ]
        + both(1)
        + both(chips),
        (slabs, tokens, w_out),
        0,
        0,
    )


def middle_kernel(zc, n_ref, ca_ref, cb_ref, cc_ref, cd_ref, *rest):
    f_refs, rest = rest[: zc // 2 + 1], rest[zc // 2 + 1 :]
    oa_ref, ob_ref, oc_ref, od_ref, cs_ref, sh_ref, rows, cots, gate_w, up_w, down_w, *rest = rest
    hid, dgate, dup, c_out, c_in, passed, stage, o_out, ls, n0, n1, c0, c1, f0, f1, h0, h1 = rest
    me = Place(zc)
    width = n_ref.shape[1]
    met = greet([me.plane(k) for k in range(1, 4)] + [me.line(1), me.sibling()])
    move(n_ref, rows.at[0], ls, 15).wait()
    met()
    farthest = send(rows.at[0], rows.at[3], (n0, n1), 3, me.plane(3))
    def places(there):
        return (
            gate_w.at[:, there, :, me.c],
            up_w.at[:, there, :, me.c],
            down_w.at[there, me.c],
        )

    given = dict(zip([1, *range(0, zc, 2)], f_refs))
    hops, loads = [], []
    for k in range(2, zc, 2):
        for i, place in enumerate(places(me.z ^ k)):
            hops.append(send(given[k].at[:, :, i], place, (h0, h1), 3 * k + i, me.line(1)))
    for k, ref in given.items():
        for i, place in enumerate(places(me.z ^ k)):
            loads.append(send(ref.at[:, :, i], place, (f0, f1), 3 * k + i, me.sibling()))
            loads.append(move(ref.at[:, :, i], place, ls, 21 + 3 * k + i))
    for k, ref in enumerate((ca_ref, cb_ref, cc_ref, cd_ref)):
        loads.append(move(ref, cots.at[k], ls, 16 + k))
    farthest.wait_send()
    near_rows = [send(rows.at[0], rows.at[k], (n0, n1), k, me.plane(k)) for k in (1, 2)]
    for copy in hops:
        copy.wait()
    for k in range(3, zc, 2):
        for i, place in enumerate(places(me.z ^ k)):
            loads.append(send(place, place, (f0, f1), 3 * k + i, me.sibling()))
    for copy in loads:
        copy.wait()
    square = (width, width)
    half = n_ref.shape[0] // 2
    upper, lower = pl.ds(0, half), pl.ds(half, half)
    c_sems = (c0, c1)
    far_parts = [
        trip(c_out.at[3, upper], passed.at[0], c_sems, 0, me.plane(2)),
        trip(c_out.at[3, lower], passed.at[1], c_sems, 1, me.plane(1)),
    ]
    near_parts = [
        trip(c_out.at[1, lower], c_in.at[0, lower], c_sems, 2, me.plane(1)),
        trip(c_out.at[2, upper], c_in.at[1, upper], c_sems, 3, me.plane(2)),
        trip(c_out.at[1, upper], c_in.at[0, upper], c_sems, 4, me.plane(1)),
        trip(c_out.at[2, lower], c_in.at[1, lower], c_sems, 5, me.plane(2)),
    ]

    def block(step, carry):
        k = jnp.where(step == 0, 3, jnp.where(step == 3, 0, step))

        @pl.when(step < 3)
        def _():
            trip(rows.at[0], rows.at[k], (n0, n1), k, me.plane(k)).wait_recv()

        gate_mat, up_mat = gate_w[...].reshape(square), up_w[...].reshape(square)
        gate = dot(rows[k], gate_mat)
        up = dot(rows[k], up_mat)
        back = nt_dot(cots[k], down_w[...].reshape(square))
        sig = jax.nn.sigmoid(gate)
        soft = gate * sig
        hid[k] = (soft * up).astype(BF16)
        dgate[k] = (back * up * sig * (1.0 + gate * (1.0 - sig))).astype(BF16)
        dup[k] = (back * soft).astype(BF16)
        c_out[k] = (nt_dot(dgate[k], gate_mat) + nt_dot(dup[k], up_mat)).astype(BF16)

        @pl.when(step == 0)
        def _():
            for copy in far_parts:
                copy.start()

        @pl.when(step == 1)
        def _():
            near_parts[0].start()

        @pl.when(step == 2)
        def _():
            near_parts[1].start()

        return carry

    lax.fori_loop(0, 4, block, 0)
    far_parts[0].wait_recv()
    c_out[1, upper] = c_out[1, upper] + passed[0]
    near_parts[2].start()
    far_parts[1].wait_recv()
    c_out[2, lower] = c_out[2, lower] + passed[1]
    near_parts[3].start()
    all_rows = (4 * n_ref.shape[0], width)

    def weight_grad(left, right, slot):
        chunk = 256
        for first in range(0, width, chunk):
            value = tn_dot(left[:, first : first + chunk], right).astype(BF16)
            stage[slot, first : first + chunk] = value

    shares = []
    piece = width // (8 * zc)

    def share(slot, which):
        parts = stage.at[slot].reshape(2, zc, 2, 2, piece, width)
        for g in range(4):
            x, y = g // 2, g % 2
            shares.append(
                move(parts.at[x, :, y], sh_ref.at[:, :, 2 * g + which], ls, 12 + 2 * g + which)
            )

    flat = lambda ref: ref[...].reshape(all_rows)
    weight_grad(flat(rows), flat(dgate), 0)
    share(0, 0)
    weight_grad(flat(rows), flat(dup), 1)
    share(1, 1)
    weight_grad(flat(hid), flat(cots), 2)
    shares.append(
        move(stage.at[2].reshape(zc, 2, 4, piece, width), sh_ref.at[:, :, 8:], ls, 20)
    )

    for k, ref in enumerate((oa_ref, ob_ref, oc_ref, od_ref)):
        o_out[k] = dot(hid[k], down_w[...].reshape(square)).astype(BF16).reshape(ref.shape)
        shares.append(move(o_out.at[k], ref, ls, k))
    for copy in far_parts:
        copy.wait_send()
    for copy in near_parts:
        copy.wait()
    cs_ref[...] = c_out[0].astype(F32) + c_in[0].astype(F32) + c_in[1].astype(F32)
    for copy in shares:
        copy.wait()
    for copy in near_rows:
        copy.wait_send()


def middle_exchange(zc, normed, cots, weights):
    own, width = normed.shape
    piece = width // (8 * zc)
    blocks = pltpu.VMEM((4, own, width), BF16)
    wide = pltpu.VMEM((2, zc, 2, 2, piece, width), BF16)
    return exchange(
        functools.partial(middle_kernel, zc),
        3,
        (
            *[struct((zc, 2, piece, width))] * 4,
            struct((own, width), F32),
            struct((zc, 2, 12, piece, width)),
        ),
        [ANY] * (5 + len(weights)),
        (ANY,) * 4 + (VM, ANY),
        [blocks, blocks, wide, wide, pltpu.VMEM((zc, 2, 2, 2, piece, width), BF16)]
        + [blocks] * 4
        + [pltpu.VMEM((2, own, width), BF16), pltpu.VMEM((2, own // 2, width), BF16)]
        + [pltpu.VMEM((3, width, width), BF16), pltpu.VMEM((4, zc, 2, piece, width), BF16), DMA((21 + 3 * zc,))]
        + both(4)
        + both(6)
        + both(3 * zc)
        + both(3 * zc),
        (normed, *cots, *weights),
        2 * 4 * own * width * width * 9,
        64 << 20,
    )


def turn_kernel(
    zc,
    c_ref,
    t_ref,
    r_ref,
    wo_ref,
    ob_ref,
    yb_ref,
    yc_ref,
    dr_ref,
    do_ref,
    va_ref,
    vb_ref,
    vc_ref,
    vd_ref,
    nb_ref,
    nc_ref,
    slabs,
    stage,
    wo_in,
    ob_in,
    ls,
    d0,
    d1,
    b0,
    b1,
    y0,
    y1,
):
    me = Place(zc)
    chips = 4 * zc
    heads = slabs.shape[0]
    group = heads // 4
    per = zc // group
    width = t_ref.shape[1]
    met = greet([me.any_chip(k) for k in range(1, chips)] + [me.sibling()])
    loads = [move(wo_ref, wo_in, ls, 5), move(ob_ref, ob_in, ls, 6)]
    total, residual = c_ref[...], r_ref[...]
    scaling = lax.rsqrt(jnp.mean(residual * residual, axis=-1, keepdims=True) + EPS)
    normed = residual * scaling
    middle = jnp.mean(total * normed, axis=-1, keepdims=True)
    grad = t_ref[...].astype(F32) + scaling * (total - normed * middle)
    dr_ref[...] = grad
    narrow = grad.astype(BF16)
    loads[0].wait()
    back = nt_dot(narrow, wo_in[...])
    for pair in range(heads // 2):
        two = back[:, lanes(pair)]
        for side in range(2):
            slabs[2 * pair + side] = pair_up(two[:BLOCK], side, two[BLOCK:], side).astype(BF16)
    met()
    to = do_ref.at[me.z, me.c, me.g]
    own = move(slabs.at[me.g * group + me.z // per], to, ls, 0)
    sends = []
    for k in reversed(range(1, chips)):
        there = me.any_chip(k)
        head = (there[0] * 2 + there[2]) * group + there[1] // per
        sends.append(send(slabs.at[head], to, (d0, d1), k, there))
    sends.append(send(yb_ref, nb_ref, (y0, y1), 1, me.plane(1)))
    sends.append(send(yc_ref, nc_ref, (y0, y1), 2, me.plane(2)))
    chunk = 256
    loads[1].wait()
    attended = ob_in[...]
    for first in range(0, width, chunk):
        stage[first : first + chunk] = tn_dot(attended[:, first : first + chunk], narrow).astype(BF16)
    parts = stage.reshape(2, zc, 2, 2, width // (8 * zc), width)
    keeps = []
    for k, ref in enumerate((va_ref, vb_ref, vc_ref, vd_ref)):
        there = me.plane(k)
        keeps.append(move(parts.at[there[0], :, there[2]], ref, ls, 1 + k))
    own.wait()
    for copy in sends[:-2]:
        copy.wait()
    half = do_ref.at[:, me.c]
    relay = send(half, half, (b0, b1), 0, me.sibling())
    for copy in keeps + sends[-2:]:
        copy.wait()
    relay.wait()


def turn_exchange(zc, c_sum, cotangent, residual, w_out, attn_rows, near):
    chips = 4 * zc
    own, width = cotangent.shape
    heads = width // HEAD_DIM
    return exchange(
        functools.partial(turn_kernel, zc),
        6,
        (
            struct((own, width), F32),
            struct((zc, 2, 4, BLOCK, PAIR)),
            *[struct((zc, 2, width // (8 * zc), width))] * 6,
        ),
        [VM] * 3 + [ANY] * 4,
        (VM,) + (ANY,) * 7,
        [
            pltpu.VMEM((heads, BLOCK, PAIR), BF16),
            pltpu.VMEM((width, width), BF16),
            pltpu.VMEM((width, width), BF16),
            pltpu.VMEM((own, width), BF16),
            DMA((7,)),
        ]
        + both(chips)
        + both(1)
        + both(3),
        (c_sum, cotangent, residual, w_out, attn_rows, *near),
        2 * 2 * own * width * width,
        8 << 20,
    )


def tail_kernel(
    zc,
    d_ref,
    n_any,
    w_any,
    x_any,
    g_any,
    f_ref,
    r_ref,
    ya_ref,
    yb_ref,
    yc_ref,
    yd_ref,
    va_ref,
    vb_ref,
    vc_ref,
    vd_ref,
    tg_ref,
    gw_ref,
    go_ref,
    gf_ref,
    out_ref,
    n_ref,
    w_ref,
    x_ref,
    g_ref,
    r_in,
    y_in,
    o_mine,
    o_theirs,
    o_land,
    mine,
    theirs,
    landed,
    grads,
    c_out,
    c_in,
    stage,
    other_w,
    ls,
    b0,
    b1,
    z0,
    z1,
    c0,
    c1,
    s0,
    s1,
    w0,
    w1,
    q0,
    q1,
    f0,
    f1,
):
    me = Place(zc)
    chips = 4 * zc
    group, per = landed.shape[:2]
    qw = group * HEAD_DIM
    greet([me.any_chip(k) for k in range(1, chips)] + [me.sibling()])()
    head, place = me.z // per, me.z % per

    def slot(k):
        return (me.x ^ (k // 2)) * 2 + (me.y ^ (k % 2))

    order = (3, 2, 1, 0)
    halves = []
    for k in order:
        halves.append(
            (
                send(d_ref.at[:, 1 - me.c, slot(k)], theirs.at[k], (b0, b1), k, me.sibling()),
                move(d_ref.at[:, me.c, slot(k)], mine.at[k], ls, k),
            )
        )
    given = ((w_any, w_ref), (n_any, n_ref), (g_any, g_ref), (x_any, x_ref))
    loads = [move(source, target, ls, 20 + i) for i, (source, target) in enumerate(given)]
    f_parts = [move(f_ref.at[pl.ds(2 * me.g, 2)], gf_ref.at[me.g], ls, 10)]
    for k in (3, 1, 2):
        there = me.plane(k)
        part = f_ref.at[pl.ds(2 * (there[0] * 2 + there[2]), 2)]
        f_parts.append(send(part, gf_ref.at[me.g], (f0, f1), k, there))
    out_parts = [move(r_ref, r_in, ls, 11)]
    for i, ref in enumerate((ya_ref, yb_ref, yc_ref, yd_ref)):
        out_parts.append(move(ref, y_in.at[i, 0], ls, 12 + i))
    for i, ref in enumerate((va_ref, vb_ref, vc_ref, vd_ref)):
        out_parts.append(move(ref, y_in.at[i, 1], ls, 16 + i))
    for k, (far, near) in zip(order, halves):
        near.wait()
        far.wait()
        mine[k] = mine[k] + theirs[k]
        for over in range(1, zc):
            send(
                mine.at[k, me.z ^ over],
                landed.at[head, place, k],
                (z0, z1),
                k * zc + over,
                me.line(over),
            )
        move(mine.at[k, me.z], landed.at[head, place, k], ls, 4 + k)

    for copy in out_parts + loads:
        copy.wait()
    final = r_in[...]
    o_sum = jnp.zeros(o_mine.shape, F32)
    for i in range(4):
        final = final + y_in[i, 0].astype(F32).reshape(final.shape)
        o_sum = o_sum + y_in[i, 1].astype(F32)
    out_ref[...] = final.astype(BF16)
    o_mine[...] = o_sum.astype(BF16)
    o_swap = send(o_mine.at[:, 1 - me.c], o_theirs, (s0, s1), 1, me.sibling())

    def block(step, carry):
        k = 3 - step
        pltpu.make_async_copy(
            mine.at[k, me.z], landed.at[head, place, k], ls.at[4 + k]
        ).wait()
        for over in range(1, zc):
            trip(
                mine.at[k, me.z ^ over],
                landed.at[head, place, k],
                (z0, z1),
                k * zc + over,
                me.line(over),
            ).wait()
        for pair in range(group // 2):
            sides = []
            for side in range(2):
                h = 2 * pair + side
                slab = landed[h, 0, k]
                for extra in range(1, per):
                    slab = slab + landed[h, extra, k]
                start = qw + h * PAIR
                grads[k, :, start : start + PAIR] = slab[BLOCK:]
                sides.append(slab[:BLOCK].astype(F32))
            for b in range(2):
                grads[k, b * BLOCK : (b + 1) * BLOCK, lanes(pair)] = pair_up(
                    sides[0], b, sides[1], b
                ).astype(BF16)

        @pl.when(k > 0)
        def _():
            c_out[k] = nt_dot(grads[k], w_ref[...]).astype(BF16)
            trip(c_out.at[k], c_in.at[k], (c0, c1), k, me.plane(k)).start()

        return carry

    o_swap.wait()
    o_theirs[...] = o_theirs[...] + o_mine[:, me.c]
    sends = [
        send(o_theirs.at[me.z ^ k], o_land.at[k], (q0, q1), k, me.line(k)) for k in range(1, zc)
    ]
    lax.fori_loop(0, 4, block, 0)
    width, cols = w_ref.shape
    all_rows = 4 * n_ref.shape[1]
    normed_all = n_ref[...].reshape(all_rows, width)
    grads_all = grads[...].reshape(all_rows, cols)
    piece = stage.shape[2]
    chunk = 256
    each = chunk // (2 * piece)
    swaps = []
    for first in range(0, width, chunk):
        value = tn_dot(normed_all[:, first : first + chunk], grads_all).astype(BF16)
        at = first // (2 * piece)
        stage[at : at + each] = value.reshape(each, 2, piece, cols)
        swaps.append(
            send(
                stage.at[at : at + each, 1 - me.c],
                other_w.at[at : at + each],
                (s0, s1),
                2 + first // chunk,
                me.sibling(),
            )
        )
    c_out[0] = nt_dot(grads[0], w_ref[...]).astype(BF16)
    for swap in swaps:
        swap.wait()

    def add(i, carry):
        other_w[i] = stage[i, me.c] + other_w[i]
        return carry

    lax.fori_loop(0, chips, add, 0)
    stay = move(other_w.at[me.chip], gw_ref.at[me.z, me.g], ls, 8)
    for k in reversed(range(1, chips)):
        there = me.any_chip(k)
        chip = (there[0] * zc + there[1]) * 2 + there[2]
        sends.append(send(other_w.at[chip], gw_ref.at[me.z, me.g], (w0, w1), k, there))
    total = c_out[0].astype(F32)
    for k in range(1, 4):
        trip(c_out.at[k], c_in.at[k], (c0, c1), k, me.plane(k)).wait()
        total = total + c_in[k].astype(F32)
    x = x_ref[...].astype(F32)
    scaling = lax.rsqrt(jnp.mean(x * x, axis=-1, keepdims=True) + EPS)
    normed = x * scaling
    middle = jnp.mean(total * normed, axis=-1, keepdims=True)
    tg_ref[...] = (g_ref[...] + scaling * (total - normed * middle)).astype(BF16)
    stay.wait()
    for copy in sends + f_parts:
        copy.wait()
    o_sum = o_theirs[me.z].astype(F32)
    for k in range(1, zc):
        o_sum = o_sum + o_land[k].astype(F32)
    go_ref[...] = o_sum


def tail_exchange(zc, group, slab_grads, n_all, weights, tokens, residual_grad, shares, residual, packs):
    chips = 4 * zc
    per = zc // group
    own, width = tokens.shape
    cols = weights.shape[1]
    slab = slab_grads.shape[3:]
    piece = width // (2 * chips)
    blocks = pltpu.VMEM((4, own, width), BF16)
    return exchange(
        functools.partial(tail_kernel, zc),
        4,
        (
            struct((own, width)),
            struct((zc, 4, piece, cols)),
            struct((piece, width), F32),
            struct((4, 2, piece, width)),
            struct((own, width)),
        ),
        [ANY] * 15,
        (VM, ANY, VM, ANY, VM),
        [
            pltpu.VMEM((4, own, width), BF16),
            pltpu.VMEM((width, cols), BF16),
            pltpu.VMEM((own, width), BF16),
            pltpu.VMEM((own, width), F32),
            pltpu.VMEM((own, width), F32),
            pltpu.VMEM((4, 2, zc, 2, piece, width), BF16),
            pltpu.VMEM((zc, 2, piece, width), BF16),
            pltpu.VMEM((zc, piece, width), BF16),
            pltpu.VMEM((zc, piece, width), BF16),
            pltpu.VMEM((4, zc) + slab, BF16),
            pltpu.VMEM((4, zc) + slab, BF16),
            pltpu.VMEM((group, per, 4) + slab, BF16),
            pltpu.VMEM((4, own, cols), BF16),
            blocks,
            blocks,
            pltpu.VMEM((chips, 2, piece, cols), BF16),
            pltpu.VMEM((chips, piece, cols), BF16),
            DMA((24,)),
        ]
        + both(4)
        + both(4 * zc)
        + both(4)
        + both(2 + width // 256)
        + both(chips)
        + both(zc)
        + both(4),
        (slab_grads, n_all, weights, tokens, residual_grad, shares, residual, *packs),
        2 * 4 * own * width * cols * 2,
        24 << 20,
    )


def last_kernel(
    zc,
    group,
    t_any,
    o_any,
    wo_any,
    gw_any,
    gf_any,
    ds_any,
    q_any,
    k_any,
    v_any,
    g_any,
    u_any,
    gain1,
    gain2,
    tg_ref,
    out_ref,
    go_ref,
    g1_ref,
    q_ref,
    k_ref,
    v_ref,
    g2_ref,
    g_ref,
    u_ref,
    d_ref,
    gw_ref,
    gf_ref,
    ds_ref,
    q_w,
    k_w,
    v_w,
    g_w,
    u_w,
    ls,
):
    given = (gw_any, q_any, k_any, v_any, gf_any, g_any, u_any, ds_any, t_any, o_any, wo_any)
    taken = (gw_ref, q_w, k_w, v_w, gf_ref, g_w, u_w, ds_ref, tg_ref, out_ref, go_ref)
    copies = [move(a, b, ls, i) for i, (a, b) in enumerate(zip(given, taken))]
    for copy in copies:
        copy.wait()
    d_ref[...] = ds_ref[8:].astype(F32).reshape(d_ref.shape)
    first_gain, second_gain = column_of(low(gain1[...])), column_of(low(gain2[...]))
    count = q_w.shape[0]
    qw = group * HEAD_DIM
    score = jnp.zeros((count, PAIR), F32)
    for g in range(4):
        raw = gw_ref[0, g].astype(F32)
        for z in range(1, zc):
            raw = raw + gw_ref[z, g].astype(F32)
        for pair in range(group // 2):
            at = lanes(g * group // 2 + pair)
            start = qw + 2 * pair * PAIR
            even, odd = raw[:, start : start + PAIR], raw[:, start + PAIR : start + 2 * PAIR]
            query = raw[:, lanes(pair)]
            key, value = pair_up(even, 0, odd, 0), pair_up(even, 1, odd, 1)
            score = score + query * low(q_w[:, at]) + key * low(k_w[:, at]) + value * low(v_w[:, at])
            q_ref[:, at] = first_gain * query
            k_ref[:, at] = first_gain * key
            v_ref[:, at] = first_gain * value
    g1_ref[...] = row_of(jnp.sum(score, axis=1, keepdims=True))
    units = g_w.shape[1] // (4 * zc)
    score = jnp.zeros((count, PAIR), F32)
    for which, (weight, target) in enumerate(((g_w, g_ref), (u_w, u_ref))):
        for chunk in range(weight.shape[1] // PAIR):
            if units % PAIR == 0:
                owner, piece = divmod(chunk, units // PAIR)
                x, z, y = owner // (2 * zc), owner // 2 % zc, owner % 2
                raw = gf_ref[2 * x + y, which, :, lanes(z * units // PAIR + piece)].astype(F32)
            else:
                x, z = chunk // zc, chunk % zc
                near = gf_ref[2 * x, which, :, lanes(z // 2)].astype(F32)
                far = gf_ref[2 * x + 1, which, :, lanes(z // 2)].astype(F32)
                raw = pair_up(near, z % 2, far, z % 2)
            score = score + raw * low(weight[:, lanes(chunk)])
            target[:, lanes(chunk)] = second_gain * raw
    g2_ref[...] = row_of(jnp.sum(score, axis=1, keepdims=True))


def last_step(zc, group, tokens_grad, output, out_share, w_all, f_all, shares, matrices, gains):
    own, width = output.shape
    count, hidden = matrices[3].shape
    return pl.pallas_call(
        functools.partial(last_kernel, zc, group),
        out_shape=(
            struct((own, width)),
            struct((own, width)),
            struct((count, width), F32),
            struct((1, count), F32),
            struct((count, width), F32),
            struct((count, width), F32),
            struct((count, width), F32),
            struct((1, count), F32),
            struct((count, hidden), F32),
            struct((count, hidden), F32),
            struct((4 * count, width), F32),
        ),
        in_specs=[ANY] * 11 + [VM] * 2,
        out_specs=(VM,) * 11,
        scratch_shapes=[
            pltpu.VMEM(v.shape, v.dtype) for v in (w_all, f_all, shares, *matrices)
        ]
        + [DMA((11,))],
        compiler_params=pltpu.CompilerParams(vmem_limit_bytes=60 << 20),
    )(
        tokens_grad,
        output,
        out_share,
        w_all,
        f_all,
        shares,
        *matrices,
        *(g.reshape(1, -1) for g in gains),
    )


def segment_start(position, lens_ref):
    start = jnp.zeros_like(position)
    end = 0
    for j in range(lens_ref.shape[0]):
        end = end + lens_ref[j]
        start = jnp.where(position >= end, end, start)
    return start


def note_tiles(workers, worker, tiles, lens_ref, mine):
    turns = tiles // workers

    def snake(turn, carry):
        forward = turn * workers + worker
        backward = turn * workers + workers - 1 - worker
        mine[turn] = jnp.where((turn & 1) == 0, forward, backward)
        return carry

    def weigh(step, ahead):
        turn = turns - 1 - step
        loads = []
        for tile in (2 * turn, 2 * turn + 1):
            first, _, _, last = key_bounds(tile * QTILE, lens_ref)
            loads.append(last - first)
        lighter_first = loads[0] <= loads[1]
        first_to_zero = jnp.where(ahead > 0, lighter_first, loads[0] > loads[1])
        mine[turn] = 2 * turn + jnp.where(first_to_zero, worker, 1 - worker)
        return ahead + jnp.where(first_to_zero, loads[0] - loads[1], loads[1] - loads[0])

    if workers == 2:
        lax.fori_loop(0, turns, weigh, 0)
    else:
        lax.fori_loop(0, turns, snake, 0)


def key_bounds(first, lens_ref):
    low_start = segment_start(first, lens_ref)
    high_start = segment_start(first + QTILE - 1, lens_ref)
    low = low_start // KTILE
    high = (first + QTILE + KTILE - 1) // KTILE
    plain = jnp.clip((high_start + KTILE - 1) // KTILE, low, high)
    stop = jnp.clip((first + 1) // KTILE, plain, high)
    return low, plain, stop, high


def visible(first, tile, starts):
    key = tile * KTILE + lax.broadcasted_iota(jnp.int32, (KTILE, QTILE), 0)
    query = first + lax.broadcasted_iota(jnp.int32, (KTILE, QTILE), 1)
    return (key <= query) & (key >= starts)


def note_places(anchor_ref, inv):
    def note(i, carry):
        inv[anchor_ref[i]] = i
        return carry

    lax.fori_loop(0, anchor_ref.shape[0], note, 0)


def half_lanes(rows, half):
    lane = lax.broadcasted_iota(jnp.int32, rows.shape, 1)
    return jnp.where((lane // HEAD_DIM) == half, rows, jnp.zeros_like(rows))


def fold(rows, columns, first):
    row = lax.broadcasted_iota(jnp.int32, (rows, columns), 0)
    column = lax.broadcasted_iota(jnp.int32, (rows, columns), 1)
    return (row % HEAD_DIM == column - first).astype(F32).astype(BF16)


def unfold(rows, columns, first):
    row = lax.broadcasted_iota(jnp.int32, (rows, columns), 0)
    column = lax.broadcasted_iota(jnp.int32, (rows, columns), 1)
    return (column % HEAD_DIM == row - first).astype(F32).astype(BF16)


def forward_kernel(
    workers, anchor_ref, lens_ref, who_ref, a_ref, o_ref, kv_ref, kvt_ref, q_ref, qt_ref, ot_ref, l_ref, inv, mine, raw
):
    blocks = anchor_ref.shape[0]
    turns = qt_ref.shape[0]
    per = QTILE // BLOCK
    worker = who_ref[0]
    note_places(anchor_ref, inv)
    note_tiles(workers, worker, turns * workers, lens_ref, mine)
    o_ref[...] = jnp.zeros_like(o_ref)
    same = selection(PAIR, PAIR, 0)

    def order(step, carry):
        for b in range(per):
            i = step * per + b
            where = inv[i]
            slab, half = where >> 1, where & 1
            at = pl.ds(pl.multiple_of(i * BLOCK, BLOCK), BLOCK)
            kv_ref[at, :] = a_ref[slab, pl.ds(pl.multiple_of(BLOCK + half * BLOCK, BLOCK), BLOCK), :]
        return carry

    lax.fori_loop(0, blocks // per, order, 0)

    def flip(step, carry):
        at = pl.ds(pl.multiple_of(step * TURNED, TURNED), TURNED)
        kvt_ref[:, at] = nt_dot(same, kv_ref[at, :]).astype(BF16)
        return carry

    lax.fori_loop(0, blocks * BLOCK // TURNED, flip, 0)

    def one_tile(turn, carry):
        tile = mine[turn]
        first = tile * QTILE
        for b in range(per):
            where = inv[tile * per + b]
            raw[b * BLOCK : (b + 1) * BLOCK, :] = half_lanes(a_ref[where >> 1, :BLOCK, :], where & 1)
        q_ref[turn] = (dot(raw[...], fold(PAIR, PAIR, 0)) * 0.125).astype(BF16)
        qt_ref[turn] = (nt_dot(unfold(PAIR, PAIR, 0), raw[...]) * 0.125).astype(BF16)
        query = qt_ref[turn]
        starts = segment_start(first + lax.broadcasted_iota(jnp.int32, (1, QTILE), 1), lens_ref)
        low, plain, stop, high = key_bounds(first, lens_ref)

        def step(masked, kt, state):
            top, total, acc = state
            at = pl.ds(pl.multiple_of(kt * KTILE, KTILE), KTILE)
            scores = dot(kv_ref[at, :], query)
            if masked:
                scores = jnp.where(visible(first, kt, starts), scores, MASKED)
            new_top = jnp.maximum(top, jnp.max(scores, axis=0, keepdims=True))
            factor = jnp.exp(top - new_top)
            weights = jnp.exp(scores - new_top)
            total = total * factor + jnp.sum(weights, axis=0, keepdims=True)
            acc = acc * factor + dot(kvt_ref[HEAD_DIM:, at], weights.astype(BF16))
            return (new_top, total, acc)

        state = (
            jnp.full((1, QTILE), LOWEST, F32),
            jnp.zeros((1, QTILE), F32),
            jnp.zeros((HEAD_DIM, QTILE), F32),
        )
        state = lax.fori_loop(low, plain, functools.partial(step, True), state)
        state = lax.fori_loop(plain, stop, functools.partial(step, False), state)
        top, total, acc = lax.fori_loop(stop, high, functools.partial(step, True), state)
        out = acc / total
        ot_ref[turn] = out
        l_ref[turn] = top + jnp.log(total)
        wide = tn_dot(out.astype(BF16), unfold(HEAD_DIM, PAIR, 0)).astype(BF16)
        for b in range(per):
            where = inv[tile * per + b]
            slab = where >> 1
            o_ref[slab] = o_ref[slab] + half_lanes(wide[b * BLOCK : (b + 1) * BLOCK], where & 1)
        return carry

    lax.fori_loop(0, turns, one_tile, 0)


def attention_forward(workers, anchors, lengths, who, packed):
    slabs = packed.shape[0]
    rows = slabs * 2 * BLOCK
    turns = rows // QTILE // workers
    return pl.pallas_call(
        functools.partial(forward_kernel, workers),
        out_shape=(
            struct((slabs, BLOCK, PAIR)),
            struct((rows, PAIR)),
            struct((PAIR, rows)),
            struct((turns, QTILE, PAIR)),
            struct((turns, PAIR, QTILE)),
            struct((turns, HEAD_DIM, QTILE), F32),
            struct((turns, 1, QTILE), F32),
        ),
        in_specs=[SM, SM, SM, VM],
        out_specs=(VM,) * 7,
        scratch_shapes=[
            pltpu.SMEM((2 * slabs,), jnp.int32),
            pltpu.SMEM((turns,), jnp.int32),
            pltpu.VMEM((QTILE, PAIR), BF16),
        ],
        compiler_params=pltpu.CompilerParams(vmem_limit_bytes=60 << 20),
        cost_estimate=pl.CostEstimate(
            flops=rows * rows * 64, bytes_accessed=rows * 1024, transcendentals=rows * rows // 8
        ),
    )(anchors, lengths, who, packed)


def backward_kernel(
    workers,
    anchor_ref,
    lens_ref,
    who_ref,
    d_ref,
    kv_ref,
    kvt_ref,
    q_ref,
    qt_ref,
    ot_ref,
    l_ref,
    g_ref,
    inv,
    mine,
    raw,
    both_rows,
    dt,
    acc,
):
    blocks = anchor_ref.shape[0]
    turns = qt_ref.shape[0]
    per = QTILE // BLOCK
    worker = who_ref[0]
    note_places(anchor_ref, inv)
    note_tiles(workers, worker, turns * workers, lens_ref, mine)
    acc[...] = jnp.zeros_like(acc)
    g_ref[:, :BLOCK, :] = jnp.zeros((g_ref.shape[0], BLOCK, PAIR), BF16)

    def one_tile(turn, carry):
        tile = mine[turn]
        first = tile * QTILE
        for b in range(per):
            where = inv[tile * per + b]
            raw[b * BLOCK : (b + 1) * BLOCK, :] = half_lanes(d_ref[where >> 1], where & 1)
        both_rows[:QTILE] = q_ref[turn]
        both_rows[QTILE:] = dot(raw[...], fold(PAIR, PAIR, HEAD_DIM)).astype(BF16)
        dt[...] = nt_dot(unfold(PAIR, PAIR, HEAD_DIM), raw[...]).astype(BF16)
        query, grad = qt_ref[turn], dt[...]
        norm = l_ref[turn]
        delta = jnp.sum(grad[HEAD_DIM:].astype(F32) * ot_ref[turn], axis=0, keepdims=True)
        starts = segment_start(first + lax.broadcasted_iota(jnp.int32, (1, QTILE), 1), lens_ref)
        low, plain, stop, high = key_bounds(first, lens_ref)

        def step(masked, kt, total):
            at = pl.ds(pl.multiple_of(kt * KTILE, KTILE), KTILE)
            keys = kv_ref[at, :]
            scores = dot(keys, query)
            if masked:
                scores = jnp.where(visible(first, kt, starts), scores, MASKED)
            weights = jnp.exp(scores - norm)
            score_grad = (weights * (dot(keys, grad) - delta)).astype(BF16)
            both_grads = jnp.concatenate([score_grad, weights.astype(BF16)], axis=1)
            acc[at, :] += dot(both_grads, both_rows[...])
            return total + dot(kvt_ref[:HEAD_DIM, at], score_grad)

        total = jnp.zeros((HEAD_DIM, QTILE), F32)
        total = lax.fori_loop(low, plain, functools.partial(step, True), total)
        total = lax.fori_loop(plain, stop, functools.partial(step, False), total)
        total = lax.fori_loop(stop, high, functools.partial(step, True), total)
        wide = tn_dot((total * 0.125).astype(BF16), unfold(HEAD_DIM, PAIR, 0)).astype(BF16)
        for b in range(per):
            where = inv[tile * per + b]
            slab = where >> 1
            g_ref[slab, :BLOCK] = g_ref[slab, :BLOCK] + half_lanes(
                wide[b * BLOCK : (b + 1) * BLOCK], where & 1
            )
        return carry

    lax.fori_loop(0, turns, one_tile, 0)

    def place(step, carry):
        for b in range(per):
            i = step * per + b
            where = inv[i]
            slab, half = where >> 1, where & 1
            at = pl.ds(pl.multiple_of(i * BLOCK, BLOCK), BLOCK)
            to = pl.ds(pl.multiple_of(BLOCK + half * BLOCK, BLOCK), BLOCK)
            g_ref[slab, to, :] = acc[at, :].astype(BF16)
        return carry

    lax.fori_loop(0, blocks // per, place, 0)


def attention_backward(workers, anchors, lengths, who, grads, kept):
    slabs = grads.shape[0]
    rows = slabs * 2 * BLOCK
    return pl.pallas_call(
        functools.partial(backward_kernel, workers),
        out_shape=struct((slabs, 3 * BLOCK, PAIR)),
        in_specs=[SM, SM, SM] + [VM] * 7,
        out_specs=VM,
        scratch_shapes=[
            pltpu.SMEM((2 * slabs,), jnp.int32),
            pltpu.SMEM((rows // QTILE // workers,), jnp.int32),
            pltpu.VMEM((QTILE, PAIR), BF16),
            pltpu.VMEM((2 * QTILE, PAIR), BF16),
            pltpu.VMEM((PAIR, QTILE), BF16),
            pltpu.VMEM((rows, PAIR), F32),
        ],
        compiler_params=pltpu.CompilerParams(vmem_limit_bytes=60 << 20),
        cost_estimate=pl.CostEstimate(
            flops=rows * rows * 160, bytes_accessed=rows * 1024, transcendentals=rows * rows // 8
        ),
    )(anchors, lengths, who, grads, *kept)


def around(value, k):
    return lax.ppermute(value, ("head", "y"), [(i, i ^ k) for i in range(4)])


def along(value, k):
    return lax.ppermute(value, "z", [(i, i ^ k) for i in range(lax.axis_size("z"))])


def doubling(pieces, first, last):
    while first >= last:
        pieces = {**pieces, **{k + first: along(pieces[k], first) for k in pieces}}
        first //= 2
    return pieces


def body(
    zc,
    tokens,
    cotangent,
    norm1_gain,
    w_query,
    w_key,
    w_value,
    w_out,
    norm2_gain,
    w_gate,
    w_up,
    w_down,
    block_anchor,
    seq_lengths,
):
    width = tokens.shape[1]
    heads = width // HEAD_DIM
    group = heads // 4
    per_head = zc // group
    workers = 2 * per_head
    feature_rows = w_query.shape[0]

    n1_all, qkv_w, ffn_own, by_head, out_mat = head_exchange(
        zc,
        group,
        tokens,
        (w_query, w_key, w_value, w_gate, w_up, w_down, w_out),
        (norm1_gain, norm2_gain),
    )
    qkv_w = qkv_w.reshape(width, 3 * group * HEAD_DIM)

    out_mat, sent = lax.optimization_barrier((out_mat.reshape(width, width), cotangent))
    cots = [cotangent] + [around(sent, k) for k in range(1, 4)]
    ffn_parts = doubling({0: ffn_own}, zc // 2, 2)
    close = along(ffn_own, 1)

    anchors = jnp.transpose(block_anchor.reshape(2, zc, 2, 2, 2), (1, 3, 0, 2, 4)).reshape(-1)
    who = ((lax.axis_index("z") % per_head) * 2 + lax.axis_index("core")).astype(jnp.int32).reshape(1)
    slab_count = zc * 8
    o_slabs, *kept = attention_forward(
        workers, anchors, seq_lengths, who, by_head.reshape((slab_count,) + by_head.shape[3:])
    )
    attn_rows, residual, normed_two = join_exchange(
        zc, heads, o_slabs.reshape(zc, 2, 4, BLOCK, PAIR), tokens, out_mat
    )
    *out_parts, c_sum, shares = middle_exchange(
        zc, normed_two, cots, [close] + [ffn_parts[k] for k in range(0, zc, 2)]
    )
    shares = lax.psum_scatter(
        shares.reshape(zc * 2 * 12, feature_rows, width), ("z", "core"), scatter_dimension=0, tiled=True
    )
    residual_grad, do_heads, *packs = turn_exchange(
        zc, c_sum, cotangent, residual, out_mat, attn_rows, out_parts[1:3]
    )
    w_grads, near = packs[:4], packs[4:]
    do_heads, far = lax.optimization_barrier((do_heads, out_parts[3]))
    packs = [out_parts[0], *near, around(far, 3), w_grads[0]]
    packs += [around(w_grads[k], k) for k in range(1, 4)]
    grad_heads = attention_backward(
        workers, anchors, seq_lengths, who, do_heads.reshape(slab_count, BLOCK, PAIR), kept
    )
    tokens_grad, w_all, out_share, f_all, output = tail_exchange(
        zc,
        group,
        grad_heads.reshape(zc, 2, 4, 3 * BLOCK, PAIR),
        n1_all,
        qkv_w,
        tokens,
        residual_grad,
        shares,
        residual,
        packs,
    )
    (
        tokens_grad,
        output,
        out_grad,
        gain1_grad,
        query_grad,
        key_grad,
        value_grad,
        gain2_grad,
        gate_grad,
        up_grad,
        down_grad,
    ) = last_step(
        zc,
        group,
        tokens_grad,
        output,
        out_share,
        w_all,
        f_all,
        shares,
        (w_query, w_key, w_value, w_gate, w_up),
        (norm1_gain, norm2_gain),
    )
    return (
        output,
        tokens_grad,
        gain1_grad.reshape(-1),
        query_grad,
        key_grad,
        value_grad,
        out_grad,
        gain2_grad.reshape(-1),
        gate_grad,
        up_grad,
        down_grad,
    )


def solution(mesh):
    blk = mesh.shape["blk"]
    grid = Mesh(mesh.devices.reshape(mesh.shape["head"], blk // 4, 2, 2), AXES)
    rows, vector, whole = P(AXES, None), P(AXES), P()
    return jax.shard_map(
        functools.partial(body, blk // 4),
        mesh=grid,
        in_specs=(rows, rows, vector, rows, rows, rows, rows, vector, rows, rows, rows, whole, whole),
        out_specs=(rows, rows, vector, rows, rows, rows, rows, vector, rows, rows, rows),
        check_vma=False,
    )
```

```python
import functools

import jax
import jax.numpy as jnp
from jax import lax
from jax.experimental import pallas as pl
from jax.experimental.pallas import tpu as pltpu
from jax.sharding import Mesh
from jax.sharding import PartitionSpec as P

HEAD_DIM = 64
BLOCK = 128
PAIR = 128
EPS = 1e-06
MASKED = -1e30
LOWEST = -1e20
QTILE = 512
KTILE = 512
TURNED = 2048
AXES = ("head", "z", "y", "core")
IDS = pl.DeviceIdType.MESH
F32 = jnp.float32
BF16 = jnp.bfloat16
ANY = pl.BlockSpec(memory_space=pl.ANY)
VM = pl.BlockSpec(memory_space=pltpu.VMEM)
SM = pl.BlockSpec(memory_space=pltpu.SMEM)


def struct(shape, dtype=BF16):
    return jax.ShapeDtypeStruct(tuple(shape), dtype)


def nt_dot(a, b):
    return lax.dot_general(a, b, (((1,), (1,)), ((), ())), preferred_element_type=F32)


def tn_dot(a, b):
    return lax.dot_general(a, b, (((0,), (0,)), ((), ())), preferred_element_type=F32)


def dot(a, b):
    return jnp.dot(a, b, preferred_element_type=F32)


def selection(rows, columns, shift, first=0, last=None):
    last = columns if last is None else last
    row = lax.broadcasted_iota(jnp.int32, (rows, columns), 0)
    column = lax.broadcasted_iota(jnp.int32, (rows, columns), 1)
    hit = (row == column + shift) & (column >= first) & (column < last)
    return hit.astype(F32).astype(BF16)


def pair_up(first, first_half, second, second_half):
    lane = lax.broadcasted_iota(jnp.int32, first.shape, 1)
    left = first if first_half == 0 else pltpu.roll(first, HEAD_DIM, 1)
    right = second if second_half == 1 else pltpu.roll(second, HEAD_DIM, 1)
    return jnp.where(lane < HEAD_DIM, left, right)


def column_of(row):
    count = row.shape[1]
    i = lax.broadcasted_iota(jnp.int32, (count, count), 0)
    j = lax.broadcasted_iota(jnp.int32, (count, count), 1)
    return jnp.sum(jnp.where(i == j, row, 0.0), axis=1, keepdims=True)


def row_of(column):
    count = column.shape[0]
    i = lax.broadcasted_iota(jnp.int32, (count, count), 0)
    j = lax.broadcasted_iota(jnp.int32, (count, count), 1)
    return jnp.sum(jnp.where(i == j, column, 0.0), axis=0, keepdims=True)


def low(value):
    return value.astype(BF16).astype(F32)


def lanes(index):
    return slice(index * PAIR, (index + 1) * PAIR)


class Place:
    def __init__(self, z_count):
        self.x, self.z, self.y, self.c = (lax.axis_index(a) for a in AXES)
        self.g = self.x * 2 + self.y
        self.chip = (self.x * z_count + self.z) * 2 + self.y

    def sibling(self):
        return (self.x, self.z, self.y, 1 - self.c)

    def plane(self, k):
        return (self.x ^ (k // 2), self.z, self.y ^ (k % 2), self.c)

    def line(self, k):
        return (self.x, self.z ^ k, self.y, self.c)

    def any_chip(self, k):
        return (self.x ^ (k // 2 % 2), self.z ^ (k // 4), self.y ^ (k % 2), self.c)


def greet(peers):
    barrier = pltpu.get_barrier_semaphore()
    for peer in peers:
        pl.semaphore_signal(barrier, inc=1, device_id=peer, device_id_type=IDS)
    return lambda: pl.semaphore_wait(barrier, len(peers))


def trip(source, target, sems, index, device):
    return pltpu.make_async_remote_copy(
        src_ref=source,
        dst_ref=target,
        send_sem=sems[0].at[index],
        recv_sem=sems[1].at[index],
        device_id=device,
        device_id_type=IDS,
    )


def send(*given):
    copy = trip(*given)
    copy.start()
    return copy


def move(source, target, sems, index):
    copy = pltpu.make_async_copy(source, target, sems.at[index])
    copy.start()
    return copy


DMA = pltpu.SemaphoreType.DMA


def both(count):
    return [DMA((count,)), DMA((count,))]


def exchange(kernel, ident, out_shape, in_specs, out_specs, scratch, args, flops, sent):
    return pl.pallas_call(
        kernel,
        out_shape=out_shape,
        in_specs=in_specs,
        out_specs=out_specs,
        scratch_shapes=scratch,
        compiler_params=pltpu.CompilerParams(
            collective_id=ident, has_side_effects=True, vmem_limit_bytes=60 << 20
        ),
        cost_estimate=pl.CostEstimate(flops=flops, bytes_accessed=sent, transcendentals=0),
    )(*args)


def head_kernel(
    zc,
    group,
    t_ref,
    q_w,
    k_w,
    v_w,
    g_w,
    u_w,
    d_w,
    o_w,
    gain1,
    gain2,
    ng_ref,
    wg_ref,
    fg_ref,
    a_ref,
    og_ref,
    w_ref,
    f_ref,
    e_ref,
    wo_ref,
    rows,
    weights,
    packed,
    ls,
    w0,
    w1,
    n0,
    n1,
    f0,
    f1,
    z0,
    z1,
    b0,
    b1,
    s0,
    s1,
    o0,
    o1,
    p0,
    p1,
):
    me = Place(zc)
    chips = 4 * zc
    per = zc // group
    qw = group * HEAD_DIM
    width = t_ref.shape[1]
    met = greet([me.any_chip(k) for k in range(1, chips)] + [me.sibling()])
    first_gain, second_gain = column_of(low(gain1[...])), column_of(low(gain2[...]))
    for g in range(4):
        at = slice(g * qw, (g + 1) * qw)
        w_ref[g, :, :qw] = (first_gain * low(q_w[:, at])).astype(BF16)
        for pair in range(group // 2):
            at = lanes(g * group // 2 + pair)
            key, value = first_gain * low(k_w[:, at]), first_gain * low(v_w[:, at])
            for half in range(2):
                start = qw + (2 * pair + half) * PAIR
                w_ref[g, :, start : start + PAIR] = pair_up(key, half, value, half).astype(BF16)
    e_ref[...] = d_w[...].astype(BF16).reshape(e_ref.shape)
    wo_ref[...] = o_w[...].astype(BF16)
    x = t_ref[...].astype(F32)
    rows[0] = (x * lax.rsqrt(jnp.mean(x * x, axis=-1, keepdims=True) + EPS)).astype(BF16)
    met()
    here = og_ref.at[me.x, me.z, me.y, me.c]
    local = [move(w_ref.at[me.g], weights.at[me.chip, me.c], ls, 0), move(wo_ref, here, ls, 1)]
    pieces = []
    for k in reversed(range(1, chips)):
        there = me.any_chip(k)
        their_g = there[0] * 2 + there[2]
        pieces.append(
            send(w_ref.at[their_g], weights.at[me.chip, me.c], (w0, w1), k, there)
        )
    outs = [send(wo_ref, here, (o0, o1), k, me.line(k)) for k in range(1, zc)]
    blocks = [send(rows.at[0], rows.at[k], (n0, n1), k, me.plane(k)) for k in range(1, 4)]
    units = g_w.shape[1] // (4 * zc)
    for which, ref in enumerate((g_w, u_w)):
        for g in range(4):
            px, py = g // 2, g % 2
            if units % PAIR == 0:
                for z in range(zc):
                    at = ((px * zc + z) * 2 + py) * units
                    f_ref[g, which, :, z * units : (z + 1) * units] = (
                        second_gain * low(ref[:, at : at + units])
                    ).astype(BF16)
            else:
                for z in range(0, zc, 2):
                    near, far = (second_gain * low(ref[:, lanes(px * zc + i)]) for i in (z, z + 1))
                    f_ref[g, which, :, lanes(z // 2)] = pair_up(near, py, far, py).astype(BF16)
    wide = [
        move(f_ref.at[me.g], fg_ref.at[me.x, me.y, pl.ds(0, 2)], ls, 2),
        move(e_ref, fg_ref.at[:, :, 2], ls, 9),
    ]
    for k in range(1, 4):
        there = me.plane(k)
        their_g = there[0] * 2 + there[2]
        wide.append(
            send(f_ref.at[their_g], fg_ref.at[me.x, me.y, pl.ds(0, 2)], (f0, f1), k, there)
        )
    local[0].wait()
    for copy in pieces:
        copy.wait()
    relay = send(
        weights.at[:, me.c], weights.at[:, me.c], (s0, s1), 0, me.sibling()
    )
    relay.wait()
    kept = [move(weights, wg_ref, ls, 3)]

    def project(k, carry):
        @pl.when(k > 0)
        def _():
            trip(rows.at[0], rows.at[k], (n0, n1), k, me.plane(k)).wait_recv()

        at = (me.x ^ (k // 2)) * 2 + (me.y ^ (k % 2))
        out = dot(rows[k], weights[...].reshape(width, 3 * qw))
        for head in range(group):
            two, half = out[:, lanes(head // 2)], head % 2
            packed[head, k, :BLOCK] = pair_up(two[:BLOCK], half, two[BLOCK:], half).astype(BF16)
            start = qw + head * PAIR
            packed[head, k, BLOCK:] = out[:, start : start + PAIR].astype(BF16)
        for over in range(1, zc):
            trip(
                packed.at[(me.z ^ over) // per, k],
                a_ref.at[me.z, me.c, at],
                (z0, z1),
                k * zc + over,
                me.line(over),
            ).start()
        trip(
            packed.at[me.z // per, k], a_ref.at[me.z, me.c, at], (b0, b1), k * zc, me.sibling()
        ).start()
        pltpu.make_async_copy(
            packed.at[me.z // per, k], a_ref.at[me.z, me.c, at], ls.at[4 + k]
        ).start()
        return carry

    lax.fori_loop(0, 4, project, 0)
    kept.append(move(rows, ng_ref, ls, 8))
    for copy in outs + local[1:]:
        copy.wait()
    column = og_ref.at[me.x, :, me.y, me.c]
    out_rows = [send(column, column, (p0, p1), k, me.plane(k)) for k in range(1, 4)]

    def pass_on(step, carry):
        k, over = step // (zc - 1), step % (zc - 1) + 1
        at = (me.x ^ (k // 2)) * 2 + (me.y ^ (k % 2))
        there = me.z ^ over
        trip(
            packed.at[there // per, k],
            a_ref.at[me.z, me.c, at],
            (z0, z1),
            k * zc + over,
            me.line(over),
        ).wait()
        landed = a_ref.at[there, me.c, at]
        trip(landed, landed, (b0, b1), k * zc + over, me.sibling()).start()
        return carry

    lax.fori_loop(0, 4 * (zc - 1), pass_on, 0)
    for copy in out_rows:
        copy.wait()
    every = og_ref.at[:, :, :, me.c]
    last = send(every, every, (s0, s1), 1, me.sibling())

    def finish(step, carry):
        k, over = step // zc, step % zc
        at = (me.x ^ (k // 2)) * 2 + (me.y ^ (k % 2))
        landed = a_ref.at[me.z ^ over, me.c, at]
        trip(landed, landed, (b0, b1), k * zc + over, me.sibling()).wait()
        return carry

    lax.fori_loop(0, 4 * zc, finish, 0)
    for k in range(4):
        pltpu.make_async_copy(
            packed.at[me.z // per, k], a_ref.at[me.z, me.c, me.g], ls.at[4 + k]
        ).wait()
    for copy in [last] + kept + wide:
        copy.wait()
    for copy in blocks:
        copy.wait_send()


def head_exchange(zc, group, tokens, matrices, gains):
    chips = 4 * zc
    own, width = tokens.shape
    count = matrices[0].shape[0]
    piece = (count, 3 * group * HEAD_DIM)
    return exchange(
        functools.partial(head_kernel, zc, group),
        1,
        (
            struct((4, own, width)),
            struct((chips, 2) + piece),
            struct((2, 2, 3, count, width)),
            struct((zc, 2, 4, BLOCK + own, PAIR)),
            struct((2, zc, 2, 2, count, width)),
        ),
        [VM] * 10,
        (ANY,) * 5,
        [
            pltpu.VMEM((4,) + piece, BF16),
            pltpu.VMEM((4, 2, count, width), BF16),
            pltpu.VMEM((2, 2, count, width), BF16),
            pltpu.VMEM((count, width), BF16),
            pltpu.VMEM((4, own, width), BF16),
            pltpu.VMEM((chips, 2) + piece, BF16),
            pltpu.VMEM((group, 4, BLOCK + own, PAIR), BF16),
            DMA((10,)),
        ]
        + both(chips)
        + both(4)
        + both(4)
        + both(4 * zc)
        + both(4 * zc)
        + both(2)
        + both(zc)
        + both(4),
        (tokens, *matrices, *(g.reshape(1, -1) for g in gains)),
        2 * 4 * own * width * width,
        16 << 20,
    )


def join_kernel(zc, s_ref, x_ref, w_ref, ob_ref, r_ref, n_ref, mine, theirs, slabs, x_in, w_in, ls, b0, b1, c0, c1):
    me = Place(zc)
    chips = 4 * zc
    heads, per = slabs.shape[:2]
    loads = [move(w_ref, w_in, ls, 2), move(x_ref, x_in, ls, 3)]
    greet([me.any_chip(k) for k in range(1, chips)] + [me.sibling()])()
    other = send(s_ref.at[:, 1 - me.c], theirs, (b0, b1), 0, me.sibling())
    own = move(s_ref.at[:, me.c], mine, ls, 0)
    own.wait()
    other.wait()
    mine[...] = mine[...] + theirs[...]
    head = me.g * (heads // 4) + me.z // per
    place = me.z % per
    keep = move(mine.at[me.z, me.g], slabs.at[head, place], ls, 1)
    sends = []
    for k in reversed(range(1, chips)):
        there = me.any_chip(k)
        their_g = there[0] * 2 + there[2]
        sends.append(
            send(mine.at[there[1], their_g], slabs.at[head, place], (c0, c1), k, there)
        )
    keep.wait()
    for copy in sends:
        copy.wait()
    for block in range(2):
        for pair in range(heads // 2):
            sides = []
            for side in range(2):
                slab = slabs[2 * pair + side, 0].astype(F32)
                for extra in range(1, per):
                    slab = slab + slabs[2 * pair + side, extra].astype(F32)
                sides.append(slab)
            ob_ref[block * BLOCK : (block + 1) * BLOCK, lanes(pair)] = pair_up(
                sides[0], block, sides[1], block
            ).astype(BF16)
    for copy in loads:
        copy.wait()
    residual = x_in[...].astype(F32) + dot(ob_ref[...], w_in[...])
    r_ref[...] = residual
    mean = jnp.mean(residual * residual, axis=-1, keepdims=True)
    n_ref[...] = (residual * lax.rsqrt(mean + EPS)).astype(BF16)


def join_exchange(zc, heads, slabs, tokens, w_out):
    chips = 4 * zc
    per = 4 * zc // heads
    half = (zc,) + slabs.shape[2:]
    shape = tokens.shape
    return exchange(
        functools.partial(join_kernel, zc),
        2,
        (struct(shape), struct(shape, F32), struct(shape)),
        [ANY, ANY, ANY],
        (VM,) * 3,
        [
            pltpu.VMEM(half, BF16),
            pltpu.VMEM(half, BF16),
            pltpu.VMEM((heads, per) + slabs.shape[3:], BF16),
            pltpu.VMEM(shape, BF16),
            pltpu.VMEM(w_out.shape, BF16),
            DMA((4,)),
        ]
        + both(1)
        + both(chips),
        (slabs, tokens, w_out),
        0,
        0,
    )


def middle_kernel(zc, n_ref, ca_ref, cb_ref, cc_ref, cd_ref, *rest):
    f_refs, rest = rest[: zc // 2 + 1], rest[zc // 2 + 1 :]
    oa_ref, ob_ref, oc_ref, od_ref, cs_ref, sh_ref, rows, cots, gate_w, up_w, down_w, *rest = rest
    hid, dgate, dup, c_out, c_in, passed, stage, o_out, ls, n0, n1, c0, c1, f0, f1, h0, h1 = rest
    me = Place(zc)
    width = n_ref.shape[1]
    met = greet([me.plane(k) for k in range(1, 4)] + [me.line(1), me.sibling()])
    move(n_ref, rows.at[0], ls, 15).wait()
    met()
    farthest = send(rows.at[0], rows.at[3], (n0, n1), 3, me.plane(3))
    def places(there):
        return (
            gate_w.at[:, there, :, me.c],
            up_w.at[:, there, :, me.c],
            down_w.at[there, me.c],
        )

    given = dict(zip([1, *range(0, zc, 2)], f_refs))
    hops, loads = [], []
    for k in range(2, zc, 2):
        for i, place in enumerate(places(me.z ^ k)):
            hops.append(send(given[k].at[:, :, i], place, (h0, h1), 3 * k + i, me.line(1)))
    for k, ref in given.items():
        for i, place in enumerate(places(me.z ^ k)):
            loads.append(send(ref.at[:, :, i], place, (f0, f1), 3 * k + i, me.sibling()))
            loads.append(move(ref.at[:, :, i], place, ls, 21 + 3 * k + i))
    for k, ref in enumerate((ca_ref, cb_ref, cc_ref, cd_ref)):
        loads.append(move(ref, cots.at[k], ls, 16 + k))
    farthest.wait_send()
    near_rows = [send(rows.at[0], rows.at[k], (n0, n1), k, me.plane(k)) for k in (1, 2)]
    for copy in hops:
        copy.wait()
    for k in range(3, zc, 2):
        for i, place in enumerate(places(me.z ^ k)):
            loads.append(send(place, place, (f0, f1), 3 * k + i, me.sibling()))
    for copy in loads:
        copy.wait()
    square = (width, width)
    half = n_ref.shape[0] // 2
    upper, lower = pl.ds(0, half), pl.ds(half, half)
    c_sems = (c0, c1)
    far_parts = [
        trip(c_out.at[3, upper], passed.at[0], c_sems, 0, me.plane(2)),
        trip(c_out.at[3, lower], passed.at[1], c_sems, 1, me.plane(1)),
    ]
    near_parts = [
        trip(c_out.at[1, lower], c_in.at[0, lower], c_sems, 2, me.plane(1)),
        trip(c_out.at[2, upper], c_in.at[1, upper], c_sems, 3, me.plane(2)),
        trip(c_out.at[1, upper], c_in.at[0, upper], c_sems, 4, me.plane(1)),
        trip(c_out.at[2, lower], c_in.at[1, lower], c_sems, 5, me.plane(2)),
    ]

    def block(step, carry):
        k = jnp.where(step == 0, 3, jnp.where(step == 3, 0, step))

        @pl.when(step < 3)
        def _():
            trip(rows.at[0], rows.at[k], (n0, n1), k, me.plane(k)).wait_recv()

        gate_mat, up_mat = gate_w[...].reshape(square), up_w[...].reshape(square)
        gate = dot(rows[k], gate_mat)
        up = dot(rows[k], up_mat)
        back = nt_dot(cots[k], down_w[...].reshape(square))
        sig = jax.nn.sigmoid(gate)
        soft = gate * sig
        hid[k] = (soft * up).astype(BF16)
        dgate[k] = (back * up * sig * (1.0 + gate * (1.0 - sig))).astype(BF16)
        dup[k] = (back * soft).astype(BF16)
        c_out[k] = (nt_dot(dgate[k], gate_mat) + nt_dot(dup[k], up_mat)).astype(BF16)

        @pl.when(step == 0)
        def _():
            for copy in far_parts:
                copy.start()

        @pl.when(step == 1)
        def _():
            near_parts[0].start()

        @pl.when(step == 2)
        def _():
            near_parts[1].start()

        return carry

    lax.fori_loop(0, 4, block, 0)
    far_parts[0].wait_recv()
    c_out[1, upper] = c_out[1, upper] + passed[0]
    near_parts[2].start()
    far_parts[1].wait_recv()
    c_out[2, lower] = c_out[2, lower] + passed[1]
    near_parts[3].start()
    all_rows = (4 * n_ref.shape[0], width)

    def weight_grad(left, right, slot):
        chunk = 256
        for first in range(0, width, chunk):
            value = tn_dot(left[:, first : first + chunk], right).astype(BF16)
            stage[slot, first : first + chunk] = value

    shares = []
    piece = width // (8 * zc)

    def share(slot, which):
        parts = stage.at[slot].reshape(2, zc, 2, 2, piece, width)
        for g in range(4):
            x, y = g // 2, g % 2
            shares.append(
                move(parts.at[x, :, y], sh_ref.at[:, :, 2 * g + which], ls, 12 + 2 * g + which)
            )

    flat = lambda ref: ref[...].reshape(all_rows)
    weight_grad(flat(rows), flat(dgate), 0)
    share(0, 0)
    weight_grad(flat(rows), flat(dup), 1)
    share(1, 1)
    weight_grad(flat(hid), flat(cots), 2)
    shares.append(
        move(stage.at[2].reshape(zc, 2, 4, piece, width), sh_ref.at[:, :, 8:], ls, 20)
    )

    for k, ref in enumerate((oa_ref, ob_ref, oc_ref, od_ref)):
        o_out[k] = dot(hid[k], down_w[...].reshape(square)).astype(BF16).reshape(ref.shape)
        shares.append(move(o_out.at[k], ref, ls, k))
    for copy in far_parts:
        copy.wait_send()
    for copy in near_parts:
        copy.wait()
    cs_ref[...] = c_out[0].astype(F32) + c_in[0].astype(F32) + c_in[1].astype(F32)
    for copy in shares:
        copy.wait()
    for copy in near_rows:
        copy.wait_send()


def middle_exchange(zc, normed, cots, weights):
    own, width = normed.shape
    piece = width // (8 * zc)
    blocks = pltpu.VMEM((4, own, width), BF16)
    wide = pltpu.VMEM((2, zc, 2, 2, piece, width), BF16)
    return exchange(
        functools.partial(middle_kernel, zc),
        3,
        (
            *[struct((zc, 2, piece, width))] * 4,
            struct((own, width), F32),
            struct((zc, 2, 12, piece, width)),
        ),
        [ANY] * (5 + len(weights)),
        (ANY,) * 4 + (VM, ANY),
        [blocks, blocks, wide, wide, pltpu.VMEM((zc, 2, 2, 2, piece, width), BF16)]
        + [blocks] * 4
        + [pltpu.VMEM((2, own, width), BF16), pltpu.VMEM((2, own // 2, width), BF16)]
        + [pltpu.VMEM((3, width, width), BF16), pltpu.VMEM((4, zc, 2, piece, width), BF16), DMA((21 + 3 * zc,))]
        + both(4)
        + both(6)
        + both(3 * zc)
        + both(3 * zc),
        (normed, *cots, *weights),
        2 * 4 * own * width * width * 9,
        64 << 20,
    )


def turn_kernel(
    zc,
    c_ref,
    t_ref,
    r_ref,
    wo_ref,
    ob_ref,
    yb_ref,
    yc_ref,
    dr_ref,
    do_ref,
    va_ref,
    vb_ref,
    vc_ref,
    vd_ref,
    nb_ref,
    nc_ref,
    slabs,
    stage,
    wo_in,
    ob_in,
    ls,
    d0,
    d1,
    b0,
    b1,
    y0,
    y1,
):
    me = Place(zc)
    chips = 4 * zc
    heads = slabs.shape[0]
    group = heads // 4
    per = zc // group
    width = t_ref.shape[1]
    met = greet([me.any_chip(k) for k in range(1, chips)] + [me.sibling()])
    loads = [move(wo_ref, wo_in, ls, 5), move(ob_ref, ob_in, ls, 6)]
    total, residual = c_ref[...], r_ref[...]
    scaling = lax.rsqrt(jnp.mean(residual * residual, axis=-1, keepdims=True) + EPS)
    normed = residual * scaling
    middle = jnp.mean(total * normed, axis=-1, keepdims=True)
    grad = t_ref[...].astype(F32) + scaling * (total - normed * middle)
    dr_ref[...] = grad
    narrow = grad.astype(BF16)
    loads[0].wait()
    back = nt_dot(narrow, wo_in[...])
    for pair in range(heads // 2):
        two = back[:, lanes(pair)]
        for side in range(2):
            slabs[2 * pair + side] = pair_up(two[:BLOCK], side, two[BLOCK:], side).astype(BF16)
    met()
    to = do_ref.at[me.z, me.c, me.g]
    own = move(slabs.at[me.g * group + me.z // per], to, ls, 0)
    sends = []
    for k in reversed(range(1, chips)):
        there = me.any_chip(k)
        head = (there[0] * 2 + there[2]) * group + there[1] // per
        sends.append(send(slabs.at[head], to, (d0, d1), k, there))
    sends.append(send(yb_ref, nb_ref, (y0, y1), 1, me.plane(1)))
    sends.append(send(yc_ref, nc_ref, (y0, y1), 2, me.plane(2)))
    chunk = 256
    loads[1].wait()
    attended = ob_in[...]
    for first in range(0, width, chunk):
        stage[first : first + chunk] = tn_dot(attended[:, first : first + chunk], narrow).astype(BF16)
    parts = stage.reshape(2, zc, 2, 2, width // (8 * zc), width)
    keeps = []
    for k, ref in enumerate((va_ref, vb_ref, vc_ref, vd_ref)):
        there = me.plane(k)
        keeps.append(move(parts.at[there[0], :, there[2]], ref, ls, 1 + k))
    own.wait()
    for copy in sends[:-2]:
        copy.wait()
    half = do_ref.at[:, me.c]
    relay = send(half, half, (b0, b1), 0, me.sibling())
    for copy in keeps + sends[-2:]:
        copy.wait()
    relay.wait()


def turn_exchange(zc, c_sum, cotangent, residual, w_out, attn_rows, near):
    chips = 4 * zc
    own, width = cotangent.shape
    heads = width // HEAD_DIM
    return exchange(
        functools.partial(turn_kernel, zc),
        6,
        (
            struct((own, width), F32),
            struct((zc, 2, 4, BLOCK, PAIR)),
            *[struct((zc, 2, width // (8 * zc), width))] * 6,
        ),
        [VM] * 3 + [ANY] * 4,
        (VM,) + (ANY,) * 7,
        [
            pltpu.VMEM((heads, BLOCK, PAIR), BF16),
            pltpu.VMEM((width, width), BF16),
            pltpu.VMEM((width, width), BF16),
            pltpu.VMEM((own, width), BF16),
            DMA((7,)),
        ]
        + both(chips)
        + both(1)
        + both(3),
        (c_sum, cotangent, residual, w_out, attn_rows, *near),
        2 * 2 * own * width * width,
        8 << 20,
    )


def tail_kernel(
    zc,
    d_ref,
    n_any,
    w_any,
    x_any,
    g_any,
    f_ref,
    r_ref,
    ya_ref,
    yb_ref,
    yc_ref,
    yd_ref,
    va_ref,
    vb_ref,
    vc_ref,
    vd_ref,
    tg_ref,
    gw_ref,
    go_ref,
    gf_ref,
    out_ref,
    n_ref,
    w_ref,
    x_ref,
    g_ref,
    r_in,
    y_in,
    o_mine,
    o_theirs,
    o_land,
    mine,
    theirs,
    landed,
    grads,
    c_out,
    c_in,
    stage,
    other_w,
    ls,
    b0,
    b1,
    z0,
    z1,
    c0,
    c1,
    s0,
    s1,
    w0,
    w1,
    q0,
    q1,
    f0,
    f1,
):
    me = Place(zc)
    chips = 4 * zc
    group, per = landed.shape[:2]
    qw = group * HEAD_DIM
    greet([me.any_chip(k) for k in range(1, chips)] + [me.sibling()])()
    head, place = me.z // per, me.z % per

    def slot(k):
        return (me.x ^ (k // 2)) * 2 + (me.y ^ (k % 2))

    order = (3, 2, 1, 0)
    halves = []
    for k in order:
        halves.append(
            (
                send(d_ref.at[:, 1 - me.c, slot(k)], theirs.at[k], (b0, b1), k, me.sibling()),
                move(d_ref.at[:, me.c, slot(k)], mine.at[k], ls, k),
            )
        )
    given = ((w_any, w_ref), (n_any, n_ref), (g_any, g_ref), (x_any, x_ref))
    loads = [move(source, target, ls, 20 + i) for i, (source, target) in enumerate(given)]
    f_parts = [move(f_ref.at[pl.ds(2 * me.g, 2)], gf_ref.at[me.g], ls, 10)]
    for k in (3, 1, 2):
        there = me.plane(k)
        part = f_ref.at[pl.ds(2 * (there[0] * 2 + there[2]), 2)]
        f_parts.append(send(part, gf_ref.at[me.g], (f0, f1), k, there))
    out_parts = [move(r_ref, r_in, ls, 11)]
    for i, ref in enumerate((ya_ref, yb_ref, yc_ref, yd_ref)):
        out_parts.append(move(ref, y_in.at[i, 0], ls, 12 + i))
    for i, ref in enumerate((va_ref, vb_ref, vc_ref, vd_ref)):
        out_parts.append(move(ref, y_in.at[i, 1], ls, 16 + i))
    for k, (far, near) in zip(order, halves):
        near.wait()
        far.wait()
        mine[k] = mine[k] + theirs[k]
        for over in range(1, zc):
            send(
                mine.at[k, me.z ^ over],
                landed.at[head, place, k],
                (z0, z1),
                k * zc + over,
                me.line(over),
            )
        move(mine.at[k, me.z], landed.at[head, place, k], ls, 4 + k)

    for copy in out_parts + loads:
        copy.wait()
    final = r_in[...]
    o_sum = jnp.zeros(o_mine.shape, F32)
    for i in range(4):
        final = final + y_in[i, 0].astype(F32).reshape(final.shape)
        o_sum = o_sum + y_in[i, 1].astype(F32)
    out_ref[...] = final.astype(BF16)
    o_mine[...] = o_sum.astype(BF16)
    o_swap = send(o_mine.at[:, 1 - me.c], o_theirs, (s0, s1), 1, me.sibling())

    def block(step, carry):
        k = 3 - step
        pltpu.make_async_copy(
            mine.at[k, me.z], landed.at[head, place, k], ls.at[4 + k]
        ).wait()
        for over in range(1, zc):
            trip(
                mine.at[k, me.z ^ over],
                landed.at[head, place, k],
                (z0, z1),
                k * zc + over,
                me.line(over),
            ).wait()
        for pair in range(group // 2):
            sides = []
            for side in range(2):
                h = 2 * pair + side
                slab = landed[h, 0, k]
                for extra in range(1, per):
                    slab = slab + landed[h, extra, k]
                start = qw + h * PAIR
                grads[k, :, start : start + PAIR] = slab[BLOCK:]
                sides.append(slab[:BLOCK].astype(F32))
            for b in range(2):
                grads[k, b * BLOCK : (b + 1) * BLOCK, lanes(pair)] = pair_up(
                    sides[0], b, sides[1], b
                ).astype(BF16)

        @pl.when(k > 0)
        def _():
            c_out[k] = nt_dot(grads[k], w_ref[...]).astype(BF16)
            trip(c_out.at[k], c_in.at[k], (c0, c1), k, me.plane(k)).start()

        return carry

    o_swap.wait()
    o_theirs[...] = o_theirs[...] + o_mine[:, me.c]
    sends = [
        send(o_theirs.at[me.z ^ k], o_land.at[k], (q0, q1), k, me.line(k)) for k in range(1, zc)
    ]
    lax.fori_loop(0, 4, block, 0)
    width, cols = w_ref.shape
    all_rows = 4 * n_ref.shape[1]
    normed_all = n_ref[...].reshape(all_rows, width)
    grads_all = grads[...].reshape(all_rows, cols)
    piece = stage.shape[2]
    chunk = 256
    each = chunk // (2 * piece)
    swaps = []
    for first in range(0, width, chunk):
        value = tn_dot(normed_all[:, first : first + chunk], grads_all).astype(BF16)
        at = first // (2 * piece)
        stage[at : at + each] = value.reshape(each, 2, piece, cols)
        swaps.append(
            send(
                stage.at[at : at + each, 1 - me.c],
                other_w.at[at : at + each],
                (s0, s1),
                2 + first // chunk,
                me.sibling(),
            )
        )
    c_out[0] = nt_dot(grads[0], w_ref[...]).astype(BF16)
    for swap in swaps:
        swap.wait()

    def add(i, carry):
        other_w[i] = stage[i, me.c] + other_w[i]
        return carry

    lax.fori_loop(0, chips, add, 0)
    stay = move(other_w.at[me.chip], gw_ref.at[me.z, me.g], ls, 8)
    for k in reversed(range(1, chips)):
        there = me.any_chip(k)
        chip = (there[0] * zc + there[1]) * 2 + there[2]
        sends.append(send(other_w.at[chip], gw_ref.at[me.z, me.g], (w0, w1), k, there))
    total = c_out[0].astype(F32)
    for k in range(1, 4):
        trip(c_out.at[k], c_in.at[k], (c0, c1), k, me.plane(k)).wait()
        total = total + c_in[k].astype(F32)
    x = x_ref[...].astype(F32)
    scaling = lax.rsqrt(jnp.mean(x * x, axis=-1, keepdims=True) + EPS)
    normed = x * scaling
    middle = jnp.mean(total * normed, axis=-1, keepdims=True)
    tg_ref[...] = (g_ref[...] + scaling * (total - normed * middle)).astype(BF16)
    stay.wait()
    for copy in sends + f_parts:
        copy.wait()
    o_sum = o_theirs[me.z].astype(F32)
    for k in range(1, zc):
        o_sum = o_sum + o_land[k].astype(F32)
    go_ref[...] = o_sum


def tail_exchange(zc, group, slab_grads, n_all, weights, tokens, residual_grad, shares, residual, packs):
    chips = 4 * zc
    per = zc // group
    own, width = tokens.shape
    cols = weights.shape[1]
    slab = slab_grads.shape[3:]
    piece = width // (2 * chips)
    blocks = pltpu.VMEM((4, own, width), BF16)
    return exchange(
        functools.partial(tail_kernel, zc),
        4,
        (
            struct((own, width)),
            struct((zc, 4, piece, cols)),
            struct((piece, width), F32),
            struct((4, 2, piece, width)),
            struct((own, width)),
        ),
        [ANY] * 15,
        (VM, ANY, VM, ANY, VM),
        [
            pltpu.VMEM((4, own, width), BF16),
            pltpu.VMEM((width, cols), BF16),
            pltpu.VMEM((own, width), BF16),
            pltpu.VMEM((own, width), F32),
            pltpu.VMEM((own, width), F32),
            pltpu.VMEM((4, 2, zc, 2, piece, width), BF16),
            pltpu.VMEM((zc, 2, piece, width), BF16),
            pltpu.VMEM((zc, piece, width), BF16),
            pltpu.VMEM((zc, piece, width), BF16),
            pltpu.VMEM((4, zc) + slab, BF16),
            pltpu.VMEM((4, zc) + slab, BF16),
            pltpu.VMEM((group, per, 4) + slab, BF16),
            pltpu.VMEM((4, own, cols), BF16),
            blocks,
            blocks,
            pltpu.VMEM((chips, 2, piece, cols), BF16),
            pltpu.VMEM((chips, piece, cols), BF16),
            DMA((24,)),
        ]
        + both(4)
        + both(4 * zc)
        + both(4)
        + both(2 + width // 256)
        + both(chips)
        + both(zc)
        + both(4),
        (slab_grads, n_all, weights, tokens, residual_grad, shares, residual, *packs),
        2 * 4 * own * width * cols * 2,
        24 << 20,
    )


def last_kernel(
    zc,
    group,
    t_any,
    o_any,
    wo_any,
    gw_any,
    gf_any,
    ds_any,
    q_any,
    k_any,
    v_any,
    g_any,
    u_any,
    gain1,
    gain2,
    tg_ref,
    out_ref,
    go_ref,
    g1_ref,
    q_ref,
    k_ref,
    v_ref,
    g2_ref,
    g_ref,
    u_ref,
    d_ref,
    gw_ref,
    gf_ref,
    ds_ref,
    q_w,
    k_w,
    v_w,
    g_w,
    u_w,
    ls,
):
    given = (gw_any, q_any, k_any, v_any, gf_any, g_any, u_any, ds_any, t_any, o_any, wo_any)
    taken = (gw_ref, q_w, k_w, v_w, gf_ref, g_w, u_w, ds_ref, tg_ref, out_ref, go_ref)
    copies = [move(a, b, ls, i) for i, (a, b) in enumerate(zip(given, taken))]
    for copy in copies:
        copy.wait()
    d_ref[...] = ds_ref[8:].astype(F32).reshape(d_ref.shape)
    first_gain, second_gain = column_of(low(gain1[...])), column_of(low(gain2[...]))
    count = q_w.shape[0]
    qw = group * HEAD_DIM
    score = jnp.zeros((count, PAIR), F32)
    for g in range(4):
        raw = gw_ref[0, g].astype(F32)
        for z in range(1, zc):
            raw = raw + gw_ref[z, g].astype(F32)
        for pair in range(group // 2):
            at = lanes(g * group // 2 + pair)
            start = qw + 2 * pair * PAIR
            even, odd = raw[:, start : start + PAIR], raw[:, start + PAIR : start + 2 * PAIR]
            query = raw[:, lanes(pair)]
            key, value = pair_up(even, 0, odd, 0), pair_up(even, 1, odd, 1)
            score = score + query * low(q_w[:, at]) + key * low(k_w[:, at]) + value * low(v_w[:, at])
            q_ref[:, at] = first_gain * query
            k_ref[:, at] = first_gain * key
            v_ref[:, at] = first_gain * value
    g1_ref[...] = row_of(jnp.sum(score, axis=1, keepdims=True))
    units = g_w.shape[1] // (4 * zc)
    score = jnp.zeros((count, PAIR), F32)
    for which, (weight, target) in enumerate(((g_w, g_ref), (u_w, u_ref))):
        for chunk in range(weight.shape[1] // PAIR):
            if units % PAIR == 0:
                owner, piece = divmod(chunk, units // PAIR)
                x, z, y = owner // (2 * zc), owner // 2 % zc, owner % 2
                raw = gf_ref[2 * x + y, which, :, lanes(z * units // PAIR + piece)].astype(F32)
            else:
                x, z = chunk // zc, chunk % zc
                near = gf_ref[2 * x, which, :, lanes(z // 2)].astype(F32)
                far = gf_ref[2 * x + 1, which, :, lanes(z // 2)].astype(F32)
                raw = pair_up(near, z % 2, far, z % 2)
            score = score + raw * low(weight[:, lanes(chunk)])
            target[:, lanes(chunk)] = second_gain * raw
    g2_ref[...] = row_of(jnp.sum(score, axis=1, keepdims=True))


def last_step(zc, group, tokens_grad, output, out_share, w_all, f_all, shares, matrices, gains):
    own, width = output.shape
    count, hidden = matrices[3].shape
    return pl.pallas_call(
        functools.partial(last_kernel, zc, group),
        out_shape=(
            struct((own, width)),
            struct((own, width)),
            struct((count, width), F32),
            struct((1, count), F32),
            struct((count, width), F32),
            struct((count, width), F32),
            struct((count, width), F32),
            struct((1, count), F32),
            struct((count, hidden), F32),
            struct((count, hidden), F32),
            struct((4 * count, width), F32),
        ),
        in_specs=[ANY] * 11 + [VM] * 2,
        out_specs=(VM,) * 11,
        scratch_shapes=[
            pltpu.VMEM(v.shape, v.dtype) for v in (w_all, f_all, shares, *matrices)
        ]
        + [DMA((11,))],
        compiler_params=pltpu.CompilerParams(vmem_limit_bytes=60 << 20),
    )(
        tokens_grad,
        output,
        out_share,
        w_all,
        f_all,
        shares,
        *matrices,
        *(g.reshape(1, -1) for g in gains),
    )


def segment_start(position, lens_ref):
    start = jnp.zeros_like(position)
    end = 0
    for j in range(lens_ref.shape[0]):
        end = end + lens_ref[j]
        start = jnp.where(position >= end, end, start)
    return start


def note_tiles(workers, worker, tiles, lens_ref, mine):
    turns = tiles // workers

    def snake(turn, carry):
        forward = turn * workers + worker
        backward = turn * workers + workers - 1 - worker
        mine[turn] = jnp.where((turn & 1) == 0, forward, backward)
        return carry

    def weigh(step, ahead):
        turn = turns - 1 - step
        loads = []
        for tile in (2 * turn, 2 * turn + 1):
            first, _, _, last = key_bounds(tile * QTILE, lens_ref)
            loads.append(last - first)
        lighter_first = loads[0] <= loads[1]
        first_to_zero = jnp.where(ahead > 0, lighter_first, loads[0] > loads[1])
        mine[turn] = 2 * turn + jnp.where(first_to_zero, worker, 1 - worker)
        return ahead + jnp.where(first_to_zero, loads[0] - loads[1], loads[1] - loads[0])

    if workers == 2:
        lax.fori_loop(0, turns, weigh, 0)
    else:
        lax.fori_loop(0, turns, snake, 0)


def key_bounds(first, lens_ref):
    low_start = segment_start(first, lens_ref)
    high_start = segment_start(first + QTILE - 1, lens_ref)
    low = low_start // KTILE
    high = (first + QTILE + KTILE - 1) // KTILE
    plain = jnp.clip((high_start + KTILE - 1) // KTILE, low, high)
    stop = jnp.clip((first + 1) // KTILE, plain, high)
    return low, plain, stop, high


def visible(first, tile, starts):
    key = tile * KTILE + lax.broadcasted_iota(jnp.int32, (KTILE, QTILE), 0)
    query = first + lax.broadcasted_iota(jnp.int32, (KTILE, QTILE), 1)
    return (key <= query) & (key >= starts)


def note_places(anchor_ref, inv):
    def note(i, carry):
        inv[anchor_ref[i]] = i
        return carry

    lax.fori_loop(0, anchor_ref.shape[0], note, 0)


def half_lanes(rows, half):
    lane = lax.broadcasted_iota(jnp.int32, rows.shape, 1)
    return jnp.where((lane // HEAD_DIM) == half, rows, jnp.zeros_like(rows))


def fold(rows, columns, first):
    row = lax.broadcasted_iota(jnp.int32, (rows, columns), 0)
    column = lax.broadcasted_iota(jnp.int32, (rows, columns), 1)
    return (row % HEAD_DIM == column - first).astype(F32).astype(BF16)


def unfold(rows, columns, first):
    row = lax.broadcasted_iota(jnp.int32, (rows, columns), 0)
    column = lax.broadcasted_iota(jnp.int32, (rows, columns), 1)
    return (column % HEAD_DIM == row - first).astype(F32).astype(BF16)


def forward_kernel(
    workers,
    anchor_ref,
    lens_ref,
    who_ref,
    a_any,
    o_ref,
    kv_any,
    kvt_any,
    q_any,
    qt_any,
    ot_any,
    l_any,
    inv,
    mine,
    raw,
    a_ref,
    kv_ref,
    kvt_ref,
    q_ref,
    qt_ref,
    ot_ref,
    l_ref,
    ls,
    ts,
):
    load = move(a_any, a_ref, ls, 0)
    blocks = anchor_ref.shape[0]
    turns = qt_ref.shape[0]
    per = QTILE // BLOCK
    worker = who_ref[0]
    note_places(anchor_ref, inv)
    note_tiles(workers, worker, turns * workers, lens_ref, mine)
    o_ref[...] = jnp.zeros_like(o_ref)
    same = selection(PAIR, PAIR, 0)
    load.wait()

    def order(step, carry):
        for b in range(per):
            i = step * per + b
            where = inv[i]
            slab, half = where >> 1, where & 1
            at = pl.ds(pl.multiple_of(i * BLOCK, BLOCK), BLOCK)
            kv_ref[at, :] = a_ref[slab, pl.ds(pl.multiple_of(BLOCK + half * BLOCK, BLOCK), BLOCK), :]
        return carry

    lax.fori_loop(0, blocks // per, order, 0)
    leaving = [move(kv_ref, kv_any, ls, 1)]

    def flip(step, carry):
        at = pl.ds(pl.multiple_of(step * TURNED, TURNED), TURNED)
        kvt_ref[:, at] = nt_dot(same, kv_ref[at, :]).astype(BF16)
        return carry

    lax.fori_loop(0, blocks * BLOCK // TURNED, flip, 0)
    leaving.append(move(kvt_ref, kvt_any, ls, 2))
    kept = ((q_ref, q_any), (qt_ref, qt_any), (ot_ref, ot_any), (l_ref, l_any))

    def leave(turn, i):
        source, target = kept[i]
        return pltpu.make_async_copy(source.at[turn], target.at[turn], ts.at[i, turn])

    def one_tile(turn, carry):
        tile = mine[turn]
        first = tile * QTILE
        for b in range(per):
            where = inv[tile * per + b]
            raw[b * BLOCK : (b + 1) * BLOCK, :] = half_lanes(a_ref[where >> 1, :BLOCK, :], where & 1)
        q_ref[turn] = (dot(raw[...], fold(PAIR, PAIR, 0)) * 0.125).astype(BF16)
        qt_ref[turn] = (nt_dot(unfold(PAIR, PAIR, 0), raw[...]) * 0.125).astype(BF16)
        query = qt_ref[turn]
        starts = segment_start(first + lax.broadcasted_iota(jnp.int32, (1, QTILE), 1), lens_ref)
        low, plain, stop, high = key_bounds(first, lens_ref)

        def step(masked, kt, state):
            top, total, acc = state
            at = pl.ds(pl.multiple_of(kt * KTILE, KTILE), KTILE)
            scores = dot(kv_ref[at, :], query)
            if masked:
                scores = jnp.where(visible(first, kt, starts), scores, MASKED)
            new_top = jnp.maximum(top, jnp.max(scores, axis=0, keepdims=True))
            factor = jnp.exp(top - new_top)
            weights = jnp.exp(scores - new_top)
            total = total * factor + jnp.sum(weights, axis=0, keepdims=True)
            acc = acc * factor + dot(kvt_ref[HEAD_DIM:, at], weights.astype(BF16))
            return (new_top, total, acc)

        state = (
            jnp.full((1, QTILE), LOWEST, F32),
            jnp.zeros((1, QTILE), F32),
            jnp.zeros((HEAD_DIM, QTILE), F32),
        )
        state = lax.fori_loop(low, plain, functools.partial(step, True), state)
        state = lax.fori_loop(plain, stop, functools.partial(step, False), state)
        top, total, acc = lax.fori_loop(stop, high, functools.partial(step, True), state)
        out = acc / total
        ot_ref[turn] = out
        l_ref[turn] = top + jnp.log(total)
        for i in range(4):
            leave(turn, i).start()
        wide = tn_dot(out.astype(BF16), unfold(HEAD_DIM, PAIR, 0)).astype(BF16)
        for b in range(per):
            where = inv[tile * per + b]
            slab = where >> 1
            o_ref[slab] = o_ref[slab] + half_lanes(wide[b * BLOCK : (b + 1) * BLOCK], where & 1)
        return carry

    lax.fori_loop(0, turns, one_tile, 0)

    def left(turn, carry):
        for i in range(4):
            leave(turn, i).wait()
        return carry

    lax.fori_loop(0, turns, left, 0)
    for copy in leaving:
        copy.wait()


def attention_forward(workers, anchors, lengths, who, packed):
    slabs = packed.shape[0]
    rows = slabs * 2 * BLOCK
    turns = rows // QTILE // workers
    return pl.pallas_call(
        functools.partial(forward_kernel, workers),
        out_shape=(
            struct((slabs, BLOCK, PAIR)),
            struct((rows, PAIR)),
            struct((PAIR, rows)),
            struct((turns, QTILE, PAIR)),
            struct((turns, PAIR, QTILE)),
            struct((turns, HEAD_DIM, QTILE), F32),
            struct((turns, 1, QTILE), F32),
        ),
        in_specs=[SM, SM, SM, ANY],
        out_specs=(VM,) + (ANY,) * 6,
        scratch_shapes=[
            pltpu.SMEM((2 * slabs,), jnp.int32),
            pltpu.SMEM((turns,), jnp.int32),
            pltpu.VMEM((QTILE, PAIR), BF16),
            pltpu.VMEM(packed.shape, BF16),
            pltpu.VMEM((rows, PAIR), BF16),
            pltpu.VMEM((PAIR, rows), BF16),
            pltpu.VMEM((turns, QTILE, PAIR), BF16),
            pltpu.VMEM((turns, PAIR, QTILE), BF16),
            pltpu.VMEM((turns, HEAD_DIM, QTILE), F32),
            pltpu.VMEM((turns, 1, QTILE), F32),
            DMA((3,)),
            DMA((4, turns)),
        ],
        compiler_params=pltpu.CompilerParams(vmem_limit_bytes=60 << 20),
        cost_estimate=pl.CostEstimate(
            flops=rows * rows * 64, bytes_accessed=rows * 1024, transcendentals=rows * rows // 8
        ),
    )(anchors, lengths, who, packed)


def backward_kernel(
    workers,
    anchor_ref,
    lens_ref,
    who_ref,
    d_ref,
    kv_ref,
    kvt_ref,
    q_ref,
    qt_ref,
    ot_ref,
    l_ref,
    g_ref,
    inv,
    mine,
    raw,
    both_rows,
    dt,
    acc,
):
    blocks = anchor_ref.shape[0]
    turns = qt_ref.shape[0]
    per = QTILE // BLOCK
    worker = who_ref[0]
    note_places(anchor_ref, inv)
    note_tiles(workers, worker, turns * workers, lens_ref, mine)
    acc[...] = jnp.zeros_like(acc)
    g_ref[:, :BLOCK, :] = jnp.zeros((g_ref.shape[0], BLOCK, PAIR), BF16)

    def one_tile(turn, carry):
        tile = mine[turn]
        first = tile * QTILE
        for b in range(per):
            where = inv[tile * per + b]
            raw[b * BLOCK : (b + 1) * BLOCK, :] = half_lanes(d_ref[where >> 1], where & 1)
        both_rows[:QTILE] = q_ref[turn]
        both_rows[QTILE:] = dot(raw[...], fold(PAIR, PAIR, HEAD_DIM)).astype(BF16)
        dt[...] = nt_dot(unfold(PAIR, PAIR, HEAD_DIM), raw[...]).astype(BF16)
        query, grad = qt_ref[turn], dt[...]
        norm = l_ref[turn]
        delta = jnp.sum(grad[HEAD_DIM:].astype(F32) * ot_ref[turn], axis=0, keepdims=True)
        starts = segment_start(first + lax.broadcasted_iota(jnp.int32, (1, QTILE), 1), lens_ref)
        low, plain, stop, high = key_bounds(first, lens_ref)

        def step(masked, kt, total):
            at = pl.ds(pl.multiple_of(kt * KTILE, KTILE), KTILE)
            keys = kv_ref[at, :]
            scores = dot(keys, query)
            if masked:
                scores = jnp.where(visible(first, kt, starts), scores, MASKED)
            weights = jnp.exp(scores - norm)
            score_grad = (weights * (dot(keys, grad) - delta)).astype(BF16)
            both_grads = jnp.concatenate([score_grad, weights.astype(BF16)], axis=1)
            acc[at, :] += dot(both_grads, both_rows[...])
            return total + dot(kvt_ref[:HEAD_DIM, at], score_grad)

        total = jnp.zeros((HEAD_DIM, QTILE), F32)
        total = lax.fori_loop(low, plain, functools.partial(step, True), total)
        total = lax.fori_loop(plain, stop, functools.partial(step, False), total)
        total = lax.fori_loop(stop, high, functools.partial(step, True), total)
        wide = tn_dot((total * 0.125).astype(BF16), unfold(HEAD_DIM, PAIR, 0)).astype(BF16)
        for b in range(per):
            where = inv[tile * per + b]
            slab = where >> 1
            g_ref[slab, :BLOCK] = g_ref[slab, :BLOCK] + half_lanes(
                wide[b * BLOCK : (b + 1) * BLOCK], where & 1
            )
        return carry

    lax.fori_loop(0, turns, one_tile, 0)

    def place(step, carry):
        for b in range(per):
            i = step * per + b
            where = inv[i]
            slab, half = where >> 1, where & 1
            at = pl.ds(pl.multiple_of(i * BLOCK, BLOCK), BLOCK)
            to = pl.ds(pl.multiple_of(BLOCK + half * BLOCK, BLOCK), BLOCK)
            g_ref[slab, to, :] = acc[at, :].astype(BF16)
        return carry

    lax.fori_loop(0, blocks // per, place, 0)


def attention_backward(workers, anchors, lengths, who, grads, kept):
    slabs = grads.shape[0]
    rows = slabs * 2 * BLOCK
    return pl.pallas_call(
        functools.partial(backward_kernel, workers),
        out_shape=struct((slabs, 3 * BLOCK, PAIR)),
        in_specs=[SM, SM, SM] + [VM] * 7,
        out_specs=VM,
        scratch_shapes=[
            pltpu.SMEM((2 * slabs,), jnp.int32),
            pltpu.SMEM((rows // QTILE // workers,), jnp.int32),
            pltpu.VMEM((QTILE, PAIR), BF16),
            pltpu.VMEM((2 * QTILE, PAIR), BF16),
            pltpu.VMEM((PAIR, QTILE), BF16),
            pltpu.VMEM((rows, PAIR), F32),
        ],
        compiler_params=pltpu.CompilerParams(vmem_limit_bytes=60 << 20),
        cost_estimate=pl.CostEstimate(
            flops=rows * rows * 160, bytes_accessed=rows * 1024, transcendentals=rows * rows // 8
        ),
    )(anchors, lengths, who, grads, *kept)


def around(value, k):
    return lax.ppermute(value, ("head", "y"), [(i, i ^ k) for i in range(4)])


def along(value, k):
    return lax.ppermute(value, "z", [(i, i ^ k) for i in range(lax.axis_size("z"))])


def doubling(pieces, first, last):
    while first >= last:
        pieces = {**pieces, **{k + first: along(pieces[k], first) for k in pieces}}
        first //= 2
    return pieces


def body(
    zc,
    tokens,
    cotangent,
    norm1_gain,
    w_query,
    w_key,
    w_value,
    w_out,
    norm2_gain,
    w_gate,
    w_up,
    w_down,
    block_anchor,
    seq_lengths,
):
    width = tokens.shape[1]
    heads = width // HEAD_DIM
    group = heads // 4
    per_head = zc // group
    workers = 2 * per_head
    feature_rows = w_query.shape[0]

    n1_all, qkv_w, ffn_own, by_head, out_mat = head_exchange(
        zc,
        group,
        tokens,
        (w_query, w_key, w_value, w_gate, w_up, w_down, w_out),
        (norm1_gain, norm2_gain),
    )
    qkv_w = qkv_w.reshape(width, 3 * group * HEAD_DIM)

    out_mat, sent = lax.optimization_barrier((out_mat.reshape(width, width), cotangent))
    cots = [cotangent] + [around(sent, k) for k in range(1, 4)]
    ffn_parts = doubling({0: ffn_own}, zc // 2, 2)
    close = along(ffn_own, 1)

    anchors = jnp.transpose(block_anchor.reshape(2, zc, 2, 2, 2), (1, 3, 0, 2, 4)).reshape(-1)
    who = ((lax.axis_index("z") % per_head) * 2 + lax.axis_index("core")).astype(jnp.int32).reshape(1)
    slab_count = zc * 8
    o_slabs, *kept = attention_forward(
        workers, anchors, seq_lengths, who, by_head.reshape((slab_count,) + by_head.shape[3:])
    )
    attn_rows, residual, normed_two = join_exchange(
        zc, heads, o_slabs.reshape(zc, 2, 4, BLOCK, PAIR), tokens, out_mat
    )
    *out_parts, c_sum, shares = middle_exchange(
        zc, normed_two, cots, [close] + [ffn_parts[k] for k in range(0, zc, 2)]
    )
    shares = lax.psum_scatter(
        shares.reshape(zc * 2 * 12, feature_rows, width), ("z", "core"), scatter_dimension=0, tiled=True
    )
    residual_grad, do_heads, *packs = turn_exchange(
        zc, c_sum, cotangent, residual, out_mat, attn_rows, out_parts[1:3]
    )
    w_grads, near = packs[:4], packs[4:]
    do_heads, far = lax.optimization_barrier((do_heads, out_parts[3]))
    packs = [out_parts[0], *near, around(far, 3), w_grads[0]]
    packs += [around(w_grads[k], k) for k in range(1, 4)]
    grad_heads = attention_backward(
        workers, anchors, seq_lengths, who, do_heads.reshape(slab_count, BLOCK, PAIR), kept
    )
    tokens_grad, w_all, out_share, f_all, output = tail_exchange(
        zc,
        group,
        grad_heads.reshape(zc, 2, 4, 3 * BLOCK, PAIR),
        n1_all,
        qkv_w,
        tokens,
        residual_grad,
        shares,
        residual,
        packs,
    )
    (
        tokens_grad,
        output,
        out_grad,
        gain1_grad,
        query_grad,
        key_grad,
        value_grad,
        gain2_grad,
        gate_grad,
        up_grad,
        down_grad,
    ) = last_step(
        zc,
        group,
        tokens_grad,
        output,
        out_share,
        w_all,
        f_all,
        shares,
        (w_query, w_key, w_value, w_gate, w_up),
        (norm1_gain, norm2_gain),
    )
    return (
        output,
        tokens_grad,
        gain1_grad.reshape(-1),
        query_grad,
        key_grad,
        value_grad,
        out_grad,
        gain2_grad.reshape(-1),
        gate_grad,
        up_grad,
        down_grad,
    )


def solution(mesh):
    blk = mesh.shape["blk"]
    grid = Mesh(mesh.devices.reshape(mesh.shape["head"], blk // 4, 2, 2), AXES)
    rows, vector, whole = P(AXES, None), P(AXES), P()
    return jax.shard_map(
        functools.partial(body, blk // 4),
        mesh=grid,
        in_specs=(rows, rows, vector, rows, rows, rows, rows, vector, rows, rows, rows, whole, whole),
        out_specs=(rows, rows, vector, rows, rows, rows, rows, vector, rows, rows, rows),
        check_vma=False,
    )
```

```python
import functools

import jax
import jax.numpy as jnp
from jax import lax
from jax.experimental import pallas as pl
from jax.experimental.pallas import tpu as pltpu
from jax.sharding import Mesh
from jax.sharding import PartitionSpec as P

HEAD_DIM = 64
BLOCK = 128
PAIR = 128
EPS = 1e-06
MASKED = -1e30
LOWEST = -1e20
QTILE = 512
KTILE = 512
TURNED = 2048
AXES = ("head", "z", "y", "core")
IDS = pl.DeviceIdType.MESH
F32 = jnp.float32
BF16 = jnp.bfloat16
ANY = pl.BlockSpec(memory_space=pl.ANY)
VM = pl.BlockSpec(memory_space=pltpu.VMEM)
SM = pl.BlockSpec(memory_space=pltpu.SMEM)


def struct(shape, dtype=BF16):
    return jax.ShapeDtypeStruct(tuple(shape), dtype)


def nt_dot(a, b):
    return lax.dot_general(a, b, (((1,), (1,)), ((), ())), preferred_element_type=F32)


def tn_dot(a, b):
    return lax.dot_general(a, b, (((0,), (0,)), ((), ())), preferred_element_type=F32)


def dot(a, b):
    return jnp.dot(a, b, preferred_element_type=F32)


def selection(rows, columns, shift, first=0, last=None):
    last = columns if last is None else last
    row = lax.broadcasted_iota(jnp.int32, (rows, columns), 0)
    column = lax.broadcasted_iota(jnp.int32, (rows, columns), 1)
    hit = (row == column + shift) & (column >= first) & (column < last)
    return hit.astype(F32).astype(BF16)


def pair_up(first, first_half, second, second_half):
    lane = lax.broadcasted_iota(jnp.int32, first.shape, 1)
    left = first if first_half == 0 else pltpu.roll(first, HEAD_DIM, 1)
    right = second if second_half == 1 else pltpu.roll(second, HEAD_DIM, 1)
    return jnp.where(lane < HEAD_DIM, left, right)


def column_of(row):
    count = row.shape[1]
    i = lax.broadcasted_iota(jnp.int32, (count, count), 0)
    j = lax.broadcasted_iota(jnp.int32, (count, count), 1)
    return jnp.sum(jnp.where(i == j, row, 0.0), axis=1, keepdims=True)


def row_of(column):
    count = column.shape[0]
    i = lax.broadcasted_iota(jnp.int32, (count, count), 0)
    j = lax.broadcasted_iota(jnp.int32, (count, count), 1)
    return jnp.sum(jnp.where(i == j, column, 0.0), axis=0, keepdims=True)


def low(value):
    return value.astype(BF16).astype(F32)


def lanes(index):
    return slice(index * PAIR, (index + 1) * PAIR)


class Place:
    def __init__(self, z_count):
        self.x, self.z, self.y, self.c = (lax.axis_index(a) for a in AXES)
        self.g = self.x * 2 + self.y
        self.chip = (self.x * z_count + self.z) * 2 + self.y

    def sibling(self):
        return (self.x, self.z, self.y, 1 - self.c)

    def plane(self, k):
        return (self.x ^ (k // 2), self.z, self.y ^ (k % 2), self.c)

    def line(self, k):
        return (self.x, self.z ^ k, self.y, self.c)

    def any_chip(self, k):
        return (self.x ^ (k // 2 % 2), self.z ^ (k // 4), self.y ^ (k % 2), self.c)


def greet(peers):
    barrier = pltpu.get_barrier_semaphore()
    for peer in peers:
        pl.semaphore_signal(barrier, inc=1, device_id=peer, device_id_type=IDS)
    return lambda: pl.semaphore_wait(barrier, len(peers))


def trip(source, target, sems, index, device):
    return pltpu.make_async_remote_copy(
        src_ref=source,
        dst_ref=target,
        send_sem=sems[0].at[index],
        recv_sem=sems[1].at[index],
        device_id=device,
        device_id_type=IDS,
    )


def send(*given):
    copy = trip(*given)
    copy.start()
    return copy


def move(source, target, sems, index):
    copy = pltpu.make_async_copy(source, target, sems.at[index])
    copy.start()
    return copy


DMA = pltpu.SemaphoreType.DMA


def both(count):
    return [DMA((count,)), DMA((count,))]


def exchange(kernel, ident, out_shape, in_specs, out_specs, scratch, args, flops, sent):
    return pl.pallas_call(
        kernel,
        out_shape=out_shape,
        in_specs=in_specs,
        out_specs=out_specs,
        scratch_shapes=scratch,
        compiler_params=pltpu.CompilerParams(
            collective_id=ident, has_side_effects=True, vmem_limit_bytes=60 << 20
        ),
        cost_estimate=pl.CostEstimate(flops=flops, bytes_accessed=sent, transcendentals=0),
    )(*args)


def head_kernel(
    zc,
    group,
    t_ref,
    q_w,
    k_w,
    v_w,
    g_w,
    u_w,
    d_w,
    o_w,
    gain1,
    gain2,
    ng_ref,
    wg_ref,
    fg_ref,
    a_ref,
    og_ref,
    w_ref,
    f_ref,
    e_ref,
    wo_ref,
    rows,
    weights,
    packed,
    ls,
    w0,
    w1,
    n0,
    n1,
    f0,
    f1,
    z0,
    z1,
    b0,
    b1,
    s0,
    s1,
    o0,
    o1,
    p0,
    p1,
):
    me = Place(zc)
    chips = 4 * zc
    per = zc // group
    qw = group * HEAD_DIM
    width = t_ref.shape[1]
    met = greet([me.any_chip(k) for k in range(1, chips)] + [me.sibling()])
    first_gain, second_gain = column_of(low(gain1[...])), column_of(low(gain2[...]))
    for g in range(4):
        at = slice(g * qw, (g + 1) * qw)
        w_ref[g, :, :qw] = (first_gain * low(q_w[:, at])).astype(BF16)
        for pair in range(group // 2):
            at = lanes(g * group // 2 + pair)
            key, value = first_gain * low(k_w[:, at]), first_gain * low(v_w[:, at])
            for half in range(2):
                start = qw + (2 * pair + half) * PAIR
                w_ref[g, :, start : start + PAIR] = pair_up(key, half, value, half).astype(BF16)
    e_ref[...] = d_w[...].astype(BF16).reshape(e_ref.shape)
    wo_ref[...] = o_w[...].astype(BF16)
    x = t_ref[...].astype(F32)
    rows[0] = (x * lax.rsqrt(jnp.mean(x * x, axis=-1, keepdims=True) + EPS)).astype(BF16)
    met()
    here = og_ref.at[me.x, me.z, me.y, me.c]
    local = [move(w_ref.at[me.g], weights.at[me.x, me.z, me.y, me.c], ls, 0), move(wo_ref, here, ls, 1)]
    pieces = []
    for k in reversed(range(1, chips)):
        there = me.any_chip(k)
        their_g = there[0] * 2 + there[2]
        pieces.append(
            send(w_ref.at[their_g], weights.at[me.x, me.z, me.y, me.c], (w0, w1), k, there)
        )
    outs = [send(wo_ref, here, (o0, o1), k, me.line(k)) for k in range(1, zc)]
    blocks = [send(rows.at[0], rows.at[k], (n0, n1), k, me.plane(k)) for k in range(1, 4)]
    units = g_w.shape[1] // (4 * zc)
    for which, ref in enumerate((g_w, u_w)):
        for g in range(4):
            px, py = g // 2, g % 2
            if units % PAIR == 0:
                for z in range(zc):
                    at = ((px * zc + z) * 2 + py) * units
                    f_ref[g, which, :, z * units : (z + 1) * units] = (
                        second_gain * low(ref[:, at : at + units])
                    ).astype(BF16)
            else:
                for z in range(0, zc, 2):
                    near, far = (second_gain * low(ref[:, lanes(px * zc + i)]) for i in (z, z + 1))
                    f_ref[g, which, :, lanes(z // 2)] = pair_up(near, py, far, py).astype(BF16)
    wide = [
        move(f_ref.at[me.g], fg_ref.at[me.x, me.y, pl.ds(0, 2)], ls, 2),
        move(e_ref, fg_ref.at[:, :, 2], ls, 9),
    ]
    for k in range(1, 4):
        there = me.plane(k)
        their_g = there[0] * 2 + there[2]
        wide.append(
            send(f_ref.at[their_g], fg_ref.at[me.x, me.y, pl.ds(0, 2)], (f0, f1), k, there)
        )
    local[0].wait()
    arrivals = [pieces[chips - 1 - k] for k in range(1, chips)]
    relays = []
    for away in range(zc):
        for k in range(max(1, 4 * away), 4 * away + 4):
            arrivals[k - 1].wait()
        got = weights.at[:, me.z ^ away, :, me.c]
        relays.append(send(got, got, (s0, s1), 1 + away, me.sibling()))
    for copy in relays:
        copy.wait()
    kept = [move(weights, wg_ref, ls, 3)]

    def project(k, carry):
        @pl.when(k > 0)
        def _():
            trip(rows.at[0], rows.at[k], (n0, n1), k, me.plane(k)).wait_recv()

        at = (me.x ^ (k // 2)) * 2 + (me.y ^ (k % 2))
        out = dot(rows[k], weights[...].reshape(width, 3 * qw))
        for head in range(group):
            two, half = out[:, lanes(head // 2)], head % 2
            packed[head, k, :BLOCK] = pair_up(two[:BLOCK], half, two[BLOCK:], half).astype(BF16)
            start = qw + head * PAIR
            packed[head, k, BLOCK:] = out[:, start : start + PAIR].astype(BF16)
        for over in range(1, zc):
            trip(
                packed.at[(me.z ^ over) // per, k],
                a_ref.at[me.z, me.c, at],
                (z0, z1),
                k * zc + over,
                me.line(over),
            ).start()
        trip(
            packed.at[me.z // per, k], a_ref.at[me.z, me.c, at], (b0, b1), k * zc, me.sibling()
        ).start()
        pltpu.make_async_copy(
            packed.at[me.z // per, k], a_ref.at[me.z, me.c, at], ls.at[4 + k]
        ).start()
        return carry

    lax.fori_loop(0, 4, project, 0)
    kept.append(move(rows, ng_ref, ls, 8))
    for copy in outs + local[1:]:
        copy.wait()
    column = og_ref.at[me.x, :, me.y, me.c]
    out_rows = [send(column, column, (p0, p1), k, me.plane(k)) for k in range(1, 4)]

    def pass_on(step, carry):
        k, over = step // (zc - 1), step % (zc - 1) + 1
        at = (me.x ^ (k // 2)) * 2 + (me.y ^ (k % 2))
        there = me.z ^ over
        trip(
            packed.at[there // per, k],
            a_ref.at[me.z, me.c, at],
            (z0, z1),
            k * zc + over,
            me.line(over),
        ).wait()
        landed = a_ref.at[there, me.c, at]
        trip(landed, landed, (b0, b1), k * zc + over, me.sibling()).start()
        return carry

    lax.fori_loop(0, 4 * (zc - 1), pass_on, 0)
    for copy in out_rows:
        copy.wait()
    every = og_ref.at[:, :, :, me.c]
    last = send(every, every, (s0, s1), 0, me.sibling())

    def finish(step, carry):
        k, over = step // zc, step % zc
        at = (me.x ^ (k // 2)) * 2 + (me.y ^ (k % 2))
        landed = a_ref.at[me.z ^ over, me.c, at]
        trip(landed, landed, (b0, b1), k * zc + over, me.sibling()).wait()
        return carry

    lax.fori_loop(0, 4 * zc, finish, 0)
    for k in range(4):
        pltpu.make_async_copy(
            packed.at[me.z // per, k], a_ref.at[me.z, me.c, me.g], ls.at[4 + k]
        ).wait()
    for copy in [last] + kept + wide:
        copy.wait()
    for copy in blocks:
        copy.wait_send()


def head_exchange(zc, group, tokens, matrices, gains):
    chips = 4 * zc
    own, width = tokens.shape
    count = matrices[0].shape[0]
    piece = (count, 3 * group * HEAD_DIM)
    return exchange(
        functools.partial(head_kernel, zc, group),
        1,
        (
            struct((4, own, width)),
            struct((2, zc, 2, 2) + piece),
            struct((2, 2, 3, count, width)),
            struct((zc, 2, 4, BLOCK + own, PAIR)),
            struct((2, zc, 2, 2, count, width)),
        ),
        [VM] * 10,
        (ANY,) * 5,
        [
            pltpu.VMEM((4,) + piece, BF16),
            pltpu.VMEM((4, 2, count, width), BF16),
            pltpu.VMEM((2, 2, count, width), BF16),
            pltpu.VMEM((count, width), BF16),
            pltpu.VMEM((4, own, width), BF16),
            pltpu.VMEM((2, zc, 2, 2) + piece, BF16),
            pltpu.VMEM((group, 4, BLOCK + own, PAIR), BF16),
            DMA((10,)),
        ]
        + both(chips)
        + both(4)
        + both(4)
        + both(4 * zc)
        + both(4 * zc)
        + both(1 + zc)
        + both(zc)
        + both(4),
        (tokens, *matrices, *(g.reshape(1, -1) for g in gains)),
        2 * 4 * own * width * width,
        16 << 20,
    )


def join_kernel(zc, s_ref, x_ref, w_ref, ob_ref, r_ref, n_ref, mine, theirs, slabs, x_in, w_in, ls, b0, b1, c0, c1):
    me = Place(zc)
    chips = 4 * zc
    heads, per = slabs.shape[:2]
    loads = [move(w_ref, w_in, ls, 2), move(x_ref, x_in, ls, 3)]
    greet([me.any_chip(k) for k in range(1, chips)] + [me.sibling()])()
    other = send(s_ref.at[:, 1 - me.c], theirs, (b0, b1), 0, me.sibling())
    own = move(s_ref.at[:, me.c], mine, ls, 0)
    own.wait()
    other.wait()
    mine[...] = mine[...] + theirs[...]
    head = me.g * (heads // 4) + me.z // per
    place = me.z % per
    keep = move(mine.at[me.z, me.g], slabs.at[head, place], ls, 1)
    sends = []
    for k in reversed(range(1, chips)):
        there = me.any_chip(k)
        their_g = there[0] * 2 + there[2]
        sends.append(
            send(mine.at[there[1], their_g], slabs.at[head, place], (c0, c1), k, there)
        )
    keep.wait()
    for copy in sends:
        copy.wait()
    for block in range(2):
        for pair in range(heads // 2):
            sides = []
            for side in range(2):
                slab = slabs[2 * pair + side, 0].astype(F32)
                for extra in range(1, per):
                    slab = slab + slabs[2 * pair + side, extra].astype(F32)
                sides.append(slab)
            ob_ref[block * BLOCK : (block + 1) * BLOCK, lanes(pair)] = pair_up(
                sides[0], block, sides[1], block
            ).astype(BF16)
    for copy in loads:
        copy.wait()
    residual = x_in[...].astype(F32) + dot(ob_ref[...], w_in[...])
    r_ref[...] = residual
    mean = jnp.mean(residual * residual, axis=-1, keepdims=True)
    n_ref[...] = (residual * lax.rsqrt(mean + EPS)).astype(BF16)


def join_exchange(zc, heads, slabs, tokens, w_out):
    chips = 4 * zc
    per = 4 * zc // heads
    half = (zc,) + slabs.shape[2:]
    shape = tokens.shape
    return exchange(
        functools.partial(join_kernel, zc),
        2,
        (struct(shape), struct(shape, F32), struct(shape)),
        [ANY, ANY, ANY],
        (VM,) * 3,
        [
            pltpu.VMEM(half, BF16),
            pltpu.VMEM(half, BF16),
            pltpu.VMEM((heads, per) + slabs.shape[3:], BF16),
            pltpu.VMEM(shape, BF16),
            pltpu.VMEM(w_out.shape, BF16),
            DMA((4,)),
        ]
        + both(1)
        + both(chips),
        (slabs, tokens, w_out),
        0,
        0,
    )


def middle_kernel(zc, n_ref, ca_ref, cb_ref, cc_ref, cd_ref, *rest):
    f_refs, rest = rest[: zc // 2 + 1], rest[zc // 2 + 1 :]
    oa_ref, ob_ref, oc_ref, od_ref, cs_ref, sh_ref, rows, cots, gate_w, up_w, down_w, *rest = rest
    hid, dgate, dup, c_out, c_in, passed, early, stage, o_out, ls, n0, n1, c0, c1, f0, f1, h0, h1 = rest
    me = Place(zc)
    width = n_ref.shape[1]
    met = greet([me.plane(k) for k in range(1, 4)] + [me.line(1), me.sibling()])
    move(n_ref, rows.at[0], ls, 15).wait()
    met()
    farthest = send(rows.at[0], rows.at[3], (n0, n1), 3, me.plane(3))
    def places(there):
        return (
            gate_w.at[:, there, :, me.c],
            up_w.at[:, there, :, me.c],
            down_w.at[there, me.c],
        )

    given = dict(zip([1, *range(0, zc, 2)], f_refs))
    hops, loads = [[], [], []], [[], [], []]
    for k in range(2, zc, 2):
        for i, place in enumerate(places(me.z ^ k)):
            hops[i].append(send(given[k].at[:, :, i], place, (h0, h1), 3 * k + i, me.line(1)))
    for k, ref in given.items():
        for i, place in enumerate(places(me.z ^ k)):
            loads[i].append(send(ref.at[:, :, i], place, (f0, f1), 3 * k + i, me.sibling()))
            loads[i].append(move(ref.at[:, :, i], place, ls, 21 + 3 * k + i))
    for k, ref in enumerate((ca_ref, cb_ref, cc_ref, cd_ref)):
        loads[2].append(move(ref, cots.at[k], ls, 16 + k))
    farthest.wait_send()
    near_rows = [send(rows.at[0], rows.at[k], (n0, n1), k, me.plane(k)) for k in (1, 2)]

    def settle(i):
        for copy in hops[i]:
            copy.wait()
        for k in range(3, zc, 2):
            place = places(me.z ^ k)[i]
            loads[i].append(send(place, place, (f0, f1), 3 * k + i, me.sibling()))
        for copy in loads[i]:
            copy.wait()

    square = (width, width)
    half = n_ref.shape[0] // 2
    upper, lower = pl.ds(0, half), pl.ds(half, half)
    c_sems = (c0, c1)
    far_parts = [
        trip(c_out.at[3, upper], passed.at[0], c_sems, 0, me.plane(2)),
        trip(c_out.at[3, lower], passed.at[1], c_sems, 1, me.plane(1)),
    ]
    near_parts = [
        trip(c_out.at[1, lower], c_in.at[0, lower], c_sems, 2, me.plane(1)),
        trip(c_out.at[2, upper], c_in.at[1, upper], c_sems, 3, me.plane(2)),
        trip(c_out.at[1, upper], c_in.at[0, upper], c_sems, 4, me.plane(1)),
        trip(c_out.at[2, lower], c_in.at[1, lower], c_sems, 5, me.plane(2)),
    ]

    def both_products(k):
        gate_mat, up_mat = gate_w[...].reshape(square), up_w[...].reshape(square)
        return dot(rows[k], gate_mat), dot(rows[k], up_mat)

    def finish(k, gate, up):
        back = nt_dot(cots[k], down_w[...].reshape(square))
        sig = jax.nn.sigmoid(gate)
        soft = gate * sig
        hid[k] = (soft * up).astype(BF16)
        dgate[k] = (back * up * sig * (1.0 + gate * (1.0 - sig))).astype(BF16)
        dup[k] = (back * soft).astype(BF16)
        gate_mat, up_mat = gate_w[...].reshape(square), up_w[...].reshape(square)
        c_out[k] = (nt_dot(dgate[k], gate_mat) + nt_dot(dup[k], up_mat)).astype(BF16)

    settle(0)
    settle(1)
    trip(rows.at[0], rows.at[3], (n0, n1), 3, me.plane(3)).wait_recv()
    early[0], early[1] = both_products(3)
    settle(2)
    finish(3, early[0], early[1])
    for copy in far_parts:
        copy.start()

    def block(step, carry):
        k = jnp.where(step == 3, 0, step)

        @pl.when(step < 3)
        def _():
            trip(rows.at[0], rows.at[k], (n0, n1), k, me.plane(k)).wait_recv()

        finish(k, *both_products(k))

        @pl.when(step == 1)
        def _():
            near_parts[0].start()

        @pl.when(step == 2)
        def _():
            near_parts[1].start()

        return carry

    lax.fori_loop(1, 4, block, 0)
    far_parts[0].wait_recv()
    c_out[1, upper] = c_out[1, upper] + passed[0]
    near_parts[2].start()
    far_parts[1].wait_recv()
    c_out[2, lower] = c_out[2, lower] + passed[1]
    near_parts[3].start()
    all_rows = (4 * n_ref.shape[0], width)

    def weight_grad(left, right, slot):
        chunk = 256
        for first in range(0, width, chunk):
            value = tn_dot(left[:, first : first + chunk], right).astype(BF16)
            stage[slot, first : first + chunk] = value

    shares = []
    piece = width // (8 * zc)

    def share(slot, which):
        parts = stage.at[slot].reshape(2, zc, 2, 2, piece, width)
        for g in range(4):
            x, y = g // 2, g % 2
            shares.append(
                move(parts.at[x, :, y], sh_ref.at[:, :, 2 * g + which], ls, 12 + 2 * g + which)
            )

    flat = lambda ref: ref[...].reshape(all_rows)
    weight_grad(flat(rows), flat(dgate), 0)
    share(0, 0)
    weight_grad(flat(rows), flat(dup), 1)
    share(1, 1)
    weight_grad(flat(hid), flat(cots), 2)
    shares.append(
        move(stage.at[2].reshape(zc, 2, 4, piece, width), sh_ref.at[:, :, 8:], ls, 20)
    )

    for k, ref in enumerate((oa_ref, ob_ref, oc_ref, od_ref)):
        o_out[k] = dot(hid[k], down_w[...].reshape(square)).astype(BF16).reshape(ref.shape)
        shares.append(move(o_out.at[k], ref, ls, k))
    for copy in far_parts:
        copy.wait_send()
    for copy in near_parts:
        copy.wait()
    cs_ref[...] = c_out[0].astype(F32) + c_in[0].astype(F32) + c_in[1].astype(F32)
    for copy in shares:
        copy.wait()
    for copy in near_rows:
        copy.wait_send()


def middle_exchange(zc, normed, cots, weights):
    own, width = normed.shape
    piece = width // (8 * zc)
    blocks = pltpu.VMEM((4, own, width), BF16)
    wide = pltpu.VMEM((2, zc, 2, 2, piece, width), BF16)
    return exchange(
        functools.partial(middle_kernel, zc),
        3,
        (
            *[struct((zc, 2, piece, width))] * 4,
            struct((own, width), F32),
            struct((zc, 2, 12, piece, width)),
        ),
        [ANY] * (5 + len(weights)),
        (ANY,) * 4 + (VM, ANY),
        [blocks, blocks, wide, wide, pltpu.VMEM((zc, 2, 2, 2, piece, width), BF16)]
        + [blocks] * 4
        + [pltpu.VMEM((2, own, width), BF16), pltpu.VMEM((2, own // 2, width), BF16)]
        + [pltpu.VMEM((2, own, width), F32)]
        + [pltpu.VMEM((3, width, width), BF16), pltpu.VMEM((4, zc, 2, piece, width), BF16), DMA((21 + 3 * zc,))]
        + both(4)
        + both(6)
        + both(3 * zc)
        + both(3 * zc),
        (normed, *cots, *weights),
        2 * 4 * own * width * width * 9,
        64 << 20,
    )


def turn_kernel(
    zc,
    c_ref,
    t_ref,
    r_ref,
    wo_ref,
    ob_ref,
    yb_ref,
    yc_ref,
    dr_ref,
    do_ref,
    va_ref,
    vb_ref,
    vc_ref,
    vd_ref,
    nb_ref,
    nc_ref,
    slabs,
    stage,
    wo_in,
    ob_in,
    ls,
    d0,
    d1,
    b0,
    b1,
    y0,
    y1,
):
    me = Place(zc)
    chips = 4 * zc
    heads = slabs.shape[0]
    group = heads // 4
    per = zc // group
    width = t_ref.shape[1]
    met = greet([me.any_chip(k) for k in range(1, chips)] + [me.sibling()])
    loads = [move(wo_ref, wo_in, ls, 5), move(ob_ref, ob_in, ls, 6)]
    total, residual = c_ref[...], r_ref[...]
    scaling = lax.rsqrt(jnp.mean(residual * residual, axis=-1, keepdims=True) + EPS)
    normed = residual * scaling
    middle = jnp.mean(total * normed, axis=-1, keepdims=True)
    grad = t_ref[...].astype(F32) + scaling * (total - normed * middle)
    dr_ref[...] = grad
    narrow = grad.astype(BF16)
    loads[0].wait()
    back = nt_dot(narrow, wo_in[...])
    for pair in range(heads // 2):
        two = back[:, lanes(pair)]
        for side in range(2):
            slabs[2 * pair + side] = pair_up(two[:BLOCK], side, two[BLOCK:], side).astype(BF16)
    met()
    to = do_ref.at[me.z, me.c, me.g]
    own = move(slabs.at[me.g * group + me.z // per], to, ls, 0)
    sends = []
    for k in reversed(range(1, chips)):
        there = me.any_chip(k)
        head = (there[0] * 2 + there[2]) * group + there[1] // per
        sends.append(send(slabs.at[head], to, (d0, d1), k, there))
    sends.append(send(yb_ref, nb_ref, (y0, y1), 1, me.plane(1)))
    sends.append(send(yc_ref, nc_ref, (y0, y1), 2, me.plane(2)))
    chunk = 256
    loads[1].wait()
    attended = ob_in[...]
    for first in range(0, width, chunk):
        stage[first : first + chunk] = tn_dot(attended[:, first : first + chunk], narrow).astype(BF16)
    parts = stage.reshape(2, zc, 2, 2, width // (8 * zc), width)
    keeps = []
    for k, ref in enumerate((va_ref, vb_ref, vc_ref, vd_ref)):
        there = me.plane(k)
        keeps.append(move(parts.at[there[0], :, there[2]], ref, ls, 1 + k))
    own.wait()
    for copy in sends[:-2]:
        copy.wait()
    half = do_ref.at[:, me.c]
    relay = send(half, half, (b0, b1), 0, me.sibling())
    for copy in keeps + sends[-2:]:
        copy.wait()
    relay.wait()


def turn_exchange(zc, c_sum, cotangent, residual, w_out, attn_rows, near):
    chips = 4 * zc
    own, width = cotangent.shape
    heads = width // HEAD_DIM
    return exchange(
        functools.partial(turn_kernel, zc),
        6,
        (
            struct((own, width), F32),
            struct((zc, 2, 4, BLOCK, PAIR)),
            *[struct((zc, 2, width // (8 * zc), width))] * 6,
        ),
        [VM] * 3 + [ANY] * 4,
        (VM,) + (ANY,) * 7,
        [
            pltpu.VMEM((heads, BLOCK, PAIR), BF16),
            pltpu.VMEM((width, width), BF16),
            pltpu.VMEM((width, width), BF16),
            pltpu.VMEM((own, width), BF16),
            DMA((7,)),
        ]
        + both(chips)
        + both(1)
        + both(3),
        (c_sum, cotangent, residual, w_out, attn_rows, *near),
        2 * 2 * own * width * width,
        8 << 20,
    )


def tail_kernel(
    zc,
    d_ref,
    n_any,
    w_any,
    x_any,
    g_any,
    f_ref,
    r_ref,
    ya_ref,
    yb_ref,
    yc_ref,
    yd_ref,
    va_ref,
    vb_ref,
    vc_ref,
    vd_ref,
    tg_ref,
    gw_ref,
    go_ref,
    gf_ref,
    out_ref,
    n_ref,
    w_ref,
    x_ref,
    g_ref,
    r_in,
    y_in,
    o_mine,
    o_theirs,
    o_land,
    mine,
    theirs,
    landed,
    grads,
    c_out,
    c_in,
    stage,
    other_w,
    ls,
    b0,
    b1,
    z0,
    z1,
    c0,
    c1,
    s0,
    s1,
    w0,
    w1,
    q0,
    q1,
    f0,
    f1,
):
    me = Place(zc)
    chips = 4 * zc
    group, per = landed.shape[:2]
    qw = group * HEAD_DIM
    greet([me.any_chip(k) for k in range(1, chips)] + [me.sibling()])()
    head, place = me.z // per, me.z % per

    def slot(k):
        return (me.x ^ (k // 2)) * 2 + (me.y ^ (k % 2))

    order = (3, 2, 1, 0)
    halves = []
    for k in order:
        halves.append(
            (
                send(d_ref.at[:, 1 - me.c, slot(k)], theirs.at[k], (b0, b1), k, me.sibling()),
                move(d_ref.at[:, me.c, slot(k)], mine.at[k], ls, k),
            )
        )
    given = ((w_any, w_ref), (n_any, n_ref), (g_any, g_ref), (x_any, x_ref))
    loads = [move(source, target, ls, 20 + i) for i, (source, target) in enumerate(given)]
    f_parts = [move(f_ref.at[pl.ds(2 * me.g, 2)], gf_ref.at[me.g], ls, 10)]
    for k in (3, 1, 2):
        there = me.plane(k)
        part = f_ref.at[pl.ds(2 * (there[0] * 2 + there[2]), 2)]
        f_parts.append(send(part, gf_ref.at[me.g], (f0, f1), k, there))
    out_parts = [move(r_ref, r_in, ls, 11)]
    for i, ref in enumerate((ya_ref, yb_ref, yc_ref, yd_ref)):
        out_parts.append(move(ref, y_in.at[i, 0], ls, 12 + i))
    for i, ref in enumerate((va_ref, vb_ref, vc_ref, vd_ref)):
        out_parts.append(move(ref, y_in.at[i, 1], ls, 16 + i))
    for k, (far, near) in zip(order, halves):
        near.wait()
        far.wait()
        mine[k] = mine[k] + theirs[k]
        for over in range(1, zc):
            send(
                mine.at[k, me.z ^ over],
                landed.at[head, place, k],
                (z0, z1),
                k * zc + over,
                me.line(over),
            )
        move(mine.at[k, me.z], landed.at[head, place, k], ls, 4 + k)

    for copy in out_parts + loads:
        copy.wait()
    final = r_in[...]
    o_sum = jnp.zeros(o_mine.shape, F32)
    for i in range(4):
        final = final + y_in[i, 0].astype(F32).reshape(final.shape)
        o_sum = o_sum + y_in[i, 1].astype(F32)
    out_ref[...] = final.astype(BF16)
    o_mine[...] = o_sum.astype(BF16)
    o_swap = send(o_mine.at[:, 1 - me.c], o_theirs, (s0, s1), 1, me.sibling())

    def block(step, carry):
        k = 3 - step
        pltpu.make_async_copy(
            mine.at[k, me.z], landed.at[head, place, k], ls.at[4 + k]
        ).wait()
        for over in range(1, zc):
            trip(
                mine.at[k, me.z ^ over],
                landed.at[head, place, k],
                (z0, z1),
                k * zc + over,
                me.line(over),
            ).wait()
        for pair in range(group // 2):
            sides = []
            for side in range(2):
                h = 2 * pair + side
                slab = landed[h, 0, k]
                for extra in range(1, per):
                    slab = slab + landed[h, extra, k]
                start = qw + h * PAIR
                grads[k, :, start : start + PAIR] = slab[BLOCK:]
                sides.append(slab[:BLOCK].astype(F32))
            for b in range(2):
                grads[k, b * BLOCK : (b + 1) * BLOCK, lanes(pair)] = pair_up(
                    sides[0], b, sides[1], b
                ).astype(BF16)

        @pl.when(k > 0)
        def _():
            c_out[k] = nt_dot(grads[k], w_ref[...]).astype(BF16)
            trip(c_out.at[k], c_in.at[k], (c0, c1), k, me.plane(k)).start()

        return carry

    o_swap.wait()
    o_theirs[...] = o_theirs[...] + o_mine[:, me.c]
    sends = [
        send(o_theirs.at[me.z ^ k], o_land.at[k], (q0, q1), k, me.line(k)) for k in range(1, zc)
    ]
    lax.fori_loop(0, 4, block, 0)
    width, cols = w_ref.shape
    all_rows = 4 * n_ref.shape[1]
    normed_all = n_ref[...].reshape(all_rows, width)
    grads_all = grads[...].reshape(all_rows, cols)
    piece = stage.shape[2]
    chunk = 256
    each = chunk // (2 * piece)
    swaps = []
    for first in range(0, width, chunk):
        value = tn_dot(normed_all[:, first : first + chunk], grads_all).astype(BF16)
        at = first // (2 * piece)
        stage[at : at + each] = value.reshape(each, 2, piece, cols)
        swaps.append(
            send(
                stage.at[at : at + each, 1 - me.c],
                other_w.at[at : at + each],
                (s0, s1),
                2 + first // chunk,
                me.sibling(),
            )
        )
    c_out[0] = nt_dot(grads[0], w_ref[...]).astype(BF16)
    for swap in swaps:
        swap.wait()

    def add(i, carry):
        other_w[i] = stage[i, me.c] + other_w[i]
        return carry

    lax.fori_loop(0, chips, add, 0)
    stay = move(other_w.at[me.chip], gw_ref.at[me.z, me.g], ls, 8)
    for k in reversed(range(1, chips)):
        there = me.any_chip(k)
        chip = (there[0] * zc + there[1]) * 2 + there[2]
        sends.append(send(other_w.at[chip], gw_ref.at[me.z, me.g], (w0, w1), k, there))
    total = c_out[0].astype(F32)
    for k in range(1, 4):
        trip(c_out.at[k], c_in.at[k], (c0, c1), k, me.plane(k)).wait()
        total = total + c_in[k].astype(F32)
    x = x_ref[...].astype(F32)
    scaling = lax.rsqrt(jnp.mean(x * x, axis=-1, keepdims=True) + EPS)
    normed = x * scaling
    middle = jnp.mean(total * normed, axis=-1, keepdims=True)
    tg_ref[...] = (g_ref[...] + scaling * (total - normed * middle)).astype(BF16)
    stay.wait()
    for copy in sends + f_parts:
        copy.wait()
    o_sum = o_theirs[me.z].astype(F32)
    for k in range(1, zc):
        o_sum = o_sum + o_land[k].astype(F32)
    go_ref[...] = o_sum


def tail_exchange(zc, group, slab_grads, n_all, weights, tokens, residual_grad, shares, residual, packs):
    chips = 4 * zc
    per = zc // group
    own, width = tokens.shape
    cols = weights.shape[1]
    slab = slab_grads.shape[3:]
    piece = width // (2 * chips)
    blocks = pltpu.VMEM((4, own, width), BF16)
    return exchange(
        functools.partial(tail_kernel, zc),
        4,
        (
            struct((own, width)),
            struct((zc, 4, piece, cols)),
            struct((piece, width), F32),
            struct((4, 2, piece, width)),
            struct((own, width)),
        ),
        [ANY] * 15,
        (VM, ANY, VM, ANY, VM),
        [
            pltpu.VMEM((4, own, width), BF16),
            pltpu.VMEM((width, cols), BF16),
            pltpu.VMEM((own, width), BF16),
            pltpu.VMEM((own, width), F32),
            pltpu.VMEM((own, width), F32),
            pltpu.VMEM((4, 2, zc, 2, piece, width), BF16),
            pltpu.VMEM((zc, 2, piece, width), BF16),
            pltpu.VMEM((zc, piece, width), BF16),
            pltpu.VMEM((zc, piece, width), BF16),
            pltpu.VMEM((4, zc) + slab, BF16),
            pltpu.VMEM((4, zc) + slab, BF16),
            pltpu.VMEM((group, per, 4) + slab, BF16),
            pltpu.VMEM((4, own, cols), BF16),
            blocks,
            blocks,
            pltpu.VMEM((chips, 2, piece, cols), BF16),
            pltpu.VMEM((chips, piece, cols), BF16),
            DMA((24,)),
        ]
        + both(4)
        + both(4 * zc)
        + both(4)
        + both(2 + width // 256)
        + both(chips)
        + both(zc)
        + both(4),
        (slab_grads, n_all, weights, tokens, residual_grad, shares, residual, *packs),
        2 * 4 * own * width * cols * 2,
        24 << 20,
    )


def last_kernel(
    zc,
    group,
    t_any,
    o_any,
    wo_any,
    gw_any,
    gf_any,
    ds_any,
    q_any,
    k_any,
    v_any,
    g_any,
    u_any,
    gain1,
    gain2,
    tg_ref,
    out_ref,
    go_ref,
    g1_ref,
    q_ref,
    k_ref,
    v_ref,
    g2_ref,
    g_ref,
    u_ref,
    d_ref,
    gw_ref,
    gf_ref,
    ds_ref,
    q_w,
    k_w,
    v_w,
    g_w,
    u_w,
    ls,
):
    given = (gw_any, q_any, k_any, v_any, gf_any, g_any, u_any, ds_any, t_any, o_any, wo_any)
    taken = (gw_ref, q_w, k_w, v_w, gf_ref, g_w, u_w, ds_ref, tg_ref, out_ref, go_ref)
    copies = [move(a, b, ls, i) for i, (a, b) in enumerate(zip(given, taken))]
    for copy in copies:
        copy.wait()
    d_ref[...] = ds_ref[8:].astype(F32).reshape(d_ref.shape)
    first_gain, second_gain = column_of(low(gain1[...])), column_of(low(gain2[...]))
    count = q_w.shape[0]
    qw = group * HEAD_DIM
    score = jnp.zeros((count, PAIR), F32)
    for g in range(4):
        raw = gw_ref[0, g].astype(F32)
        for z in range(1, zc):
            raw = raw + gw_ref[z, g].astype(F32)
        for pair in range(group // 2):
            at = lanes(g * group // 2 + pair)
            start = qw + 2 * pair * PAIR
            even, odd = raw[:, start : start + PAIR], raw[:, start + PAIR : start + 2 * PAIR]
            query = raw[:, lanes(pair)]
            key, value = pair_up(even, 0, odd, 0), pair_up(even, 1, odd, 1)
            score = score + query * low(q_w[:, at]) + key * low(k_w[:, at]) + value * low(v_w[:, at])
            q_ref[:, at] = first_gain * query
            k_ref[:, at] = first_gain * key
            v_ref[:, at] = first_gain * value
    g1_ref[...] = row_of(jnp.sum(score, axis=1, keepdims=True))
    units = g_w.shape[1] // (4 * zc)
    score = jnp.zeros((count, PAIR), F32)
    for which, (weight, target) in enumerate(((g_w, g_ref), (u_w, u_ref))):
        for chunk in range(weight.shape[1] // PAIR):
            if units % PAIR == 0:
                owner, piece = divmod(chunk, units // PAIR)
                x, z, y = owner // (2 * zc), owner // 2 % zc, owner % 2
                raw = gf_ref[2 * x + y, which, :, lanes(z * units // PAIR + piece)].astype(F32)
            else:
                x, z = chunk // zc, chunk % zc
                near = gf_ref[2 * x, which, :, lanes(z // 2)].astype(F32)
                far = gf_ref[2 * x + 1, which, :, lanes(z // 2)].astype(F32)
                raw = pair_up(near, z % 2, far, z % 2)
            score = score + raw * low(weight[:, lanes(chunk)])
            target[:, lanes(chunk)] = second_gain * raw
    g2_ref[...] = row_of(jnp.sum(score, axis=1, keepdims=True))


def last_step(zc, group, tokens_grad, output, out_share, w_all, f_all, shares, matrices, gains):
    own, width = output.shape
    count, hidden = matrices[3].shape
    return pl.pallas_call(
        functools.partial(last_kernel, zc, group),
        out_shape=(
            struct((own, width)),
            struct((own, width)),
            struct((count, width), F32),
            struct((1, count), F32),
            struct((count, width), F32),
            struct((count, width), F32),
            struct((count, width), F32),
            struct((1, count), F32),
            struct((count, hidden), F32),
            struct((count, hidden), F32),
            struct((4 * count, width), F32),
        ),
        in_specs=[ANY] * 11 + [VM] * 2,
        out_specs=(VM,) * 11,
        scratch_shapes=[
            pltpu.VMEM(v.shape, v.dtype) for v in (w_all, f_all, shares, *matrices)
        ]
        + [DMA((11,))],
        compiler_params=pltpu.CompilerParams(vmem_limit_bytes=60 << 20),
    )(
        tokens_grad,
        output,
        out_share,
        w_all,
        f_all,
        shares,
        *matrices,
        *(g.reshape(1, -1) for g in gains),
    )


def segment_start(position, lens_ref):
    start = jnp.zeros_like(position)
    end = 0
    for j in range(lens_ref.shape[0]):
        end = end + lens_ref[j]
        start = jnp.where(position >= end, end, start)
    return start


def note_tiles(workers, worker, tiles, lens_ref, mine):
    turns = tiles // workers

    def snake(turn, carry):
        forward = turn * workers + worker
        backward = turn * workers + workers - 1 - worker
        mine[turn] = jnp.where((turn & 1) == 0, forward, backward)
        return carry

    def weigh(step, ahead):
        turn = turns - 1 - step
        loads = []
        for tile in (2 * turn, 2 * turn + 1):
            first, _, _, last = key_bounds(tile * QTILE, lens_ref)
            loads.append(last - first)
        lighter_first = loads[0] <= loads[1]
        first_to_zero = jnp.where(ahead > 0, lighter_first, loads[0] > loads[1])
        mine[turn] = 2 * turn + jnp.where(first_to_zero, worker, 1 - worker)
        return ahead + jnp.where(first_to_zero, loads[0] - loads[1], loads[1] - loads[0])

    if workers == 2:
        lax.fori_loop(0, turns, weigh, 0)
    else:
        lax.fori_loop(0, turns, snake, 0)


def key_bounds(first, lens_ref):
    low_start = segment_start(first, lens_ref)
    high_start = segment_start(first + QTILE - 1, lens_ref)
    low = low_start // KTILE
    high = (first + QTILE + KTILE - 1) // KTILE
    plain = jnp.clip((high_start + KTILE - 1) // KTILE, low, high)
    stop = jnp.clip((first + 1) // KTILE, plain, high)
    return low, plain, stop, high


def visible(first, tile, starts):
    key = tile * KTILE + lax.broadcasted_iota(jnp.int32, (KTILE, QTILE), 0)
    query = first + lax.broadcasted_iota(jnp.int32, (KTILE, QTILE), 1)
    return (key <= query) & (key >= starts)


def note_places(anchor_ref, inv):
    def note(i, carry):
        inv[anchor_ref[i]] = i
        return carry

    lax.fori_loop(0, anchor_ref.shape[0], note, 0)


def half_lanes(rows, half):
    lane = lax.broadcasted_iota(jnp.int32, rows.shape, 1)
    return jnp.where((lane // HEAD_DIM) == half, rows, jnp.zeros_like(rows))


def fold(rows, columns, first):
    row = lax.broadcasted_iota(jnp.int32, (rows, columns), 0)
    column = lax.broadcasted_iota(jnp.int32, (rows, columns), 1)
    return (row % HEAD_DIM == column - first).astype(F32).astype(BF16)


def unfold(rows, columns, first):
    row = lax.broadcasted_iota(jnp.int32, (rows, columns), 0)
    column = lax.broadcasted_iota(jnp.int32, (rows, columns), 1)
    return (column % HEAD_DIM == row - first).astype(F32).astype(BF16)


def forward_kernel(
    workers,
    anchor_ref,
    lens_ref,
    who_ref,
    a_any,
    o_ref,
    kv_any,
    kvt_any,
    q_any,
    qt_any,
    ot_any,
    l_any,
    inv,
    mine,
    raw,
    a_ref,
    kv_ref,
    kvt_ref,
    q_ref,
    qt_ref,
    ot_ref,
    l_ref,
    ls,
    ts,
):
    load = move(a_any, a_ref, ls, 0)
    blocks = anchor_ref.shape[0]
    turns = qt_ref.shape[0]
    per = QTILE // BLOCK
    worker = who_ref[0]
    note_places(anchor_ref, inv)
    note_tiles(workers, worker, turns * workers, lens_ref, mine)
    o_ref[...] = jnp.zeros_like(o_ref)
    same = selection(PAIR, PAIR, 0)
    load.wait()

    def order(step, carry):
        for b in range(per):
            i = step * per + b
            where = inv[i]
            slab, half = where >> 1, where & 1
            at = pl.ds(pl.multiple_of(i * BLOCK, BLOCK), BLOCK)
            kv_ref[at, :] = a_ref[slab, pl.ds(pl.multiple_of(BLOCK + half * BLOCK, BLOCK), BLOCK), :]
        return carry

    lax.fori_loop(0, blocks // per, order, 0)
    leaving = [move(kv_ref, kv_any, ls, 1)]

    def flip(step, carry):
        at = pl.ds(pl.multiple_of(step * TURNED, TURNED), TURNED)
        kvt_ref[:, at] = nt_dot(same, kv_ref[at, :]).astype(BF16)
        return carry

    lax.fori_loop(0, blocks * BLOCK // TURNED, flip, 0)
    leaving.append(move(kvt_ref, kvt_any, ls, 2))
    kept = ((q_ref, q_any), (qt_ref, qt_any), (ot_ref, ot_any), (l_ref, l_any))

    def leave(turn, i):
        source, target = kept[i]
        return pltpu.make_async_copy(source.at[turn], target.at[turn], ts.at[i, turn])

    def one_tile(turn, carry):
        tile = mine[turn]
        first = tile * QTILE
        for b in range(per):
            where = inv[tile * per + b]
            raw[b * BLOCK : (b + 1) * BLOCK, :] = half_lanes(a_ref[where >> 1, :BLOCK, :], where & 1)
        q_ref[turn] = (dot(raw[...], fold(PAIR, PAIR, 0)) * 0.125).astype(BF16)
        qt_ref[turn] = (nt_dot(unfold(PAIR, PAIR, 0), raw[...]) * 0.125).astype(BF16)
        query = qt_ref[turn]
        starts = segment_start(first + lax.broadcasted_iota(jnp.int32, (1, QTILE), 1), lens_ref)
        low, plain, stop, high = key_bounds(first, lens_ref)

        def step(masked, kt, state):
            top, total, acc = state
            at = pl.ds(pl.multiple_of(kt * KTILE, KTILE), KTILE)
            scores = dot(kv_ref[at, :], query)
            if masked:
                scores = jnp.where(visible(first, kt, starts), scores, MASKED)
            new_top = jnp.maximum(top, jnp.max(scores, axis=0, keepdims=True))
            factor = jnp.exp(top - new_top)
            weights = jnp.exp(scores - new_top)
            total = total * factor + jnp.sum(weights, axis=0, keepdims=True)
            acc = acc * factor + dot(kvt_ref[HEAD_DIM:, at], weights.astype(BF16))
            return (new_top, total, acc)

        state = (
            jnp.full((1, QTILE), LOWEST, F32),
            jnp.zeros((1, QTILE), F32),
            jnp.zeros((HEAD_DIM, QTILE), F32),
        )
        state = lax.fori_loop(low, plain, functools.partial(step, True), state)
        state = lax.fori_loop(plain, stop, functools.partial(step, False), state)
        top, total, acc = lax.fori_loop(stop, high, functools.partial(step, True), state)
        out = acc / total
        ot_ref[turn] = out
        l_ref[turn] = top + jnp.log(total)
        for i in range(4):
            leave(turn, i).start()
        wide = tn_dot(out.astype(BF16), unfold(HEAD_DIM, PAIR, 0)).astype(BF16)
        for b in range(per):
            where = inv[tile * per + b]
            slab = where >> 1
            o_ref[slab] = o_ref[slab] + half_lanes(wide[b * BLOCK : (b + 1) * BLOCK], where & 1)
        return carry

    lax.fori_loop(0, turns, one_tile, 0)

    def left(turn, carry):
        for i in range(4):
            leave(turn, i).wait()
        return carry

    lax.fori_loop(0, turns, left, 0)
    for copy in leaving:
        copy.wait()


def attention_forward(workers, anchors, lengths, who, packed):
    slabs = packed.shape[0]
    rows = slabs * 2 * BLOCK
    turns = rows // QTILE // workers
    return pl.pallas_call(
        functools.partial(forward_kernel, workers),
        out_shape=(
            struct((slabs, BLOCK, PAIR)),
            struct((rows, PAIR)),
            struct((PAIR, rows)),
            struct((turns, QTILE, PAIR)),
            struct((turns, PAIR, QTILE)),
            struct((turns, HEAD_DIM, QTILE), F32),
            struct((turns, 1, QTILE), F32),
        ),
        in_specs=[SM, SM, SM, ANY],
        out_specs=(VM,) + (ANY,) * 6,
        scratch_shapes=[
            pltpu.SMEM((2 * slabs,), jnp.int32),
            pltpu.SMEM((turns,), jnp.int32),
            pltpu.VMEM((QTILE, PAIR), BF16),
            pltpu.VMEM(packed.shape, BF16),
            pltpu.VMEM((rows, PAIR), BF16),
            pltpu.VMEM((PAIR, rows), BF16),
            pltpu.VMEM((turns, QTILE, PAIR), BF16),
            pltpu.VMEM((turns, PAIR, QTILE), BF16),
            pltpu.VMEM((turns, HEAD_DIM, QTILE), F32),
            pltpu.VMEM((turns, 1, QTILE), F32),
            DMA((3,)),
            DMA((4, turns)),
        ],
        compiler_params=pltpu.CompilerParams(vmem_limit_bytes=60 << 20),
        cost_estimate=pl.CostEstimate(
            flops=rows * rows * 64, bytes_accessed=rows * 1024, transcendentals=rows * rows // 8
        ),
    )(anchors, lengths, who, packed)


def backward_kernel(
    workers,
    anchor_ref,
    lens_ref,
    who_ref,
    d_ref,
    kv_ref,
    kvt_ref,
    q_ref,
    qt_ref,
    ot_ref,
    l_ref,
    g_ref,
    inv,
    mine,
    raw,
    both_rows,
    dt,
    acc,
):
    blocks = anchor_ref.shape[0]
    turns = qt_ref.shape[0]
    per = QTILE // BLOCK
    worker = who_ref[0]
    note_places(anchor_ref, inv)
    note_tiles(workers, worker, turns * workers, lens_ref, mine)
    acc[...] = jnp.zeros_like(acc)
    g_ref[:, :BLOCK, :] = jnp.zeros((g_ref.shape[0], BLOCK, PAIR), BF16)

    def one_tile(turn, carry):
        tile = mine[turn]
        first = tile * QTILE
        for b in range(per):
            where = inv[tile * per + b]
            raw[b * BLOCK : (b + 1) * BLOCK, :] = half_lanes(d_ref[where >> 1], where & 1)
        both_rows[:QTILE] = q_ref[turn]
        both_rows[QTILE:] = dot(raw[...], fold(PAIR, PAIR, HEAD_DIM)).astype(BF16)
        dt[...] = nt_dot(unfold(PAIR, PAIR, HEAD_DIM), raw[...]).astype(BF16)
        query, grad = qt_ref[turn], dt[...]
        norm = l_ref[turn]
        delta = jnp.sum(grad[HEAD_DIM:].astype(F32) * ot_ref[turn], axis=0, keepdims=True)
        starts = segment_start(first + lax.broadcasted_iota(jnp.int32, (1, QTILE), 1), lens_ref)
        low, plain, stop, high = key_bounds(first, lens_ref)

        def step(masked, kt, total):
            at = pl.ds(pl.multiple_of(kt * KTILE, KTILE), KTILE)
            keys = kv_ref[at, :]
            scores = dot(keys, query)
            if masked:
                scores = jnp.where(visible(first, kt, starts), scores, MASKED)
            weights = jnp.exp(scores - norm)
            score_grad = (weights * (dot(keys, grad) - delta)).astype(BF16)
            both_grads = jnp.concatenate([score_grad, weights.astype(BF16)], axis=1)
            acc[at, :] += dot(both_grads, both_rows[...])
            return total + dot(kvt_ref[:HEAD_DIM, at], score_grad)

        total = jnp.zeros((HEAD_DIM, QTILE), F32)
        total = lax.fori_loop(low, plain, functools.partial(step, True), total)
        total = lax.fori_loop(plain, stop, functools.partial(step, False), total)
        total = lax.fori_loop(stop, high, functools.partial(step, True), total)
        wide = tn_dot((total * 0.125).astype(BF16), unfold(HEAD_DIM, PAIR, 0)).astype(BF16)
        for b in range(per):
            where = inv[tile * per + b]
            slab = where >> 1
            g_ref[slab, :BLOCK] = g_ref[slab, :BLOCK] + half_lanes(
                wide[b * BLOCK : (b + 1) * BLOCK], where & 1
            )
        return carry

    lax.fori_loop(0, turns, one_tile, 0)

    def place(step, carry):
        for b in range(per):
            i = step * per + b
            where = inv[i]
            slab, half = where >> 1, where & 1
            at = pl.ds(pl.multiple_of(i * BLOCK, BLOCK), BLOCK)
            to = pl.ds(pl.multiple_of(BLOCK + half * BLOCK, BLOCK), BLOCK)
            g_ref[slab, to, :] = acc[at, :].astype(BF16)
        return carry

    lax.fori_loop(0, blocks // per, place, 0)


def attention_backward(workers, anchors, lengths, who, grads, kept):
    slabs = grads.shape[0]
    rows = slabs * 2 * BLOCK
    return pl.pallas_call(
        functools.partial(backward_kernel, workers),
        out_shape=struct((slabs, 3 * BLOCK, PAIR)),
        in_specs=[SM, SM, SM] + [VM] * 7,
        out_specs=VM,
        scratch_shapes=[
            pltpu.SMEM((2 * slabs,), jnp.int32),
            pltpu.SMEM((rows // QTILE // workers,), jnp.int32),
            pltpu.VMEM((QTILE, PAIR), BF16),
            pltpu.VMEM((2 * QTILE, PAIR), BF16),
            pltpu.VMEM((PAIR, QTILE), BF16),
            pltpu.VMEM((rows, PAIR), F32),
        ],
        compiler_params=pltpu.CompilerParams(vmem_limit_bytes=60 << 20),
        cost_estimate=pl.CostEstimate(
            flops=rows * rows * 160, bytes_accessed=rows * 1024, transcendentals=rows * rows // 8
        ),
    )(anchors, lengths, who, grads, *kept)


def around(value, k):
    return lax.ppermute(value, ("head", "y"), [(i, i ^ k) for i in range(4)])


def along(value, k):
    return lax.ppermute(value, "z", [(i, i ^ k) for i in range(lax.axis_size("z"))])


def doubling(pieces, first, last):
    while first >= last:
        pieces = {**pieces, **{k + first: along(pieces[k], first) for k in pieces}}
        first //= 2
    return pieces


def body(
    zc,
    tokens,
    cotangent,
    norm1_gain,
    w_query,
    w_key,
    w_value,
    w_out,
    norm2_gain,
    w_gate,
    w_up,
    w_down,
    block_anchor,
    seq_lengths,
):
    width = tokens.shape[1]
    heads = width // HEAD_DIM
    group = heads // 4
    per_head = zc // group
    workers = 2 * per_head
    feature_rows = w_query.shape[0]

    n1_all, qkv_w, ffn_own, by_head, out_mat = head_exchange(
        zc,
        group,
        tokens,
        (w_query, w_key, w_value, w_gate, w_up, w_down, w_out),
        (norm1_gain, norm2_gain),
    )
    qkv_w = qkv_w.reshape(width, 3 * group * HEAD_DIM)

    out_mat, sent = lax.optimization_barrier((out_mat.reshape(width, width), cotangent))
    cots = [cotangent] + [around(sent, k) for k in range(1, 4)]
    ffn_parts = doubling({0: ffn_own}, zc // 2, 2)
    close = along(ffn_own, 1)

    anchors = jnp.transpose(block_anchor.reshape(2, zc, 2, 2, 2), (1, 3, 0, 2, 4)).reshape(-1)
    who = ((lax.axis_index("z") % per_head) * 2 + lax.axis_index("core")).astype(jnp.int32).reshape(1)
    slab_count = zc * 8
    o_slabs, *kept = attention_forward(
        workers, anchors, seq_lengths, who, by_head.reshape((slab_count,) + by_head.shape[3:])
    )
    attn_rows, residual, normed_two = join_exchange(
        zc, heads, o_slabs.reshape(zc, 2, 4, BLOCK, PAIR), tokens, out_mat
    )
    *out_parts, c_sum, shares = middle_exchange(
        zc, normed_two, cots, [close] + [ffn_parts[k] for k in range(0, zc, 2)]
    )
    shares = lax.psum_scatter(
        shares.reshape(zc * 2 * 12, feature_rows, width), ("z", "core"), scatter_dimension=0, tiled=True
    )
    residual_grad, do_heads, *packs = turn_exchange(
        zc, c_sum, cotangent, residual, out_mat, attn_rows, out_parts[1:3]
    )
    w_grads, near = packs[:4], packs[4:]
    do_heads, far = lax.optimization_barrier((do_heads, out_parts[3]))
    packs = [out_parts[0], *near, around(far, 3), w_grads[0]]
    packs += [around(w_grads[k], k) for k in range(1, 4)]
    grad_heads = attention_backward(
        workers, anchors, seq_lengths, who, do_heads.reshape(slab_count, BLOCK, PAIR), kept
    )
    tokens_grad, w_all, out_share, f_all, output = tail_exchange(
        zc,
        group,
        grad_heads.reshape(zc, 2, 4, 3 * BLOCK, PAIR),
        n1_all,
        qkv_w,
        tokens,
        residual_grad,
        shares,
        residual,
        packs,
    )
    (
        tokens_grad,
        output,
        out_grad,
        gain1_grad,
        query_grad,
        key_grad,
        value_grad,
        gain2_grad,
        gate_grad,
        up_grad,
        down_grad,
    ) = last_step(
        zc,
        group,
        tokens_grad,
        output,
        out_share,
        w_all,
        f_all,
        shares,
        (w_query, w_key, w_value, w_gate, w_up),
        (norm1_gain, norm2_gain),
    )
    return (
        output,
        tokens_grad,
        gain1_grad.reshape(-1),
        query_grad,
        key_grad,
        value_grad,
        out_grad,
        gain2_grad.reshape(-1),
        gate_grad,
        up_grad,
        down_grad,
    )


def solution(mesh):
    blk = mesh.shape["blk"]
    grid = Mesh(mesh.devices.reshape(mesh.shape["head"], blk // 4, 2, 2), AXES)
    rows, vector, whole = P(AXES, None), P(AXES), P()
    return jax.shard_map(
        functools.partial(body, blk // 4),
        mesh=grid,
        in_specs=(rows, rows, vector, rows, rows, rows, rows, vector, rows, rows, rows, whole, whole),
        out_specs=(rows, rows, vector, rows, rows, rows, rows, vector, rows, rows, rows),
        check_vma=False,
    )
```

```python
import functools

import jax
import jax.numpy as jnp
from jax import lax
from jax.experimental import pallas as pl
from jax.experimental.pallas import tpu as pltpu
from jax.sharding import Mesh
from jax.sharding import PartitionSpec as P

HEAD_DIM = 64
BLOCK = 128
PAIR = 128
EPS = 1e-06
MASKED = -1e30
LOWEST = -1e20
QTILE = 512
KTILE = 512
TURNED = 2048
AXES = ("head", "z", "y", "core")
IDS = pl.DeviceIdType.MESH
F32 = jnp.float32
BF16 = jnp.bfloat16
ANY = pl.BlockSpec(memory_space=pl.ANY)
VM = pl.BlockSpec(memory_space=pltpu.VMEM)
SM = pl.BlockSpec(memory_space=pltpu.SMEM)


def struct(shape, dtype=BF16):
    return jax.ShapeDtypeStruct(tuple(shape), dtype)


def nt_dot(a, b):
    return lax.dot_general(a, b, (((1,), (1,)), ((), ())), preferred_element_type=F32)


def tn_dot(a, b):
    return lax.dot_general(a, b, (((0,), (0,)), ((), ())), preferred_element_type=F32)


def dot(a, b):
    return jnp.dot(a, b, preferred_element_type=F32)


def selection(rows, columns, shift, first=0, last=None):
    last = columns if last is None else last
    row = lax.broadcasted_iota(jnp.int32, (rows, columns), 0)
    column = lax.broadcasted_iota(jnp.int32, (rows, columns), 1)
    hit = (row == column + shift) & (column >= first) & (column < last)
    return hit.astype(F32).astype(BF16)


def pair_up(first, first_half, second, second_half):
    lane = lax.broadcasted_iota(jnp.int32, first.shape, 1)
    left = first if first_half == 0 else pltpu.roll(first, HEAD_DIM, 1)
    right = second if second_half == 1 else pltpu.roll(second, HEAD_DIM, 1)
    return jnp.where(lane < HEAD_DIM, left, right)


def column_of(row):
    count = row.shape[1]
    i = lax.broadcasted_iota(jnp.int32, (count, count), 0)
    j = lax.broadcasted_iota(jnp.int32, (count, count), 1)
    return jnp.sum(jnp.where(i == j, row, 0.0), axis=1, keepdims=True)


def row_of(column):
    count = column.shape[0]
    i = lax.broadcasted_iota(jnp.int32, (count, count), 0)
    j = lax.broadcasted_iota(jnp.int32, (count, count), 1)
    return jnp.sum(jnp.where(i == j, column, 0.0), axis=0, keepdims=True)


def low(value):
    return value.astype(BF16).astype(F32)


def lanes(index):
    return slice(index * PAIR, (index + 1) * PAIR)


class Place:
    def __init__(self, z_count):
        self.x, self.z, self.y, self.c = (lax.axis_index(a) for a in AXES)
        self.g = self.x * 2 + self.y
        self.chip = (self.x * z_count + self.z) * 2 + self.y

    def sibling(self):
        return (self.x, self.z, self.y, 1 - self.c)

    def plane(self, k):
        return (self.x ^ (k // 2), self.z, self.y ^ (k % 2), self.c)

    def line(self, k):
        return (self.x, self.z ^ k, self.y, self.c)

    def any_chip(self, k):
        return (self.x ^ (k // 2 % 2), self.z ^ (k // 4), self.y ^ (k % 2), self.c)


def greet(peers):
    barrier = pltpu.get_barrier_semaphore()
    for peer in peers:
        pl.semaphore_signal(barrier, inc=1, device_id=peer, device_id_type=IDS)
    return lambda: pl.semaphore_wait(barrier, len(peers))


def trip(source, target, sems, index, device):
    return pltpu.make_async_remote_copy(
        src_ref=source,
        dst_ref=target,
        send_sem=sems[0].at[index],
        recv_sem=sems[1].at[index],
        device_id=device,
        device_id_type=IDS,
    )


def send(*given):
    copy = trip(*given)
    copy.start()
    return copy


def move(source, target, sems, index):
    copy = pltpu.make_async_copy(source, target, sems.at[index])
    copy.start()
    return copy


DMA = pltpu.SemaphoreType.DMA


def both(count):
    return [DMA((count,)), DMA((count,))]


def exchange(kernel, ident, out_shape, in_specs, out_specs, scratch, args, flops, sent):
    return pl.pallas_call(
        kernel,
        out_shape=out_shape,
        in_specs=in_specs,
        out_specs=out_specs,
        scratch_shapes=scratch,
        compiler_params=pltpu.CompilerParams(
            collective_id=ident, has_side_effects=True, vmem_limit_bytes=60 << 20
        ),
        cost_estimate=pl.CostEstimate(flops=flops, bytes_accessed=sent, transcendentals=0),
    )(*args)


def head_kernel(
    zc,
    group,
    t_ref,
    q_w,
    k_w,
    v_w,
    g_any,
    u_any,
    d_any,
    o_w,
    gain1,
    gain2,
    ng_ref,
    wg_ref,
    fg_ref,
    a_ref,
    og_ref,
    w_ref,
    f_ref,
    e_ref,
    wo_ref,
    rows,
    weights,
    packed,
    g_w,
    u_w,
    d_w,
    ls,
    w0,
    w1,
    n0,
    n1,
    f0,
    f1,
    z0,
    z1,
    b0,
    b1,
    s0,
    s1,
    o0,
    o1,
    p0,
    p1,
):
    me = Place(zc)
    chips = 4 * zc
    per = zc // group
    qw = group * HEAD_DIM
    width = t_ref.shape[1]
    met = greet([me.any_chip(k) for k in range(1, chips)] + [me.sibling()])
    loads = [move(f, t, ls, 4 + i) for i, (f, t) in enumerate(((g_any, g_w), (u_any, u_w), (d_any, d_w)))]
    first_gain, second_gain = column_of(low(gain1[...])), column_of(low(gain2[...]))
    for g in range(4):
        at = slice(g * qw, (g + 1) * qw)
        w_ref[g, :, :qw] = (first_gain * low(q_w[:, at])).astype(BF16)
        for pair in range(group // 2):
            at = lanes(g * group // 2 + pair)
            key, value = first_gain * low(k_w[:, at]), first_gain * low(v_w[:, at])
            for half in range(2):
                start = qw + (2 * pair + half) * PAIR
                w_ref[g, :, start : start + PAIR] = pair_up(key, half, value, half).astype(BF16)
    wo_ref[...] = o_w[...].astype(BF16)
    x = t_ref[...].astype(F32)
    rows[0] = (x * lax.rsqrt(jnp.mean(x * x, axis=-1, keepdims=True) + EPS)).astype(BF16)
    met()
    here = og_ref.at[me.x, me.z, me.y, me.c]
    local = [move(w_ref.at[me.g], weights.at[me.x, me.z, me.y, me.c], ls, 0), move(wo_ref, here, ls, 1)]
    pieces = []
    for k in reversed(range(1, chips)):
        there = me.any_chip(k)
        their_g = there[0] * 2 + there[2]
        pieces.append(
            send(w_ref.at[their_g], weights.at[me.x, me.z, me.y, me.c], (w0, w1), k, there)
        )
    outs = [send(wo_ref, here, (o0, o1), k, me.line(k)) for k in range(1, zc)]
    blocks = [send(rows.at[0], rows.at[k], (n0, n1), k, me.plane(k)) for k in range(1, 4)]
    for copy in loads:
        copy.wait()
    e_ref[...] = d_w[...].astype(BF16).reshape(e_ref.shape)
    units = g_w.shape[1] // (4 * zc)
    for which, ref in enumerate((g_w, u_w)):
        for g in range(4):
            px, py = g // 2, g % 2
            if units % PAIR == 0:
                for z in range(zc):
                    at = ((px * zc + z) * 2 + py) * units
                    f_ref[g, which, :, z * units : (z + 1) * units] = (
                        second_gain * low(ref[:, at : at + units])
                    ).astype(BF16)
            else:
                for z in range(0, zc, 2):
                    near, far = (second_gain * low(ref[:, lanes(px * zc + i)]) for i in (z, z + 1))
                    f_ref[g, which, :, lanes(z // 2)] = pair_up(near, py, far, py).astype(BF16)
    wide = [
        move(f_ref.at[me.g], fg_ref.at[me.x, me.y, pl.ds(0, 2)], ls, 2),
        move(e_ref, fg_ref.at[:, :, 2], ls, 9),
    ]
    for k in range(1, 4):
        there = me.plane(k)
        their_g = there[0] * 2 + there[2]
        wide.append(
            send(f_ref.at[their_g], fg_ref.at[me.x, me.y, pl.ds(0, 2)], (f0, f1), k, there)
        )
    local[0].wait()
    arrivals = [pieces[chips - 1 - k] for k in range(1, chips)]
    relays = []
    for away in range(zc):
        for k in range(max(1, 4 * away), 4 * away + 4):
            arrivals[k - 1].wait()
        got = weights.at[:, me.z ^ away, :, me.c]
        relays.append(send(got, got, (s0, s1), 1 + away, me.sibling()))
    for copy in relays:
        copy.wait()
    kept = [move(weights, wg_ref, ls, 3)]

    def project(k, carry):
        @pl.when(k > 0)
        def _():
            trip(rows.at[0], rows.at[k], (n0, n1), k, me.plane(k)).wait_recv()

        at = (me.x ^ (k // 2)) * 2 + (me.y ^ (k % 2))
        out = dot(rows[k], weights[...].reshape(width, 3 * qw))
        for head in range(group):
            two, half = out[:, lanes(head // 2)], head % 2
            packed[head, k, :BLOCK] = pair_up(two[:BLOCK], half, two[BLOCK:], half).astype(BF16)
            start = qw + head * PAIR
            packed[head, k, BLOCK:] = out[:, start : start + PAIR].astype(BF16)
        for over in range(1, zc):
            trip(
                packed.at[(me.z ^ over) // per, k],
                a_ref.at[me.z, me.c, at],
                (z0, z1),
                k * zc + over,
                me.line(over),
            ).start()
        trip(
            packed.at[me.z // per, k], a_ref.at[me.z, me.c, at], (b0, b1), k * zc, me.sibling()
        ).start()
        pltpu.make_async_copy(
            packed.at[me.z // per, k], a_ref.at[me.z, me.c, at], ls.at[4 + k]
        ).start()
        return carry

    lax.fori_loop(0, 4, project, 0)
    kept.append(move(rows, ng_ref, ls, 8))
    for copy in outs + local[1:]:
        copy.wait()
    column = og_ref.at[me.x, :, me.y, me.c]
    out_rows = [send(column, column, (p0, p1), k, me.plane(k)) for k in range(1, 4)]

    def pass_on(step, carry):
        k, over = step // (zc - 1), step % (zc - 1) + 1
        at = (me.x ^ (k // 2)) * 2 + (me.y ^ (k % 2))
        there = me.z ^ over
        trip(
            packed.at[there // per, k],
            a_ref.at[me.z, me.c, at],
            (z0, z1),
            k * zc + over,
            me.line(over),
        ).wait()
        landed = a_ref.at[there, me.c, at]
        trip(landed, landed, (b0, b1), k * zc + over, me.sibling()).start()
        return carry

    lax.fori_loop(0, 4 * (zc - 1), pass_on, 0)
    for copy in out_rows:
        copy.wait()
    every = og_ref.at[:, :, :, me.c]
    last = send(every, every, (s0, s1), 0, me.sibling())

    def finish(step, carry):
        k, over = step // zc, step % zc
        at = (me.x ^ (k // 2)) * 2 + (me.y ^ (k % 2))
        landed = a_ref.at[me.z ^ over, me.c, at]
        trip(landed, landed, (b0, b1), k * zc + over, me.sibling()).wait()
        return carry

    lax.fori_loop(0, 4 * zc, finish, 0)
    for k in range(4):
        pltpu.make_async_copy(
            packed.at[me.z // per, k], a_ref.at[me.z, me.c, me.g], ls.at[4 + k]
        ).wait()
    for copy in [last] + kept + wide:
        copy.wait()
    for copy in blocks:
        copy.wait_send()


def head_exchange(zc, group, tokens, matrices, gains):
    chips = 4 * zc
    own, width = tokens.shape
    count = matrices[0].shape[0]
    piece = (count, 3 * group * HEAD_DIM)
    return exchange(
        functools.partial(head_kernel, zc, group),
        1,
        (
            struct((4, own, width)),
            struct((2, zc, 2, 2) + piece),
            struct((2, 2, 3, count, width)),
            struct((zc, 2, 4, BLOCK + own, PAIR)),
            struct((2, zc, 2, 2, count, width)),
        ),
        [VM] * 4 + [ANY] * 3 + [VM] * 3,
        (ANY,) * 5,
        [
            pltpu.VMEM((4,) + piece, BF16),
            pltpu.VMEM((4, 2, count, width), BF16),
            pltpu.VMEM((2, 2, count, width), BF16),
            pltpu.VMEM((count, width), BF16),
            pltpu.VMEM((4, own, width), BF16),
            pltpu.VMEM((2, zc, 2, 2) + piece, BF16),
            pltpu.VMEM((group, 4, BLOCK + own, PAIR), BF16),
            *[pltpu.VMEM(w.shape, F32) for w in matrices[3:6]],
            DMA((10,)),
        ]
        + both(chips)
        + both(4)
        + both(4)
        + both(4 * zc)
        + both(4 * zc)
        + both(1 + zc)
        + both(zc)
        + both(4),
        (tokens, *matrices, *(g.reshape(1, -1) for g in gains)),
        2 * 4 * own * width * width,
        16 << 20,
    )


def join_kernel(zc, s_ref, x_ref, w_ref, ob_ref, r_ref, n_ref, mine, theirs, slabs, x_in, w_in, ls, b0, b1, c0, c1):
    me = Place(zc)
    chips = 4 * zc
    heads, per = slabs.shape[:2]
    loads = [move(w_ref, w_in, ls, 2), move(x_ref, x_in, ls, 3)]
    greet([me.any_chip(k) for k in range(1, chips)] + [me.sibling()])()
    other = send(s_ref.at[:, 1 - me.c], theirs, (b0, b1), 0, me.sibling())
    own = move(s_ref.at[:, me.c], mine, ls, 0)
    own.wait()
    other.wait()
    mine[...] = mine[...] + theirs[...]
    head = me.g * (heads // 4) + me.z // per
    place = me.z % per
    keep = move(mine.at[me.z, me.g], slabs.at[head, place], ls, 1)
    sends = []
    for k in reversed(range(1, chips)):
        there = me.any_chip(k)
        their_g = there[0] * 2 + there[2]
        sends.append(
            send(mine.at[there[1], their_g], slabs.at[head, place], (c0, c1), k, there)
        )
    keep.wait()
    for copy in sends:
        copy.wait()
    for block in range(2):
        for pair in range(heads // 2):
            sides = []
            for side in range(2):
                slab = slabs[2 * pair + side, 0].astype(F32)
                for extra in range(1, per):
                    slab = slab + slabs[2 * pair + side, extra].astype(F32)
                sides.append(slab)
            ob_ref[block * BLOCK : (block + 1) * BLOCK, lanes(pair)] = pair_up(
                sides[0], block, sides[1], block
            ).astype(BF16)
    for copy in loads:
        copy.wait()
    residual = x_in[...].astype(F32) + dot(ob_ref[...], w_in[...])
    r_ref[...] = residual
    mean = jnp.mean(residual * residual, axis=-1, keepdims=True)
    n_ref[...] = (residual * lax.rsqrt(mean + EPS)).astype(BF16)


def join_exchange(zc, heads, slabs, tokens, w_out):
    chips = 4 * zc
    per = 4 * zc // heads
    half = (zc,) + slabs.shape[2:]
    shape = tokens.shape
    return exchange(
        functools.partial(join_kernel, zc),
        2,
        (struct(shape), struct(shape, F32), struct(shape)),
        [ANY, ANY, ANY],
        (VM,) * 3,
        [
            pltpu.VMEM(half, BF16),
            pltpu.VMEM(half, BF16),
            pltpu.VMEM((heads, per) + slabs.shape[3:], BF16),
            pltpu.VMEM(shape, BF16),
            pltpu.VMEM(w_out.shape, BF16),
            DMA((4,)),
        ]
        + both(1)
        + both(chips),
        (slabs, tokens, w_out),
        0,
        0,
    )


def middle_kernel(zc, n_ref, ca_ref, cb_ref, cc_ref, cd_ref, *rest):
    f_refs, rest = rest[: zc // 2 + 1], rest[zc // 2 + 1 :]
    oa_ref, ob_ref, oc_ref, od_ref, cs_ref, sh_ref, rows, cots, gate_w, up_w, down_w, *rest = rest
    hid, dgate, dup, c_out, c_in, passed, early, stage, o_out, ls, n0, n1, c0, c1, f0, f1, h0, h1 = rest
    me = Place(zc)
    width = n_ref.shape[1]
    met = greet([me.plane(k) for k in range(1, 4)] + [me.line(1), me.sibling()])
    move(n_ref, rows.at[0], ls, 15).wait()
    met()
    farthest = send(rows.at[0], rows.at[3], (n0, n1), 3, me.plane(3))
    def places(there):
        return (
            gate_w.at[:, there, :, me.c],
            up_w.at[:, there, :, me.c],
            down_w.at[there, me.c],
        )

    given = dict(zip([1, *range(0, zc, 2)], f_refs))
    hops, loads = [[], [], []], [[], [], []]
    for k in range(2, zc, 2):
        for i, place in enumerate(places(me.z ^ k)):
            hops[i].append(send(given[k].at[:, :, i], place, (h0, h1), 3 * k + i, me.line(1)))
    for k, ref in given.items():
        for i, place in enumerate(places(me.z ^ k)):
            loads[i].append(send(ref.at[:, :, i], place, (f0, f1), 3 * k + i, me.sibling()))
            loads[i].append(move(ref.at[:, :, i], place, ls, 21 + 3 * k + i))
    for k, ref in enumerate((ca_ref, cb_ref, cc_ref, cd_ref)):
        loads[2].append(move(ref, cots.at[k], ls, 16 + k))
    farthest.wait_send()
    near_rows = [send(rows.at[0], rows.at[k], (n0, n1), k, me.plane(k)) for k in (1, 2)]

    def settle(i):
        for copy in hops[i]:
            copy.wait()
        for k in range(3, zc, 2):
            place = places(me.z ^ k)[i]
            loads[i].append(send(place, place, (f0, f1), 3 * k + i, me.sibling()))
        for copy in loads[i]:
            copy.wait()

    square = (width, width)
    half = n_ref.shape[0] // 2
    upper, lower = pl.ds(0, half), pl.ds(half, half)
    c_sems = (c0, c1)
    far_parts = [
        trip(c_out.at[3, upper], passed.at[0], c_sems, 0, me.plane(2)),
        trip(c_out.at[3, lower], passed.at[1], c_sems, 1, me.plane(1)),
    ]
    near_parts = [
        trip(c_out.at[1, lower], c_in.at[0, lower], c_sems, 2, me.plane(1)),
        trip(c_out.at[2, upper], c_in.at[1, upper], c_sems, 3, me.plane(2)),
        trip(c_out.at[1, upper], c_in.at[0, upper], c_sems, 4, me.plane(1)),
        trip(c_out.at[2, lower], c_in.at[1, lower], c_sems, 5, me.plane(2)),
    ]

    def both_products(k):
        gate_mat, up_mat = gate_w[...].reshape(square), up_w[...].reshape(square)
        return dot(rows[k], gate_mat), dot(rows[k], up_mat)

    def finish(k, gate, up):
        back = nt_dot(cots[k], down_w[...].reshape(square))
        sig = jax.nn.sigmoid(gate)
        soft = gate * sig
        hid[k] = (soft * up).astype(BF16)
        dgate[k] = (back * up * sig * (1.0 + gate * (1.0 - sig))).astype(BF16)
        dup[k] = (back * soft).astype(BF16)
        gate_mat, up_mat = gate_w[...].reshape(square), up_w[...].reshape(square)
        c_out[k] = (nt_dot(dgate[k], gate_mat) + nt_dot(dup[k], up_mat)).astype(BF16)

    settle(0)
    settle(1)
    trip(rows.at[0], rows.at[3], (n0, n1), 3, me.plane(3)).wait_recv()
    early[0], early[1] = both_products(3)
    settle(2)
    finish(3, early[0], early[1])
    for copy in far_parts:
        copy.start()

    def block(step, carry):
        k = jnp.where(step == 3, 0, step)

        @pl.when(step < 3)
        def _():
            trip(rows.at[0], rows.at[k], (n0, n1), k, me.plane(k)).wait_recv()

        finish(k, *both_products(k))

        @pl.when(step == 1)
        def _():
            near_parts[0].start()

        @pl.when(step == 2)
        def _():
            near_parts[1].start()

        return carry

    lax.fori_loop(1, 4, block, 0)
    far_parts[0].wait_recv()
    c_out[1, upper] = c_out[1, upper] + passed[0]
    near_parts[2].start()
    far_parts[1].wait_recv()
    c_out[2, lower] = c_out[2, lower] + passed[1]
    near_parts[3].start()
    all_rows = (4 * n_ref.shape[0], width)

    def weight_grad(left, right, slot):
        chunk = 256
        for first in range(0, width, chunk):
            value = tn_dot(left[:, first : first + chunk], right).astype(BF16)
            stage[slot, first : first + chunk] = value

    shares = []
    piece = width // (8 * zc)

    def share(slot, which):
        parts = stage.at[slot].reshape(2, zc, 2, 2, piece, width)
        for g in range(4):
            x, y = g // 2, g % 2
            shares.append(
                move(parts.at[x, :, y], sh_ref.at[:, :, 2 * g + which], ls, 12 + 2 * g + which)
            )

    flat = lambda ref: ref[...].reshape(all_rows)
    weight_grad(flat(rows), flat(dgate), 0)
    share(0, 0)
    weight_grad(flat(rows), flat(dup), 1)
    share(1, 1)
    weight_grad(flat(hid), flat(cots), 2)
    shares.append(
        move(stage.at[2].reshape(zc, 2, 4, piece, width), sh_ref.at[:, :, 8:], ls, 20)
    )

    for k, ref in enumerate((oa_ref, ob_ref, oc_ref, od_ref)):
        o_out[k] = dot(hid[k], down_w[...].reshape(square)).astype(BF16).reshape(ref.shape)
        shares.append(move(o_out.at[k], ref, ls, k))
    for copy in far_parts:
        copy.wait_send()
    for copy in near_parts:
        copy.wait()
    cs_ref[...] = c_out[0].astype(F32) + c_in[0].astype(F32) + c_in[1].astype(F32)
    for copy in shares:
        copy.wait()
    for copy in near_rows:
        copy.wait_send()


def middle_exchange(zc, normed, cots, weights):
    own, width = normed.shape
    piece = width // (8 * zc)
    blocks = pltpu.VMEM((4, own, width), BF16)
    wide = pltpu.VMEM((2, zc, 2, 2, piece, width), BF16)
    return exchange(
        functools.partial(middle_kernel, zc),
        3,
        (
            *[struct((zc, 2, piece, width))] * 4,
            struct((own, width), F32),
            struct((zc, 2, 12, piece, width)),
        ),
        [ANY] * (5 + len(weights)),
        (ANY,) * 4 + (VM, ANY),
        [blocks, blocks, wide, wide, pltpu.VMEM((zc, 2, 2, 2, piece, width), BF16)]
        + [blocks] * 4
        + [pltpu.VMEM((2, own, width), BF16), pltpu.VMEM((2, own // 2, width), BF16)]
        + [pltpu.VMEM((2, own, width), F32)]
        + [pltpu.VMEM((3, width, width), BF16), pltpu.VMEM((4, zc, 2, piece, width), BF16), DMA((21 + 3 * zc,))]
        + both(4)
        + both(6)
        + both(3 * zc)
        + both(3 * zc),
        (normed, *cots, *weights),
        2 * 4 * own * width * width * 9,
        64 << 20,
    )


def turn_kernel(
    zc,
    c_ref,
    t_ref,
    r_ref,
    wo_ref,
    ob_ref,
    yb_ref,
    yc_ref,
    dr_ref,
    do_ref,
    va_ref,
    vb_ref,
    vc_ref,
    vd_ref,
    nb_ref,
    nc_ref,
    slabs,
    stage,
    wo_in,
    ob_in,
    ls,
    d0,
    d1,
    b0,
    b1,
    y0,
    y1,
):
    me = Place(zc)
    chips = 4 * zc
    heads = slabs.shape[0]
    group = heads // 4
    per = zc // group
    width = t_ref.shape[1]
    met = greet([me.any_chip(k) for k in range(1, chips)] + [me.sibling()])
    loads = [move(wo_ref, wo_in, ls, 5), move(ob_ref, ob_in, ls, 6)]
    total, residual = c_ref[...], r_ref[...]
    scaling = lax.rsqrt(jnp.mean(residual * residual, axis=-1, keepdims=True) + EPS)
    normed = residual * scaling
    middle = jnp.mean(total * normed, axis=-1, keepdims=True)
    grad = t_ref[...].astype(F32) + scaling * (total - normed * middle)
    dr_ref[...] = grad
    narrow = grad.astype(BF16)
    loads[0].wait()
    back = nt_dot(narrow, wo_in[...])
    for pair in range(heads // 2):
        two = back[:, lanes(pair)]
        for side in range(2):
            slabs[2 * pair + side] = pair_up(two[:BLOCK], side, two[BLOCK:], side).astype(BF16)
    met()
    to = do_ref.at[me.z, me.c, me.g]
    own = move(slabs.at[me.g * group + me.z // per], to, ls, 0)
    sends = []
    for k in reversed(range(1, chips)):
        there = me.any_chip(k)
        head = (there[0] * 2 + there[2]) * group + there[1] // per
        sends.append(send(slabs.at[head], to, (d0, d1), k, there))
    sends.append(send(yb_ref, nb_ref, (y0, y1), 1, me.plane(1)))
    sends.append(send(yc_ref, nc_ref, (y0, y1), 2, me.plane(2)))
    chunk = 256
    loads[1].wait()
    attended = ob_in[...]
    for first in range(0, width, chunk):
        stage[first : first + chunk] = tn_dot(attended[:, first : first + chunk], narrow).astype(BF16)
    parts = stage.reshape(2, zc, 2, 2, width // (8 * zc), width)
    keeps = []
    for k, ref in enumerate((va_ref, vb_ref, vc_ref, vd_ref)):
        there = me.plane(k)
        keeps.append(move(parts.at[there[0], :, there[2]], ref, ls, 1 + k))
    own.wait()
    for copy in sends[:-2]:
        copy.wait()
    half = do_ref.at[:, me.c]
    relay = send(half, half, (b0, b1), 0, me.sibling())
    for copy in keeps + sends[-2:]:
        copy.wait()
    relay.wait()


def turn_exchange(zc, c_sum, cotangent, residual, w_out, attn_rows, near):
    chips = 4 * zc
    own, width = cotangent.shape
    heads = width // HEAD_DIM
    return exchange(
        functools.partial(turn_kernel, zc),
        6,
        (
            struct((own, width), F32),
            struct((zc, 2, 4, BLOCK, PAIR)),
            *[struct((zc, 2, width // (8 * zc), width))] * 6,
        ),
        [VM] * 3 + [ANY] * 4,
        (VM,) + (ANY,) * 7,
        [
            pltpu.VMEM((heads, BLOCK, PAIR), BF16),
            pltpu.VMEM((width, width), BF16),
            pltpu.VMEM((width, width), BF16),
            pltpu.VMEM((own, width), BF16),
            DMA((7,)),
        ]
        + both(chips)
        + both(1)
        + both(3),
        (c_sum, cotangent, residual, w_out, attn_rows, *near),
        2 * 2 * own * width * width,
        8 << 20,
    )


def tail_kernel(
    zc,
    d_ref,
    n_any,
    w_any,
    x_any,
    g_any,
    f_ref,
    r_ref,
    ya_ref,
    yb_ref,
    yc_ref,
    yd_ref,
    va_ref,
    vb_ref,
    vc_ref,
    vd_ref,
    tg_ref,
    gw_ref,
    go_ref,
    gf_ref,
    out_ref,
    n_ref,
    w_ref,
    x_ref,
    g_ref,
    r_in,
    y_in,
    o_mine,
    o_theirs,
    o_land,
    mine,
    theirs,
    landed,
    grads,
    c_out,
    c_in,
    stage,
    other_w,
    ls,
    b0,
    b1,
    z0,
    z1,
    c0,
    c1,
    s0,
    s1,
    w0,
    w1,
    q0,
    q1,
    f0,
    f1,
):
    me = Place(zc)
    chips = 4 * zc
    group, per = landed.shape[:2]
    qw = group * HEAD_DIM
    greet([me.any_chip(k) for k in range(1, chips)] + [me.sibling()])()
    head, place = me.z // per, me.z % per

    def slot(k):
        return (me.x ^ (k // 2)) * 2 + (me.y ^ (k % 2))

    order = (3, 2, 1, 0)
    halves = []
    for k in order:
        halves.append(
            (
                send(d_ref.at[:, 1 - me.c, slot(k)], theirs.at[k], (b0, b1), k, me.sibling()),
                move(d_ref.at[:, me.c, slot(k)], mine.at[k], ls, k),
            )
        )
    given = ((w_any, w_ref), (n_any, n_ref), (g_any, g_ref), (x_any, x_ref))
    loads = [move(source, target, ls, 20 + i) for i, (source, target) in enumerate(given)]
    f_parts = [move(f_ref.at[pl.ds(2 * me.g, 2)], gf_ref.at[me.g], ls, 10)]
    for k in (3, 1, 2):
        there = me.plane(k)
        part = f_ref.at[pl.ds(2 * (there[0] * 2 + there[2]), 2)]
        f_parts.append(send(part, gf_ref.at[me.g], (f0, f1), k, there))
    out_parts = [move(r_ref, r_in, ls, 11)]
    for i, ref in enumerate((ya_ref, yb_ref, yc_ref, yd_ref)):
        out_parts.append(move(ref, y_in.at[i, 0], ls, 12 + i))
    for i, ref in enumerate((va_ref, vb_ref, vc_ref, vd_ref)):
        out_parts.append(move(ref, y_in.at[i, 1], ls, 16 + i))
    for k, (far, near) in zip(order, halves):
        near.wait()
        far.wait()
        mine[k] = mine[k] + theirs[k]
        for over in range(1, zc):
            send(
                mine.at[k, me.z ^ over],
                landed.at[head, place, k],
                (z0, z1),
                k * zc + over,
                me.line(over),
            )
        move(mine.at[k, me.z], landed.at[head, place, k], ls, 4 + k)

    for copy in out_parts + loads:
        copy.wait()
    final = r_in[...]
    o_sum = jnp.zeros(o_mine.shape, F32)
    for i in range(4):
        final = final + y_in[i, 0].astype(F32).reshape(final.shape)
        o_sum = o_sum + y_in[i, 1].astype(F32)
    out_ref[...] = final.astype(BF16)
    o_mine[...] = o_sum.astype(BF16)
    o_swap = send(o_mine.at[:, 1 - me.c], o_theirs, (s0, s1), 1, me.sibling())

    def block(step, carry):
        k = 3 - step
        pltpu.make_async_copy(
            mine.at[k, me.z], landed.at[head, place, k], ls.at[4 + k]
        ).wait()
        for over in range(1, zc):
            trip(
                mine.at[k, me.z ^ over],
                landed.at[head, place, k],
                (z0, z1),
                k * zc + over,
                me.line(over),
            ).wait()
        for pair in range(group // 2):
            sides = []
            for side in range(2):
                h = 2 * pair + side
                slab = landed[h, 0, k]
                for extra in range(1, per):
                    slab = slab + landed[h, extra, k]
                start = qw + h * PAIR
                grads[k, :, start : start + PAIR] = slab[BLOCK:]
                sides.append(slab[:BLOCK].astype(F32))
            for b in range(2):
                grads[k, b * BLOCK : (b + 1) * BLOCK, lanes(pair)] = pair_up(
                    sides[0], b, sides[1], b
                ).astype(BF16)

        @pl.when(k > 0)
        def _():
            c_out[k] = nt_dot(grads[k], w_ref[...]).astype(BF16)
            trip(c_out.at[k], c_in.at[k], (c0, c1), k, me.plane(k)).start()

        return carry

    o_swap.wait()
    o_theirs[...] = o_theirs[...] + o_mine[:, me.c]
    sends = [
        send(o_theirs.at[me.z ^ k], o_land.at[k], (q0, q1), k, me.line(k)) for k in range(1, zc)
    ]
    lax.fori_loop(0, 4, block, 0)
    width, cols = w_ref.shape
    all_rows = 4 * n_ref.shape[1]
    normed_all = n_ref[...].reshape(all_rows, width)
    grads_all = grads[...].reshape(all_rows, cols)
    piece = stage.shape[2]
    chunk = 256
    each = chunk // (2 * piece)
    swaps = []
    for first in range(0, width, chunk):
        value = tn_dot(normed_all[:, first : first + chunk], grads_all).astype(BF16)
        at = first // (2 * piece)
        stage[at : at + each] = value.reshape(each, 2, piece, cols)
        swaps.append(
            send(
                stage.at[at : at + each, 1 - me.c],
                other_w.at[at : at + each],
                (s0, s1),
                2 + first // chunk,
                me.sibling(),
            )
        )
    c_out[0] = nt_dot(grads[0], w_ref[...]).astype(BF16)
    for swap in swaps:
        swap.wait()

    def add(i, carry):
        other_w[i] = stage[i, me.c] + other_w[i]
        return carry

    lax.fori_loop(0, chips, add, 0)
    stay = move(other_w.at[me.chip], gw_ref.at[me.z, me.g], ls, 8)
    for k in reversed(range(1, chips)):
        there = me.any_chip(k)
        chip = (there[0] * zc + there[1]) * 2 + there[2]
        sends.append(send(other_w.at[chip], gw_ref.at[me.z, me.g], (w0, w1), k, there))
    total = c_out[0].astype(F32)
    for k in range(1, 4):
        trip(c_out.at[k], c_in.at[k], (c0, c1), k, me.plane(k)).wait()
        total = total + c_in[k].astype(F32)
    x = x_ref[...].astype(F32)
    scaling = lax.rsqrt(jnp.mean(x * x, axis=-1, keepdims=True) + EPS)
    normed = x * scaling
    middle = jnp.mean(total * normed, axis=-1, keepdims=True)
    tg_ref[...] = (g_ref[...] + scaling * (total - normed * middle)).astype(BF16)
    stay.wait()
    for copy in sends + f_parts:
        copy.wait()
    o_sum = o_theirs[me.z].astype(F32)
    for k in range(1, zc):
        o_sum = o_sum + o_land[k].astype(F32)
    go_ref[...] = o_sum


def tail_exchange(zc, group, slab_grads, n_all, weights, tokens, residual_grad, shares, residual, packs):
    chips = 4 * zc
    per = zc // group
    own, width = tokens.shape
    cols = weights.shape[1]
    slab = slab_grads.shape[3:]
    piece = width // (2 * chips)
    blocks = pltpu.VMEM((4, own, width), BF16)
    return exchange(
        functools.partial(tail_kernel, zc),
        4,
        (
            struct((own, width)),
            struct((zc, 4, piece, cols)),
            struct((piece, width), F32),
            struct((4, 2, piece, width)),
            struct((own, width)),
        ),
        [ANY] * 15,
        (VM, ANY, VM, ANY, VM),
        [
            pltpu.VMEM((4, own, width), BF16),
            pltpu.VMEM((width, cols), BF16),
            pltpu.VMEM((own, width), BF16),
            pltpu.VMEM((own, width), F32),
            pltpu.VMEM((own, width), F32),
            pltpu.VMEM((4, 2, zc, 2, piece, width), BF16),
            pltpu.VMEM((zc, 2, piece, width), BF16),
            pltpu.VMEM((zc, piece, width), BF16),
            pltpu.VMEM((zc, piece, width), BF16),
            pltpu.VMEM((4, zc) + slab, BF16),
            pltpu.VMEM((4, zc) + slab, BF16),
            pltpu.VMEM((group, per, 4) + slab, BF16),
            pltpu.VMEM((4, own, cols), BF16),
            blocks,
            blocks,
            pltpu.VMEM((chips, 2, piece, cols), BF16),
            pltpu.VMEM((chips, piece, cols), BF16),
            DMA((24,)),
        ]
        + both(4)
        + both(4 * zc)
        + both(4)
        + both(2 + width // 256)
        + both(chips)
        + both(zc)
        + both(4),
        (slab_grads, n_all, weights, tokens, residual_grad, shares, residual, *packs),
        2 * 4 * own * width * cols * 2,
        24 << 20,
    )


def last_kernel(
    zc,
    group,
    t_any,
    o_any,
    wo_any,
    gw_any,
    gf_any,
    ds_any,
    q_any,
    k_any,
    v_any,
    g_any,
    u_any,
    gain1,
    gain2,
    tg_ref,
    out_ref,
    go_ref,
    g1_ref,
    q_ref,
    k_ref,
    v_ref,
    g2_ref,
    g_ref,
    u_ref,
    d_ref,
    gw_ref,
    gf_ref,
    ds_ref,
    q_w,
    k_w,
    v_w,
    g_w,
    u_w,
    ls,
):
    given = (gw_any, q_any, k_any, v_any, gf_any, g_any, u_any, ds_any, t_any, o_any, wo_any)
    taken = (gw_ref, q_w, k_w, v_w, gf_ref, g_w, u_w, ds_ref, tg_ref, out_ref, go_ref)
    copies = [move(a, b, ls, i) for i, (a, b) in enumerate(zip(given, taken))]
    for copy in copies:
        copy.wait()
    d_ref[...] = ds_ref[8:].astype(F32).reshape(d_ref.shape)
    first_gain, second_gain = column_of(low(gain1[...])), column_of(low(gain2[...]))
    count = q_w.shape[0]
    qw = group * HEAD_DIM
    score = jnp.zeros((count, PAIR), F32)
    for g in range(4):
        raw = gw_ref[0, g].astype(F32)
        for z in range(1, zc):
            raw = raw + gw_ref[z, g].astype(F32)
        for pair in range(group // 2):
            at = lanes(g * group // 2 + pair)
            start = qw + 2 * pair * PAIR
            even, odd = raw[:, start : start + PAIR], raw[:, start + PAIR : start + 2 * PAIR]
            query = raw[:, lanes(pair)]
            key, value = pair_up(even, 0, odd, 0), pair_up(even, 1, odd, 1)
            score = score + query * low(q_w[:, at]) + key * low(k_w[:, at]) + value * low(v_w[:, at])
            q_ref[:, at] = first_gain * query
            k_ref[:, at] = first_gain * key
            v_ref[:, at] = first_gain * value
    g1_ref[...] = row_of(jnp.sum(score, axis=1, keepdims=True))
    units = g_w.shape[1] // (4 * zc)
    score = jnp.zeros((count, PAIR), F32)
    for which, (weight, target) in enumerate(((g_w, g_ref), (u_w, u_ref))):
        for chunk in range(weight.shape[1] // PAIR):
            if units % PAIR == 0:
                owner, piece = divmod(chunk, units // PAIR)
                x, z, y = owner // (2 * zc), owner // 2 % zc, owner % 2
                raw = gf_ref[2 * x + y, which, :, lanes(z * units // PAIR + piece)].astype(F32)
            else:
                x, z = chunk // zc, chunk % zc
                near = gf_ref[2 * x, which, :, lanes(z // 2)].astype(F32)
                far = gf_ref[2 * x + 1, which, :, lanes(z // 2)].astype(F32)
                raw = pair_up(near, z % 2, far, z % 2)
            score = score + raw * low(weight[:, lanes(chunk)])
            target[:, lanes(chunk)] = second_gain * raw
    g2_ref[...] = row_of(jnp.sum(score, axis=1, keepdims=True))


def last_step(zc, group, tokens_grad, output, out_share, w_all, f_all, shares, matrices, gains):
    own, width = output.shape
    count, hidden = matrices[3].shape
    return pl.pallas_call(
        functools.partial(last_kernel, zc, group),
        out_shape=(
            struct((own, width)),
            struct((own, width)),
            struct((count, width), F32),
            struct((1, count), F32),
            struct((count, width), F32),
            struct((count, width), F32),
            struct((count, width), F32),
            struct((1, count), F32),
            struct((count, hidden), F32),
            struct((count, hidden), F32),
            struct((4 * count, width), F32),
        ),
        in_specs=[ANY] * 11 + [VM] * 2,
        out_specs=(VM,) * 11,
        scratch_shapes=[
            pltpu.VMEM(v.shape, v.dtype) for v in (w_all, f_all, shares, *matrices)
        ]
        + [DMA((11,))],
        compiler_params=pltpu.CompilerParams(vmem_limit_bytes=60 << 20),
    )(
        tokens_grad,
        output,
        out_share,
        w_all,
        f_all,
        shares,
        *matrices,
        *(g.reshape(1, -1) for g in gains),
    )


def segment_start(position, lens_ref):
    start = jnp.zeros_like(position)
    end = 0
    for j in range(lens_ref.shape[0]):
        end = end + lens_ref[j]
        start = jnp.where(position >= end, end, start)
    return start


def note_tiles(workers, worker, tiles, lens_ref, mine):
    turns = tiles // workers

    def snake(turn, carry):
        forward = turn * workers + worker
        backward = turn * workers + workers - 1 - worker
        mine[turn] = jnp.where((turn & 1) == 0, forward, backward)
        return carry

    def weigh(step, ahead):
        turn = turns - 1 - step
        loads = []
        for tile in (2 * turn, 2 * turn + 1):
            first, _, _, last = key_bounds(tile * QTILE, lens_ref)
            loads.append(last - first)
        lighter_first = loads[0] <= loads[1]
        first_to_zero = jnp.where(ahead > 0, lighter_first, loads[0] > loads[1])
        mine[turn] = 2 * turn + jnp.where(first_to_zero, worker, 1 - worker)
        return ahead + jnp.where(first_to_zero, loads[0] - loads[1], loads[1] - loads[0])

    if workers == 2:
        lax.fori_loop(0, turns, weigh, 0)
    else:
        lax.fori_loop(0, turns, snake, 0)


def key_bounds(first, lens_ref):
    low_start = segment_start(first, lens_ref)
    high_start = segment_start(first + QTILE - 1, lens_ref)
    low = low_start // KTILE
    high = (first + QTILE + KTILE - 1) // KTILE
    plain = jnp.clip((high_start + KTILE - 1) // KTILE, low, high)
    stop = jnp.clip((first + 1) // KTILE, plain, high)
    return low, plain, stop, high


def visible(first, tile, starts):
    key = tile * KTILE + lax.broadcasted_iota(jnp.int32, (KTILE, QTILE), 0)
    query = first + lax.broadcasted_iota(jnp.int32, (KTILE, QTILE), 1)
    return (key <= query) & (key >= starts)


def note_places(anchor_ref, inv):
    def note(i, carry):
        inv[anchor_ref[i]] = i
        return carry

    lax.fori_loop(0, anchor_ref.shape[0], note, 0)


def half_lanes(rows, half):
    lane = lax.broadcasted_iota(jnp.int32, rows.shape, 1)
    return jnp.where((lane // HEAD_DIM) == half, rows, jnp.zeros_like(rows))


def fold(rows, columns, first):
    row = lax.broadcasted_iota(jnp.int32, (rows, columns), 0)
    column = lax.broadcasted_iota(jnp.int32, (rows, columns), 1)
    return (row % HEAD_DIM == column - first).astype(F32).astype(BF16)


def unfold(rows, columns, first):
    row = lax.broadcasted_iota(jnp.int32, (rows, columns), 0)
    column = lax.broadcasted_iota(jnp.int32, (rows, columns), 1)
    return (column % HEAD_DIM == row - first).astype(F32).astype(BF16)


def forward_kernel(
    workers,
    anchor_ref,
    lens_ref,
    who_ref,
    a_any,
    o_ref,
    kv_any,
    kvt_any,
    q_any,
    qt_any,
    ot_any,
    l_any,
    inv,
    mine,
    raw,
    a_ref,
    kv_ref,
    kvt_ref,
    q_ref,
    qt_ref,
    ot_ref,
    l_ref,
    ls,
    ts,
):
    load = move(a_any, a_ref, ls, 0)
    blocks = anchor_ref.shape[0]
    turns = qt_ref.shape[0]
    per = QTILE // BLOCK
    worker = who_ref[0]
    note_places(anchor_ref, inv)
    note_tiles(workers, worker, turns * workers, lens_ref, mine)
    o_ref[...] = jnp.zeros_like(o_ref)
    same = selection(PAIR, PAIR, 0)
    load.wait()

    def order(step, carry):
        for b in range(per):
            i = step * per + b
            where = inv[i]
            slab, half = where >> 1, where & 1
            at = pl.ds(pl.multiple_of(i * BLOCK, BLOCK), BLOCK)
            kv_ref[at, :] = a_ref[slab, pl.ds(pl.multiple_of(BLOCK + half * BLOCK, BLOCK), BLOCK), :]
        return carry

    lax.fori_loop(0, blocks // per, order, 0)
    leaving = [move(kv_ref, kv_any, ls, 1)]

    def flip(step, carry):
        at = pl.ds(pl.multiple_of(step * TURNED, TURNED), TURNED)
        kvt_ref[:, at] = nt_dot(same, kv_ref[at, :]).astype(BF16)
        return carry

    lax.fori_loop(0, blocks * BLOCK // TURNED, flip, 0)
    leaving.append(move(kvt_ref, kvt_any, ls, 2))
    kept = ((q_ref, q_any), (qt_ref, qt_any), (ot_ref, ot_any), (l_ref, l_any))

    def leave(turn, i):
        source, target = kept[i]
        return pltpu.make_async_copy(source.at[turn], target.at[turn], ts.at[i, turn])

    def one_tile(turn, carry):
        tile = mine[turn]
        first = tile * QTILE
        for b in range(per):
            where = inv[tile * per + b]
            raw[b * BLOCK : (b + 1) * BLOCK, :] = half_lanes(a_ref[where >> 1, :BLOCK, :], where & 1)
        q_ref[turn] = (dot(raw[...], fold(PAIR, PAIR, 0)) * 0.125).astype(BF16)
        qt_ref[turn] = (nt_dot(unfold(PAIR, PAIR, 0), raw[...]) * 0.125).astype(BF16)
        query = qt_ref[turn]
        starts = segment_start(first + lax.broadcasted_iota(jnp.int32, (1, QTILE), 1), lens_ref)
        low, plain, stop, high = key_bounds(first, lens_ref)

        def step(masked, kt, state):
            top, total, acc = state
            at = pl.ds(pl.multiple_of(kt * KTILE, KTILE), KTILE)
            scores = dot(kv_ref[at, :], query)
            if masked:
                scores = jnp.where(visible(first, kt, starts), scores, MASKED)
            new_top = jnp.maximum(top, jnp.max(scores, axis=0, keepdims=True))
            factor = jnp.exp(top - new_top)
            weights = jnp.exp(scores - new_top)
            total = total * factor + jnp.sum(weights, axis=0, keepdims=True)
            acc = acc * factor + dot(kvt_ref[HEAD_DIM:, at], weights.astype(BF16))
            return (new_top, total, acc)

        state = (
            jnp.full((1, QTILE), LOWEST, F32),
            jnp.zeros((1, QTILE), F32),
            jnp.zeros((HEAD_DIM, QTILE), F32),
        )
        state = lax.fori_loop(low, plain, functools.partial(step, True), state)
        state = lax.fori_loop(plain, stop, functools.partial(step, False), state)
        top, total, acc = lax.fori_loop(stop, high, functools.partial(step, True), state)
        out = acc / total
        ot_ref[turn] = out
        l_ref[turn] = top + jnp.log(total)
        for i in range(4):
            leave(turn, i).start()
        wide = tn_dot(out.astype(BF16), unfold(HEAD_DIM, PAIR, 0)).astype(BF16)
        for b in range(per):
            where = inv[tile * per + b]
            slab = where >> 1
            o_ref[slab] = o_ref[slab] + half_lanes(wide[b * BLOCK : (b + 1) * BLOCK], where & 1)
        return carry

    lax.fori_loop(0, turns, one_tile, 0)

    def left(turn, carry):
        for i in range(4):
            leave(turn, i).wait()
        return carry

    lax.fori_loop(0, turns, left, 0)
    for copy in leaving:
        copy.wait()


def attention_forward(workers, anchors, lengths, who, packed):
    slabs = packed.shape[0]
    rows = slabs * 2 * BLOCK
    turns = rows // QTILE // workers
    return pl.pallas_call(
        functools.partial(forward_kernel, workers),
        out_shape=(
            struct((slabs, BLOCK, PAIR)),
            struct((rows, PAIR)),
            struct((PAIR, rows)),
            struct((turns, QTILE, PAIR)),
            struct((turns, PAIR, QTILE)),
            struct((turns, HEAD_DIM, QTILE), F32),
            struct((turns, 1, QTILE), F32),
        ),
        in_specs=[SM, SM, SM, ANY],
        out_specs=(VM,) + (ANY,) * 6,
        scratch_shapes=[
            pltpu.SMEM((2 * slabs,), jnp.int32),
            pltpu.SMEM((turns,), jnp.int32),
            pltpu.VMEM((QTILE, PAIR), BF16),
            pltpu.VMEM(packed.shape, BF16),
            pltpu.VMEM((rows, PAIR), BF16),
            pltpu.VMEM((PAIR, rows), BF16),
            pltpu.VMEM((turns, QTILE, PAIR), BF16),
            pltpu.VMEM((turns, PAIR, QTILE), BF16),
            pltpu.VMEM((turns, HEAD_DIM, QTILE), F32),
            pltpu.VMEM((turns, 1, QTILE), F32),
            DMA((3,)),
            DMA((4, turns)),
        ],
        compiler_params=pltpu.CompilerParams(vmem_limit_bytes=60 << 20),
        cost_estimate=pl.CostEstimate(
            flops=rows * rows * 64, bytes_accessed=rows * 1024, transcendentals=rows * rows // 8
        ),
    )(anchors, lengths, who, packed)


def backward_kernel(
    workers,
    anchor_ref,
    lens_ref,
    who_ref,
    d_ref,
    kv_ref,
    kvt_ref,
    q_ref,
    qt_ref,
    ot_ref,
    l_ref,
    g_ref,
    inv,
    mine,
    raw,
    both_rows,
    dt,
    acc,
):
    blocks = anchor_ref.shape[0]
    turns = qt_ref.shape[0]
    per = QTILE // BLOCK
    worker = who_ref[0]
    note_places(anchor_ref, inv)
    note_tiles(workers, worker, turns * workers, lens_ref, mine)
    acc[...] = jnp.zeros_like(acc)
    g_ref[:, :BLOCK, :] = jnp.zeros((g_ref.shape[0], BLOCK, PAIR), BF16)

    def one_tile(turn, carry):
        tile = mine[turn]
        first = tile * QTILE
        for b in range(per):
            where = inv[tile * per + b]
            raw[b * BLOCK : (b + 1) * BLOCK, :] = half_lanes(d_ref[where >> 1], where & 1)
        both_rows[:QTILE] = q_ref[turn]
        both_rows[QTILE:] = dot(raw[...], fold(PAIR, PAIR, HEAD_DIM)).astype(BF16)
        dt[...] = nt_dot(unfold(PAIR, PAIR, HEAD_DIM), raw[...]).astype(BF16)
        query, grad = qt_ref[turn], dt[...]
        norm = l_ref[turn]
        delta = jnp.sum(grad[HEAD_DIM:].astype(F32) * ot_ref[turn], axis=0, keepdims=True)
        starts = segment_start(first + lax.broadcasted_iota(jnp.int32, (1, QTILE), 1), lens_ref)
        low, plain, stop, high = key_bounds(first, lens_ref)

        def step(masked, kt, total):
            at = pl.ds(pl.multiple_of(kt * KTILE, KTILE), KTILE)
            keys = kv_ref[at, :]
            scores = dot(keys, query)
            if masked:
                scores = jnp.where(visible(first, kt, starts), scores, MASKED)
            weights = jnp.exp(scores - norm)
            score_grad = (weights * (dot(keys, grad) - delta)).astype(BF16)
            both_grads = jnp.concatenate([score_grad, weights.astype(BF16)], axis=1)
            acc[at, :] += dot(both_grads, both_rows[...])
            return total + dot(kvt_ref[:HEAD_DIM, at], score_grad)

        total = jnp.zeros((HEAD_DIM, QTILE), F32)
        total = lax.fori_loop(low, plain, functools.partial(step, True), total)
        total = lax.fori_loop(plain, stop, functools.partial(step, False), total)
        total = lax.fori_loop(stop, high, functools.partial(step, True), total)
        wide = tn_dot((total * 0.125).astype(BF16), unfold(HEAD_DIM, PAIR, 0)).astype(BF16)
        for b in range(per):
            where = inv[tile * per + b]
            slab = where >> 1
            g_ref[slab, :BLOCK] = g_ref[slab, :BLOCK] + half_lanes(
                wide[b * BLOCK : (b + 1) * BLOCK], where & 1
            )
        return carry

    lax.fori_loop(0, turns, one_tile, 0)

    def place(step, carry):
        for b in range(per):
            i = step * per + b
            where = inv[i]
            slab, half = where >> 1, where & 1
            at = pl.ds(pl.multiple_of(i * BLOCK, BLOCK), BLOCK)
            to = pl.ds(pl.multiple_of(BLOCK + half * BLOCK, BLOCK), BLOCK)
            g_ref[slab, to, :] = acc[at, :].astype(BF16)
        return carry

    lax.fori_loop(0, blocks // per, place, 0)


def attention_backward(workers, anchors, lengths, who, grads, kept):
    slabs = grads.shape[0]
    rows = slabs * 2 * BLOCK
    return pl.pallas_call(
        functools.partial(backward_kernel, workers),
        out_shape=struct((slabs, 3 * BLOCK, PAIR)),
        in_specs=[SM, SM, SM] + [VM] * 7,
        out_specs=VM,
        scratch_shapes=[
            pltpu.SMEM((2 * slabs,), jnp.int32),
            pltpu.SMEM((rows // QTILE // workers,), jnp.int32),
            pltpu.VMEM((QTILE, PAIR), BF16),
            pltpu.VMEM((2 * QTILE, PAIR), BF16),
            pltpu.VMEM((PAIR, QTILE), BF16),
            pltpu.VMEM((rows, PAIR), F32),
        ],
        compiler_params=pltpu.CompilerParams(vmem_limit_bytes=60 << 20),
        cost_estimate=pl.CostEstimate(
            flops=rows * rows * 160, bytes_accessed=rows * 1024, transcendentals=rows * rows // 8
        ),
    )(anchors, lengths, who, grads, *kept)


def around(value, k):
    return lax.ppermute(value, ("head", "y"), [(i, i ^ k) for i in range(4)])


def along(value, k):
    return lax.ppermute(value, "z", [(i, i ^ k) for i in range(lax.axis_size("z"))])


def doubling(pieces, first, last):
    while first >= last:
        pieces = {**pieces, **{k + first: along(pieces[k], first) for k in pieces}}
        first //= 2
    return pieces


def body(
    zc,
    tokens,
    cotangent,
    norm1_gain,
    w_query,
    w_key,
    w_value,
    w_out,
    norm2_gain,
    w_gate,
    w_up,
    w_down,
    block_anchor,
    seq_lengths,
):
    width = tokens.shape[1]
    heads = width // HEAD_DIM
    group = heads // 4
    per_head = zc // group
    workers = 2 * per_head
    feature_rows = w_query.shape[0]

    n1_all, qkv_w, ffn_own, by_head, out_mat = head_exchange(
        zc,
        group,
        tokens,
        (w_query, w_key, w_value, w_gate, w_up, w_down, w_out),
        (norm1_gain, norm2_gain),
    )
    qkv_w = qkv_w.reshape(width, 3 * group * HEAD_DIM)

    out_mat, sent = lax.optimization_barrier((out_mat.reshape(width, width), cotangent))
    cots = [cotangent] + [around(sent, k) for k in range(1, 4)]
    ffn_parts = doubling({0: ffn_own}, zc // 2, 2)
    close = along(ffn_own, 1)

    anchors = jnp.transpose(block_anchor.reshape(2, zc, 2, 2, 2), (1, 3, 0, 2, 4)).reshape(-1)
    who = ((lax.axis_index("z") % per_head) * 2 + lax.axis_index("core")).astype(jnp.int32).reshape(1)
    slab_count = zc * 8
    o_slabs, *kept = attention_forward(
        workers, anchors, seq_lengths, who, by_head.reshape((slab_count,) + by_head.shape[3:])
    )
    attn_rows, residual, normed_two = join_exchange(
        zc, heads, o_slabs.reshape(zc, 2, 4, BLOCK, PAIR), tokens, out_mat
    )
    *out_parts, c_sum, shares = middle_exchange(
        zc, normed_two, cots, [close] + [ffn_parts[k] for k in range(0, zc, 2)]
    )
    shares = lax.psum_scatter(
        shares.reshape(zc * 2 * 12, feature_rows, width), ("z", "core"), scatter_dimension=0, tiled=True
    )
    residual_grad, do_heads, *packs = turn_exchange(
        zc, c_sum, cotangent, residual, out_mat, attn_rows, out_parts[1:3]
    )
    w_grads, near = packs[:4], packs[4:]
    do_heads, far = lax.optimization_barrier((do_heads, out_parts[3]))
    packs = [out_parts[0], *near, around(far, 3), w_grads[0]]
    packs += [around(w_grads[k], k) for k in range(1, 4)]
    grad_heads = attention_backward(
        workers, anchors, seq_lengths, who, do_heads.reshape(slab_count, BLOCK, PAIR), kept
    )
    tokens_grad, w_all, out_share, f_all, output = tail_exchange(
        zc,
        group,
        grad_heads.reshape(zc, 2, 4, 3 * BLOCK, PAIR),
        n1_all,
        qkv_w,
        tokens,
        residual_grad,
        shares,
        residual,
        packs,
    )
    (
        tokens_grad,
        output,
        out_grad,
        gain1_grad,
        query_grad,
        key_grad,
        value_grad,
        gain2_grad,
        gate_grad,
        up_grad,
        down_grad,
    ) = last_step(
        zc,
        group,
        tokens_grad,
        output,
        out_share,
        w_all,
        f_all,
        shares,
        (w_query, w_key, w_value, w_gate, w_up),
        (norm1_gain, norm2_gain),
    )
    return (
        output,
        tokens_grad,
        gain1_grad.reshape(-1),
        query_grad,
        key_grad,
        value_grad,
        out_grad,
        gain2_grad.reshape(-1),
        gate_grad,
        up_grad,
        down_grad,
    )


def solution(mesh):
    blk = mesh.shape["blk"]
    grid = Mesh(mesh.devices.reshape(mesh.shape["head"], blk // 4, 2, 2), AXES)
    rows, vector, whole = P(AXES, None), P(AXES), P()
    return jax.shard_map(
        functools.partial(body, blk // 4),
        mesh=grid,
        in_specs=(rows, rows, vector, rows, rows, rows, rows, vector, rows, rows, rows, whole, whole),
        out_specs=(rows, rows, vector, rows, rows, rows, rows, vector, rows, rows, rows),
        check_vma=False,
    )
```
